32 devices in a mesh: dp: 16 (over z, x, core), tensor: 2 (over y).
Axes of the slice: x: 2, y: 2, z: 4, core: 2. Of those that a mesh axis runs over, the one named last changes fastest.
Arguments:
- features: bfloat16 [512, 16, 4096], P('tensor', 'dp'), may hold values from -6 to 6
- cotangent: bfloat16 [512, 16, 4096], P('tensor', 'dp'), may hold values from -6 to 6
- embedding: bfloat16 [16, 2048], P('dp'), may hold values from -6 to 6
- context: bfloat16 [16, 260, 2048], P('dp'), may hold values from -6 to 6
- lengths: int32 [16], P('dp'), may hold values from 5 to 256, as said below
- norm1_gain: float32 [512], P('tensor'), may hold values from 0.25 to 1.75
- norm1_bias: float32 [512], P('tensor'), may hold values from -2 to 2
- conv1_weight: bfloat16 [512, 4608], P('tensor'), may hold values from -0.09375 to 0.09375
- conv1_bias: float32 [512], P('tensor'), may hold values from -2 to 2
- emb_weight: bfloat16 [2, 2048, 512], P(None, None, 'tensor'), may hold values from -0.125 to 0.125
- emb_bias: float32 [2, 512], P(None, 'tensor'), may hold values from -2 to 2
- norm2_gain: float32 [512], P('tensor'), may hold values from 0.25 to 1.75
- norm2_bias: float32 [512], P('tensor'), may hold values from -2 to 2
- conv2_weight: bfloat16 [512, 4608], P('tensor'), may hold values from -0.09375 to 0.09375
- conv2_bias: float32 [512], P('tensor'), may hold values from -2 to 2
- norm3_gain: float32 [512], P('tensor'), may hold values from 0.25 to 1.75
- norm3_bias: float32 [512], P('tensor'), may hold values from -2 to 2
- qkv_weight: bfloat16 [3, 512, 512], P(None, 'tensor'), may hold values from -0.25 to 0.25
- qkv_bias: float32 [3, 512], P(None, 'tensor'), may hold values from -2 to 2
- context_weight: bfloat16 [2, 512, 2048], P(None, 'tensor'), may hold values from -0.125 to 0.125
- context_bias: float32 [2, 512], P(None, 'tensor'), may hold values from -2 to 2
- out_weight: bfloat16 [512, 512], P('tensor'), may hold values from -2 to 2
- out_bias: float32 [512], P('tensor'), may hold values from -2 to 2
Outputs:
- output: bfloat16 [512, 16, 4096], P('tensor', 'dp')
- input_grad: float32 [512, 16, 4096], P('tensor', 'dp')
- norm1_gain_grad: float32 [512], P('tensor')
- norm1_bias_grad: float32 [512], P('tensor')
- conv1_weight_grad: float32 [512, 4608], P('tensor')
- conv1_bias_grad: float32 [512], P('tensor')
- emb_weight_grad: float32 [2, 2048, 512], P(None, None, 'tensor')
- emb_bias_grad: float32 [2, 512], P(None, 'tensor')
- norm2_gain_grad: float32 [512], P('tensor')
- norm2_bias_grad: float32 [512], P('tensor')
- conv2_weight_grad: float32 [512, 4608], P('tensor')
- conv2_bias_grad: float32 [512], P('tensor')
- norm3_gain_grad: float32 [512], P('tensor')
- norm3_bias_grad: float32 [512], P('tensor')
- qkv_weight_grad: float32 [3, 512, 512], P(None, 'tensor')
- qkv_bias_grad: float32 [3, 512], P(None, 'tensor')
- context_weight_grad: float32 [2, 512, 2048], P(None, 'tensor')
- context_bias_grad: float32 [2, 512], P(None, 'tensor')
- out_weight_grad: float32 [512, 512], P('tensor')
- out_bias_grad: float32 [512], P('tensor')
The draws below stay inside these ranges and needn't reach their ends.
Inputs may be any that keep to these rules, and one draw needn't show every extreme that they name: `lengths`: each image's number of real text tokens; some image has 256.
All inputs are finite; a program needn't handle non-finite values.
Results may differ from the reference program's by a relative error of at most 0.025.
Values may be sent and summed in bfloat16 or wider, within the bound.
No kernel may reach another device: no remote copies, remote signals or barrier semaphores. Data moves between devices by JAX's collectives and lax.ppermute only.
A program may use at most 384 MiB of HBM per device.

```python
import jax
import jax.numpy as jnp
from jax import lax

C = 512
HEAD_DIM = 64
HEADS = 8
GROUPS = 32
EMB = 2048
SIDE = 64
HW = 4096
TXT = 256
CTX = 260
IMAGES = 16


def draw_lengths(key, part):
    first_key, second_key = jax.random.split(jax.random.fold_in(key, 17))
    drawn = jax.random.randint(first_key, (IMAGES,), 5, TXT + 1)
    place = jax.random.randint(second_key, (), 0, IMAGES)
    return jnp.where(jnp.arange(IMAGES) == place, TXT, drawn).astype(jnp.int32)


def levels(own_key, dims, cuts, low, largest):
    def one(axis_at, blocks):
        heights = jax.random.uniform(jax.random.fold_in(jax.random.fold_in(own_key, 6), axis_at), (blocks,), jnp.float32, low / len(cuts), largest / len(cuts))
        return jnp.repeat(jnp.exp(heights), dims[axis_at] // blocks).reshape((-1,) + (1,) * (len(dims) - axis_at - 1))

    factor_of = one(*cuts[0])
    for cut in cuts[1:]:
        factor_of = factor_of * one(*cut)
    return factor_of


def noise(key, dims, width, bound, cuts=(), kind=jnp.bfloat16):
    values = jax.random.normal(key, dims, jnp.float32) * width
    if len(cuts) > 0:
        values = levels(key, dims, cuts, -0.22, 0.18) * values
    return jnp.clip(values, min=-bound, max=bound).astype(kind)


def setup_inputs(seed: int = 0) -> dict:
    arg_keys = jax.random.split(jax.random.key(seed), 24)
    features = noise(arg_keys[0], (C, IMAGES, HW), 1.0, 6.0, ((0, 2), (1, 16)))
    cotangent = noise(arg_keys[1], (C, IMAGES, HW), 1.0, 6.0, ((0, 2), (1, 16)))
    embedding = noise(arg_keys[2], (IMAGES, EMB), 1.0, 6.0, ((0, 16),))
    context = noise(arg_keys[3], (IMAGES, CTX, EMB), 1.0, 6.0, ((0, 16),))
    lengths = draw_lengths(jax.random.fold_in(arg_keys[23], 71), 0)
    norm1_gain = jnp.clip(1.0 + 0.15 * jax.random.normal(arg_keys[5], (C,), jnp.float32), 0.25, 1.75)
    norm1_bias = noise(arg_keys[6], (C,), 0.3, 2.0, ((0, 2),), jnp.float32)
    conv1_weight = noise(arg_keys[7], (C, 9 * C), (9 * C) ** -0.5, 0.09375, ((0, 2),))
    conv1_bias = noise(arg_keys[8], (C,), 0.3, 2.0, ((0, 2),), jnp.float32)
    emb_weight = noise(arg_keys[9], (2, EMB, C), EMB ** -0.5, 0.125, ((2, 2),))
    emb_bias = noise(arg_keys[10], (2, C), 0.3, 2.0, ((1, 2),), jnp.float32)
    norm2_gain = jnp.clip(1.0 + 0.15 * jax.random.normal(arg_keys[11], (C,), jnp.float32), 0.25, 1.75)
    norm2_bias = noise(arg_keys[12], (C,), 0.3, 2.0, ((0, 2),), jnp.float32)
    conv2_weight = noise(arg_keys[13], (C, 9 * C), (9 * C) ** -0.5, 0.09375, ((0, 2),))
    conv2_bias = noise(arg_keys[14], (C,), 0.3, 2.0, ((0, 2),), jnp.float32)
    norm3_gain = jnp.clip(1.0 + 0.15 * jax.random.normal(arg_keys[15], (C,), jnp.float32), 0.25, 1.75)
    norm3_bias = noise(arg_keys[16], (C,), 0.3, 2.0, ((0, 2),), jnp.float32)
    qkv_weight = noise(arg_keys[17], (3, C, C), C ** -0.5, 0.25, ((1, 2),))
    qkv_bias = noise(arg_keys[18], (3, C), 0.3, 2.0, ((1, 2),), jnp.float32)
    context_weight = noise(arg_keys[19], (2, C, EMB), EMB ** -0.5, 0.125, ((1, 2),))
    context_bias = noise(arg_keys[20], (2, C), 0.3, 2.0, ((1, 2),), jnp.float32)
    out_weight = noise(arg_keys[21], (C, C), (max(C // 64, 4)) ** -0.5, 2.0, ((0, 2),))
    out_bias = noise(arg_keys[22], (C,), 0.3, 2.0, ((0, 2),), jnp.float32)
    return dict(features=features, cotangent=cotangent, embedding=embedding, context=context, lengths=lengths, norm1_gain=norm1_gain, norm1_bias=norm1_bias, conv1_weight=conv1_weight, conv1_bias=conv1_bias, emb_weight=emb_weight, emb_bias=emb_bias, norm2_gain=norm2_gain, norm2_bias=norm2_bias, conv2_weight=conv2_weight, conv2_bias=conv2_bias, norm3_gain=norm3_gain, norm3_bias=norm3_bias, qkv_weight=qkv_weight, qkv_bias=qkv_bias, context_weight=context_weight, context_bias=context_bias, out_weight=out_weight, out_bias=out_bias)


@jax.custom_vjp
def low(v):
    return lax.optimization_barrier(v.astype(jnp.bfloat16)).astype(jnp.float32)

@jax.custom_vjp
def low_back(v):
    return v

def low_keep(v):
    return (low(v), None)

def low_pass(kept, grad):
    return (grad,)

def back_keep(v):
    return (v, None)

def back_low(kept, grad):
    return (low(grad),)
low.defvjp(low_keep, low_pass)
low_back.defvjp(back_keep, back_low)
PRECISE = lax.Precision.HIGHEST
EPSILON = 1e-05
NEG_FILL = -1e+30

def group_norm(values, gain_vec, bias_vec):
    per_group = C // GROUPS
    grouped = values.reshape(GROUPS, per_group, HW)
    group_mean = lax.optimization_barrier(jnp.mean(grouped, axis=(1, 2), keepdims=True))
    group_var = lax.optimization_barrier(jnp.mean(jnp.square(grouped - group_mean), axis=(1, 2), keepdims=True))
    normal_vals = ((grouped - group_mean) * lax.rsqrt(group_var + EPSILON)).reshape(C, HW)
    return normal_vals * gain_vec[:, None] + bias_vec[:, None]

def shifted(values, kernel_tap):
    row_off, col_off = (kernel_tap // 3, kernel_tap % 3)
    channels = values.shape[0]
    padded = jnp.pad(values.reshape(channels, SIDE, SIDE), ((0, 0), (1, 1), (1, 1)))
    return padded[:, row_off:row_off + SIDE, col_off:col_off + SIDE].reshape(channels, HW)

def convolve(values, weight, bias_vec):
    kernel = weight.reshape(C, 9, C)
    result = jnp.zeros((C, HW), jnp.float32) + bias_vec[:, None]
    for kernel_tap in range(9):
        result = result + jnp.dot(kernel[:, kernel_tap], shifted(values, kernel_tap), precision=PRECISE, preferred_element_type=jnp.float32)
    return result

def attend(queries, key_rows, value_rows, key_valid):
    block_len = min(512, HW)
    blocks_q = queries.reshape(HEADS, HEAD_DIM, HW // block_len, block_len).transpose(2, 0, 1, 3)
    head_keys = key_rows.reshape(HEADS, HEAD_DIM, -1)
    head_values = value_rows.reshape(HEADS, HEAD_DIM, -1)
    scale_val = HEAD_DIM ** (-0.5)

    def one_block(q_block):
        scores = low_back(jnp.einsum('hdi,hdj->hij', q_block, head_keys, precision=PRECISE) * scale_val)
        scores = jnp.where(key_valid[None, None, :], scores, NEG_FILL)
        row_top = lax.optimization_barrier(jnp.max(scores, axis=-1, keepdims=True))
        raised = jnp.exp(scores - row_top)
        probs_low = low(raised / lax.optimization_barrier(jnp.sum(raised, axis=-1, keepdims=True)))
        return jnp.einsum('hdj,hij->hdi', head_values, probs_low, precision=PRECISE)
    result = lax.map(jax.checkpoint(one_block), blocks_q)
    return result.transpose(1, 2, 0, 3).reshape(C, HW)

def forward(image, params, emb_row, context_rows, length_val):
    gain_one, shift_one, kernel_one, bias_one, emb_proj, emb_shift, gain_two, shift_two, kernel_two, bias_two, gain_three, shift_three, qkv_proj, qkv_shift, ctx_proj, ctx_shift, out_proj, out_shift = params
    act_one = low(jax.nn.silu(group_norm(image, gain_one, shift_one)))
    conv_one = low_back(convolve(act_one, kernel_one, bias_one))
    emb_act = low(jax.nn.silu(emb_row))
    scale_shift = low_back(jnp.einsum('e,teo->to', emb_act, emb_proj, precision=PRECISE) + emb_shift)
    mid = group_norm(conv_one, gain_two, shift_two) * (1.0 + scale_shift[0][:, None]) + scale_shift[1][:, None]
    act_two = low(jax.nn.silu(mid))
    hidden = image + low_back(convolve(act_two, kernel_two, bias_two))
    normed = low(group_norm(hidden, gain_three, shift_three))
    qkv = low(low_back(jnp.einsum('toc,cp->top', qkv_proj, normed, precision=PRECISE) + qkv_shift[:, :, None]))
    ctx_kv = low(low_back(jnp.einsum('toe,ne->ton', ctx_proj, context_rows, precision=PRECISE) + ctx_shift[:, :, None]))
    key_rows = jnp.concatenate([qkv[1], ctx_kv[0]], axis=1)
    value_rows = jnp.concatenate([qkv[2], ctx_kv[1]], axis=1)
    key_valid = jnp.arange(HW + CTX) < HW + 4 + length_val
    heads_out = low(low_back(attend(qkv[0], key_rows, value_rows, key_valid)))
    return hidden + jnp.dot(out_proj, heads_out, precision=PRECISE, preferred_element_type=jnp.float32) + out_shift[:, None]

def reference(features, cotangent, embedding, context, lengths, norm1_gain, norm1_bias, conv1_weight, conv1_bias, emb_weight, emb_bias, norm2_gain, norm2_bias, conv2_weight, conv2_bias, norm3_gain, norm3_bias, qkv_weight, qkv_bias, context_weight, context_bias, out_weight, out_bias):
    params = tuple((item_val.astype(jnp.float32) for item_val in (norm1_gain, norm1_bias, conv1_weight, conv1_bias, emb_weight, emb_bias, norm2_gain, norm2_bias, conv2_weight, conv2_bias, norm3_gain, norm3_bias, qkv_weight, qkv_bias, context_weight, context_bias, out_weight, out_bias)))
    images = jnp.moveaxis(features.astype(jnp.float32), 1, 0)
    grad_images = jnp.moveaxis(cotangent.astype(jnp.float32), 1, 0)

    def per_image(totals, packed):
        image, grad_image, emb_row, context_rows, length_val = packed

        def run(value_in, param_in):
            return forward(value_in, param_in, emb_row, context_rows, length_val)
        result, pull_back = jax.vjp(run, image, params)
        grad_in, grad_params = pull_back(grad_image)
        totals = jax.tree.map(lambda left, right: left + right, totals, grad_params)
        return (totals, (result.astype(jnp.bfloat16), grad_in))
    start_vals = jax.tree.map(jnp.zeros_like, params)
    totals, (results, grads_in) = lax.scan(per_image, start_vals, (images, grad_images, embedding.astype(jnp.float32), context.astype(jnp.float32), lengths))
    output = jnp.moveaxis(results, 0, 1)
    input_grad = jnp.moveaxis(grads_in, 0, 1)
    return (output, input_grad, totals[0], totals[1], totals[2], totals[3], totals[4], totals[5], totals[6], totals[7], totals[8], totals[9], totals[10], totals[11], totals[12], totals[13], totals[14], totals[15], totals[16], totals[17])
```

```python
import functools

import jax
import jax.numpy as jnp
from jax import lax
from jax.experimental import pallas as pl
from jax.experimental.pallas import tpu as pltpu
from jax.sharding import PartitionSpec as P

C = 512
HEAD_DIM = 64
GROUPS = 32
SIDE = 64
HW = 4096
CTX = 260


EPSILON = 1e-05
NEG_FILL = -1e30


def group_norm(values, gain_vec, bias_vec):
    channels, images, pixels = values.shape
    per_group = C // GROUPS
    grouped = values.reshape(channels // per_group, per_group, images, pixels)
    group_mean = jnp.mean(grouped, axis=(1, 3), keepdims=True)
    group_var = jnp.mean(jnp.square(grouped - group_mean), axis=(1, 3), keepdims=True)
    normal_vals = ((grouped - group_mean) * lax.rsqrt(group_var + EPSILON)).reshape(values.shape)
    return normal_vals * gain_vec[:, None, None] + bias_vec[:, None, None]


def shifted(values, kernel_tap):
    row_off, col_off = (kernel_tap // 3, kernel_tap % 3)
    channels, images, pixels = values.shape
    padded = jnp.pad(values.reshape(channels, images, SIDE, SIDE), ((0, 0), (0, 0), (1, 1), (1, 1)))
    return padded[:, :, row_off : row_off + SIDE, col_off : col_off + SIDE].reshape(
        channels, images, pixels
    )


def convolve(full_act, weight, bias_vec):
    kernel = weight.reshape(weight.shape[0], 9, C)
    result = (
        jnp.zeros((weight.shape[0],) + full_act.shape[1:], jnp.float32) + bias_vec[:, None, None]
    )
    for kernel_tap in range(9):
        result = result + jnp.einsum(
            "oc,cip->oip",
            kernel[:, kernel_tap],
            shifted(full_act, kernel_tap),
            preferred_element_type=jnp.float32,
        )
    return result


def kernel_grad(grad_low, full_act):
    pieces = [
        jnp.einsum(
            "oip,cip->oc",
            grad_low,
            shifted(full_act, kernel_tap),
            preferred_element_type=jnp.float32,
        )
        for kernel_tap in range(9)
    ]
    return jnp.stack(pieces, axis=1).reshape(grad_low.shape[0], 9 * C)


def conv_input_grad(grad_low, weight):
    channels = grad_low.shape[0]
    kernel = weight.reshape(channels, 9, C)
    moved_grads = [shifted(grad_low, 8 - kernel_tap) for kernel_tap in range(9)]
    result = jnp.zeros((lax.axis_size("tensor") * channels,) + grad_low.shape[1:], jnp.float32)
    for kernel_tap in range(9):
        cols_part = kernel[:, kernel_tap]
        result = result + jnp.einsum(
            "oc,oip->cip", cols_part, moved_grads[kernel_tap], preferred_element_type=jnp.float32
        )
    return lax.psum_scatter(
        result.astype(jnp.bfloat16), "tensor", scatter_dimension=0, tiled=True
    ).astype(jnp.float32)


def to_heads(values):
    channels, images, length_n = values.shape
    return (
        values.reshape(channels // HEAD_DIM, HEAD_DIM, images, length_n)
        .transpose(2, 0, 1, 3)
        .reshape(-1, HEAD_DIM, length_n)
    )


def from_heads(values, images):
    groups_n, head_dims, length_n = values.shape
    heads_here = groups_n // images
    return (
        values.reshape(images, heads_here, head_dims, length_n)
        .transpose(1, 2, 0, 3)
        .reshape(heads_here * head_dims, images, length_n)
    )


CTXP = 384
KP = HW + CTXP


def chunks(ck):
    out=[(c,ck,False) for c in range(0,HW,ck)]
    out.append((HW,CTXP,True))
    return out

def attn_kernel(lim_ref,q_ref,k_ref,v_ref,g_ref,o_ref,dq_ref,dk_ref,dv_ref,kt,vt,s_sc,p_sc,dka,dva,*,ck):
    i=pl.program_id(1); n=pl.num_programs(1)
    bq=q_ref.shape[2]
    @pl.when(i==0)
    def _():
        kt[...]=k_ref[0].astype(jnp.float32).T.astype(jnp.bfloat16)
        vt[...]=v_ref[0].astype(jnp.float32).T.astype(jnp.bfloat16)
        dka[...]=jnp.zeros_like(dka); dva[...]=jnp.zeros_like(dva)
    scale=HEAD_DIM**-0.5
    q=(q_ref[0].astype(jnp.float32)*scale).astype(jnp.bfloat16)
    g=g_ref[0]
    f32=jnp.float32
    lim=lim_ref[0]
    m=jnp.full((8,bq),-jnp.inf,f32)
    for c,w,masked in chunks(ck):
        s=jnp.dot(kt[c:c+w,:],q,preferred_element_type=f32)
        if masked:
            row=lax.broadcasted_iota(jnp.int32,(w,bq),0)
            s=jnp.where(row<lim,s,-1e30)
        s_sc[c:c+w,:]=s
        m=jnp.maximum(m,jnp.max(s.reshape(w//8,8,bq),axis=0))
    mm=jnp.max(m,axis=0,keepdims=True)
    l=jnp.zeros((8,bq),f32)
    o=jnp.zeros((HEAD_DIM,bq),f32)
    for c,w,_ in chunks(ck):
        p=jnp.exp(s_sc[c:c+w,:]-mm)
        l=l+jnp.sum(p.reshape(w//8,8,bq),axis=0)
        pb=p.astype(jnp.bfloat16)
        p_sc[c:c+w,:]=pb
        o=o+jnp.dot(v_ref[0,:,c:c+w],pb,preferred_element_type=f32)
    inv=1.0/jnp.sum(l,axis=0,keepdims=True)
    o=o*inv
    o_ref[0]=o.astype(jnp.bfloat16)
    gf=g.astype(f32)
    delta=jnp.sum(gf*o,axis=0,keepdims=True)*inv
    gs=(gf*inv).astype(jnp.bfloat16)
    dq=jnp.zeros((HEAD_DIM,bq),f32)
    nt=(((1,),(1,)),((),()))
    for c,w,_ in chunks(ck):
        dp=jnp.dot(vt[c:c+w,:],gs,preferred_element_type=f32)
        pb=p_sc[c:c+w,:]
        ds=(dp-delta).astype(jnp.bfloat16)*pb
        dq=dq+jnp.dot(k_ref[0,:,c:c+w],ds,preferred_element_type=f32)
        dka[:,c:c+w]+=lax.dot_general(q,ds,nt,preferred_element_type=f32)
        dva[:,c:c+w]+=lax.dot_general(gs,pb,nt,preferred_element_type=f32)
    dq_ref[0]=(dq*scale).astype(jnp.bfloat16)
    @pl.when(i==n-1)
    def _():
        dk_ref[0]=dka[...].astype(jnp.bfloat16)
        dv_ref[0]=dva[...].astype(jnp.bfloat16)

def attention(lim,q,k,v,g,bq=1024, ck=512):
    H=q.shape[0]
    bs=lambda w,im: pl.BlockSpec((1,HEAD_DIM,w),im)
    qm=lambda h,i:(h,0,i); km=lambda h,i:(h,0,0)
    sd=jax.ShapeDtypeStruct
    fl=6*2*H*HW*KP*HEAD_DIM
    return pl.pallas_call(functools.partial(attn_kernel,ck=ck),
        grid=(H,HW//bq),
        in_specs=[pl.BlockSpec(memory_space=pltpu.SMEM),bs(bq,qm),bs(KP,km),bs(KP,km),bs(bq,qm)],
        out_specs=[bs(bq,qm),bs(bq,qm),bs(KP,km),bs(KP,km)],
        out_shape=[sd((H,HEAD_DIM,HW),jnp.bfloat16)]*2+[sd((H,HEAD_DIM,KP),jnp.bfloat16)]*2,
        scratch_shapes=[pltpu.VMEM((KP,HEAD_DIM),jnp.bfloat16)]*2+[pltpu.VMEM((KP,bq),jnp.float32),pltpu.VMEM((KP,bq),jnp.bfloat16)]+[pltpu.VMEM((HEAD_DIM,KP),jnp.float32)]*2,
        compiler_params=pltpu.CompilerParams(vmem_limit_bytes=60<<20,dimension_semantics=("arbitrary","arbitrary")),
        cost_estimate=pl.CostEstimate(flops=fl,transcendentals=H*HW*KP,bytes_accessed=H*64*(4*HW+4*KP)*2),
    )(lim,q,k,v,g)


def first_section(values, gain_vec, bias_vec):
    return jax.nn.silu(group_norm(values, gain_vec, bias_vec))


def second_section(values, gain_vec, bias_vec, modulation):
    normal_vals = group_norm(values, gain_vec, bias_vec)
    return jax.nn.silu(normal_vals * (1.0 + modulation[0][:, :, None]) + modulation[1][:, :, None])


def local(
    features,
    cotangent,
    embedding,
    context,
    lengths,
    norm1_gain,
    norm1_bias,
    conv1_weight,
    conv1_bias,
    emb_weight,
    emb_bias,
    norm2_gain,
    norm2_bias,
    conv2_weight,
    conv2_bias,
    norm3_gain,
    norm3_bias,
    qkv_weight,
    qkv_bias,
    context_weight,
    context_bias,
    out_weight,
    out_bias,
):
    channels, images, pixels = features.shape
    feat_f32 = features.astype(jnp.float32)
    act_one = first_section(feat_f32, norm1_gain, norm1_bias).astype(jnp.bfloat16)
    full_one = lax.all_gather(act_one, "tensor", axis=0, tiled=True)
    conv_one = convolve(full_one, conv1_weight, conv1_bias)
    emb_act = jax.nn.silu(embedding.astype(jnp.float32)).astype(jnp.bfloat16)
    scale_shift = (
        jnp.einsum("ie,teo->toi", emb_act, emb_weight, preferred_element_type=jnp.float32)
        + emb_bias[:, :, None]
    )
    act_two = second_section(conv_one, norm2_gain, norm2_bias, scale_shift).astype(jnp.bfloat16)
    full_two = lax.all_gather(act_two, "tensor", axis=0, tiled=True)
    hidden = feat_f32 + convolve(full_two, conv2_weight, conv2_bias)
    normed = group_norm(hidden, norm3_gain, norm3_bias).astype(jnp.bfloat16)
    full_three = lax.all_gather(normed, "tensor", axis=0, tiled=True)
    qkv_low = (
        jnp.einsum("toc,cip->toip", qkv_weight, full_three, preferred_element_type=jnp.float32)
        + qkv_bias[:, :, None, None]
    ).astype(jnp.bfloat16)
    ctx_low = (
        jnp.einsum("toe,ine->toin", context_weight, context, preferred_element_type=jnp.float32)
        + context_bias[:, :, None, None]
    ).astype(jnp.bfloat16)
    queries = to_heads(qkv_low[0])
    pad = ((0, 0), (0, 0), (0, CTXP - CTX))
    key_rows = jnp.concatenate([to_heads(qkv_low[1]), jnp.pad(to_heads(ctx_low[0]), pad)], axis=2)
    value_rows = jnp.concatenate([to_heads(qkv_low[2]), jnp.pad(to_heads(ctx_low[1]), pad)], axis=2)
    grad_heads = lax.psum_scatter(
        jnp.einsum("oc,oip->cip", out_weight, cotangent, preferred_element_type=jnp.float32).astype(
            jnp.bfloat16
        ),
        "tensor",
        scatter_dimension=0,
        tiled=True,
    )
    heads_mixed, query_grad, key_grad, value_grad = attention(
        4 + lengths, queries, key_rows, value_rows, to_heads(grad_heads)
    )
    heads_out = from_heads(heads_mixed, images)
    full_heads = lax.all_gather(heads_out, "tensor", axis=0, tiled=True)
    output = (
        hidden
        + jnp.einsum("oc,cip->oip", out_weight, full_heads, preferred_element_type=jnp.float32)
        + out_bias[:, None, None]
    ).astype(jnp.bfloat16)
    grad_top = cotangent.astype(jnp.float32)
    out_weight_grad = jnp.einsum(
        "oip,cip->oc", cotangent, full_heads, preferred_element_type=jnp.float32
    )
    out_bias_grad = jnp.sum(grad_top, axis=(1, 2))
    grad_qkv = jnp.stack(
        [
            from_heads(query_grad, images),
            from_heads(key_grad[:, :, :HW], images),
            from_heads(value_grad[:, :, :HW], images),
        ]
    ).astype(jnp.bfloat16)
    grad_ctx = jnp.stack(
        [from_heads(key_grad[:, :, HW : HW + CTX], images), from_heads(value_grad[:, :, HW : HW + CTX], images)]
    ).astype(jnp.bfloat16)
    qkv_weight_grad = jnp.einsum(
        "toip,cip->toc", grad_qkv, full_three, preferred_element_type=jnp.float32
    )
    qkv_bias_grad = jnp.sum(grad_qkv.astype(jnp.float32), axis=(2, 3))
    context_weight_grad = jnp.einsum(
        "toin,ine->toe", grad_ctx, context, preferred_element_type=jnp.float32
    )
    context_bias_grad = jnp.sum(grad_ctx.astype(jnp.float32), axis=(2, 3))
    cols_part = qkv_weight
    grad_normed = lax.psum_scatter(
        jnp.einsum("toc,toip->cip", cols_part, grad_qkv, preferred_element_type=jnp.float32).astype(
            jnp.bfloat16
        ),
        "tensor",
        scatter_dimension=0,
        tiled=True,
    ).astype(jnp.float32)
    unused_three, pull_three = jax.vjp(group_norm, hidden, norm3_gain, norm3_bias)
    grad_branch, norm3_gain_grad, norm3_bias_grad = pull_three(grad_normed)
    grad_hidden = grad_top + grad_branch
    attention_grads = (
        lax.psum(out_weight_grad.astype(jnp.bfloat16), "dp").astype(jnp.float32),
        lax.psum(out_bias_grad.astype(jnp.bfloat16), "dp").astype(jnp.float32),
        lax.psum(qkv_weight_grad.astype(jnp.bfloat16), "dp").astype(jnp.float32),
        lax.psum(qkv_bias_grad.astype(jnp.bfloat16), "dp").astype(jnp.float32),
        lax.psum(context_weight_grad.astype(jnp.bfloat16), "dp").astype(jnp.float32),
        lax.psum(context_bias_grad.astype(jnp.bfloat16), "dp").astype(jnp.float32),
        lax.psum(norm3_gain_grad.astype(jnp.bfloat16), "dp").astype(jnp.float32),
        lax.psum(norm3_bias_grad.astype(jnp.bfloat16), "dp").astype(jnp.float32),
    )
    grad_conv_two = grad_hidden.astype(jnp.bfloat16)
    conv2_bias_grad = jnp.sum(grad_conv_two.astype(jnp.float32), axis=(1, 2))
    conv2_weight_grad = kernel_grad(grad_conv_two, full_two)
    grad_act_two = conv_input_grad(grad_conv_two, conv2_weight)
    unused_two, pull_two = jax.vjp(second_section, conv_one, norm2_gain, norm2_bias, scale_shift)
    grad_conv_one, norm2_gain_grad, norm2_bias_grad, grad_modulation = pull_two(grad_act_two)
    grad_mod_low = grad_modulation.astype(jnp.bfloat16)
    emb_weight_grad = jnp.einsum(
        "ie,toi->teo", emb_act, grad_mod_low, preferred_element_type=jnp.float32
    )
    emb_bias_grad = jnp.sum(grad_mod_low.astype(jnp.float32), axis=2)
    grad_conv_low = grad_conv_one.astype(jnp.bfloat16)
    conv1_bias_grad = jnp.sum(grad_conv_low.astype(jnp.float32), axis=(1, 2))
    conv1_weight_grad = kernel_grad(grad_conv_low, full_one)
    grad_act_one = conv_input_grad(grad_conv_low, conv1_weight)
    unused_one, pull_one = jax.vjp(first_section, feat_f32, norm1_gain, norm1_bias)
    grad_feat, norm1_gain_grad, norm1_bias_grad = pull_one(grad_act_one)
    input_grad = grad_hidden + grad_feat
    residual_grads = (
        lax.psum(norm1_gain_grad.astype(jnp.bfloat16), "dp").astype(jnp.float32),
        lax.psum(norm1_bias_grad.astype(jnp.bfloat16), "dp").astype(jnp.float32),
        lax.psum(conv1_weight_grad.astype(jnp.bfloat16), "dp").astype(jnp.float32),
        lax.psum(conv1_bias_grad.astype(jnp.bfloat16), "dp").astype(jnp.float32),
        lax.psum(emb_weight_grad.astype(jnp.bfloat16), "dp").astype(jnp.float32),
        lax.psum(emb_bias_grad.astype(jnp.bfloat16), "dp").astype(jnp.float32),
        lax.psum(norm2_gain_grad.astype(jnp.bfloat16), "dp").astype(jnp.float32),
        lax.psum(norm2_bias_grad.astype(jnp.bfloat16), "dp").astype(jnp.float32),
        lax.psum(conv2_weight_grad.astype(jnp.bfloat16), "dp").astype(jnp.float32),
        lax.psum(conv2_bias_grad.astype(jnp.bfloat16), "dp").astype(jnp.float32),
    )
    return (
        output,
        input_grad,
        residual_grads[0],
        residual_grads[1],
        residual_grads[2],
        residual_grads[3],
        residual_grads[4],
        residual_grads[5],
        residual_grads[6],
        residual_grads[7],
        residual_grads[8],
        residual_grads[9],
        attention_grads[6],
        attention_grads[7],
        attention_grads[2],
        attention_grads[3],
        attention_grads[4],
        attention_grads[5],
        attention_grads[0],
        attention_grads[1],
    )


def solution(mesh):
    placed = (
        P("tensor", "dp", None),
        P("tensor", "dp", None),
        P("dp", None),
        P("dp", None, None),
        P("dp"),
        P("tensor"),
        P("tensor"),
        P("tensor", None),
        P("tensor"),
        P(None, None, "tensor"),
        P(None, "tensor"),
        P("tensor"),
        P("tensor"),
        P("tensor", None),
        P("tensor"),
        P("tensor"),
        P("tensor"),
        P(None, "tensor", None),
        P(None, "tensor"),
        P(None, "tensor", None),
        P(None, "tensor"),
        P("tensor", None),
        P("tensor"),
    )
    return jax.shard_map(
        local,
        mesh=mesh,
        in_specs=placed,
        out_specs=(
            P("tensor", "dp", None),
            P("tensor", "dp", None),
            P("tensor"),
            P("tensor"),
            P("tensor", None),
            P("tensor"),
            P(None, None, "tensor"),
            P(None, "tensor"),
            P("tensor"),
            P("tensor"),
            P("tensor", None),
            P("tensor"),
            P("tensor"),
            P("tensor"),
            P(None, "tensor", None),
            P(None, "tensor"),
            P(None, "tensor", None),
            P(None, "tensor"),
            P("tensor", None),
            P("tensor"),
        ),
        check_vma=False,
    )
```

```python
import functools

import jax
import jax.numpy as jnp
from jax import lax
from jax.experimental import pallas as pl
from jax.experimental.pallas import tpu as pltpu
from jax.sharding import PartitionSpec as P

C = 512
HEAD_DIM = 64
PER_GROUP = 16
SIDE = 64
HW = 4096
CTX = 260
CTXP = 384
PAD = 128
EPSILON = 1e-05
NEG_FILL = -1e30
F32 = jnp.float32
BF = jnp.bfloat16
NT = (((1,), (1,)), ((), ()))
VMEM_BYTES = 62 << 20


def dot(a, b):
    return jnp.dot(a, b, preferred_element_type=F32)


def dot_nt(a, b):
    return lax.dot_general(a, b, NT, preferred_element_type=F32)


def whole():
    return pl.BlockSpec(memory_space=pltpu.VMEM)


def params(**kwargs):
    return pltpu.CompilerParams(vmem_limit_bytes=VMEM_BYTES, **kwargs)


def cost(flops, nbytes, transcendentals=0):
    return pl.CostEstimate(flops=flops, bytes_accessed=nbytes, transcendentals=transcendentals)


def struct(shape, dtype):
    return jax.ShapeDtypeStruct(shape, dtype)


def group_scalar(column):
    return jnp.sum(column, axis=0, keepdims=True) * (1.0 / (PER_GROUP * HW))


def group_stats(vals):
    mean = group_scalar(jnp.sum(vals, axis=1, keepdims=True))
    centred = vals - mean
    var = group_scalar(jnp.sum(centred * centred, axis=1, keepdims=True))
    rstd = lax.rsqrt(var + EPSILON)
    return mean, rstd


def norm_backward(dy_sum, dyx_sum, gain):
    return group_scalar(dy_sum * gain), group_scalar(dyx_sum * gain)


def for_groups(channels, body):
    def step(g, carry):
        body(pl.ds(pl.multiple_of(g * PER_GROUP, PER_GROUP), PER_GROUP))
        return carry

    lax.fori_loop(0, channels // PER_GROUP, step, 0)


def columns(values):
    lane = lax.broadcasted_iota(jnp.int32, (PER_GROUP, 128), 1)
    tile = jnp.zeros((PER_GROUP, 128), F32)
    for at, val in enumerate(values):
        tile = jnp.where(lane == at, val, tile)
    return tile


def act_one_kernel(x_ref, par_ref, act_ref, stat_ref):
    def body(rows):
        vals = x_ref[rows, :].astype(F32)
        mean, rstd = group_stats(vals)
        par = par_ref[rows, :]
        out = (vals - mean) * rstd * par[:, 0:1] + par[:, 1:2]
        act_ref[rows, :] = (out * jax.nn.sigmoid(out)).astype(BF)
        stat_ref[rows, :] = columns([mean, rstd])

    for_groups(x_ref.shape[0], body)


def first_activation(x, par):
    ch = x.shape[0]
    return pl.pallas_call(
        act_one_kernel,
        out_shape=[struct((ch, HW), BF), struct((ch, 128), F32)],
        in_specs=[whole()] * 2,
        out_specs=[whole()] * 2,
        compiler_params=params(),
        cost_estimate=cost(20 * ch * HW, 4 * ch * HW, ch * HW),
    )(x, par)


def fill_shifted(xs, pieces):
    row = 0
    for x_ref in pieces:
        rows = x_ref.shape[0]
        for r in range(0, rows, 64):
            x = x_ref[r : r + 64, :].astype(F32)
            col = lax.broadcasted_iota(jnp.int32, x.shape, 1) % SIDE
            zero = jnp.zeros_like(x)
            at = slice(row + r, row + r + 64)
            for d in range(3):
                if d == 0:
                    y = jnp.where(col == 0, zero, pltpu.roll(x, 1, 1))
                elif d == 1:
                    y = x
                else:
                    y = jnp.where(col == SIDE - 1, zero, pltpu.roll(x, HW - 1, 1))
                xs[2 * d, at, PAD : PAD + HW] = y.astype(BF)
                turned = pltpu.roll(y, 64, 1)
                lane = lax.broadcasted_iota(jnp.int32, x.shape, 1)
                xs[2 * d + 1, at, PAD : PAD + HW] = jnp.where(lane < 64, zero, turned).astype(BF)
                tail = turned[:, :128]
                xs[2 * d + 1, at, PAD + HW :] = jnp.where(
                    lane[:, :128] < 64, tail, jnp.zeros_like(tail)
                ).astype(BF)
        row += rows
    edge = jnp.zeros((xs.shape[1], PAD), BF)
    for d in range(3):
        xs[2 * d, :, :PAD] = edge
        xs[2 * d, :, PAD + HW :] = edge
        xs[2 * d + 1, :, :PAD] = edge


def window(xs, tap, start, width):
    row_off, col_off = tap // 3, tap % 3
    off = (row_off - 1) * SIDE
    if off == 0:
        return xs[2 * col_off, :, PAD + start : PAD + start + width]
    first = PAD + start + off + 64
    return xs[2 * col_off + 1, :, first : first + width]


def convolve(xs, w_ref, out_ref, add, width=1024):
    depth = xs.shape[1]
    for p in range(0, HW, width):
        acc = dot(w_ref[:, :depth], window(xs, 0, p, width))
        for tap in range(1, 9):
            acc = acc + dot(w_ref[:, tap * depth : (tap + 1) * depth], window(xs, tap, p, width))
        out_ref[:, p : p + width] = add(acc, slice(p, p + width))


def conv_call(kernel, weight, pieces, others, outs, scratch, name):
    out_ch, depth = weight.shape[0], C
    nbytes = weight.size * 2 + sum(a.size * a.dtype.itemsize for a in tuple(pieces) + tuple(others))
    return pl.pallas_call(
        functools.partial(kernel, len(pieces)),
        out_shape=outs,
        in_specs=[whole()] * (1 + len(pieces) + len(others)),
        out_specs=[whole()] * len(outs),
        scratch_shapes=[pltpu.VMEM((6, depth, HW + 2 * PAD), BF)] + scratch,
        compiler_params=params(),
        cost_estimate=cost(2 * out_ch * 9 * depth * HW, nbytes, out_ch * HW),
        name=name,
    )(weight, *pieces, *others)


def conv_one_kernel(n, w_ref, *refs):
    pieces, (par_ref, conv_ref, act_ref, stat_ref, xs) = refs[:n], refs[n:]
    fill_shifted(xs, pieces)
    bias = par_ref[:, 0:1]
    convolve(xs, w_ref, conv_ref, lambda acc, at: acc + bias)

    def body(rows):
        vals = conv_ref[rows, :]
        mean, rstd = group_stats(vals)
        par = par_ref[rows, :]
        normal = (vals - mean) * rstd * par[:, 1:2] + par[:, 2:3]
        mid = normal * (1.0 + par[:, 3:4]) + par[:, 4:5]
        act_ref[rows, :] = (mid * jax.nn.sigmoid(mid)).astype(BF)
        stat_ref[rows, :] = columns([mean, rstd])

    for_groups(conv_ref.shape[0], body)


def conv_two_kernel(n, w_ref, *refs):
    pieces, (par_ref, feat_ref, hidden_ref, normed_ref, stat_ref, xs) = refs[:n], refs[n:]
    fill_shifted(xs, pieces)
    bias = par_ref[:, 0:1]
    convolve(xs, w_ref, hidden_ref, lambda acc, at: acc + bias + feat_ref[:, at].astype(F32))

    def body(rows):
        vals = hidden_ref[rows, :]
        mean, rstd = group_stats(vals)
        par = par_ref[rows, :]
        normed_ref[rows, :] = ((vals - mean) * rstd * par[:, 1:2] + par[:, 2:3]).astype(BF)
        stat_ref[rows, :] = columns([mean, rstd])

    for_groups(hidden_ref.shape[0], body)


def silu_slope(mid):
    sig = jax.nn.sigmoid(mid)
    return sig * (1.0 + mid * (1.0 - sig))


def conv_two_back_kernel(n, w_ref, *refs):
    pieces, (par_ref, conv_ref, stat_ref, grad_ref, sums_ref, xs, acc_ref) = refs[:n], refs[n:]
    fill_shifted(xs, pieces)
    convolve(xs, w_ref, acc_ref, lambda acc, at: acc)

    def body(rows):
        par, stat = par_ref[rows, :], stat_ref[rows, :]
        gain, shift, factor = par[:, 1:2], par[:, 2:3], 1.0 + par[:, 3:4]
        rstd = stat[:, 1:2]
        hat = (conv_ref[rows, :] - stat[:, 0:1]) * rstd
        mid = (hat * gain + shift) * factor + par[:, 4:5]
        grad = acc_ref[rows, :] * silu_slope(mid)
        total = jnp.sum(grad, axis=1, keepdims=True)
        total_hat = jnp.sum(grad * hat, axis=1, keepdims=True)
        mean_u, mean_uhat = norm_backward(total * factor, total_hat * factor, gain)
        out = ((grad * (factor * gain) - mean_u - hat * mean_uhat) * rstd).astype(BF)
        grad_ref[rows, :] = out
        bias_grad = jnp.sum(out.astype(F32), axis=1, keepdims=True)
        sums_ref[rows, :] = columns(
            [
                total_hat * factor,
                total * factor,
                total_hat * gain + total * shift,
                total,
                bias_grad,
            ]
        )

    for_groups(acc_ref.shape[0], body)


def conv_one_back_kernel(n, w_ref, *refs):
    pieces, (par_ref, feat_ref, stat_ref, hid_ref, grad_ref, sums_ref, xs, acc_ref) = (
        refs[:n],
        refs[n:],
    )
    fill_shifted(xs, pieces)
    convolve(xs, w_ref, acc_ref, lambda acc, at: acc)

    def body(rows):
        par, stat = par_ref[rows, :], stat_ref[rows, :]
        gain, shift = par[:, 0:1], par[:, 1:2]
        rstd = stat[:, 1:2]
        hat = (feat_ref[rows, :].astype(F32) - stat[:, 0:1]) * rstd
        grad = acc_ref[rows, :] * silu_slope(hat * gain + shift)
        total = jnp.sum(grad, axis=1, keepdims=True)
        total_hat = jnp.sum(grad * hat, axis=1, keepdims=True)
        mean_u, mean_uhat = norm_backward(total, total_hat, gain)
        out = hid_ref[rows, :] + (grad * gain - mean_u - hat * mean_uhat) * rstd
        grad_ref[rows, :] = out.astype(grad_ref.dtype)
        sums_ref[rows, :] = columns([total_hat, total])

    for_groups(acc_ref.shape[0], body)


def weight_grad_kernel(n, grad_ref, *refs):
    pieces, (out_ref, gs) = refs[:n], refs[n:]
    fill_shifted(gs, (grad_ref,))
    for tap in range(9):
        moved = window(gs, 8 - tap, 0, HW)
        at = tap * C
        for x_ref in pieces:
            rows = x_ref.shape[0]
            out_ref[:, at : at + rows] = dot_nt(moved, x_ref[...]).astype(BF)
            at += rows


def conv_weight_grad(grad, pieces, name):
    out_ch = grad.shape[0]
    return pl.pallas_call(
        functools.partial(weight_grad_kernel, len(pieces)),
        out_shape=struct((out_ch, 9 * C), BF),
        in_specs=[whole()] * (1 + len(pieces)),
        out_specs=whole(),
        scratch_shapes=[pltpu.VMEM((6, out_ch, HW + 2 * PAD), BF)],
        compiler_params=params(),
        cost_estimate=cost(2 * out_ch * 9 * C * HW, (out_ch + C) * HW * 2 + out_ch * 9 * C * 2),
        name=name,
    )(grad, *pieces)


def norm_three_back_kernel(n, *refs):
    addends, (hidden_ref, stat_ref, par_ref, cot_ref, hid_ref, grad_ref, sums_ref) = (
        refs[:n],
        refs[n:],
    )

    def body(rows):
        dy = addends[0][rows, :].astype(F32)
        for extra in addends[1:]:
            dy = dy + extra[rows, :].astype(F32)
        par, stat = par_ref[rows, :], stat_ref[rows, :]
        gain, rstd = par[:, 1:2], stat[:, 1:2]
        hat = (hidden_ref[rows, :] - stat[:, 0:1]) * rstd
        total = jnp.sum(dy, axis=1, keepdims=True)
        total_hat = jnp.sum(dy * hat, axis=1, keepdims=True)
        mean_u, mean_uhat = norm_backward(total, total_hat, gain)
        top = cot_ref[rows, :].astype(F32)
        out = top + (dy * gain - mean_u - hat * mean_uhat) * rstd
        hid_ref[rows, :] = out
        low = out.astype(BF)
        grad_ref[rows, :] = low
        sums_ref[rows, :] = columns(
            [
                total_hat,
                total,
                jnp.sum(low.astype(F32), axis=1, keepdims=True),
                jnp.sum(top, axis=1, keepdims=True),
            ]
        )

    for_groups(hidden_ref.shape[0], body)


def norm_three_back(addends, hidden, stat, par, cot):
    ch = hidden.shape[0]
    return pl.pallas_call(
        functools.partial(norm_three_back_kernel, len(addends)),
        out_shape=[struct((ch, HW), F32), struct((ch, HW), BF), struct((ch, 128), F32)],
        in_specs=[whole()] * (len(addends) + 4),
        out_specs=[whole()] * 3,
        compiler_params=params(),
        cost_estimate=cost(20 * ch * HW, 16 * ch * HW),
    )(*addends, hidden, stat, par, cot)


def product_kernel(n, w_ref, *refs):
    pieces, (bias_ref, out_ref) = refs[:n], refs[n:]
    acc = bias_ref[...]
    at = 0
    for x_ref in pieces:
        rows = x_ref.shape[0]
        acc = acc + dot(w_ref[:, at : at + rows], x_ref[...])
        at += rows
    out_ref[...] = acc.astype(BF)


def product(weight, pieces, bias, width=1024, name=None):
    rows, depth = weight.shape
    return pl.pallas_call(
        functools.partial(product_kernel, len(pieces)),
        grid=(HW // width,),
        out_shape=struct((rows, HW), BF),
        in_specs=[pl.BlockSpec((rows, depth), lambda p: (0, 0))]
        + [pl.BlockSpec((x.shape[0], width), lambda p: (0, p)) for x in pieces]
        + [pl.BlockSpec((rows, 1), lambda p: (0, 0))],
        out_specs=pl.BlockSpec((rows, width), lambda p: (0, p)),
        compiler_params=params(),
        cost_estimate=cost(2 * rows * depth * HW, (rows + depth) * HW * 2),
        name=name,
    )(weight, *pieces, bias)


def output_kernel(n, w_ref, *refs):
    pieces, (bias_ref, hidden_ref, out_ref) = refs[:n], refs[n:]
    acc = hidden_ref[...] + bias_ref[...]
    at = 0
    for x_ref in pieces:
        rows = x_ref.shape[0]
        acc = acc + dot(w_ref[:, at : at + rows], x_ref[...])
        at += rows
    out_ref[...] = acc.astype(BF)


def output_product(weight, pieces, bias, hidden, width=1024):
    rows, depth = weight.shape
    return pl.pallas_call(
        functools.partial(output_kernel, len(pieces)),
        grid=(HW // width,),
        out_shape=struct((rows, HW), BF),
        in_specs=[pl.BlockSpec((rows, depth), lambda p: (0, 0))]
        + [pl.BlockSpec((x.shape[0], width), lambda p: (0, p)) for x in pieces]
        + [
            pl.BlockSpec((rows, 1), lambda p: (0, 0)),
            pl.BlockSpec((rows, width), lambda p: (0, p)),
        ],
        out_specs=pl.BlockSpec((rows, width), lambda p: (0, p)),
        compiler_params=params(),
        cost_estimate=cost(2 * rows * depth * HW, (rows * 3 + depth) * HW * 2),
    )(weight, *pieces, bias, hidden)


def outer_kernel(n_left, n_right, *refs):
    lefts, rights = refs[:n_left], refs[n_left : n_left + n_right]
    out_ref, sums_ref = refs[n_left + n_right : n_left + n_right + 2]
    acc_ref, tot_ref = refs[n_left + n_right + 2 :]
    step = pl.program_id(0)

    @pl.when(step == 0)
    def _():
        acc_ref[...] = jnp.zeros_like(acc_ref)
        tot_ref[...] = jnp.zeros_like(tot_ref)

    row = 0
    for left in lefts:
        rows = left.shape[0]
        val = left[...]
        at = 0
        for right in rights:
            cols = right.shape[0]
            acc_ref[row : row + rows, at : at + cols] += dot_nt(val, right[...])
            at += cols
        tot_ref[row : row + rows, :] += jnp.sum(val.astype(F32), axis=1, keepdims=True)
        row += rows

    @pl.when(step == pl.num_programs(0) - 1)
    def _():
        out_ref[...] = acc_ref[...].astype(BF)
        sums_ref[...] = tot_ref[...]


def outer(lefts, rights, width=1024, name=None):
    rows, cols = sum(a.shape[0] for a in lefts), sum(a.shape[0] for a in rights)
    fixed = lambda p: (0, 0)
    return pl.pallas_call(
        functools.partial(outer_kernel, len(lefts), len(rights)),
        grid=(HW // width,),
        out_shape=[struct((rows, cols), BF), struct((rows, 128), F32)],
        in_specs=[pl.BlockSpec((a.shape[0], width), lambda p: (0, p)) for a in (*lefts, *rights)],
        out_specs=[pl.BlockSpec((rows, cols), fixed), pl.BlockSpec((rows, 128), fixed)],
        scratch_shapes=[pltpu.VMEM((rows, cols), F32), pltpu.VMEM((rows, 128), F32)],
        compiler_params=params(),
        cost_estimate=cost(2 * rows * cols * HW, (rows + cols) * HW * 2),
        name=name,
    )(*lefts, *rights)


def key_chunks(width):
    return [(c, width, False) for c in range(0, HW, width)] + [(0, CTXP, True)]


def attention_kernel(
    lim_ref, q_ref, k_ref, v_ref, kc_ref, vc_ref, g_ref,
    o_ref, dq_ref, dk_ref, dv_ref, dkc_ref, dvc_ref,
    kt, vt, s_sc, p_sc, dk_acc, dv_acc, *, chunk,
):
    step, last = pl.program_id(1), pl.num_programs(1) - 1
    width = q_ref.shape[-1]

    @pl.when(step == 0)
    def _():
        kt[:HW, :] = k_ref[0, 0].astype(F32).T.astype(BF)
        kt[HW:, :] = kc_ref[0, 0].astype(F32).T.astype(BF)
        vt[:HW, :] = v_ref[0, 0].astype(F32).T.astype(BF)
        vt[HW:, :] = vc_ref[0, 0].astype(F32).T.astype(BF)
        dk_acc[...] = jnp.zeros_like(dk_acc)
        dv_acc[...] = jnp.zeros_like(dv_acc)

    scale = HEAD_DIM ** (-0.5)
    q = (q_ref[0, 0].astype(F32) * scale).astype(BF)
    limit = lim_ref[0]
    top = jnp.full((8, width), -jnp.inf, F32)
    for c, w, masked in key_chunks(chunk):
        at = slice(c + HW, c + HW + w) if masked else slice(c, c + w)
        scores = dot(kt[at, :], q)
        if masked:
            key = lax.broadcasted_iota(jnp.int32, (w, width), 0)
            scores = jnp.where(key < limit, scores, NEG_FILL)
        s_sc[at, :] = scores
        top = jnp.maximum(top, jnp.max(scores.reshape(w // 8, 8, width), axis=0))
    row_top = jnp.max(top, axis=0, keepdims=True)
    total = jnp.zeros((8, width), F32)
    mixed = jnp.zeros((HEAD_DIM, width), F32)
    for c, w, masked in key_chunks(chunk):
        at = slice(c + HW, c + HW + w) if masked else slice(c, c + w)
        vals = vc_ref[0, 0, :, c : c + w] if masked else v_ref[0, 0, :, c : c + w]
        raised = jnp.exp(s_sc[at, :] - row_top)
        total = total + jnp.sum(raised.reshape(w // 8, 8, width), axis=0)
        low = raised.astype(BF)
        p_sc[at, :] = low
        mixed = mixed + dot(vals, low)
    inverse = 1.0 / jnp.sum(total, axis=0, keepdims=True)
    mixed = mixed * inverse
    o_ref[0] = mixed.astype(BF)
    grad = g_ref[0].astype(F32)
    delta = jnp.sum(grad * mixed, axis=0, keepdims=True) * inverse
    grad_low = (grad * inverse).astype(BF)
    dq = jnp.zeros((HEAD_DIM, width), F32)
    for c, w, masked in key_chunks(chunk):
        at = slice(c + HW, c + HW + w) if masked else slice(c, c + w)
        keys = kc_ref[0, 0, :, c : c + w] if masked else k_ref[0, 0, :, c : c + w]
        probs = p_sc[at, :]
        slope = (dot(vt[at, :], grad_low) - delta).astype(BF) * probs
        dq = dq + dot(keys, slope)
        dk_acc[:, at] += dot_nt(q, slope)
        dv_acc[:, at] += dot_nt(grad_low, probs)
    dq_ref[0] = (dq * scale).astype(BF)

    @pl.when(step == last)
    def _():
        dk_ref[0] = dk_acc[:, :HW].astype(BF)
        dv_ref[0] = dv_acc[:, :HW].astype(BF)
        dkc_ref[0] = dk_acc[:, HW:].astype(BF)
        dvc_ref[0] = dv_acc[:, HW:].astype(BF)


def attention(limit, qkv, ctx_kv, grads, width=1024, chunk=512):
    heads = qkv.shape[1]
    keys = HW + CTXP

    def part(t, w, moving):
        return pl.BlockSpec(
            (1, 1, HEAD_DIM, w), (lambda h, i: (t, h, 0, i)) if moving else (lambda h, i: (t, h, 0, 0))
        )

    def row(w, moving):
        return pl.BlockSpec(
            (1, HEAD_DIM, w), (lambda h, i: (h, 0, i)) if moving else (lambda h, i: (h, 0, 0))
        )

    big, small = struct((heads, HEAD_DIM, HW), BF), struct((heads, HEAD_DIM, CTXP), BF)
    return pl.pallas_call(
        functools.partial(attention_kernel, chunk=chunk),
        grid=(heads, HW // width),
        in_specs=[
            pl.BlockSpec(memory_space=pltpu.SMEM),
            part(0, width, True),
            part(1, HW, False),
            part(2, HW, False),
            part(0, CTXP, False),
            part(1, CTXP, False),
            row(width, True),
        ],
        out_specs=[
            row(width, True),
            row(width, True),
            row(HW, False),
            row(HW, False),
            row(CTXP, False),
            row(CTXP, False),
        ],
        out_shape=[big, big, big, big, small, small],
        scratch_shapes=[
            pltpu.VMEM((keys, HEAD_DIM), BF),
            pltpu.VMEM((keys, HEAD_DIM), BF),
            pltpu.VMEM((keys, width), F32),
            pltpu.VMEM((keys, width), BF),
            pltpu.VMEM((HEAD_DIM, keys), F32),
            pltpu.VMEM((HEAD_DIM, keys), F32),
        ],
        compiler_params=params(dimension_semantics=("arbitrary", "arbitrary")),
        cost_estimate=cost(
            24 * heads * HW * keys * HEAD_DIM, heads * HEAD_DIM * 8 * HW * 2, heads * HW * keys
        ),
        name="attention",
    )(limit, qkv, qkv, qkv, ctx_kv, ctx_kv, grads)


class Alone:
    def __init__(self, mesh):
        self.size = mesh.shape["tensor"]

    def move(self, x):
        return x

    def gather(self, x):
        return (lax.all_gather(x, "tensor", axis=0, tiled=True),)

    def scatter(self, x):
        return (lax.psum_scatter(x, "tensor", scatter_dimension=0, tiled=True),)

    def arrange(self, x, axis):
        return x

    def restore(self, x, axis):
        return x

    def turn(self, w):
        return lax.all_to_all(w, "tensor", split_axis=2, concat_axis=0, tiled=True)


class Paired:
    def __init__(self, mesh):
        dp = mesh.shape["dp"]
        self.near = [(i, i ^ 1) for i in range(dp)]
        self.far = [
            ((2 * k + core) * 2 + t, (2 * k + t) * 2 + core)
            for k in range(dp // 2)
            for core in range(2)
            for t in range(2)
        ]

    def half(self):
        return lax.axis_index("dp") % 2

    def move(self, x):
        return lax.ppermute(x, ("dp", "tensor"), self.far)

    def trade(self, x):
        return lax.ppermute(x, "dp", self.near)

    def gather(self, x):
        return (x, self.trade(x))

    def scatter(self, x):
        rows = x.shape[0] // 2
        return (x[:rows], self.trade(x[rows:]))

    def arrange(self, x, axis):
        size = x.shape[axis] // 2
        own = lax.dynamic_slice_in_dim(x, self.half() * size, size, axis)
        other = lax.dynamic_slice_in_dim(x, (1 - self.half()) * size, size, axis)
        return jnp.concatenate([own, other], axis)

    def restore(self, x, axis):
        size = x.shape[axis] // 2
        low = lax.slice_in_dim(x, 0, size, axis=axis)
        high = lax.slice_in_dim(x, size, 2 * size, axis=axis)
        return jnp.where(lax.axis_index("tensor") == 0, x, jnp.concatenate([high, low], axis))

    def turn(self, w):
        size = w.shape[2] // 2
        own = lax.dynamic_slice_in_dim(w, self.half() * size, size, 2)
        other = lax.dynamic_slice_in_dim(w, (1 - self.half()) * size, size, 2)
        return jnp.concatenate([own, self.trade(other)], 0)


def after(first, *later):
    held = lax.optimization_barrier((first, *later))
    return held[1:] if len(later) > 1 else held[1]


def local(plan, features, cotangent, embedding, context, lengths, norm1_gain, norm1_bias,
    conv1_weight, conv1_bias, emb_weight, emb_bias, norm2_gain, norm2_bias, conv2_weight,
    conv2_bias, norm3_gain, norm3_bias, qkv_weight, qkv_bias, context_weight, context_bias,
    out_weight, out_bias,
):
    ch, images, pixels = features.shape
    heads = ch // HEAD_DIM
    features = plan.move(features.reshape(ch, pixels))
    w1 = plan.move(conv1_weight)

    emb_act = jax.nn.silu(embedding.astype(F32)).astype(BF)
    scale_shift = (
        jnp.einsum("ie,teo->to", emb_act, emb_weight, preferred_element_type=F32) + emb_bias
    )
    ctx_kv = (
        jnp.einsum("toe,ne->ton", context_weight, context[0], preferred_element_type=F32)
        + context_bias[:, :, None]
    ).astype(BF)
    ctx_kv = jnp.pad(ctx_kv, ((0, 0), (0, 0), (0, CTXP - CTX)))
    length_row = jnp.broadcast_to(lengths.astype(F32)[:, None], (1, ch))
    vectors = jnp.concatenate(
        [
            jnp.stack([norm1_gain, norm1_bias, conv1_bias, norm2_gain, norm2_bias]),
            scale_shift,
            jnp.stack([conv2_bias, norm3_gain, norm3_bias, out_bias]),
            qkv_bias,
            length_row,
        ]
    )
    vectors = plan.move(vectors)
    w2 = plan.move(after(features, conv2_weight))
    cot = plan.move(after(w1, cotangent.reshape(ch, pixels)))
    w_out = plan.move(after(w1, out_weight))
    w_qkv = plan.move(after(w1, qkv_weight))
    ctx_kv = plan.move(after(w1, ctx_kv))

    length = vectors[14, :1].astype(jnp.int32)
    par = jnp.pad(vectors[:14].T, ((0, 0), (0, 2)))
    par_one, par_two, par_three = par[:, 0:2], par[:, 2:7], par[:, 7:10]
    bias_out, bias_qkv = par[:, 10:11], vectors[11:14].reshape(3 * ch, 1)

    def conv_weight(w):
        return plan.arrange(w.reshape(ch, 9, C), 2).reshape(ch, 9 * C)

    def turned_weight(w):
        return plan.turn(w.reshape(ch, 9, C))[:, ::-1].transpose(2, 1, 0).reshape(ch, 9 * C)

    act_one, stat_one = first_activation(features, par_one)
    full_one = plan.gather(act_one)
    conv_one, act_two, stat_two = conv_call(
        conv_one_kernel, conv_weight(w1), full_one, (par_two,),
        [struct((ch, HW), F32), struct((ch, HW), BF), struct((ch, 128), F32)], [], "conv_one",
    )
    full_two = plan.gather(act_two)
    hidden, normed, stat_three = conv_call(
        conv_two_kernel, conv_weight(w2), full_two, (par_three, features),
        [struct((ch, HW), F32), struct((ch, HW), BF), struct((ch, 128), F32)], [], "conv_two",
    )
    full_three = plan.gather(normed)
    zeros = jnp.zeros((C, 1), F32)
    grad_heads = product(plan.arrange(w_out, 1).T, (cot,), zeros, name="grad_heads")
    grad_heads = sum(a.astype(F32) for a in plan.scatter(grad_heads)).astype(BF)
    w_in = plan.arrange(w_qkv, 2)
    qkv = product(w_in.reshape(3 * ch, C), full_three, bias_qkv, name="qkv")
    mixed, dq, dk, dv, dkc, dvc = attention(
        4 + length,
        qkv.reshape(3, heads, HEAD_DIM, HW),
        ctx_kv.reshape(2, heads, HEAD_DIM, CTXP),
        grad_heads.reshape(heads, HEAD_DIM, HW),
    )

    flat = lambda a: a.reshape(ch, HW)
    dq, dk, dv = flat(dq), flat(dk), flat(dv)
    grad_normed = product(w_in.reshape(3 * ch, C).T, (dq, dk, dv), zeros, name="grad_normed")
    addends = plan.scatter(grad_normed)
    full_heads = plan.gather(flat(mixed))
    dw_qkv, db_qkv = outer((dq, dk, dv), full_three, name="qkv_grad")
    grad_hidden, grad_two, sums_three = norm_three_back(addends, hidden, stat_three, par_three, cot)
    full_grad_two = plan.gather(grad_two)
    dw_two = conv_weight_grad(grad_two, full_two, "conv_two_weight_grad")
    output = output_product(plan.arrange(w_out, 1), full_heads, bias_out, hidden)
    output = plan.move(output)
    dw_out, _ = outer((cot,), full_heads, name="out_grad")
    grad_one, sums_two = conv_call(
        conv_two_back_kernel, turned_weight(w2), full_grad_two, (par_two, conv_one, stat_two),
        [struct((ch, HW), BF), struct((ch, 128), F32)], [pltpu.VMEM((ch, HW), F32)], "conv_two_back",
    )
    full_grad_one = plan.gather(grad_one)
    dw_one = conv_weight_grad(grad_one, full_one, "conv_one_weight_grad")
    moved = isinstance(plan, Paired)
    input_grad, sums_one = conv_call(
        conv_one_back_kernel, turned_weight(w1), full_grad_one,
        (par_one, features, stat_one, grad_hidden),
        [struct((ch, HW), BF if moved else F32), struct((ch, 128), F32)],
        [pltpu.VMEM((ch, HW), F32)], "conv_one_back",
    )
    input_grad = plan.move(input_grad).astype(F32)

    grad_ctx = jnp.stack([flat_ctx.reshape(ch, CTXP) for flat_ctx in (dkc, dvc)])
    grad_ctx = plan.move(grad_ctx)[:, :, :CTX]
    small = jnp.concatenate(
        [
            sums_three[:, :4].T,
            db_qkv[:, 0].reshape(3, ch),
            sums_two[:, :5].T,
        ]
    )
    small = plan.move(small)
    last = plan.move(sums_one[:, :2].T)
    grad_mod = small[9:11].astype(BF)
    dw_emb = emb_act.astype(F32).reshape(1, -1, 1) * grad_mod.astype(F32)[:, None, :]
    dw_ctx = jnp.einsum("ton,ne->toe", grad_ctx, context[0], preferred_element_type=F32)
    db_ctx = jnp.sum(grad_ctx.astype(F32), axis=2)
    moved_grads = [plan.move(a) for a in (dw_out, dw_qkv.reshape(3, ch, C), dw_two)]
    dw_one = plan.move(dw_one)
    early = lax.psum((dw_ctx.astype(BF), *moved_grads, dw_emb.astype(BF)), "dp")
    rest = jnp.concatenate([small[:7], small[7:9], grad_mod.astype(F32), small[11:12], db_ctx, last])
    late = lax.psum((after(early[-1], dw_one), rest), "dp")
    dw_ctx, dw_out, dw_qkv, dw_two, dw_emb = early
    dw_one, rest = late

    def restored(a, axis):
        return plan.restore(a, axis).astype(F32)

    def conv_grad(a):
        return restored(a.reshape(ch, 9, C), 2).reshape(ch, 9 * C)

    return (
        output.reshape(ch, images, pixels),
        input_grad.reshape(ch, images, pixels),
        rest[14],
        rest[15],
        conv_grad(dw_one),
        rest[11],
        dw_emb.astype(F32),
        rest[9:11],
        rest[7],
        rest[8],
        conv_grad(dw_two),
        rest[2],
        rest[0],
        rest[1],
        restored(dw_qkv, 2),
        rest[4:7],
        dw_ctx.astype(F32),
        rest[12:14],
        restored(dw_out, 1),
        rest[3],
    )


def solution(mesh):
    paired = mesh.shape["tensor"] == 2 and mesh.shape["dp"] % 2 == 0
    plan = Paired(mesh) if paired else Alone(mesh)
    placed = (
        P("tensor", "dp", None),
        P("tensor", "dp", None),
        P("dp", None),
        P("dp", None, None),
        P("dp"),
        P("tensor"),
        P("tensor"),
        P("tensor", None),
        P("tensor"),
        P(None, None, "tensor"),
        P(None, "tensor"),
        P("tensor"),
        P("tensor"),
        P("tensor", None),
        P("tensor"),
        P("tensor"),
        P("tensor"),
        P(None, "tensor", None),
        P(None, "tensor"),
        P(None, "tensor", None),
        P(None, "tensor"),
        P("tensor", None),
        P("tensor"),
    )
    return jax.shard_map(
        functools.partial(local, plan),
        mesh=mesh,
        in_specs=placed,
        out_specs=(
            P("tensor", "dp", None),
            P("tensor", "dp", None),
            P("tensor"),
            P("tensor"),
            P("tensor", None),
            P("tensor"),
            P(None, None, "tensor"),
            P(None, "tensor"),
            P("tensor"),
            P("tensor"),
            P("tensor", None),
            P("tensor"),
            P("tensor"),
            P("tensor"),
            P(None, "tensor", None),
            P(None, "tensor"),
            P(None, "tensor", None),
            P(None, "tensor"),
            P("tensor", None),
            P("tensor"),
        ),
        check_vma=False,
    )
```

```python
import functools

import jax
import jax.numpy as jnp
from jax import lax
from jax.experimental import pallas as pl
from jax.experimental.pallas import tpu as pltpu
from jax.sharding import PartitionSpec as P

C = 512
HEAD_DIM = 64
PER_GROUP = 16
SIDE = 64
HW = 4096
CTX = 260
CTXP = 384
BLOCK = 256
KEYS = 4608
PAD = 128
FILL = 32
EPSILON = 1e-05
NEG_FILL = -1e30
F32 = jnp.float32
BF = jnp.bfloat16
NT = (((1,), (1,)), ((), ()))
VMEM_BYTES = 62 << 20


def dot(a, b):
    return jnp.dot(a, b, preferred_element_type=F32)


def dot_nt(a, b):
    return lax.dot_general(a, b, NT, preferred_element_type=F32)


def whole():
    return pl.BlockSpec(memory_space=pltpu.VMEM)


def placed():
    return pl.BlockSpec(memory_space=pl.ANY)


def scalars():
    return pl.BlockSpec(memory_space=pltpu.SMEM)


def params(**kwargs):
    return pltpu.CompilerParams(vmem_limit_bytes=VMEM_BYTES, **kwargs)


def cost(flops, nbytes, transcendentals=0):
    return pl.CostEstimate(flops=flops, bytes_accessed=nbytes, transcendentals=transcendentals)


def struct(shape, dtype):
    return jax.ShapeDtypeStruct(shape, dtype)


def fetch(meta, own_ref, got_ref, buf, sem):
    @pl.when(meta[1] == 1)
    def _():
        pltpu.make_async_copy(own_ref, buf, sem).start()

    @pl.when(meta[1] != 1)
    def _():
        pltpu.make_async_copy(got_ref, buf, sem).start()


def arrive(own_ref, buf, sem):
    pltpu.make_async_copy(own_ref, buf, sem).wait()


def group_scalar(column):
    return jnp.sum(column, axis=0, keepdims=True) * (1.0 / (PER_GROUP * HW))


def group_stats(vals):
    mean = group_scalar(jnp.sum(vals, axis=1, keepdims=True))
    centred = vals - mean
    var = group_scalar(jnp.sum(centred * centred, axis=1, keepdims=True))
    rstd = lax.rsqrt(var + EPSILON)
    return mean, rstd


def norm_backward(dy_sum, dyx_sum, gain):
    return group_scalar(dy_sum * gain), group_scalar(dyx_sum * gain)


def for_groups(channels, body, together=2):
    def step(g, carry):
        for u in range(together):
            first = pl.multiple_of((g * together + u) * PER_GROUP, PER_GROUP)
            body(pl.ds(first, PER_GROUP))
        return carry

    lax.fori_loop(0, channels // PER_GROUP // together, step, 0)


def columns(values):
    lane = lax.broadcasted_iota(jnp.int32, (PER_GROUP, 128), 1)
    tile = jnp.zeros((PER_GROUP, 128), F32)
    for at, val in enumerate(values):
        tile = jnp.where(lane == at, val, tile)
    return tile


ROWS = SIDE // 2


def lanes(x, n):
    return x[:, 128 * n : 128 * n + 128]


def low_lanes(x):
    return lax.broadcasted_iota(jnp.int32, (x.shape[0], 128), 1) < SIDE


def fold(x):
    low = low_lanes(x)
    out = []
    for r in range(ROWS):
        upper, lower = lanes(x, r // 2), lanes(x, r // 2 + ROWS // 2)
        if r % 2 == 0:
            out.append(jnp.where(low, upper, pltpu.roll(lower, SIDE, 1)))
        else:
            out.append(jnp.where(low, pltpu.roll(upper, SIDE, 1), lower))
    return jnp.concatenate(out, 1)


def unfold(x):
    low = low_lanes(x)
    pairs = range(x.shape[1] // 256)
    top = [jnp.where(low, lanes(x, 2 * n), pltpu.roll(lanes(x, 2 * n + 1), SIDE, 1)) for n in pairs]
    bottom = [
        jnp.where(low, pltpu.roll(lanes(x, 2 * n), SIDE, 1), lanes(x, 2 * n + 1)) for n in pairs
    ]
    return jnp.concatenate(top, 1), jnp.concatenate(bottom, 1)


def fold_kernel(meta, own_ref, got_ref, out_ref, x_buf, sem):
    fetch(meta, own_ref, got_ref, x_buf, sem)
    arrive(own_ref, x_buf, sem)

    def body(rows):
        out_ref[rows, :] = fold(x_buf[rows, :].astype(F32)).astype(BF)

    for_groups(out_ref.shape[0], body)


def folded(meta, own, got):
    return pl.pallas_call(
        fold_kernel,
        out_shape=struct(own.shape, BF),
        in_specs=[scalars(), placed(), placed()],
        out_specs=whole(),
        scratch_shapes=[pltpu.VMEM(own.shape, BF), pltpu.SemaphoreType.DMA(())],
        compiler_params=params(),
        cost_estimate=cost(8 * own.size, 4 * own.size),
        name="fold",
    )(meta, own, got)


def act_one_kernel(meta, own_ref, got_ref, par_ref, act_ref, stat_ref, fold_ref, x_buf, sem):
    fetch(meta, own_ref, got_ref, x_buf, sem)
    arrive(own_ref, x_buf, sem)

    def body(rows):
        vals = fold(x_buf[rows, :].astype(F32))
        fold_ref[rows, :] = vals.astype(BF)
        mean, rstd = group_stats(vals)
        par = par_ref[rows, :]
        out = (vals - mean) * (rstd * par[:, 0:1]) + par[:, 1:2]
        act_ref[rows, :] = (out * jax.nn.sigmoid(out)).astype(BF)
        stat_ref[rows, :] = columns([mean, rstd])

    for_groups(act_ref.shape[0], body)


def first_activation(meta, own, got, par):
    ch = own.shape[0]
    return pl.pallas_call(
        act_one_kernel,
        out_shape=[struct((ch, HW), BF), struct((ch, 128), F32), struct((ch, HW), BF)],
        in_specs=[scalars(), placed(), placed(), whole()],
        out_specs=[whole()] * 3,
        scratch_shapes=[pltpu.VMEM((ch, HW), BF), pltpu.SemaphoreType.DMA(())],
        compiler_params=params(),
        cost_estimate=cost(20 * ch * HW, 6 * ch * HW, ch * HW),
        name="act_one",
    )(meta, own, got, par)


def fill_shifted(xs, pieces, first):
    start = first
    for x_ref in pieces:
        rows = x_ref.shape[0]

        def step(r, carry, x_ref=x_ref, start=start):
            off = pl.multiple_of(r * FILL, FILL)
            at = pl.ds(pl.multiple_of(start + off, FILL), FILL)
            lane = lax.broadcasted_iota(jnp.int32, (FILL, 128), 1)
            low = lane < SIDE
            left, right = lane % SIDE == 0, lane % SIDE == SIDE - 1
            zero = jnp.zeros((FILL, 128), F32)
            here = pl.ds(off, FILL)
            for n in range(ROWS):
                x = x_ref[here, 128 * n : 128 * n + 128].astype(F32)
                kinds = (
                    jnp.where(left, zero, pltpu.roll(x, 1, 1)),
                    x,
                    jnp.where(right, zero, pltpu.roll(x, 127, 1)),
                )
                for d, y in enumerate(kinds):
                    xs[d, at, PAD + 128 * n : PAD + 128 * n + 128] = y.astype(BF)
                    if n == ROWS - 1:
                        xs[d, at, :PAD] = jnp.where(low, zero, pltpu.roll(y, SIDE, 1)).astype(BF)
                    if n == 0:
                        xs[d, at, PAD + HW :] = jnp.where(
                            low, pltpu.roll(y, SIDE, 1), zero
                        ).astype(BF)
            return carry

        lax.fori_loop(0, rows // FILL, step, 0)
        start = xs.shape[1] - rows - start if len(pieces) == 2 else start + rows


def window(xs, tap, start, width):
    first = PAD + start + (tap // 3 - 1) * 128
    if not isinstance(start, int):
        first = pl.multiple_of(first, 128)
    return xs[tap % 3, :, pl.ds(first, width)]


def convolve(xs, w_ref, out_ref, add, width=1024):
    depth = xs.shape[1]

    def step(n, carry):
        p = n * width
        acc = dot(w_ref[:, :depth], window(xs, 0, p, width))
        for tap in range(1, 9):
            acc = acc + dot(w_ref[:, tap * depth : (tap + 1) * depth], window(xs, tap, p, width))
        at = pl.ds(pl.multiple_of(p, width), width)
        out_ref[:, at] = add(acc, at)
        return carry

    lax.fori_loop(0, HW // width, step, 0)


def conv_call(kernel, meta, weights, pieces, vmem_in, any_in, outs, any_outs, scratch, name):
    out_ch, depth = weights[0].shape[0], C
    arrays = (weights[0], *pieces, *vmem_in, *any_in)
    nbytes = sum(a.size * a.dtype.itemsize for a in arrays) + out_ch * HW * 4
    return pl.pallas_call(
        functools.partial(kernel, len(pieces)),
        out_shape=[*outs, *any_outs],
        in_specs=[scalars(), placed(), placed()]
        + [whole()] * (len(pieces) + len(vmem_in))
        + [placed()] * len(any_in),
        out_specs=[whole()] * len(outs) + [placed()] * len(any_outs),
        scratch_shapes=[
            pltpu.VMEM((3, depth, HW + 2 * PAD), BF),
            pltpu.VMEM((out_ch, 9 * depth), BF),
            pltpu.VMEM((out_ch, HW), F32),
            pltpu.SemaphoreType.DMA((4,)),
            *scratch,
        ],
        compiler_params=params(),
        cost_estimate=cost(2 * out_ch * 9 * depth * HW, nbytes, out_ch * HW),
        name=name,
    )(meta, *weights, *pieces, *vmem_in, *any_in)


def conv_one_kernel(n, meta, w_own, w_got, *refs):
    pieces, refs = refs[:n], refs[n:]
    par_ref, act_ref, stat_ref, conv_ref, w_ref, xs, w_buf, acc, sems = refs
    fetch(meta, w_own, w_got, w_buf, sems.at[0])
    fill_shifted(xs, pieces, meta[0])
    arrive(w_own, w_buf, sems.at[0])
    keep = pltpu.make_async_copy(w_buf, w_ref, sems.at[2])
    keep.start()
    bias = par_ref[:, 0:1]
    convolve(xs, w_buf, acc, lambda val, at: val + bias)
    store = pltpu.make_async_copy(acc, conv_ref, sems.at[1])
    store.start()

    def body(rows):
        vals = acc[rows, :]
        mean, rstd = group_stats(vals)
        par = par_ref[rows, :]
        gain, shift, factor = par[:, 1:2], par[:, 2:3], 1.0 + par[:, 3:4]
        mid = (vals - mean) * (rstd * gain * factor) + (shift * factor + par[:, 4:5])
        act_ref[rows, :] = (mid * jax.nn.sigmoid(mid)).astype(BF)
        stat_ref[rows, :] = columns([mean, rstd])

    for_groups(acc.shape[0], body)
    store.wait()
    keep.wait()


def conv_two_kernel(n, meta, w_own, w_got, *refs):
    pieces, refs = refs[:n], refs[n:]
    par_ref, f_ref, normed_ref, stat_ref, hidden_ref, w_ref, xs, w_buf, acc, sems = refs
    fetch(meta, w_own, w_got, w_buf, sems.at[0])
    fill_shifted(xs, pieces, meta[0])
    arrive(w_own, w_buf, sems.at[0])
    keep = pltpu.make_async_copy(w_buf, w_ref, sems.at[2])
    keep.start()
    bias = par_ref[:, 0:1]
    convolve(xs, w_buf, acc, lambda val, at: val + bias + f_ref[:, at].astype(F32))
    store = pltpu.make_async_copy(acc, hidden_ref, sems.at[1])
    store.start()

    def body(rows):
        vals = acc[rows, :]
        mean, rstd = group_stats(vals)
        par = par_ref[rows, :]
        normed_ref[rows, :] = ((vals - mean) * (rstd * par[:, 1:2]) + par[:, 2:3]).astype(BF)
        stat_ref[rows, :] = columns([mean, rstd])

    for_groups(acc.shape[0], body)
    store.wait()
    keep.wait()


def silu_slope(mid):
    sig = jax.nn.sigmoid(mid)
    return sig * (1.0 + mid * (1.0 - sig))


def conv_two_back_kernel(n, meta, w_own, w_got, *refs):
    pieces, refs = refs[:n], refs[n:]
    par_ref, stat_ref, conv_ref, grad_ref, sums_ref, xs, w_buf, acc, sems, conv_buf = refs
    fetch(meta, w_own, w_got, w_buf, sems.at[0])
    load = pltpu.make_async_copy(conv_ref, conv_buf, sems.at[1])
    load.start()
    fill_shifted(xs, pieces, meta[0])
    arrive(w_own, w_buf, sems.at[0])
    convolve(xs, w_buf, acc, lambda val, at: val)
    load.wait()

    def body(rows):
        par, stat = par_ref[rows, :], stat_ref[rows, :]
        gain, shift, factor = par[:, 1:2], par[:, 2:3], 1.0 + par[:, 3:4]
        rstd = stat[:, 1:2]
        hat = (conv_buf[rows, :] - stat[:, 0:1]) * rstd
        mid = hat * (gain * factor) + (shift * factor + par[:, 4:5])
        grad = acc[rows, :] * silu_slope(mid)
        total = jnp.sum(grad, axis=1, keepdims=True)
        total_hat = jnp.sum(grad * hat, axis=1, keepdims=True)
        mean_u, mean_uhat = norm_backward(total * factor, total_hat * factor, gain)
        out = ((grad * (factor * gain) - mean_u - hat * mean_uhat) * rstd).astype(BF)
        grad_ref[rows, :] = out
        bias_grad = jnp.sum(out.astype(F32), axis=1, keepdims=True)
        sums_ref[rows, :] = columns(
            [
                total_hat * factor,
                total * factor,
                total_hat * gain + total * shift,
                total,
                bias_grad,
            ]
        )

    for_groups(acc.shape[0], body)


def conv_one_back_kernel(n, meta, w_own, w_got, *refs):
    pieces, refs = refs[:n], refs[n:]
    par_ref, stat_ref, f_ref, hid_ref, grad_ref, sums_ref, xs, w_buf, acc, sems, hid_buf = refs
    fetch(meta, w_own, w_got, w_buf, sems.at[0])
    load = pltpu.make_async_copy(hid_ref, hid_buf, sems.at[1])
    load.start()
    fill_shifted(xs, pieces, meta[0])
    arrive(w_own, w_buf, sems.at[0])
    convolve(xs, w_buf, acc, lambda val, at: val)
    load.wait()

    def body(rows):
        par, stat = par_ref[rows, :], stat_ref[rows, :]
        gain, shift = par[:, 0:1], par[:, 1:2]
        rstd = stat[:, 1:2]
        hat = (f_ref[rows, :].astype(F32) - stat[:, 0:1]) * rstd
        grad = acc[rows, :] * silu_slope(hat * gain + shift)
        total = jnp.sum(grad, axis=1, keepdims=True)
        total_hat = jnp.sum(grad * hat, axis=1, keepdims=True)
        mean_u, mean_uhat = norm_backward(total, total_hat, gain)
        out = hid_buf[rows, :] + (grad * gain - mean_u - hat * mean_uhat) * rstd
        top, bottom = unfold(out)
        grad_ref[rows, : HW // 2] = top.astype(grad_ref.dtype)
        grad_ref[rows, HW // 2 :] = bottom.astype(grad_ref.dtype)
        sums_ref[rows, :] = columns([total_hat, total])

    for_groups(acc.shape[0], body)


def weight_grad_kernel(n, meta, grad_ref, *refs):
    pieces, (out_ref, gs) = refs[:n], refs[n:]
    fill_shifted(gs, (grad_ref,), 0)
    for tap in range(9):
        moved = window(gs, 8 - tap, 0, HW)
        first = meta[0]
        for x_ref in pieces:
            rows = x_ref.shape[0]
            at = pl.ds(pl.multiple_of(tap * C + first, rows), rows)
            out_ref[:, at] = dot_nt(moved, x_ref[...]).astype(BF)
            first = C - rows - first


def conv_weight_grad(meta, grad, pieces, name):
    out_ch = grad.shape[0]
    return pl.pallas_call(
        functools.partial(weight_grad_kernel, len(pieces)),
        out_shape=struct((out_ch, 9 * C), BF),
        in_specs=[scalars()] + [whole()] * (1 + len(pieces)),
        out_specs=whole(),
        scratch_shapes=[pltpu.VMEM((3, out_ch, HW + 2 * PAD), BF)],
        compiler_params=params(),
        cost_estimate=cost(2 * out_ch * 9 * C * HW, (out_ch + C) * HW * 2 + out_ch * 9 * C * 2),
        name=name,
    )(meta, grad, *pieces)


def turn_kernel(meta, own_ref, other_ref, out_ref):
    half = own_ref.shape[0]
    for tap in range(9):
        at = pl.ds(pl.multiple_of(tap * C + meta[0], half), half)
        row = meta[0]
        for ref in (own_ref, other_ref):
            to = pl.ds(pl.multiple_of((8 - tap) * C + row, half), half)
            out_ref[:, to] = ref[:, at].astype(F32).T.astype(BF)
            row = half - row


def turned_pair(meta, own, other):
    return pl.pallas_call(
        turn_kernel,
        out_shape=struct(own.shape, BF),
        in_specs=[scalars(), whole(), whole()],
        out_specs=whole(),
        compiler_params=params(),
        cost_estimate=cost(0, 3 * own.size * 2),
        name="turn",
    )(meta, own, other)


def norm_three_back_kernel(n, *refs):
    addends, (hidden_ref, stat_ref, par_ref, cot_ref, hid_ref, grad_ref, sums_ref) = (
        refs[:n],
        refs[n:],
    )

    def body(rows):
        dy = addends[0][rows, :].astype(F32)
        for extra in addends[1:]:
            dy = dy + extra[rows, :].astype(F32)
        par, stat = par_ref[rows, :], stat_ref[rows, :]
        gain, rstd = par[:, 1:2], stat[:, 1:2]
        hat = (hidden_ref[rows, :] - stat[:, 0:1]) * rstd
        total = jnp.sum(dy, axis=1, keepdims=True)
        total_hat = jnp.sum(dy * hat, axis=1, keepdims=True)
        mean_u, mean_uhat = norm_backward(total, total_hat, gain)
        top = cot_ref[rows, :].astype(F32)
        out = top + (dy * gain - mean_u - hat * mean_uhat) * rstd
        hid_ref[rows, :] = out
        low = out.astype(BF)
        grad_ref[rows, :] = low
        sums_ref[rows, :] = columns(
            [
                total_hat,
                total,
                jnp.sum(low.astype(F32), axis=1, keepdims=True),
                jnp.sum(top, axis=1, keepdims=True),
            ]
        )

    for_groups(hidden_ref.shape[0], body)


def norm_three_back(addends, hidden, stat, par, cot):
    ch = hidden.shape[0]
    rows = 32

    def part(a):
        return pl.BlockSpec((rows, a.shape[1]), lambda r: (r, 0))

    outs = [struct((ch, HW), F32), struct((ch, HW), BF), struct((ch, 128), F32)]
    ins = (*addends, hidden, stat, par, cot)
    return pl.pallas_call(
        functools.partial(norm_three_back_kernel, len(addends)),
        grid=(ch // rows,),
        out_shape=outs,
        in_specs=[part(a) for a in ins],
        out_specs=[part(a) for a in outs],
        compiler_params=params(),
        cost_estimate=cost(20 * ch * HW, 16 * ch * HW),
        name="norm_three_back",
    )(*ins)


def piece_columns(meta, w_ref, pieces):
    first = meta[0]
    acc = None
    for x_ref in pieces:
        rows = x_ref.shape[0]
        term = dot(w_ref[:, pl.ds(pl.multiple_of(first, rows), rows)], x_ref[...])
        acc = term if acc is None else acc + term
        first = w_ref.shape[1] - rows - first
    return acc


def inputs_kernel(n, meta, w_ref, *refs):
    pieces, (bias_ref, out_ref) = refs[:n], refs[n:]
    out_ref[...] = (piece_columns(meta, w_ref, pieces) + bias_ref[...]).astype(BF)


def inputs_product(meta, weight, pieces, bias, width=1024, name=None):
    rows, depth = weight.shape
    return pl.pallas_call(
        functools.partial(inputs_kernel, len(pieces)),
        grid=(HW // width,),
        out_shape=struct((rows, HW), BF),
        in_specs=[scalars(), pl.BlockSpec((rows, depth), lambda p: (0, 0))]
        + [pl.BlockSpec((x.shape[0], width), lambda p: (0, p)) for x in pieces]
        + [pl.BlockSpec((rows, 1), lambda p: (0, 0))],
        out_specs=pl.BlockSpec((rows, width), lambda p: (0, p)),
        compiler_params=params(),
        cost_estimate=cost(2 * rows * depth * HW, (rows + depth) * HW * 2),
        name=name,
    )(meta, weight, *pieces, bias)


def parts_kernel(n, meta, w_ref, *refs):
    pieces, outs = refs[:n], refs[n:]
    first = meta[0]
    for out_ref in outs:
        rows = out_ref.shape[0]
        row = pl.ds(pl.multiple_of(first, rows), rows)
        acc = None
        at = 0
        for x_ref in pieces:
            depth = x_ref.shape[0]
            term = dot(w_ref[row, at : at + depth], x_ref[...])
            acc = term if acc is None else acc + term
            at += depth
        out_ref[...] = acc.astype(BF)
        first = w_ref.shape[0] - rows - first


def parts_product(meta, weight, pieces, count, width=1024, name=None):
    rows, depth = weight.shape
    part = struct((rows // count, HW), BF)
    return pl.pallas_call(
        functools.partial(parts_kernel, len(pieces)),
        grid=(HW // width,),
        out_shape=[part] * count,
        in_specs=[scalars(), pl.BlockSpec((rows, depth), lambda p: (0, 0))]
        + [pl.BlockSpec((x.shape[0], width), lambda p: (0, p)) for x in pieces],
        out_specs=[pl.BlockSpec((rows // count, width), lambda p: (0, p))] * count,
        compiler_params=params(),
        cost_estimate=cost(2 * rows * depth * HW, (rows + depth) * HW * 2),
        name=name,
    )(meta, weight, *pieces)


def output_kernel(n, meta, w_ref, *refs):
    pieces, (bias_ref, hidden_ref, out_ref) = refs[:n], refs[n:]
    acc = hidden_ref[...] + bias_ref[...] + piece_columns(meta, w_ref, pieces)
    half = acc.shape[1] // 2
    for base, val in zip((0, HW // 2), unfold(acc)):
        first = pl.multiple_of(base + pl.program_id(0) * half, half)
        out_ref[:, pl.ds(first, half)] = val.astype(BF)


def output_product(meta, weight, pieces, bias, hidden, width=1024):
    rows, depth = weight.shape
    return pl.pallas_call(
        functools.partial(output_kernel, len(pieces)),
        grid=(HW // width,),
        out_shape=struct((rows, HW), BF),
        in_specs=[scalars(), pl.BlockSpec((rows, depth), lambda p: (0, 0))]
        + [pl.BlockSpec((x.shape[0], width), lambda p: (0, p)) for x in pieces]
        + [
            pl.BlockSpec((rows, 1), lambda p: (0, 0)),
            pl.BlockSpec((rows, width), lambda p: (0, p)),
        ],
        out_specs=pl.BlockSpec((rows, HW), lambda p: (0, 0)),
        compiler_params=params(),
        cost_estimate=cost(2 * rows * depth * HW, (rows * 3 + depth) * HW * 2),
        name="output",
    )(meta, weight, *pieces, bias, hidden)


def outer_kernel(n_left, n_right, meta, *refs):
    lefts, rights = refs[:n_left], refs[n_left : n_left + n_right]
    out_ref, sums_ref = refs[n_left + n_right : n_left + n_right + 2]
    acc_ref, tot_ref = refs[n_left + n_right + 2 :]
    step = pl.program_id(0)

    @pl.when(step == 0)
    def _():
        acc_ref[...] = jnp.zeros_like(acc_ref)
        tot_ref[...] = jnp.zeros_like(tot_ref)

    row = 0
    for left in lefts:
        rows = left.shape[0]
        val = left[...]
        first = meta[0]
        for right in rights:
            cols = right.shape[0]
            at = pl.ds(pl.multiple_of(first, cols), cols)
            acc_ref[row : row + rows, at] += dot_nt(val, right[...])
            first = acc_ref.shape[1] - cols - first
        tot_ref[row : row + rows, :] += jnp.sum(val.astype(F32), axis=1, keepdims=True)
        row += rows

    @pl.when(step == pl.num_programs(0) - 1)
    def _():
        out_ref[...] = acc_ref[...].astype(BF)
        sums_ref[...] = tot_ref[...]


def outer(meta, lefts, rights, width=1024, name=None):
    rows, cols = sum(a.shape[0] for a in lefts), sum(a.shape[0] for a in rights)
    fixed = lambda p: (0, 0)
    return pl.pallas_call(
        functools.partial(outer_kernel, len(lefts), len(rights)),
        grid=(HW // width,),
        out_shape=[struct((rows, cols), BF), struct((rows, 128), F32)],
        in_specs=[scalars()]
        + [pl.BlockSpec((a.shape[0], width), lambda p: (0, p)) for a in (*lefts, *rights)],
        out_specs=[pl.BlockSpec((rows, cols), fixed), pl.BlockSpec((rows, 128), fixed)],
        scratch_shapes=[pltpu.VMEM((rows, cols), F32), pltpu.VMEM((rows, 128), F32)],
        compiler_params=params(),
        cost_estimate=cost(2 * rows * cols * HW, (rows + cols) * HW * 2),
        name=name,
    )(meta, *lefts, *rights)


def attention_kernel(
    lim_ref, q_ref, k_ref, v_ref, kc_ref, vc_ref, g_ref,
    o_ref, dq_ref, dk_ref, dv_ref, dkc_ref, dvc_ref,
    kt, vt, kn, vn, s_even, s_odd, p_sc, tops, o_acc, dk_acc, dv_acc, *, unroll, back,
):
    step, last = pl.program_id(1), pl.num_programs(1) - 1
    width = q_ref.shape[-1]
    blocks = KEYS // BLOCK

    @pl.when(step == 0)
    def _():
        spare = jnp.zeros((HEAD_DIM, KEYS - HW - CTXP), BF)
        for ref, own, ctx in ((kn, k_ref, kc_ref), (vn, v_ref, vc_ref)):
            ref[:, :HW] = own[0, 0]
            ref[:, HW : HW + CTXP] = ctx[0, 0]
            ref[:, HW + CTXP :] = spare
        row = lax.broadcasted_iota(jnp.int32, (HEAD_DIM, BLOCK), 0)
        for n in range(blocks):
            at = slice(n * BLOCK, (n + 1) * BLOCK)
            key = lax.broadcasted_iota(jnp.int32, (HEAD_DIM, BLOCK), 1) + n * BLOCK
            fill = jnp.where((row == 0) & (key >= HW + lim_ref[0]), NEG_FILL, 0.0)
            kt[at, :] = jnp.concatenate([kn[:, at].astype(F32), fill], 0).T.astype(BF)
            vt[at, :] = jnp.concatenate([vn[:, at].astype(F32), jnp.zeros_like(fill)], 0).T.astype(BF)
        dk_acc[...] = jnp.zeros_like(dk_acc)
        dv_acc[...] = jnp.zeros_like(dv_acc)

    def keys_at(n):
        return pl.ds(pl.multiple_of(n * BLOCK, BLOCK), BLOCK)

    scale = HEAD_DIM ** (-0.5)
    q = (q_ref[0, 0].astype(F32) * scale).astype(BF)
    one = jnp.where(lax.broadcasted_iota(jnp.int32, (HEAD_DIM, width), 0) == 0, 1.0, 0.0).astype(BF)
    q_more = jnp.concatenate([q, one], 0)

    def score(n, held):
        scores = dot(kt[keys_at(n), :], q_more)
        held[...] = scores
        return jnp.max(jnp.max(scores.reshape(BLOCK // 8, 8, width), axis=0), axis=0, keepdims=True)

    o_acc[...] = jnp.zeros_like(o_acc)

    def forward(n, held, top, total, shrink):
        raised = jnp.exp(held[...] - top)
        low = raised.astype(BF)
        p_sc[keys_at(n), :] = low
        tops[n, 0:1, :] = top
        sums = jnp.sum(raised.reshape(BLOCK // 8, 8, width), axis=0)
        o_acc[...] = o_acc[...] * shrink + dot(vn[:, keys_at(n)], low)
        return total * shrink + sums

    def forward_step(n, held, ahead_held, carry):
        top, total, shrink = carry
        ahead = jnp.maximum(top, score(n + 1, ahead_held))
        total = forward(n, held, top, total, shrink)
        return ahead, total, jnp.exp(top - ahead)

    held = (s_even, s_odd)

    def forward_run(j, carry):
        for u in range(unroll):
            carry = forward_step(unroll * j + u, held[u % 2], held[1 - u % 2], carry)
        return carry

    carry = (score(0, s_even), jnp.zeros((8, width), F32), jnp.ones((1, width), F32))
    carry = lax.fori_loop(0, blocks // unroll - 1, forward_run, carry)
    for n in range(blocks - unroll, blocks - 1):
        carry = forward_step(n, held[n % 2], held[1 - n % 2], carry)
    top, total, shrink = carry
    total = forward(blocks - 1, s_odd, top, total, shrink)

    inverse = 1.0 / jnp.sum(total, axis=0, keepdims=True)
    mixed = o_acc[...] * inverse
    o_ref[0] = mixed.astype(BF)
    grad = g_ref[0].astype(F32)
    delta = jnp.sum(grad * mixed, axis=0, keepdims=True)
    dq = jnp.zeros((HEAD_DIM, width), F32)
    none = jnp.zeros((HEAD_DIM, width), BF)
    for c in range(0, KEYS, back):
        at = slice(c, c + back)
        slopes = []
        for n in range(c // BLOCK, (c + back) // BLOCK):
            sub = slice(n * BLOCK, (n + 1) * BLOCK)
            factor = inverse * jnp.exp(tops[n, 0:1, :] - top)
            grad_low = (grad * factor).astype(BF)
            both = jnp.concatenate([grad_low, none], 0)
            probs = p_sc[sub, :]
            slope = (dot(vt[sub, :], both) - delta * factor).astype(BF) * probs
            slopes.append(slope)
            dv_acc[:, sub] += dot_nt(grad_low, probs)
        slope = jnp.concatenate(slopes, 0)
        dq = dq + dot(kn[:, at], slope)
        dk_acc[:, at] += dot_nt(q, slope)
    dq_ref[0] = (dq * scale).astype(BF)

    @pl.when(step == last)
    def _():
        dk_ref[0] = dk_acc[:, :HW].astype(BF)
        dv_ref[0] = dv_acc[:, :HW].astype(BF)
        dkc_ref[0] = dk_acc[:, HW : HW + CTXP].astype(BF)
        dvc_ref[0] = dv_acc[:, HW : HW + CTXP].astype(BF)


def attention(limit, qkv, ctx_kv, grads, width=1024, unroll=6, back=512):
    heads = qkv.shape[1]
    keys = KEYS

    def part(t, w, moving):
        return pl.BlockSpec(
            (1, 1, HEAD_DIM, w), (lambda h, i: (t, h, 0, i)) if moving else (lambda h, i: (t, h, 0, 0))
        )

    def row(w, moving):
        return pl.BlockSpec(
            (1, HEAD_DIM, w), (lambda h, i: (h, 0, i)) if moving else (lambda h, i: (h, 0, 0))
        )

    big, small = struct((heads, HEAD_DIM, HW), BF), struct((heads, HEAD_DIM, CTXP), BF)
    return pl.pallas_call(
        functools.partial(attention_kernel, unroll=unroll, back=back),
        grid=(heads, HW // width),
        in_specs=[
            pl.BlockSpec(memory_space=pltpu.SMEM),
            part(0, width, True),
            part(1, HW, False),
            part(2, HW, False),
            part(0, CTXP, False),
            part(1, CTXP, False),
            row(width, True),
        ],
        out_specs=[
            row(width, True),
            row(width, True),
            row(HW, False),
            row(HW, False),
            row(CTXP, False),
            row(CTXP, False),
        ],
        out_shape=[big, big, big, big, small, small],
        scratch_shapes=[
            pltpu.VMEM((keys, 2 * HEAD_DIM), BF),
            pltpu.VMEM((keys, 2 * HEAD_DIM), BF),
            pltpu.VMEM((HEAD_DIM, keys), BF),
            pltpu.VMEM((HEAD_DIM, keys), BF),
            pltpu.VMEM((BLOCK, width), F32),
            pltpu.VMEM((BLOCK, width), F32),
            pltpu.VMEM((keys, width), BF),
            pltpu.VMEM((keys // BLOCK, 8, width), F32),
            pltpu.VMEM((HEAD_DIM, width), F32),
            pltpu.VMEM((HEAD_DIM, keys), F32),
            pltpu.VMEM((HEAD_DIM, keys), F32),
        ],
        compiler_params=params(dimension_semantics=("arbitrary", "arbitrary")),
        cost_estimate=cost(
            24 * heads * HW * keys * HEAD_DIM, heads * HEAD_DIM * 8 * HW * 2, heads * HW * keys
        ),
        name="attention",
    )(limit, qkv, qkv, qkv, ctx_kv, ctx_kv, grads)


class Alone:
    parts = 1

    def __init__(self, mesh):
        self.images = mesh.shape["dp"]

    def meta(self):
        return jnp.array([0, 1], jnp.int32)

    def image(self):
        return lax.axis_index("dp")

    def got(self, x):
        return x

    def pick(self, own, got):
        return own

    def gather(self, x):
        return (lax.all_gather(x, "tensor", axis=0, tiled=True),)

    def scatter(self, parts):
        return (lax.psum_scatter(parts[0], "tensor", scatter_dimension=0, tiled=True),)

    def turn(self, meta, w):
        ch = w.shape[0]
        cut = w.reshape(ch, 9, C)
        turned = lax.all_to_all(cut, "tensor", split_axis=2, concat_axis=0, tiled=True)
        return turned[:, ::-1].transpose(2, 1, 0).reshape(ch, 9 * C)

    def total(self, x):
        return lax.psum(x, "dp")

    def everywhere(self, x):
        return lax.psum(x, "dp")

    def sum_owned(self, x):
        return lax.psum(x, "dp")


class Paired:
    parts = 2

    def __init__(self, mesh):
        dp = mesh.shape["dp"]
        self.images = dp
        self.far = [
            ((2 * k + core) * 2 + 1 - core, (2 * k + 1 - core) * 2 + core)
            for k in range(dp // 2)
            for core in range(2)
        ]
        self.bits = [1 << b for b in range((dp - 1).bit_length())]

    def half(self):
        return lax.axis_index("dp") % 2

    def stays(self):
        return self.half() == lax.axis_index("tensor")

    def meta(self):
        return jnp.stack([self.half() * (C // 2), self.stays().astype(jnp.int32)]).astype(jnp.int32)

    def image(self):
        return lax.axis_index("dp") // 2 * 2 + lax.axis_index("tensor")

    def got(self, x):
        return lax.ppermute(x, ("dp", "tensor"), self.far)

    def pick(self, own, got):
        return jnp.where(self.stays(), own, got)

    def over(self, x, bit):
        return lax.ppermute(x, "dp", [(i, i ^ bit) for i in range(self.images)])

    def gather(self, x):
        return (x, self.over(x, 1))

    def scatter(self, parts):
        return (parts[0], self.over(parts[1], 1))

    def turn(self, meta, w):
        return turned_pair(meta, w, self.over(w, 1))

    def total(self, x):
        x = x + lax.ppermute(x, "tensor", [(0, 1), (1, 0)])
        for bit in self.bits[1:]:
            x = x + self.over(x, bit)
        return self.pick(x, self.over(x, 1))

    def everywhere(self, x):
        for bit in self.bits:
            x = x + self.over(x, bit)
        return x

    def sum_owned(self, x):
        rows = x.shape[0] // 2
        done = []
        for at, order in enumerate((self.bits, [self.bits[0], *self.bits[2:], self.bits[1]])):
            part = lax.slice_in_dim(x, at * rows, (at + 1) * rows)
            size = rows
            for bit in order:
                size //= 2
                upper = (lax.axis_index("dp") // bit) % 2
                keep = lax.dynamic_slice_in_dim(part, upper * size, size)
                send = lax.dynamic_slice_in_dim(part, (1 - upper) * size, size)
                part = (keep.astype(F32) + self.over(send, bit).astype(F32)).astype(BF)
            for bit in reversed(order):
                upper = (lax.axis_index("dp") // bit) % 2
                other = self.over(part, bit)
                part = jnp.where(
                    upper == 0,
                    jnp.concatenate([part, other]),
                    jnp.concatenate([other, part]),
                )
            done.append(part)
        return jnp.concatenate(done)


def after(first, *later):
    held = lax.optimization_barrier((first, *later))
    return held[1:] if len(later) > 1 else held[1]


def local(plan, features, cotangent, embedding, context, lengths, norm1_gain, norm1_bias,
    conv1_weight, conv1_bias, emb_weight, emb_bias, norm2_gain, norm2_bias, conv2_weight,
    conv2_bias, norm3_gain, norm3_bias, qkv_weight, qkv_bias, context_weight, context_bias,
    out_weight, out_bias,
):
    ch, images, pixels = features.shape
    heads = ch // HEAD_DIM
    meta = plan.meta()
    moved = plan.parts == 2

    length_row = jnp.broadcast_to(lengths.astype(F32)[:, None], (1, ch))
    vectors = jnp.concatenate(
        [
            jnp.stack([norm1_gain, norm1_bias, conv1_bias, norm2_gain, norm2_bias]),
            jnp.stack([conv2_bias, norm3_gain, norm3_bias, out_bias]),
            qkv_bias,
            length_row,
        ]
    )
    vectors = plan.pick(vectors, plan.got(vectors))
    f_own = features.reshape(ch, pixels)
    f_got = plan.got(f_own)
    w1_got = plan.got(conv1_weight)
    emb_act = jax.nn.silu(embedding.astype(F32)).astype(BF)
    scale_shift = (
        jnp.einsum("ie,teo->to", emb_act, emb_weight, preferred_element_type=F32) + emb_bias
    )
    ctx_kv = (
        jnp.einsum("toe,ne->ton", context_weight, context[0], preferred_element_type=F32)
        + context_bias[:, :, None]
    ).astype(BF)
    ctx_kv = jnp.pad(ctx_kv, ((0, 0), (0, 0), (0, CTXP - CTX)))
    vectors, ctx_kv = after(scale_shift, vectors, ctx_kv)
    scale_shift = plan.pick(scale_shift, plan.got(scale_shift))
    length = vectors[12, :1].astype(jnp.int32)
    par_one = vectors[0:2].T
    act_one, stat_one, f_low = first_activation(meta, f_own, f_got, par_one)
    full_one = plan.gather(act_one)
    w2_got = plan.got(after(act_one, conv2_weight))
    mats_own = jnp.concatenate([qkv_weight.reshape(3 * ch, C), out_weight])
    mats_own, ctx_own, cot_own = after(
        full_one[-1], mats_own, ctx_kv, cotangent.reshape(ch, pixels)
    )
    mats_got, ctx_got = plan.got(mats_own), plan.got(ctx_own)
    cot_got = plan.got(cot_own)

    par_two = jnp.concatenate([vectors[2:5], scale_shift]).T
    low, stat, wide = struct((ch, HW), BF), struct((ch, 128), F32), struct((ch, HW), F32)
    weight = struct((ch, 9 * C), BF)
    act_two, stat_two, conv_one, w1 = conv_call(
        conv_one_kernel, meta, (conv1_weight, w1_got), full_one, (par_two,), (),
        [low, stat], [wide, weight], [], "conv_one",
    )
    full_two = plan.gather(act_two)
    par_three = vectors[5:8].T
    normed, stat_three, hidden, w2 = conv_call(
        conv_two_kernel, meta, (conv2_weight, w2_got), full_two, (par_three, f_low), (),
        [low, stat], [wide, weight], [], "conv_two",
    )
    full_three = plan.gather(normed)
    mats = plan.pick(mats_own, mats_got)
    w_qkv, w_out = mats[: 3 * ch], mats[3 * ch :]
    qkv = inputs_product(meta, w_qkv, full_three, vectors[9:12].reshape(3 * ch, 1), name="qkv")
    cot = folded(meta, *after(normed, cot_own, cot_got))
    grad_heads = plan.scatter(
        parts_product(meta, w_out.T, (cot,), plan.parts, name="grad_heads")
    )
    turned_one = plan.turn(meta, w1)
    turned_two = plan.turn(meta, w2)
    grad_heads = sum(a.astype(F32) for a in grad_heads).astype(BF)
    ctx_kv = plan.pick(ctx_own, ctx_got)
    mixed, dq, dk, dv, dkc, dvc = attention(
        4 + length,
        qkv.reshape(3, heads, HEAD_DIM, HW),
        ctx_kv.reshape(2, heads, HEAD_DIM, CTXP),
        grad_heads.reshape(heads, HEAD_DIM, HW),
    )

    flat = lambda a: a.reshape(ch, HW)
    dq, dk, dv = flat(dq), flat(dk), flat(dv)
    addends = plan.scatter(
        parts_product(meta, w_qkv.T, (dq, dk, dv), plan.parts, name="grad_normed")
    )
    full_heads = plan.gather(flat(mixed))
    ctx_own = jnp.concatenate([a.reshape(1, ch, CTXP) for a in (dkc, dvc)])
    ctx_got = plan.got(ctx_own)
    dw_qkv, db_qkv = outer(meta, (dq, dk, dv), full_three, name="qkv_grad")
    dw_out, _ = outer(meta, (cot,), full_heads, name="out_grad")
    mats_own = jnp.concatenate([dw_qkv, dw_out])
    mats_got = plan.got(mats_own)
    grad_hidden, grad_two, sums_three = norm_three_back(addends, hidden, stat_three, par_three, cot)
    full_grad_two = plan.gather(grad_two)
    dw_two = conv_weight_grad(meta, grad_two, full_two, "conv_two_weight_grad")
    two_got = plan.got(dw_two)
    ctx_grad = plan.pick(ctx_own, ctx_got)[:, :, :CTX]
    dw_ctx = jnp.einsum("ton,ne->toe", ctx_grad, context[0], preferred_element_type=F32).astype(BF)
    full_grad_two = after(dw_two, *full_grad_two) if moved else full_grad_two
    grad_one, sums_two = conv_call(
        conv_two_back_kernel, meta, (turned_two, turned_two), full_grad_two, (par_two, stat_two),
        (conv_one,), [low, stat], [], [pltpu.VMEM((ch, HW), F32)], "conv_two_back",
    )
    full_grad_one = plan.gather(grad_one)
    mats = plan.pick(mats_own, after(dw_two, mats_got))
    early = (dw_ctx, mats, plan.pick(dw_two, after(grad_one, two_got)))
    held = after(early, grad_one)
    dw_one = conv_weight_grad(meta, held, full_one, "conv_one_weight_grad")
    early = lax.psum(early, "dp")
    one_got = plan.got(dw_one)
    full_grad_one = after(dw_one, *full_grad_one) if moved else full_grad_one
    input_grad, sums_one = conv_call(
        conv_one_back_kernel, meta, (turned_one, turned_one), full_grad_one,
        (par_one, stat_one, f_low), (grad_hidden,),
        [struct((ch, HW), BF if moved else F32), stat], [],
        [pltpu.VMEM((ch, HW), F32)], "conv_one_back",
    )
    input_got = plan.got(input_grad)
    output = output_product(
        meta, w_out, full_heads, vectors[8].reshape(ch, 1), after(grad_hidden, hidden)
    )
    output = plan.pick(output, plan.got(output))

    dw_one = plan.sum_owned(plan.pick(dw_one, one_got))
    emb_all = jnp.where(
        jnp.arange(plan.images)[:, None] == lax.axis_index("dp"), emb_act, jnp.zeros_like(emb_act)
    )
    emb_all = plan.everywhere(emb_all)
    ctx_sums = jnp.sum(ctx_own.astype(F32), axis=2)
    sums_two = sums_two[:, :5].T
    own_mod = sums_two[2:4].astype(BF).astype(F32)
    mods = jnp.where(
        (jnp.arange(plan.images) == plan.image())[:, None, None], own_mod, jnp.zeros_like(own_mod)
    ).reshape(2 * plan.images, ch)
    small = plan.total(
        jnp.concatenate(
            [
                sums_three[:, :4].T,
                db_qkv[:, 0].reshape(3, ch),
                sums_two[:2],
                sums_two[4:5],
                ctx_sums,
                mods,
            ]
        )
    )
    mods = small[12:].reshape(plan.images, 2, ch)
    mods_low = mods.astype(BF)
    dw_emb = jnp.stack(
        [
            jnp.einsum("ie,io->eo", emb_all, mods_low[:, t], preferred_element_type=F32)
            for t in range(2)
        ]
    )
    last = plan.total(sums_one[:, :2].T)
    input_grad = plan.pick(input_grad, input_got).astype(F32)
    dw_ctx, mats, dw_two = after((dw_one, last, input_grad), *early)

    return (
        output.reshape(ch, images, pixels),
        input_grad.reshape(ch, images, pixels),
        last[0],
        last[1],
        dw_one.astype(F32),
        small[9],
        dw_emb,
        jnp.sum(mods, axis=0),
        small[7],
        small[8],
        dw_two.astype(F32),
        small[2],
        small[0],
        small[1],
        mats[: 3 * ch].astype(F32).reshape(3, ch, C),
        small[4:7],
        dw_ctx.astype(F32),
        small[10:12],
        mats[3 * ch :].astype(F32),
        small[3],
    )


def solution(mesh):
    paired = mesh.shape["tensor"] == 2 and mesh.shape["dp"] % 2 == 0
    plan = Paired(mesh) if paired else Alone(mesh)
    specs = (
        P("tensor", "dp", None),
        P("tensor", "dp", None),
        P("dp", None),
        P("dp", None, None),
        P("dp"),
        P("tensor"),
        P("tensor"),
        P("tensor", None),
        P("tensor"),
        P(None, None, "tensor"),
        P(None, "tensor"),
        P("tensor"),
        P("tensor"),
        P("tensor", None),
        P("tensor"),
        P("tensor"),
        P("tensor"),
        P(None, "tensor", None),
        P(None, "tensor"),
        P(None, "tensor", None),
        P(None, "tensor"),
        P("tensor", None),
        P("tensor"),
    )
    return jax.shard_map(
        functools.partial(local, plan),
        mesh=mesh,
        in_specs=specs,
        out_specs=(
            P("tensor", "dp", None),
            P("tensor", "dp", None),
            P("tensor"),
            P("tensor"),
            P("tensor", None),
            P("tensor"),
            P(None, None, "tensor"),
            P(None, "tensor"),
            P("tensor"),
            P("tensor"),
            P("tensor", None),
            P("tensor"),
            P("tensor"),
            P("tensor"),
            P(None, "tensor", None),
            P(None, "tensor"),
            P(None, "tensor", None),
            P(None, "tensor"),
            P("tensor", None),
            P("tensor"),
        ),
        check_vma=False,
    )
```

```python
import functools

import jax
import jax.numpy as jnp
from jax import lax
from jax.experimental import pallas as pl
from jax.experimental.pallas import tpu as pltpu
from jax.sharding import PartitionSpec as P

C = 512
HEAD_DIM = 64
PER_GROUP = 16
SIDE = 64
HW = 4096
CTX = 260
CTXP = 384
CTX_EMB = 2048
BLOCK = 256
KEYS = 4608
PAD = 128
FILL = 32
SCALE = 100
EPSILON = 1e-05
NEG_FILL = -1e30
F32 = jnp.float32
BF = jnp.bfloat16
NT = (((1,), (1,)), ((), ()))
VMEM_BYTES = 62 << 20


def dot(a, b):
    return jnp.dot(a, b, preferred_element_type=F32)


def dot_nt(a, b):
    return lax.dot_general(a, b, NT, preferred_element_type=F32)


def whole():
    return pl.BlockSpec(memory_space=pltpu.VMEM)


def placed():
    return pl.BlockSpec(memory_space=pl.ANY)


def scalars():
    return pl.BlockSpec(memory_space=pltpu.SMEM)


def params(**kwargs):
    return pltpu.CompilerParams(vmem_limit_bytes=VMEM_BYTES, **kwargs)


def cost(flops, nbytes, transcendentals=0):
    return pl.CostEstimate(
        flops=flops // SCALE, bytes_accessed=nbytes // SCALE, transcendentals=transcendentals // SCALE
    )


def struct(shape, dtype):
    return jax.ShapeDtypeStruct(shape, dtype)


def fetch(meta, own_ref, got_ref, buf, sem):
    @pl.when(meta[1] == 1)
    def _():
        pltpu.make_async_copy(own_ref, buf, sem).start()

    @pl.when(meta[1] != 1)
    def _():
        pltpu.make_async_copy(got_ref, buf, sem).start()


def arrive(own_ref, buf, sem):
    pltpu.make_async_copy(own_ref, buf, sem).wait()


def group_scalar(column):
    return jnp.sum(column, axis=0, keepdims=True) * (1.0 / (PER_GROUP * HW))


def group_stats(vals):
    mean = group_scalar(jnp.sum(vals, axis=1, keepdims=True))
    centred = vals - mean
    var = group_scalar(jnp.sum(centred * centred, axis=1, keepdims=True))
    rstd = lax.rsqrt(var + EPSILON)
    return mean, rstd


def norm_backward(dy_sum, dyx_sum, gain):
    return group_scalar(dy_sum * gain), group_scalar(dyx_sum * gain)


def for_groups(channels, body, together=2):
    def step(g, carry):
        for u in range(together):
            first = pl.multiple_of((g * together + u) * PER_GROUP, PER_GROUP)
            body(pl.ds(first, PER_GROUP))
        return carry

    lax.fori_loop(0, channels // PER_GROUP // together, step, 0)


def columns(values):
    lane = lax.broadcasted_iota(jnp.int32, (PER_GROUP, 128), 1)
    tile = jnp.zeros((PER_GROUP, 128), F32)
    for at, val in enumerate(values):
        tile = jnp.where(lane == at, val, tile)
    return tile


ROWS = SIDE // 2


def lanes(x, n):
    return x[:, 128 * n : 128 * n + 128]


def low_lanes(x):
    return lax.broadcasted_iota(jnp.int32, (x.shape[0], 128), 1) < SIDE


def fold(x):
    low = low_lanes(x)
    out = []
    for r in range(ROWS):
        upper, lower = lanes(x, r // 2), lanes(x, r // 2 + ROWS // 2)
        if r % 2 == 0:
            out.append(jnp.where(low, upper, pltpu.roll(lower, SIDE, 1)))
        else:
            out.append(jnp.where(low, pltpu.roll(upper, SIDE, 1), lower))
    return jnp.concatenate(out, 1)


def unfold(x):
    low = low_lanes(x)
    pairs = range(x.shape[1] // 256)
    top = [jnp.where(low, lanes(x, 2 * n), pltpu.roll(lanes(x, 2 * n + 1), SIDE, 1)) for n in pairs]
    bottom = [
        jnp.where(low, pltpu.roll(lanes(x, 2 * n), SIDE, 1), lanes(x, 2 * n + 1)) for n in pairs
    ]
    return jnp.concatenate(top, 1), jnp.concatenate(bottom, 1)


def fold_kernel(meta, own_ref, got_ref, out_ref, x_buf, sem):
    fetch(meta, own_ref, got_ref, x_buf, sem)
    arrive(own_ref, x_buf, sem)

    def body(rows):
        out_ref[rows, :] = fold(x_buf[rows, :].astype(F32)).astype(BF)

    for_groups(out_ref.shape[0], body)


def folded(meta, own, got):
    return pl.pallas_call(
        fold_kernel,
        out_shape=struct(own.shape, BF),
        in_specs=[scalars(), placed(), placed()],
        out_specs=whole(),
        scratch_shapes=[pltpu.VMEM(own.shape, BF), pltpu.SemaphoreType.DMA(())],
        compiler_params=params(),
        cost_estimate=cost(8 * own.size, 4 * own.size),
        name="fold",
    )(meta, own, got)


def act_one_kernel(meta, own_ref, got_ref, par_ref, act_ref, stat_ref, fold_ref, x_buf, sem):
    fetch(meta, own_ref, got_ref, x_buf, sem)
    arrive(own_ref, x_buf, sem)

    def body(rows):
        vals = fold(x_buf[rows, :].astype(F32))
        fold_ref[rows, :] = vals.astype(BF)
        mean, rstd = group_stats(vals)
        par = par_ref[rows, :]
        out = (vals - mean) * (rstd * par[:, 0:1]) + par[:, 1:2]
        act_ref[rows, :] = (out * jax.nn.sigmoid(out)).astype(BF)
        stat_ref[rows, :] = columns([mean, rstd])

    for_groups(act_ref.shape[0], body)


def first_activation(meta, own, got, par):
    ch = own.shape[0]
    return pl.pallas_call(
        act_one_kernel,
        out_shape=[struct((ch, HW), BF), struct((ch, 128), F32), struct((ch, HW), BF)],
        in_specs=[scalars(), placed(), placed(), whole()],
        out_specs=[whole()] * 3,
        scratch_shapes=[pltpu.VMEM((ch, HW), BF), pltpu.SemaphoreType.DMA(())],
        compiler_params=params(),
        cost_estimate=cost(20 * ch * HW, 6 * ch * HW, ch * HW),
        name="act_one",
    )(meta, own, got, par)


def fill_shifted(xs, pieces, first):
    start = first
    for x_ref in pieces:
        rows = x_ref.shape[0]

        def step(r, carry, x_ref=x_ref, start=start):
            off = pl.multiple_of(r * FILL, FILL)
            at = pl.ds(pl.multiple_of(start + off, FILL), FILL)
            lane = lax.broadcasted_iota(jnp.int32, (FILL, 128), 1)
            low = lane < SIDE
            left, right = lane % SIDE == 0, lane % SIDE == SIDE - 1
            zero = jnp.zeros((FILL, 128), F32)
            here = pl.ds(off, FILL)
            for n in range(ROWS):
                x = x_ref[here, 128 * n : 128 * n + 128].astype(F32)
                kinds = (
                    jnp.where(left, zero, pltpu.roll(x, 1, 1)),
                    x,
                    jnp.where(right, zero, pltpu.roll(x, 127, 1)),
                )
                for d, y in enumerate(kinds):
                    xs[d, at, PAD + 128 * n : PAD + 128 * n + 128] = y.astype(BF)
                    if n == ROWS - 1:
                        xs[d, at, :PAD] = jnp.where(low, zero, pltpu.roll(y, SIDE, 1)).astype(BF)
                    if n == 0:
                        xs[d, at, PAD + HW :] = jnp.where(
                            low, pltpu.roll(y, SIDE, 1), zero
                        ).astype(BF)
            return carry

        lax.fori_loop(0, rows // FILL, step, 0)
        start = xs.shape[1] - rows - start if len(pieces) == 2 else start + rows


def window(xs, tap, start, width):
    first = PAD + start + (tap // 3 - 1) * 128
    if not isinstance(start, int):
        first = pl.multiple_of(first, 128)
    return xs[tap % 3, :, pl.ds(first, width)]


def convolve(xs, w_ref, out_ref, add, width=1024):
    depth = xs.shape[1]

    def step(n, carry):
        p = n * width
        acc = dot(w_ref[:, :depth], window(xs, 0, p, width))
        for tap in range(1, 9):
            acc = acc + dot(w_ref[:, tap * depth : (tap + 1) * depth], window(xs, tap, p, width))
        at = pl.ds(pl.multiple_of(p, width), width)
        out_ref[:, at] = add(acc, at)
        return carry

    lax.fori_loop(0, HW // width, step, 0)


def conv_call(kernel, meta, weights, pieces, vmem_in, any_in, outs, any_outs, scratch, name):
    out_ch, depth = weights[0].shape[0], C
    arrays = (weights[0], *pieces, *vmem_in, *any_in)
    nbytes = sum(a.size * a.dtype.itemsize for a in arrays) + out_ch * HW * 4
    return pl.pallas_call(
        functools.partial(kernel, len(pieces)),
        out_shape=[*outs, *any_outs],
        in_specs=[scalars(), placed(), placed()]
        + [whole()] * (len(pieces) + len(vmem_in))
        + [placed()] * len(any_in),
        out_specs=[whole()] * len(outs) + [placed()] * len(any_outs),
        scratch_shapes=[
            pltpu.VMEM((3, depth, HW + 2 * PAD), BF),
            pltpu.VMEM((out_ch, 9 * depth), BF),
            pltpu.VMEM((out_ch, HW), F32),
            pltpu.SemaphoreType.DMA((4,)),
            *scratch,
        ],
        compiler_params=params(),
        cost_estimate=cost(2 * out_ch * 9 * depth * HW, nbytes, out_ch * HW),
        name=name,
    )(meta, *weights, *pieces, *vmem_in, *any_in)


def conv_one_kernel(n, meta, w_own, w_got, *refs):
    pieces, refs = refs[:n], refs[n:]
    par_ref, act_ref, stat_ref, conv_ref, w_ref, xs, w_buf, acc, sems = refs
    fetch(meta, w_own, w_got, w_buf, sems.at[0])
    fill_shifted(xs, pieces, meta[0])
    arrive(w_own, w_buf, sems.at[0])
    keep = pltpu.make_async_copy(w_buf, w_ref, sems.at[2])
    keep.start()
    bias = par_ref[:, 0:1]
    convolve(xs, w_buf, acc, lambda val, at: val + bias)
    store = pltpu.make_async_copy(acc, conv_ref, sems.at[1])
    store.start()

    def body(rows):
        vals = acc[rows, :]
        mean, rstd = group_stats(vals)
        par = par_ref[rows, :]
        gain, shift, factor = par[:, 1:2], par[:, 2:3], 1.0 + par[:, 3:4]
        mid = (vals - mean) * (rstd * gain * factor) + (shift * factor + par[:, 4:5])
        act_ref[rows, :] = (mid * jax.nn.sigmoid(mid)).astype(BF)
        stat_ref[rows, :] = columns([mean, rstd])

    for_groups(acc.shape[0], body)
    store.wait()
    keep.wait()


def conv_two_kernel(n, meta, w_own, w_got, *refs):
    pieces, refs = refs[:n], refs[n:]
    par_ref, f_ref, normed_ref, stat_ref, hidden_ref, w_ref, xs, w_buf, acc, sems = refs
    fetch(meta, w_own, w_got, w_buf, sems.at[0])
    fill_shifted(xs, pieces, meta[0])
    arrive(w_own, w_buf, sems.at[0])
    keep = pltpu.make_async_copy(w_buf, w_ref, sems.at[2])
    keep.start()
    bias = par_ref[:, 0:1]
    convolve(xs, w_buf, acc, lambda val, at: val + bias + f_ref[:, at].astype(F32))
    store = pltpu.make_async_copy(acc, hidden_ref, sems.at[1])
    store.start()

    def body(rows):
        vals = acc[rows, :]
        mean, rstd = group_stats(vals)
        par = par_ref[rows, :]
        normed_ref[rows, :] = ((vals - mean) * (rstd * par[:, 1:2]) + par[:, 2:3]).astype(BF)
        stat_ref[rows, :] = columns([mean, rstd])

    for_groups(acc.shape[0], body)
    store.wait()
    keep.wait()


def silu_slope(mid):
    sig = jax.nn.sigmoid(mid)
    return sig * (1.0 + mid * (1.0 - sig))


def conv_two_back_kernel(n, meta, w_own, w_got, *refs):
    pieces, refs = refs[:n], refs[n:]
    par_ref, stat_ref, conv_ref, grad_ref, sums_ref, xs, w_buf, acc, sems, conv_buf = refs
    fetch(meta, w_own, w_got, w_buf, sems.at[0])
    load = pltpu.make_async_copy(conv_ref, conv_buf, sems.at[1])
    load.start()
    fill_shifted(xs, pieces, meta[0])
    arrive(w_own, w_buf, sems.at[0])
    convolve(xs, w_buf, acc, lambda val, at: val)
    load.wait()

    def body(rows):
        par, stat = par_ref[rows, :], stat_ref[rows, :]
        gain, shift, factor = par[:, 1:2], par[:, 2:3], 1.0 + par[:, 3:4]
        rstd = stat[:, 1:2]
        hat = (conv_buf[rows, :] - stat[:, 0:1]) * rstd
        mid = hat * (gain * factor) + (shift * factor + par[:, 4:5])
        grad = acc[rows, :] * silu_slope(mid)
        total = jnp.sum(grad, axis=1, keepdims=True)
        total_hat = jnp.sum(grad * hat, axis=1, keepdims=True)
        mean_u, mean_uhat = norm_backward(total * factor, total_hat * factor, gain)
        out = ((grad * (factor * gain) - mean_u - hat * mean_uhat) * rstd).astype(BF)
        grad_ref[rows, :] = out
        bias_grad = jnp.sum(out.astype(F32), axis=1, keepdims=True)
        sums_ref[rows, :] = columns(
            [
                total_hat * factor,
                total * factor,
                total_hat * gain + total * shift,
                total,
                bias_grad,
            ]
        )

    for_groups(acc.shape[0], body)


def conv_one_back_kernel(n, meta, w_own, w_got, *refs):
    pieces, refs = refs[:n], refs[n:]
    par_ref, stat_ref, f_ref, hid_ref, grad_ref, sums_ref, xs, w_buf, acc, sems, hid_buf = refs
    fetch(meta, w_own, w_got, w_buf, sems.at[0])
    load = pltpu.make_async_copy(hid_ref, hid_buf, sems.at[1])
    load.start()
    fill_shifted(xs, pieces, meta[0])
    arrive(w_own, w_buf, sems.at[0])
    convolve(xs, w_buf, acc, lambda val, at: val)
    load.wait()

    def body(rows):
        par, stat = par_ref[rows, :], stat_ref[rows, :]
        gain, shift = par[:, 0:1], par[:, 1:2]
        rstd = stat[:, 1:2]
        hat = (f_ref[rows, :].astype(F32) - stat[:, 0:1]) * rstd
        grad = acc[rows, :] * silu_slope(hat * gain + shift)
        total = jnp.sum(grad, axis=1, keepdims=True)
        total_hat = jnp.sum(grad * hat, axis=1, keepdims=True)
        mean_u, mean_uhat = norm_backward(total, total_hat, gain)
        out = hid_buf[rows, :] + (grad * gain - mean_u - hat * mean_uhat) * rstd
        top, bottom = unfold(out)
        grad_ref[rows, : HW // 2] = top.astype(grad_ref.dtype)
        grad_ref[rows, HW // 2 :] = bottom.astype(grad_ref.dtype)
        sums_ref[rows, :] = columns([total_hat, total])

    for_groups(acc.shape[0], body)


def weight_grad_kernel(n, meta, grad_ref, *refs):
    pieces, (out_ref, gs) = refs[:n], refs[n:]
    fill_shifted(gs, (grad_ref,), 0)
    for tap in range(9):
        moved = window(gs, 8 - tap, 0, HW)
        first = meta[0]
        for x_ref in pieces:
            rows = x_ref.shape[0]
            at = pl.ds(pl.multiple_of(tap * C + first, rows), rows)
            out_ref[:, at] = dot_nt(moved, x_ref[...]).astype(BF)
            first = C - rows - first


def conv_weight_grad(meta, grad, pieces, name):
    out_ch = grad.shape[0]
    return pl.pallas_call(
        functools.partial(weight_grad_kernel, len(pieces)),
        out_shape=struct((out_ch, 9 * C), BF),
        in_specs=[scalars()] + [whole()] * (1 + len(pieces)),
        out_specs=whole(),
        scratch_shapes=[pltpu.VMEM((3, out_ch, HW + 2 * PAD), BF)],
        compiler_params=params(),
        cost_estimate=cost(2 * out_ch * 9 * C * HW, (out_ch + C) * HW * 2 + out_ch * 9 * C * 2),
        name=name,
    )(meta, grad, *pieces)


def turn_kernel(meta, own_ref, other_ref, out_ref):
    half = own_ref.shape[0]
    for tap in range(9):
        at = pl.ds(pl.multiple_of(tap * C + meta[0], half), half)
        row = meta[0]
        for ref in (own_ref, other_ref):
            to = pl.ds(pl.multiple_of((8 - tap) * C + row, half), half)
            out_ref[:, to] = ref[:, at].astype(F32).T.astype(BF)
            row = half - row


def turned_pair(meta, own, other):
    return pl.pallas_call(
        turn_kernel,
        out_shape=struct(own.shape, BF),
        in_specs=[scalars(), whole(), whole()],
        out_specs=whole(),
        compiler_params=params(),
        cost_estimate=cost(0, 3 * own.size * 2),
        name="turn",
    )(meta, own, other)


def norm_three_back_kernel(n, *refs):
    addends, (hidden_ref, stat_ref, par_ref, cot_ref, hid_ref, grad_ref, sums_ref) = (
        refs[:n],
        refs[n:],
    )

    def body(rows):
        dy = addends[0][rows, :].astype(F32)
        for extra in addends[1:]:
            dy = dy + extra[rows, :].astype(F32)
        par, stat = par_ref[rows, :], stat_ref[rows, :]
        gain, rstd = par[:, 1:2], stat[:, 1:2]
        hat = (hidden_ref[rows, :] - stat[:, 0:1]) * rstd
        total = jnp.sum(dy, axis=1, keepdims=True)
        total_hat = jnp.sum(dy * hat, axis=1, keepdims=True)
        mean_u, mean_uhat = norm_backward(total, total_hat, gain)
        top = cot_ref[rows, :].astype(F32)
        out = top + (dy * gain - mean_u - hat * mean_uhat) * rstd
        hid_ref[rows, :] = out
        low = out.astype(BF)
        grad_ref[rows, :] = low
        sums_ref[rows, :] = columns(
            [
                total_hat,
                total,
                jnp.sum(low.astype(F32), axis=1, keepdims=True),
                jnp.sum(top, axis=1, keepdims=True),
            ]
        )

    for_groups(hidden_ref.shape[0], body)


def norm_three_back(addends, hidden, stat, par, cot):
    ch = hidden.shape[0]
    rows = 32

    def part(a):
        return pl.BlockSpec((rows, a.shape[1]), lambda r: (r, 0))

    outs = [struct((ch, HW), F32), struct((ch, HW), BF), struct((ch, 128), F32)]
    ins = (*addends, hidden, stat, par, cot)
    return pl.pallas_call(
        functools.partial(norm_three_back_kernel, len(addends)),
        grid=(ch // rows,),
        out_shape=outs,
        in_specs=[part(a) for a in ins],
        out_specs=[part(a) for a in outs],
        compiler_params=params(),
        cost_estimate=cost(20 * ch * HW, 16 * ch * HW),
        name="norm_three_back",
    )(*ins)


def piece_columns(meta, w_ref, pieces):
    first = meta[0]
    acc = None
    for x_ref in pieces:
        rows = x_ref.shape[0]
        term = dot(w_ref[:, pl.ds(pl.multiple_of(first, rows), rows)], x_ref[...])
        acc = term if acc is None else acc + term
        first = w_ref.shape[1] - rows - first
    return acc


def inputs_kernel(n, meta, w_ref, *refs):
    pieces, (bias_ref, out_ref) = refs[:n], refs[n:]
    out_ref[...] = (piece_columns(meta, w_ref, pieces) + bias_ref[...]).astype(BF)


def inputs_product(meta, weight, pieces, bias, width=1024, name=None):
    rows, depth = weight.shape
    return pl.pallas_call(
        functools.partial(inputs_kernel, len(pieces)),
        grid=(HW // width,),
        out_shape=struct((rows, HW), BF),
        in_specs=[scalars(), pl.BlockSpec((rows, depth), lambda p: (0, 0))]
        + [pl.BlockSpec((x.shape[0], width), lambda p: (0, p)) for x in pieces]
        + [pl.BlockSpec((rows, 1), lambda p: (0, 0))],
        out_specs=pl.BlockSpec((rows, width), lambda p: (0, p)),
        compiler_params=params(),
        cost_estimate=cost(2 * rows * depth * HW, (rows + depth) * HW * 2),
        name=name,
    )(meta, weight, *pieces, bias)


def parts_kernel(n, meta, w_ref, *refs):
    pieces, outs = refs[:n], refs[n:]
    first = meta[0]
    for out_ref in outs:
        rows = out_ref.shape[0]
        row = pl.ds(pl.multiple_of(first, rows), rows)
        acc = None
        at = 0
        for x_ref in pieces:
            depth = x_ref.shape[0]
            term = dot(w_ref[row, at : at + depth], x_ref[...])
            acc = term if acc is None else acc + term
            at += depth
        out_ref[...] = acc.astype(BF)
        first = w_ref.shape[0] - rows - first


def parts_product(meta, weight, pieces, count, width=1024, name=None):
    rows, depth = weight.shape
    part = struct((rows // count, HW), BF)
    return pl.pallas_call(
        functools.partial(parts_kernel, len(pieces)),
        grid=(HW // width,),
        out_shape=[part] * count,
        in_specs=[scalars(), pl.BlockSpec((rows, depth), lambda p: (0, 0))]
        + [pl.BlockSpec((x.shape[0], width), lambda p: (0, p)) for x in pieces],
        out_specs=[pl.BlockSpec((rows // count, width), lambda p: (0, p))] * count,
        compiler_params=params(),
        cost_estimate=cost(2 * rows * depth * HW, (rows + depth) * HW * 2),
        name=name,
    )(meta, weight, *pieces)


def output_kernel(n, meta, w_ref, *refs):
    pieces, (bias_ref, hidden_ref, out_ref) = refs[:n], refs[n:]
    acc = hidden_ref[...] + bias_ref[...] + piece_columns(meta, w_ref, pieces)
    half = acc.shape[1] // 2
    for base, val in zip((0, HW // 2), unfold(acc)):
        first = pl.multiple_of(base + pl.program_id(0) * half, half)
        out_ref[:, pl.ds(first, half)] = val.astype(BF)


def output_product(meta, weight, pieces, bias, hidden, width=1024):
    rows, depth = weight.shape
    return pl.pallas_call(
        functools.partial(output_kernel, len(pieces)),
        grid=(HW // width,),
        out_shape=struct((rows, HW), BF),
        in_specs=[scalars(), pl.BlockSpec((rows, depth), lambda p: (0, 0))]
        + [pl.BlockSpec((x.shape[0], width), lambda p: (0, p)) for x in pieces]
        + [
            pl.BlockSpec((rows, 1), lambda p: (0, 0)),
            pl.BlockSpec((rows, width), lambda p: (0, p)),
        ],
        out_specs=pl.BlockSpec((rows, HW), lambda p: (0, 0)),
        compiler_params=params(),
        cost_estimate=cost(2 * rows * depth * HW, (rows * 3 + depth) * HW * 2),
        name="output",
    )(meta, weight, *pieces, bias, hidden)


def outer_kernel(n_left, n_right, meta, *refs):
    lefts, rights = refs[:n_left], refs[n_left : n_left + n_right]
    out_ref, sums_ref = refs[n_left + n_right : n_left + n_right + 2]
    acc_ref, tot_ref = refs[n_left + n_right + 2 :]
    step = pl.program_id(0)

    @pl.when(step == 0)
    def _():
        acc_ref[...] = jnp.zeros_like(acc_ref)
        tot_ref[...] = jnp.zeros_like(tot_ref)

    row = 0
    for left in lefts:
        rows = left.shape[0]
        val = left[...]
        first = meta[0]
        for right in rights:
            cols = right.shape[0]
            at = pl.ds(pl.multiple_of(first, cols), cols)
            acc_ref[row : row + rows, at] += dot_nt(val, right[...])
            first = acc_ref.shape[1] - cols - first
        tot_ref[row : row + rows, :] += jnp.sum(val.astype(F32), axis=1, keepdims=True)
        row += rows

    @pl.when(step == pl.num_programs(0) - 1)
    def _():
        out_ref[...] = acc_ref[...].astype(BF)
        sums_ref[...] = tot_ref[...]


def outer(meta, lefts, rights, width=1024, name=None):
    rows, cols = sum(a.shape[0] for a in lefts), sum(a.shape[0] for a in rights)
    fixed = lambda p: (0, 0)
    return pl.pallas_call(
        functools.partial(outer_kernel, len(lefts), len(rights)),
        grid=(HW // width,),
        out_shape=[struct((rows, cols), BF), struct((rows, 128), F32)],
        in_specs=[scalars()]
        + [pl.BlockSpec((a.shape[0], width), lambda p: (0, p)) for a in (*lefts, *rights)],
        out_specs=[pl.BlockSpec((rows, cols), fixed), pl.BlockSpec((rows, 128), fixed)],
        scratch_shapes=[pltpu.VMEM((rows, cols), F32), pltpu.VMEM((rows, 128), F32)],
        compiler_params=params(),
        cost_estimate=cost(2 * rows * cols * HW, (rows + cols) * HW * 2),
        name=name,
    )(meta, *lefts, *rights)


def attention_kernel(
    n_grads, lim_ref, q_ref, k_ref, v_ref, kc_ref, vc_ref, *refs, unroll, back,
):
    g_refs, refs = refs[:n_grads], refs[n_grads:]
    o_ref, dq_ref, dk_ref, dv_ref, dkc_ref, dvc_ref = refs[:6]
    kt, vt, kn, vn, s_even, s_odd, p_sc, tops, o_acc, dk_acc, dv_acc = refs[6:]
    step, last = pl.program_id(1), pl.num_programs(1) - 1
    width = q_ref.shape[-1]
    blocks = KEYS // BLOCK

    @pl.when(step == 0)
    def _():
        spare = jnp.zeros((HEAD_DIM, KEYS - HW - CTXP), BF)
        for ref, own, ctx in ((kn, k_ref, kc_ref), (vn, v_ref, vc_ref)):
            ref[:, :HW] = own[0, 0]
            ref[:, HW : HW + CTXP] = ctx[0, 0]
            ref[:, HW + CTXP :] = spare
        row = lax.broadcasted_iota(jnp.int32, (HEAD_DIM, BLOCK), 0)
        for n in range(blocks):
            at = slice(n * BLOCK, (n + 1) * BLOCK)
            key = lax.broadcasted_iota(jnp.int32, (HEAD_DIM, BLOCK), 1) + n * BLOCK
            fill = jnp.where((row == 0) & (key >= HW + lim_ref[0]), NEG_FILL, 0.0)
            kt[at, :] = jnp.concatenate([kn[:, at].astype(F32), fill], 0).T.astype(BF)
            vt[at, :] = jnp.concatenate([vn[:, at].astype(F32), jnp.zeros_like(fill)], 0).T.astype(BF)
        dk_acc[...] = jnp.zeros_like(dk_acc)
        dv_acc[...] = jnp.zeros_like(dv_acc)

    def keys_at(n):
        return pl.ds(pl.multiple_of(n * BLOCK, BLOCK), BLOCK)

    scale = HEAD_DIM ** (-0.5)
    q = (q_ref[0, 0].astype(F32) * scale).astype(BF)
    one = jnp.where(lax.broadcasted_iota(jnp.int32, (HEAD_DIM, width), 0) == 0, 1.0, 0.0).astype(BF)
    q_more = jnp.concatenate([q, one], 0)

    def score(n, held):
        scores = dot(kt[keys_at(n), :], q_more)
        held[...] = scores
        return jnp.max(jnp.max(scores.reshape(BLOCK // 8, 8, width), axis=0), axis=0, keepdims=True)

    o_acc[...] = jnp.zeros_like(o_acc)

    def forward(n, held, top, total, shrink):
        raised = jnp.exp(held[...] - top)
        low = raised.astype(BF)
        p_sc[keys_at(n), :] = low
        tops[n, 0:1, :] = top
        sums = jnp.sum(raised.reshape(BLOCK // 8, 8, width), axis=0)
        o_acc[...] = o_acc[...] * shrink + dot(vn[:, keys_at(n)], low)
        return total * shrink + sums

    def forward_step(n, held, ahead_held, carry):
        top, total, shrink = carry
        ahead = jnp.maximum(top, score(n + 1, ahead_held))
        total = forward(n, held, top, total, shrink)
        return ahead, total, jnp.exp(top - ahead)

    held = (s_even, s_odd)

    def forward_run(j, carry):
        for u in range(unroll):
            carry = forward_step(unroll * j + u, held[u % 2], held[1 - u % 2], carry)
        return carry

    carry = (score(0, s_even), jnp.zeros((8, width), F32), jnp.ones((1, width), F32))
    carry = lax.fori_loop(0, blocks // unroll - 1, forward_run, carry)
    for n in range(blocks - unroll, blocks - 1):
        carry = forward_step(n, held[n % 2], held[1 - n % 2], carry)
    top, total, shrink = carry
    total = forward(blocks - 1, s_odd, top, total, shrink)

    inverse = 1.0 / jnp.sum(total, axis=0, keepdims=True)
    mixed = o_acc[...] * inverse
    o_ref[0] = mixed.astype(BF)
    grad = sum(g_ref[0].astype(F32) for g_ref in g_refs)
    if n_grads > 1:
        grad = grad.astype(BF).astype(F32)
    delta = jnp.sum(grad * mixed, axis=0, keepdims=True)
    dq = jnp.zeros((HEAD_DIM, width), F32)
    none = jnp.zeros((HEAD_DIM, width), BF)
    for c in range(0, KEYS, back):
        at = slice(c, c + back)
        slopes = []
        for n in range(c // BLOCK, (c + back) // BLOCK):
            sub = slice(n * BLOCK, (n + 1) * BLOCK)
            factor = inverse * jnp.exp(tops[n, 0:1, :] - top)
            grad_low = (grad * factor).astype(BF)
            both = jnp.concatenate([grad_low, none], 0)
            probs = p_sc[sub, :]
            slope = (dot(vt[sub, :], both) - delta * factor).astype(BF) * probs
            slopes.append(slope)
            dv_acc[:, sub] += dot_nt(grad_low, probs)
        slope = jnp.concatenate(slopes, 0)
        dq = dq + dot(kn[:, at], slope)
        dk_acc[:, at] += dot_nt(q, slope)
    dq_ref[0] = (dq * scale).astype(BF)

    @pl.when(step == last)
    def _():
        dk_ref[0] = dk_acc[:, :HW].astype(BF)
        dv_ref[0] = dv_acc[:, :HW].astype(BF)
        dkc_ref[0] = dk_acc[:, HW : HW + CTXP].astype(BF)
        dvc_ref[0] = dv_acc[:, HW : HW + CTXP].astype(BF)


def attention(limit, qkv, ctx_kv, grads, width=1024, unroll=6, back=512):
    heads = qkv.shape[1]
    keys = KEYS

    def part(t, w, moving):
        return pl.BlockSpec(
            (1, 1, HEAD_DIM, w), (lambda h, i: (t, h, 0, i)) if moving else (lambda h, i: (t, h, 0, 0))
        )

    def row(w, moving):
        return pl.BlockSpec(
            (1, HEAD_DIM, w), (lambda h, i: (h, 0, i)) if moving else (lambda h, i: (h, 0, 0))
        )

    big, small = struct((heads, HEAD_DIM, HW), BF), struct((heads, HEAD_DIM, CTXP), BF)
    return pl.pallas_call(
        functools.partial(attention_kernel, len(grads), unroll=unroll, back=back),
        grid=(heads, HW // width),
        in_specs=[
            pl.BlockSpec(memory_space=pltpu.SMEM),
            part(0, width, True),
            part(1, HW, False),
            part(2, HW, False),
            part(0, CTXP, False),
            part(1, CTXP, False),
        ]
        + [row(width, True)] * len(grads),
        out_specs=[
            row(width, True),
            row(width, True),
            row(HW, False),
            row(HW, False),
            row(CTXP, False),
            row(CTXP, False),
        ],
        out_shape=[big, big, big, big, small, small],
        scratch_shapes=[
            pltpu.VMEM((keys, 2 * HEAD_DIM), BF),
            pltpu.VMEM((keys, 2 * HEAD_DIM), BF),
            pltpu.VMEM((HEAD_DIM, keys), BF),
            pltpu.VMEM((HEAD_DIM, keys), BF),
            pltpu.VMEM((BLOCK, width), F32),
            pltpu.VMEM((BLOCK, width), F32),
            pltpu.VMEM((keys, width), BF),
            pltpu.VMEM((keys // BLOCK, 8, width), F32),
            pltpu.VMEM((HEAD_DIM, width), F32),
            pltpu.VMEM((HEAD_DIM, keys), F32),
            pltpu.VMEM((HEAD_DIM, keys), F32),
        ],
        compiler_params=params(dimension_semantics=("arbitrary", "arbitrary")),
        cost_estimate=cost(
            24 * heads * HW * keys * HEAD_DIM, heads * HEAD_DIM * 8 * HW * 2, heads * HW * keys
        ),
        name="attention",
    )(limit, qkv, qkv, qkv, ctx_kv, ctx_kv, *grads)


class Alone:
    parts = 1

    def __init__(self, mesh):
        self.images = mesh.shape["dp"]

    def meta(self):
        return jnp.array([0, 1], jnp.int32)

    def image(self):
        return lax.axis_index("dp")

    def got(self, x):
        return x

    def pick(self, own, got):
        return own

    def gather(self, x):
        return (lax.all_gather(x, "tensor", axis=0, tiled=True),)

    def scatter(self, parts):
        return (lax.psum_scatter(parts[0], "tensor", scatter_dimension=0, tiled=True),)

    def turn(self, meta, w):
        ch = w.shape[0]
        cut = w.reshape(ch, 9, C)
        turned = lax.all_to_all(cut, "tensor", split_axis=2, concat_axis=0, tiled=True)
        return turned[:, ::-1].transpose(2, 1, 0).reshape(ch, 9 * C)

    def total(self, x):
        return lax.psum(x, "dp")

    def everywhere(self, x):
        return lax.psum(x, "dp")

    def sum_owned(self, x):
        return lax.psum(x, "dp")


class Paired:
    parts = 2

    def __init__(self, mesh):
        dp = mesh.shape["dp"]
        self.images = dp
        self.far = [
            ((2 * k + core) * 2 + 1 - core, (2 * k + 1 - core) * 2 + core)
            for k in range(dp // 2)
            for core in range(2)
        ]
        self.bits = [1 << b for b in range((dp - 1).bit_length())]

    def half(self):
        return lax.axis_index("dp") % 2

    def stays(self):
        return self.half() == lax.axis_index("tensor")

    def meta(self):
        return jnp.stack([self.half() * (C // 2), self.stays().astype(jnp.int32)]).astype(jnp.int32)

    def image(self):
        return lax.axis_index("dp") // 2 * 2 + lax.axis_index("tensor")

    def got(self, x):
        return lax.ppermute(x, ("dp", "tensor"), self.far)

    def pick(self, own, got):
        return jnp.where(self.stays(), own, got)

    def over(self, x, bit):
        return lax.ppermute(x, "dp", [(i, i ^ bit) for i in range(self.images)])

    def gather(self, x):
        return (x, self.over(x, 1))

    def scatter(self, parts):
        return (parts[0], self.over(parts[1], 1))

    def turn(self, meta, w):
        return turned_pair(meta, w, self.over(w, 1))

    def total(self, x):
        x = x + lax.ppermute(x, "tensor", [(0, 1), (1, 0)])
        for bit in self.bits[1:]:
            x = x + self.over(x, bit)
        return self.pick(x, self.over(x, 1))

    def everywhere(self, x):
        for bit in self.bits:
            x = x + self.over(x, bit)
        return x

    def sum_owned(self, x):
        rows = x.shape[0] // 2
        done = []
        for at, order in enumerate((self.bits, [self.bits[0], *self.bits[2:], self.bits[1]])):
            part = lax.slice_in_dim(x, at * rows, (at + 1) * rows)
            size = rows
            for bit in order:
                size //= 2
                upper = (lax.axis_index("dp") // bit) % 2
                keep = lax.dynamic_slice_in_dim(part, upper * size, size)
                send = lax.dynamic_slice_in_dim(part, (1 - upper) * size, size)
                part = (keep.astype(F32) + self.over(send, bit).astype(F32)).astype(BF)
            for bit in reversed(order):
                upper = (lax.axis_index("dp") // bit) % 2
                other = self.over(part, bit)
                part = jnp.where(
                    upper == 0,
                    jnp.concatenate([part, other]),
                    jnp.concatenate([other, part]),
                )
            done.append(part)
        return jnp.concatenate(done)


def after(first, *later):
    held = lax.optimization_barrier((first, *later))
    return held[1:] if len(later) > 1 else held[1]


def local(plan, features, cotangent, embedding, context, lengths, norm1_gain, norm1_bias,
    conv1_weight, conv1_bias, emb_weight, emb_bias, norm2_gain, norm2_bias, conv2_weight,
    conv2_bias, norm3_gain, norm3_bias, qkv_weight, qkv_bias, context_weight, context_bias,
    out_weight, out_bias,
):
    ch, images, pixels = features.shape
    heads = ch // HEAD_DIM
    meta = plan.meta()
    moved = plan.parts == 2

    emb_act = jax.nn.silu(embedding.astype(F32)).astype(BF)
    scale_shift = (
        jnp.einsum("ie,teo->to", emb_act, emb_weight, preferred_element_type=F32) + emb_bias
    )
    length_row = jnp.broadcast_to(lengths.astype(F32)[:, None], (1, ch))
    vectors = jnp.concatenate(
        [
            jnp.stack([norm1_gain, norm1_bias, conv1_bias, norm2_gain, norm2_bias]),
            scale_shift,
            jnp.stack([conv2_bias, norm3_gain, norm3_bias, out_bias]),
            qkv_bias,
            length_row,
        ]
    )
    f_own = features.reshape(ch, pixels)
    f_got = plan.got(f_own)
    vectors, w1_own = after(scale_shift, vectors, conv1_weight)
    vectors = plan.pick(vectors, plan.got(vectors))
    w1_got = plan.got(w1_own)
    ctx_kv = (
        jnp.einsum("toe,ne->ton", context_weight, context[0], preferred_element_type=F32)
        + context_bias[:, :, None]
    ).astype(BF)
    ctx_kv = jnp.pad(ctx_kv, ((0, 0), (0, 0), (0, CTXP - CTX)))
    emb_all = jnp.where(
        jnp.arange(plan.images)[:, None] == lax.axis_index("dp"), emb_act, jnp.zeros_like(emb_act)
    )
    emb_all = plan.everywhere(emb_all)
    length = vectors[14, :1].astype(jnp.int32)
    par_one, par_two, par_three = vectors[0:2].T, vectors[2:7].T, vectors[7:10].T
    w2_got = plan.got(after(vectors, conv2_weight))
    act_one, stat_one, f_low = first_activation(meta, f_own, f_got, par_one)
    full_one = plan.gather(act_one)
    mats_own = jnp.concatenate([qkv_weight.reshape(3 * ch, C), out_weight])
    mats_own, ctx_own, cot_own = after(
        full_one[-1], mats_own, ctx_kv, cotangent.reshape(ch, pixels)
    )
    mats_got, ctx_got = plan.got(mats_own), plan.got(ctx_own)
    cot_got = plan.got(cot_own)

    par_two = after(emb_all, par_two)
    low, stat, wide = struct((ch, HW), BF), struct((ch, 128), F32), struct((ch, HW), F32)
    weight = struct((ch, 9 * C), BF)
    act_two, stat_two, conv_one, w1 = conv_call(
        conv_one_kernel, meta, (conv1_weight, w1_got), full_one, (par_two,), (),
        [low, stat], [wide, weight], [], "conv_one",
    )
    full_two = plan.gather(act_two)
    normed, stat_three, hidden, w2 = conv_call(
        conv_two_kernel, meta, (conv2_weight, w2_got), full_two, (par_three, f_low), (),
        [low, stat], [wide, weight], [], "conv_two",
    )
    full_three = plan.gather(normed)
    mats_got, ctx_got, cot_got = after(normed, mats_got, ctx_got, cot_got)
    mats = plan.pick(mats_own, mats_got)
    w_qkv, w_out = mats[: 3 * ch], mats[3 * ch :]
    cot = folded(meta, cot_own, cot_got)
    grad_heads = plan.scatter(
        parts_product(meta, w_out.T, (cot,), plan.parts, name="grad_heads")
    )
    qkv = inputs_product(meta, w_qkv, full_three, vectors[11:14].reshape(3 * ch, 1), name="qkv")
    ctx_kv = plan.pick(ctx_own, ctx_got)
    mixed, dq, dk, dv, dkc, dvc = attention(
        4 + length,
        qkv.reshape(3, heads, HEAD_DIM, HW),
        ctx_kv.reshape(2, heads, HEAD_DIM, CTXP),
        [a.reshape(heads, HEAD_DIM, HW) for a in grad_heads],
    )

    flat = lambda a: a.reshape(ch, HW)
    dq, dk, dv = flat(dq), flat(dk), flat(dv)
    addends = plan.scatter(
        parts_product(meta, w_qkv.T, (dq, dk, dv), plan.parts, name="grad_normed")
    )
    full_heads = plan.gather(flat(mixed))
    ctx_own = jnp.concatenate([a.reshape(1, ch, CTXP) for a in (dkc, dvc)])
    ctx_got = plan.got(ctx_own)
    turned_two = plan.turn(meta, after(mixed, w2))
    dw_qkv, db_qkv = outer(meta, (dq, dk, dv), full_three, name="qkv_grad")
    dw_out, _ = outer(meta, (cot,), full_heads, name="out_grad")
    mats_own = jnp.concatenate([dw_qkv, dw_out])
    mats_got = plan.got(mats_own)
    grad_hidden, grad_two, sums_three = norm_three_back(addends, hidden, stat_three, par_three, cot)
    full_grad_two = plan.gather(grad_two)
    dw_two = conv_weight_grad(meta, grad_two, full_two, "conv_two_weight_grad")
    two_got = plan.got(dw_two)
    ctx_grad = plan.pick(ctx_own, ctx_got)[:, :, :CTX]
    dw_ctx = jnp.einsum("ton,ne->toe", ctx_grad, context[0], preferred_element_type=F32).astype(BF)
    full_grad_two = after(dw_two, *full_grad_two) if moved else full_grad_two
    grad_one, sums_two = conv_call(
        conv_two_back_kernel, meta, (turned_two, turned_two), full_grad_two, (par_two, stat_two),
        (conv_one,), [low, stat], [], [pltpu.VMEM((ch, HW), F32)], "conv_two_back",
    )
    full_grad_one = plan.gather(grad_one)
    turned_one = plan.turn(meta, after(mixed, w1))
    mats = plan.pick(mats_own, mats_got)
    dw_two = plan.pick(dw_two, after(grad_one, two_got))
    early = jnp.concatenate(
        [dw_ctx[0], dw_ctx[1], *(mats[t * ch : (t + 1) * ch] for t in range(4)), dw_two], 1
    )
    held = after(early, grad_one)
    early = lax.psum_scatter(early, "dp", scatter_dimension=0, tiled=True)
    dw_one = conv_weight_grad(meta, held, full_one, "conv_one_weight_grad")
    one_got = plan.got(dw_one)
    full_grad_one = after(dw_one, *full_grad_one) if moved else full_grad_one
    input_grad, sums_one = conv_call(
        conv_one_back_kernel, meta, (turned_one, turned_one), full_grad_one,
        (par_one, stat_one, f_low), (grad_hidden,),
        [struct((ch, HW), BF if moved else F32), stat], [],
        [pltpu.VMEM((ch, HW), F32)], "conv_one_back",
    )
    input_got = plan.got(input_grad)

    output = output_product(
        meta, w_out, full_heads, vectors[10].reshape(ch, 1), after(input_grad, hidden)
    )
    output_got = plan.got(output)
    early, dw_one, one_got, sums_one = after((output, input_got), early, dw_one, one_got, sums_one)
    dw_one, one_got, sums_one = after(early, dw_one, one_got, sums_one)
    early = lax.all_gather(early, "dp", axis=0, tiled=True)
    dw_one = plan.sum_owned(plan.pick(dw_one, one_got))
    ctx_sums = jnp.sum(ctx_own.astype(F32), axis=2)
    sums_two = sums_two[:, :5].T
    own_mod = sums_two[2:4].astype(BF).astype(F32)
    mods = jnp.where(
        (jnp.arange(plan.images) == plan.image())[:, None, None], own_mod, jnp.zeros_like(own_mod)
    ).reshape(2 * plan.images, ch)
    small = plan.total(
        jnp.concatenate(
            [
                sums_three[:, :4].T,
                db_qkv[:, 0].reshape(3, ch),
                sums_two[:2],
                sums_two[4:5],
                ctx_sums,
                sums_one[:, :2].T,
                mods,
            ]
        )
    )
    mods = small[14:].reshape(plan.images, 2, ch)
    mods_low = mods.astype(BF)
    dw_emb = jnp.stack(
        [
            jnp.einsum("ie,io->eo", emb_all, mods_low[:, t], preferred_element_type=F32)
            for t in range(2)
        ]
    )
    input_grad = plan.pick(input_grad, input_got).astype(F32)
    output = plan.pick(output, output_got)
    early = after((dw_one, small, input_grad), early)
    dw_ctx = jnp.stack([early[:, n * CTX_EMB : (n + 1) * CTX_EMB] for n in range(2)])
    first = 2 * CTX_EMB
    mats = [early[:, first + n * C : first + (n + 1) * C].astype(F32) for n in range(4)]
    dw_two = early[:, first + 4 * C :]

    return (
        output.reshape(ch, images, pixels),
        input_grad.reshape(ch, images, pixels),
        small[12],
        small[13],
        dw_one.astype(F32),
        small[9],
        dw_emb,
        jnp.sum(mods, axis=0),
        small[7],
        small[8],
        dw_two.astype(F32),
        small[2],
        small[0],
        small[1],
        jnp.stack(mats[:3]),
        small[4:7],
        dw_ctx.astype(F32),
        small[10:12],
        mats[3],
        small[3],
    )


def solution(mesh):
    paired = mesh.shape["tensor"] == 2 and mesh.shape["dp"] % 2 == 0
    plan = Paired(mesh) if paired else Alone(mesh)
    specs = (
        P("tensor", "dp", None),
        P("tensor", "dp", None),
        P("dp", None),
        P("dp", None, None),
        P("dp"),
        P("tensor"),
        P("tensor"),
        P("tensor", None),
        P("tensor"),
        P(None, None, "tensor"),
        P(None, "tensor"),
        P("tensor"),
        P("tensor"),
        P("tensor", None),
        P("tensor"),
        P("tensor"),
        P("tensor"),
        P(None, "tensor", None),
        P(None, "tensor"),
        P(None, "tensor", None),
        P(None, "tensor"),
        P("tensor", None),
        P("tensor"),
    )
    return jax.shard_map(
        functools.partial(local, plan),
        mesh=mesh,
        in_specs=specs,
        out_specs=(
            P("tensor", "dp", None),
            P("tensor", "dp", None),
            P("tensor"),
            P("tensor"),
            P("tensor", None),
            P("tensor"),
            P(None, None, "tensor"),
            P(None, "tensor"),
            P("tensor"),
            P("tensor"),
            P("tensor", None),
            P("tensor"),
            P("tensor"),
            P("tensor"),
            P(None, "tensor", None),
            P(None, "tensor"),
            P(None, "tensor", None),
            P(None, "tensor"),
            P("tensor", None),
            P("tensor"),
        ),
        check_vma=False,
    )
```

```python
import functools

import jax
import jax.numpy as jnp
from jax import lax
from jax.experimental import pallas as pl
from jax.experimental.pallas import tpu as pltpu
from jax.sharding import PartitionSpec as P

C = 512
HEAD_DIM = 64
PER_GROUP = 16
SIDE = 64
HW = 4096
CTX = 260
CTXP = 384
CTX_EMB = 2048
BLOCK = 256
KEYS = 4608
PAD = 128
FILL = 32
SCALE = 100
EPSILON = 1e-05
NEG_FILL = -1e30
F32 = jnp.float32
BF = jnp.bfloat16
NT = (((1,), (1,)), ((), ()))
VMEM_BYTES = 62 << 20


def dot(a, b):
    return jnp.dot(a, b, preferred_element_type=F32)


def dot_nt(a, b):
    return lax.dot_general(a, b, NT, preferred_element_type=F32)


def whole():
    return pl.BlockSpec(memory_space=pltpu.VMEM)


def placed():
    return pl.BlockSpec(memory_space=pl.ANY)


def scalars():
    return pl.BlockSpec(memory_space=pltpu.SMEM)


def params(**kwargs):
    return pltpu.CompilerParams(vmem_limit_bytes=VMEM_BYTES, **kwargs)


def cost(flops, nbytes, transcendentals=0):
    return pl.CostEstimate(
        flops=flops // SCALE, bytes_accessed=nbytes // SCALE, transcendentals=transcendentals // SCALE
    )


def struct(shape, dtype):
    return jax.ShapeDtypeStruct(shape, dtype)


def fetch(meta, own_ref, got_ref, buf, sem):
    @pl.when(meta[1] == 1)
    def _():
        pltpu.make_async_copy(own_ref, buf, sem).start()

    @pl.when(meta[1] != 1)
    def _():
        pltpu.make_async_copy(got_ref, buf, sem).start()


def arrive(own_ref, buf, sem):
    pltpu.make_async_copy(own_ref, buf, sem).wait()


def group_scalar(column):
    return jnp.sum(column, axis=0, keepdims=True) * (1.0 / (PER_GROUP * HW))


def group_stats(vals):
    mean = group_scalar(jnp.sum(vals, axis=1, keepdims=True))
    centred = vals - mean
    var = group_scalar(jnp.sum(centred * centred, axis=1, keepdims=True))
    rstd = lax.rsqrt(var + EPSILON)
    return mean, rstd


def norm_backward(dy_sum, dyx_sum, gain):
    return group_scalar(dy_sum * gain), group_scalar(dyx_sum * gain)


def for_groups(channels, body, together=2):
    def step(g, carry):
        for u in range(together):
            first = pl.multiple_of((g * together + u) * PER_GROUP, PER_GROUP)
            body(pl.ds(first, PER_GROUP))
        return carry

    lax.fori_loop(0, channels // PER_GROUP // together, step, 0)


def columns(values):
    lane = lax.broadcasted_iota(jnp.int32, (PER_GROUP, 128), 1)
    tile = jnp.zeros((PER_GROUP, 128), F32)
    for at, val in enumerate(values):
        tile = jnp.where(lane == at, val, tile)
    return tile


ROWS = SIDE // 2


def lanes(x, n):
    return x[:, 128 * n : 128 * n + 128]


def low_lanes(x):
    return lax.broadcasted_iota(jnp.int32, (x.shape[0], 128), 1) < SIDE


def fold(x):
    low = low_lanes(x)
    out = []
    for r in range(ROWS):
        upper, lower = lanes(x, r // 2), lanes(x, r // 2 + ROWS // 2)
        if r % 2 == 0:
            out.append(jnp.where(low, upper, pltpu.roll(lower, SIDE, 1)))
        else:
            out.append(jnp.where(low, pltpu.roll(upper, SIDE, 1), lower))
    return jnp.concatenate(out, 1)


def unfold(x):
    low = low_lanes(x)
    pairs = range(x.shape[1] // 256)
    top = [jnp.where(low, lanes(x, 2 * n), pltpu.roll(lanes(x, 2 * n + 1), SIDE, 1)) for n in pairs]
    bottom = [
        jnp.where(low, pltpu.roll(lanes(x, 2 * n), SIDE, 1), lanes(x, 2 * n + 1)) for n in pairs
    ]
    return jnp.concatenate(top, 1), jnp.concatenate(bottom, 1)


def fold_kernel(meta, own_ref, got_ref, out_ref, x_buf, sem):
    fetch(meta, own_ref, got_ref, x_buf, sem)
    arrive(own_ref, x_buf, sem)

    def body(rows):
        out_ref[rows, :] = fold(x_buf[rows, :].astype(F32)).astype(BF)

    for_groups(out_ref.shape[0], body)


def folded(meta, own, got):
    return pl.pallas_call(
        fold_kernel,
        out_shape=struct(own.shape, BF),
        in_specs=[scalars(), placed(), placed()],
        out_specs=whole(),
        scratch_shapes=[pltpu.VMEM(own.shape, BF), pltpu.SemaphoreType.DMA(())],
        compiler_params=params(),
        cost_estimate=cost(8 * own.size, 4 * own.size),
        name="fold",
    )(meta, own, got)


def act_one_kernel(meta, own_ref, got_ref, par_ref, act_ref, stat_ref, fold_ref, x_buf, sem):
    fetch(meta, own_ref, got_ref, x_buf, sem)
    arrive(own_ref, x_buf, sem)

    def body(rows):
        vals = fold(x_buf[rows, :].astype(F32))
        fold_ref[rows, :] = vals.astype(BF)
        mean, rstd = group_stats(vals)
        par = par_ref[rows, :]
        out = (vals - mean) * (rstd * par[:, 0:1]) + par[:, 1:2]
        act_ref[rows, :] = (out * jax.nn.sigmoid(out)).astype(BF)
        stat_ref[rows, :] = columns([mean, rstd])

    for_groups(act_ref.shape[0], body)


def first_activation(meta, own, got, par):
    ch = own.shape[0]
    return pl.pallas_call(
        act_one_kernel,
        out_shape=[struct((ch, HW), BF), struct((ch, 128), F32), struct((ch, HW), BF)],
        in_specs=[scalars(), placed(), placed(), whole()],
        out_specs=[whole()] * 3,
        scratch_shapes=[pltpu.VMEM((ch, HW), BF), pltpu.SemaphoreType.DMA(())],
        compiler_params=params(),
        cost_estimate=cost(20 * ch * HW, 6 * ch * HW, ch * HW),
        name="act_one",
    )(meta, own, got, par)


def fill_shifted(xs, pieces, first):
    start = first
    for x_ref in pieces:
        rows = x_ref.shape[0]

        def step(r, carry, x_ref=x_ref, start=start):
            off = pl.multiple_of(r * FILL, FILL)
            at = pl.ds(pl.multiple_of(start + off, FILL), FILL)
            lane = lax.broadcasted_iota(jnp.int32, (FILL, 128), 1)
            low = lane < SIDE
            left, right = lane % SIDE == 0, lane % SIDE == SIDE - 1
            zero = jnp.zeros((FILL, 128), F32)
            here = pl.ds(off, FILL)
            for n in range(ROWS):
                x = x_ref[here, 128 * n : 128 * n + 128].astype(F32)
                kinds = (
                    jnp.where(left, zero, pltpu.roll(x, 1, 1)),
                    x,
                    jnp.where(right, zero, pltpu.roll(x, 127, 1)),
                )
                for d, y in enumerate(kinds):
                    xs[d, at, PAD + 128 * n : PAD + 128 * n + 128] = y.astype(BF)
                    if n == ROWS - 1:
                        xs[d, at, :PAD] = jnp.where(low, zero, pltpu.roll(y, SIDE, 1)).astype(BF)
                    if n == 0:
                        xs[d, at, PAD + HW :] = jnp.where(
                            low, pltpu.roll(y, SIDE, 1), zero
                        ).astype(BF)
            return carry

        lax.fori_loop(0, rows // FILL, step, 0)
        start = xs.shape[1] - rows - start if len(pieces) == 2 else start + rows


def window(xs, tap, start, width):
    first = PAD + start + (tap // 3 - 1) * 128
    if not isinstance(start, int):
        first = pl.multiple_of(first, 128)
    return xs[tap % 3, :, pl.ds(first, width)]


def convolve(xs, w_ref, out_ref, add, width=1024):
    depth = xs.shape[1]

    def step(n, carry):
        p = n * width
        acc = dot(w_ref[:, :depth], window(xs, 0, p, width))
        for tap in range(1, 9):
            acc = acc + dot(w_ref[:, tap * depth : (tap + 1) * depth], window(xs, tap, p, width))
        at = pl.ds(pl.multiple_of(p, width), width)
        out_ref[:, at] = add(acc, at)
        return carry

    lax.fori_loop(0, HW // width, step, 0)


def conv_call(kernel, meta, weights, pieces, vmem_in, any_in, outs, any_outs, scratch, name):
    out_ch, depth = weights[0].shape[0], C
    arrays = (weights[0], *pieces, *vmem_in, *any_in)
    nbytes = sum(a.size * a.dtype.itemsize for a in arrays) + out_ch * HW * 4
    return pl.pallas_call(
        functools.partial(kernel, len(pieces)),
        out_shape=[*outs, *any_outs],
        in_specs=[scalars(), placed(), placed()]
        + [whole()] * (len(pieces) + len(vmem_in))
        + [placed()] * len(any_in),
        out_specs=[whole()] * len(outs) + [placed()] * len(any_outs),
        scratch_shapes=[
            pltpu.VMEM((3, depth, HW + 2 * PAD), BF),
            pltpu.VMEM((out_ch, 9 * depth), BF),
            pltpu.VMEM((out_ch, HW), F32),
            pltpu.SemaphoreType.DMA((4,)),
            *scratch,
        ],
        compiler_params=params(),
        cost_estimate=cost(2 * out_ch * 9 * depth * HW, nbytes, out_ch * HW),
        name=name,
    )(meta, *weights, *pieces, *vmem_in, *any_in)


def conv_one_kernel(n, meta, w_own, w_got, *refs):
    pieces, refs = refs[:n], refs[n:]
    par_ref, act_ref, stat_ref, conv_ref, w_ref, xs, w_buf, acc, sems = refs
    fetch(meta, w_own, w_got, w_buf, sems.at[0])
    fill_shifted(xs, pieces, meta[0])
    arrive(w_own, w_buf, sems.at[0])
    keep = pltpu.make_async_copy(w_buf, w_ref, sems.at[2])
    keep.start()
    bias = par_ref[:, 0:1]
    convolve(xs, w_buf, acc, lambda val, at: val + bias)
    store = pltpu.make_async_copy(acc, conv_ref, sems.at[1])
    store.start()

    def body(rows):
        vals = acc[rows, :]
        mean, rstd = group_stats(vals)
        par = par_ref[rows, :]
        gain, shift, factor = par[:, 1:2], par[:, 2:3], 1.0 + par[:, 3:4]
        mid = (vals - mean) * (rstd * gain * factor) + (shift * factor + par[:, 4:5])
        act_ref[rows, :] = (mid * jax.nn.sigmoid(mid)).astype(BF)
        stat_ref[rows, :] = columns([mean, rstd])

    for_groups(acc.shape[0], body)
    store.wait()
    keep.wait()


def conv_two_kernel(n, meta, w_own, w_got, *refs):
    pieces, refs = refs[:n], refs[n:]
    par_ref, f_ref, normed_ref, stat_ref, hidden_ref, w_ref, xs, w_buf, acc, sems = refs
    fetch(meta, w_own, w_got, w_buf, sems.at[0])
    fill_shifted(xs, pieces, meta[0])
    arrive(w_own, w_buf, sems.at[0])
    keep = pltpu.make_async_copy(w_buf, w_ref, sems.at[2])
    keep.start()
    bias = par_ref[:, 0:1]
    convolve(xs, w_buf, acc, lambda val, at: val + bias + f_ref[:, at].astype(F32))
    store = pltpu.make_async_copy(acc, hidden_ref, sems.at[1])
    store.start()

    def body(rows):
        vals = acc[rows, :]
        mean, rstd = group_stats(vals)
        par = par_ref[rows, :]
        normed_ref[rows, :] = ((vals - mean) * (rstd * par[:, 1:2]) + par[:, 2:3]).astype(BF)
        stat_ref[rows, :] = columns([mean, rstd])

    for_groups(acc.shape[0], body)
    store.wait()
    keep.wait()


def silu_slope(mid):
    sig = jax.nn.sigmoid(mid)
    return sig * (1.0 + mid * (1.0 - sig))


def conv_two_back_kernel(n, meta, w_own, w_got, *refs):
    pieces, refs = refs[:n], refs[n:]
    par_ref, stat_ref, conv_ref, grad_ref, sums_ref, xs, w_buf, acc, sems, conv_buf = refs
    fetch(meta, w_own, w_got, w_buf, sems.at[0])
    load = pltpu.make_async_copy(conv_ref, conv_buf, sems.at[1])
    load.start()
    fill_shifted(xs, pieces, meta[0])
    arrive(w_own, w_buf, sems.at[0])
    convolve(xs, w_buf, acc, lambda val, at: val)
    load.wait()

    def body(rows):
        par, stat = par_ref[rows, :], stat_ref[rows, :]
        gain, shift, factor = par[:, 1:2], par[:, 2:3], 1.0 + par[:, 3:4]
        rstd = stat[:, 1:2]
        hat = (conv_buf[rows, :] - stat[:, 0:1]) * rstd
        mid = hat * (gain * factor) + (shift * factor + par[:, 4:5])
        grad = acc[rows, :] * silu_slope(mid)
        total = jnp.sum(grad, axis=1, keepdims=True)
        total_hat = jnp.sum(grad * hat, axis=1, keepdims=True)
        mean_u, mean_uhat = norm_backward(total * factor, total_hat * factor, gain)
        out = ((grad * (factor * gain) - mean_u - hat * mean_uhat) * rstd).astype(BF)
        grad_ref[rows, :] = out
        bias_grad = jnp.sum(out.astype(F32), axis=1, keepdims=True)
        sums_ref[rows, :] = columns(
            [
                total_hat * factor,
                total * factor,
                total_hat * gain + total * shift,
                total,
                bias_grad,
            ]
        )

    for_groups(acc.shape[0], body)


def conv_one_back_kernel(n, meta, w_own, w_got, *refs):
    pieces, refs = refs[:n], refs[n:]
    par_ref, stat_ref, f_ref, hid_ref, grad_ref, sums_ref, xs, w_buf, acc, sems, hid_buf = refs
    fetch(meta, w_own, w_got, w_buf, sems.at[0])
    load = pltpu.make_async_copy(hid_ref, hid_buf, sems.at[1])
    load.start()
    fill_shifted(xs, pieces, meta[0])
    arrive(w_own, w_buf, sems.at[0])
    convolve(xs, w_buf, acc, lambda val, at: val)
    load.wait()

    def body(rows):
        par, stat = par_ref[rows, :], stat_ref[rows, :]
        gain, shift = par[:, 0:1], par[:, 1:2]
        rstd = stat[:, 1:2]
        hat = (f_ref[rows, :].astype(F32) - stat[:, 0:1]) * rstd
        grad = acc[rows, :] * silu_slope(hat * gain + shift)
        total = jnp.sum(grad, axis=1, keepdims=True)
        total_hat = jnp.sum(grad * hat, axis=1, keepdims=True)
        mean_u, mean_uhat = norm_backward(total, total_hat, gain)
        out = hid_buf[rows, :] + (grad * gain - mean_u - hat * mean_uhat) * rstd
        top, bottom = unfold(out)
        grad_ref[rows, : HW // 2] = top.astype(grad_ref.dtype)
        grad_ref[rows, HW // 2 :] = bottom.astype(grad_ref.dtype)
        sums_ref[rows, :] = columns([total_hat, total])

    for_groups(acc.shape[0], body)


def weight_grad_kernel(n, meta, grad_ref, *refs):
    pieces, (out_ref, gs) = refs[:n], refs[n:]
    fill_shifted(gs, (grad_ref,), 0)
    for tap in range(9):
        moved = window(gs, 8 - tap, 0, HW)
        first = meta[0]
        for x_ref in pieces:
            rows = x_ref.shape[0]
            at = pl.ds(pl.multiple_of(tap * C + first, rows), rows)
            out_ref[:, at] = dot_nt(moved, x_ref[...]).astype(BF)
            first = C - rows - first


def conv_weight_grad(meta, grad, pieces, name):
    out_ch = grad.shape[0]
    return pl.pallas_call(
        functools.partial(weight_grad_kernel, len(pieces)),
        out_shape=struct((out_ch, 9 * C), BF),
        in_specs=[scalars()] + [whole()] * (1 + len(pieces)),
        out_specs=whole(),
        scratch_shapes=[pltpu.VMEM((3, out_ch, HW + 2 * PAD), BF)],
        compiler_params=params(),
        cost_estimate=cost(2 * out_ch * 9 * C * HW, (out_ch + C) * HW * 2 + out_ch * 9 * C * 2),
        name=name,
    )(meta, grad, *pieces)


def turn_kernel(meta, own_ref, other_ref, out_ref):
    half = own_ref.shape[0]
    for tap in range(9):
        at = pl.ds(pl.multiple_of(tap * C + meta[0], half), half)
        row = meta[0]
        for ref in (own_ref, other_ref):
            to = pl.ds(pl.multiple_of((8 - tap) * C + row, half), half)
            out_ref[:, to] = ref[:, at].astype(F32).T.astype(BF)
            row = half - row


def turned_pair(meta, own, other):
    return pl.pallas_call(
        turn_kernel,
        out_shape=struct(own.shape, BF),
        in_specs=[scalars(), whole(), whole()],
        out_specs=whole(),
        compiler_params=params(),
        cost_estimate=cost(0, 3 * own.size * 2),
        name="turn",
    )(meta, own, other)


def norm_three_back_kernel(n, *refs):
    addends, (hidden_ref, stat_ref, par_ref, cot_ref, hid_ref, grad_ref, sums_ref) = (
        refs[:n],
        refs[n:],
    )

    def body(rows):
        dy = addends[0][rows, :].astype(F32)
        for extra in addends[1:]:
            dy = dy + extra[rows, :].astype(F32)
        par, stat = par_ref[rows, :], stat_ref[rows, :]
        gain, rstd = par[:, 1:2], stat[:, 1:2]
        hat = (hidden_ref[rows, :] - stat[:, 0:1]) * rstd
        total = jnp.sum(dy, axis=1, keepdims=True)
        total_hat = jnp.sum(dy * hat, axis=1, keepdims=True)
        mean_u, mean_uhat = norm_backward(total, total_hat, gain)
        top = cot_ref[rows, :].astype(F32)
        out = top + (dy * gain - mean_u - hat * mean_uhat) * rstd
        hid_ref[rows, :] = out
        low = out.astype(BF)
        grad_ref[rows, :] = low
        sums_ref[rows, :] = columns(
            [
                total_hat,
                total,
                jnp.sum(low.astype(F32), axis=1, keepdims=True),
                jnp.sum(top, axis=1, keepdims=True),
            ]
        )

    for_groups(hidden_ref.shape[0], body)


def norm_three_back(addends, hidden, stat, par, cot):
    ch = hidden.shape[0]
    rows = 32

    def part(a):
        return pl.BlockSpec((rows, a.shape[1]), lambda r: (r, 0))

    outs = [struct((ch, HW), F32), struct((ch, HW), BF), struct((ch, 128), F32)]
    ins = (*addends, hidden, stat, par, cot)
    return pl.pallas_call(
        functools.partial(norm_three_back_kernel, len(addends)),
        grid=(ch // rows,),
        out_shape=outs,
        in_specs=[part(a) for a in ins],
        out_specs=[part(a) for a in outs],
        compiler_params=params(),
        cost_estimate=cost(20 * ch * HW, 16 * ch * HW),
        name="norm_three_back",
    )(*ins)


def piece_columns(meta, w_ref, pieces):
    first = meta[0]
    acc = None
    for x_ref in pieces:
        rows = x_ref.shape[0]
        term = dot(w_ref[:, pl.ds(pl.multiple_of(first, rows), rows)], x_ref[...])
        acc = term if acc is None else acc + term
        first = w_ref.shape[1] - rows - first
    return acc


def inputs_kernel(n, meta, w_ref, *refs):
    pieces, (bias_ref, out_ref) = refs[:n], refs[n:]
    out_ref[...] = (piece_columns(meta, w_ref, pieces) + bias_ref[...]).astype(BF)


def inputs_product(meta, weight, pieces, bias, width=1024, name=None):
    rows, depth = weight.shape
    return pl.pallas_call(
        functools.partial(inputs_kernel, len(pieces)),
        grid=(HW // width,),
        out_shape=struct((rows, HW), BF),
        in_specs=[scalars(), pl.BlockSpec((rows, depth), lambda p: (0, 0))]
        + [pl.BlockSpec((x.shape[0], width), lambda p: (0, p)) for x in pieces]
        + [pl.BlockSpec((rows, 1), lambda p: (0, 0))],
        out_specs=pl.BlockSpec((rows, width), lambda p: (0, p)),
        compiler_params=params(),
        cost_estimate=cost(2 * rows * depth * HW, (rows + depth) * HW * 2),
        name=name,
    )(meta, weight, *pieces, bias)


def parts_kernel(n, meta, w_ref, *refs):
    pieces, outs = refs[:n], refs[n:]
    first = meta[0]
    for out_ref in outs:
        rows = out_ref.shape[0]
        row = pl.ds(pl.multiple_of(first, rows), rows)
        acc = None
        at = 0
        for x_ref in pieces:
            depth = x_ref.shape[0]
            term = dot(w_ref[row, at : at + depth], x_ref[...])
            acc = term if acc is None else acc + term
            at += depth
        out_ref[...] = acc.astype(BF)
        first = w_ref.shape[0] - rows - first


def parts_product(meta, weight, pieces, count, width=1024, name=None):
    rows, depth = weight.shape
    part = struct((rows // count, HW), BF)
    return pl.pallas_call(
        functools.partial(parts_kernel, len(pieces)),
        grid=(HW // width,),
        out_shape=[part] * count,
        in_specs=[scalars(), pl.BlockSpec((rows, depth), lambda p: (0, 0))]
        + [pl.BlockSpec((x.shape[0], width), lambda p: (0, p)) for x in pieces],
        out_specs=[pl.BlockSpec((rows // count, width), lambda p: (0, p))] * count,
        compiler_params=params(),
        cost_estimate=cost(2 * rows * depth * HW, (rows + depth) * HW * 2),
        name=name,
    )(meta, weight, *pieces)


def output_kernel(n, meta, w_ref, *refs):
    pieces, (bias_ref, hidden_ref, out_ref) = refs[:n], refs[n:]
    acc = hidden_ref[...] + bias_ref[...] + piece_columns(meta, w_ref, pieces)
    half = acc.shape[1] // 2
    for base, val in zip((0, HW // 2), unfold(acc)):
        first = pl.multiple_of(base + pl.program_id(0) * half, half)
        out_ref[:, pl.ds(first, half)] = val.astype(BF)


def output_product(meta, weight, pieces, bias, hidden, width=1024):
    rows, depth = weight.shape
    return pl.pallas_call(
        functools.partial(output_kernel, len(pieces)),
        grid=(HW // width,),
        out_shape=struct((rows, HW), BF),
        in_specs=[scalars(), pl.BlockSpec((rows, depth), lambda p: (0, 0))]
        + [pl.BlockSpec((x.shape[0], width), lambda p: (0, p)) for x in pieces]
        + [
            pl.BlockSpec((rows, 1), lambda p: (0, 0)),
            pl.BlockSpec((rows, width), lambda p: (0, p)),
        ],
        out_specs=pl.BlockSpec((rows, HW), lambda p: (0, 0)),
        compiler_params=params(),
        cost_estimate=cost(2 * rows * depth * HW, (rows * 3 + depth) * HW * 2),
        name="output",
    )(meta, weight, *pieces, bias, hidden)


def outer_kernel(n_left, n_right, meta, *refs):
    lefts, rights = refs[:n_left], refs[n_left : n_left + n_right]
    out_ref, sums_ref = refs[n_left + n_right : n_left + n_right + 2]
    acc_ref, tot_ref = refs[n_left + n_right + 2 :]
    step = pl.program_id(0)

    @pl.when(step == 0)
    def _():
        acc_ref[...] = jnp.zeros_like(acc_ref)
        tot_ref[...] = jnp.zeros_like(tot_ref)

    row = 0
    for left in lefts:
        rows = left.shape[0]
        val = left[...]
        first = meta[0]
        for right in rights:
            cols = right.shape[0]
            at = pl.ds(pl.multiple_of(first, cols), cols)
            acc_ref[row : row + rows, at] += dot_nt(val, right[...])
            first = acc_ref.shape[1] - cols - first
        tot_ref[row : row + rows, :] += jnp.sum(val.astype(F32), axis=1, keepdims=True)
        row += rows

    @pl.when(step == pl.num_programs(0) - 1)
    def _():
        out_ref[...] = acc_ref[...].astype(BF)
        sums_ref[...] = tot_ref[...]


def outer(meta, lefts, rights, width=1024, name=None):
    rows, cols = sum(a.shape[0] for a in lefts), sum(a.shape[0] for a in rights)
    fixed = lambda p: (0, 0)
    return pl.pallas_call(
        functools.partial(outer_kernel, len(lefts), len(rights)),
        grid=(HW // width,),
        out_shape=[struct((rows, cols), BF), struct((rows, 128), F32)],
        in_specs=[scalars()]
        + [pl.BlockSpec((a.shape[0], width), lambda p: (0, p)) for a in (*lefts, *rights)],
        out_specs=[pl.BlockSpec((rows, cols), fixed), pl.BlockSpec((rows, 128), fixed)],
        scratch_shapes=[pltpu.VMEM((rows, cols), F32), pltpu.VMEM((rows, 128), F32)],
        compiler_params=params(),
        cost_estimate=cost(2 * rows * cols * HW, (rows + cols) * HW * 2),
        name=name,
    )(meta, *lefts, *rights)


def attention_kernel(
    n_grads, lim_ref, q_ref, k_ref, v_ref, kc_ref, vc_ref, *refs, unroll, back,
):
    g_refs, refs = refs[:n_grads], refs[n_grads:]
    o_ref, dq_ref, dk_ref, dv_ref, dkc_ref, dvc_ref = refs[:6]
    kt, vt, kn, vn, s_even, s_odd, p_sc, tops, o_acc, dk_acc, dv_acc = refs[6:]
    step, last = pl.program_id(1), pl.num_programs(1) - 1
    width = q_ref.shape[-1]
    blocks = KEYS // BLOCK

    @pl.when(step == 0)
    def _():
        spare = jnp.zeros((HEAD_DIM, KEYS - HW - CTXP), BF)
        for ref, own, ctx in ((kn, k_ref, kc_ref), (vn, v_ref, vc_ref)):
            ref[:, :HW] = own[0, 0]
            ref[:, HW : HW + CTXP] = ctx[0, 0]
            ref[:, HW + CTXP :] = spare
        row = lax.broadcasted_iota(jnp.int32, (HEAD_DIM, BLOCK), 0)
        for n in range(blocks):
            at = slice(n * BLOCK, (n + 1) * BLOCK)
            key = lax.broadcasted_iota(jnp.int32, (HEAD_DIM, BLOCK), 1) + n * BLOCK
            fill = jnp.where((row == 0) & (key >= HW + lim_ref[0]), NEG_FILL, 0.0)
            kt[at, :] = jnp.concatenate([kn[:, at].astype(F32), fill], 0).T.astype(BF)
            vt[at, :] = jnp.concatenate([vn[:, at].astype(F32), jnp.zeros_like(fill)], 0).T.astype(BF)
        dk_acc[...] = jnp.zeros_like(dk_acc)
        dv_acc[...] = jnp.zeros_like(dv_acc)

    def keys_at(n):
        return pl.ds(pl.multiple_of(n * BLOCK, BLOCK), BLOCK)

    scale = HEAD_DIM ** (-0.5)
    q = (q_ref[0, 0].astype(F32) * scale).astype(BF)
    one = jnp.where(lax.broadcasted_iota(jnp.int32, (HEAD_DIM, width), 0) == 0, 1.0, 0.0).astype(BF)
    q_more = jnp.concatenate([q, one], 0)

    def score(n, held):
        scores = dot(kt[keys_at(n), :], q_more)
        held[...] = scores
        return jnp.max(jnp.max(scores.reshape(BLOCK // 8, 8, width), axis=0), axis=0, keepdims=True)

    o_acc[...] = jnp.zeros_like(o_acc)

    def forward(n, held, top, total, shrink):
        raised = jnp.exp(held[...] - top)
        low = raised.astype(BF)
        p_sc[keys_at(n), :] = low
        tops[n, 0:1, :] = top
        sums = jnp.sum(raised.reshape(BLOCK // 8, 8, width), axis=0)
        o_acc[...] = o_acc[...] * shrink + dot(vn[:, keys_at(n)], low)
        return total * shrink + sums

    def forward_step(n, held, ahead_held, carry):
        top, total, shrink = carry
        ahead = jnp.maximum(top, score(n + 1, ahead_held))
        total = forward(n, held, top, total, shrink)
        return ahead, total, jnp.exp(top - ahead)

    held = (s_even, s_odd)

    def forward_run(j, carry):
        for u in range(unroll):
            carry = forward_step(unroll * j + u, held[u % 2], held[1 - u % 2], carry)
        return carry

    carry = (score(0, s_even), jnp.zeros((8, width), F32), jnp.ones((1, width), F32))
    carry = lax.fori_loop(0, blocks // unroll - 1, forward_run, carry)
    for n in range(blocks - unroll, blocks - 1):
        carry = forward_step(n, held[n % 2], held[1 - n % 2], carry)
    top, total, shrink = carry
    total = forward(blocks - 1, s_odd, top, total, shrink)

    inverse = 1.0 / jnp.sum(total, axis=0, keepdims=True)
    mixed = o_acc[...] * inverse
    o_ref[0] = mixed.astype(BF)
    grad = sum(g_ref[0].astype(F32) for g_ref in g_refs)
    if n_grads > 1:
        grad = grad.astype(BF).astype(F32)
    delta = jnp.sum(grad * mixed, axis=0, keepdims=True)
    dq = jnp.zeros((HEAD_DIM, width), F32)
    none = jnp.zeros((HEAD_DIM, width), BF)
    for c in range(0, KEYS, back):
        at = slice(c, c + back)
        slopes = []
        for n in range(c // BLOCK, (c + back) // BLOCK):
            sub = slice(n * BLOCK, (n + 1) * BLOCK)
            factor = inverse * jnp.exp(tops[n, 0:1, :] - top)
            grad_low = (grad * factor).astype(BF)
            both = jnp.concatenate([grad_low, none], 0)
            probs = p_sc[sub, :]
            slope = (dot(vt[sub, :], both) - delta * factor).astype(BF) * probs
            slopes.append(slope)
            dv_acc[:, sub] += dot_nt(grad_low, probs)
        slope = jnp.concatenate(slopes, 0)
        dq = dq + dot(kn[:, at], slope)
        dk_acc[:, at] += dot_nt(q, slope)
    dq_ref[0] = (dq * scale).astype(BF)

    @pl.when(step == last)
    def _():
        dk_ref[0] = dk_acc[:, :HW].astype(BF)
        dv_ref[0] = dv_acc[:, :HW].astype(BF)
        dkc_ref[0] = dk_acc[:, HW : HW + CTXP].astype(BF)
        dvc_ref[0] = dv_acc[:, HW : HW + CTXP].astype(BF)


def attention(limit, qkv, ctx_kv, grads, width=1024, unroll=6, back=512):
    heads = qkv.shape[1]
    keys = KEYS

    def part(t, w, moving):
        return pl.BlockSpec(
            (1, 1, HEAD_DIM, w), (lambda h, i: (t, h, 0, i)) if moving else (lambda h, i: (t, h, 0, 0))
        )

    def row(w, moving):
        return pl.BlockSpec(
            (1, HEAD_DIM, w), (lambda h, i: (h, 0, i)) if moving else (lambda h, i: (h, 0, 0))
        )

    big, small = struct((heads, HEAD_DIM, HW), BF), struct((heads, HEAD_DIM, CTXP), BF)
    return pl.pallas_call(
        functools.partial(attention_kernel, len(grads), unroll=unroll, back=back),
        grid=(heads, HW // width),
        in_specs=[
            pl.BlockSpec(memory_space=pltpu.SMEM),
            part(0, width, True),
            part(1, HW, False),
            part(2, HW, False),
            part(0, CTXP, False),
            part(1, CTXP, False),
        ]
        + [row(width, True)] * len(grads),
        out_specs=[
            row(width, True),
            row(width, True),
            row(HW, False),
            row(HW, False),
            row(CTXP, False),
            row(CTXP, False),
        ],
        out_shape=[big, big, big, big, small, small],
        scratch_shapes=[
            pltpu.VMEM((keys, 2 * HEAD_DIM), BF),
            pltpu.VMEM((keys, 2 * HEAD_DIM), BF),
            pltpu.VMEM((HEAD_DIM, keys), BF),
            pltpu.VMEM((HEAD_DIM, keys), BF),
            pltpu.VMEM((BLOCK, width), F32),
            pltpu.VMEM((BLOCK, width), F32),
            pltpu.VMEM((keys, width), BF),
            pltpu.VMEM((keys // BLOCK, 8, width), F32),
            pltpu.VMEM((HEAD_DIM, width), F32),
            pltpu.VMEM((HEAD_DIM, keys), F32),
            pltpu.VMEM((HEAD_DIM, keys), F32),
        ],
        compiler_params=params(dimension_semantics=("arbitrary", "arbitrary")),
        cost_estimate=cost(
            24 * heads * HW * keys * HEAD_DIM, heads * HEAD_DIM * 8 * HW * 2, heads * HW * keys
        ),
        name="attention",
    )(limit, qkv, qkv, qkv, ctx_kv, ctx_kv, *grads)


class Alone:
    parts = 1

    def __init__(self, mesh):
        self.images = mesh.shape["dp"]

    def meta(self):
        return jnp.array([0, 1], jnp.int32)

    def image(self):
        return lax.axis_index("dp")

    def got(self, x):
        return x

    def pick(self, own, got):
        return own

    def gather(self, x):
        return (lax.all_gather(x, "tensor", axis=0, tiled=True),)

    def scatter(self, parts):
        return (lax.psum_scatter(parts[0], "tensor", scatter_dimension=0, tiled=True),)

    def turn(self, meta, w):
        ch = w.shape[0]
        cut = w.reshape(ch, 9, C)
        turned = lax.all_to_all(cut, "tensor", split_axis=2, concat_axis=0, tiled=True)
        return turned[:, ::-1].transpose(2, 1, 0).reshape(ch, 9 * C)

    def total(self, x):
        return lax.psum(x, "dp")

    def everywhere(self, x):
        return lax.psum(x, "dp")

    def sum_owned(self, x):
        return lax.psum(x, "dp")


class Paired:
    parts = 2

    def __init__(self, mesh):
        dp = mesh.shape["dp"]
        self.images = dp
        self.far = [
            ((2 * k + core) * 2 + 1 - core, (2 * k + 1 - core) * 2 + core)
            for k in range(dp // 2)
            for core in range(2)
        ]
        self.bits = [1 << b for b in range((dp - 1).bit_length())]

    def half(self):
        return lax.axis_index("dp") % 2

    def stays(self):
        return self.half() == lax.axis_index("tensor")

    def meta(self):
        return jnp.stack([self.half() * (C // 2), self.stays().astype(jnp.int32)]).astype(jnp.int32)

    def image(self):
        return lax.axis_index("dp") // 2 * 2 + lax.axis_index("tensor")

    def got(self, x):
        return lax.ppermute(x, ("dp", "tensor"), self.far)

    def pick(self, own, got):
        return jnp.where(self.stays(), own, got)

    def over(self, x, bit):
        return lax.ppermute(x, "dp", [(i, i ^ bit) for i in range(self.images)])

    def gather(self, x):
        return (x, self.over(x, 1))

    def scatter(self, parts):
        return (parts[0], self.over(parts[1], 1))

    def turn(self, meta, w):
        return turned_pair(meta, w, self.over(w, 1))

    def total(self, x):
        x = x + lax.ppermute(x, "tensor", [(0, 1), (1, 0)])
        for bit in self.bits[1:]:
            x = x + self.over(x, bit)
        return self.pick(x, self.over(x, 1))

    def everywhere(self, x):
        for bit in self.bits:
            x = x + self.over(x, bit)
        return x

    def sum_owned(self, x):
        rows = x.shape[0] // 2
        order = (self.bits, [self.bits[0], *self.bits[2:], self.bits[1]])
        parts = [lax.slice_in_dim(x, at * rows, (at + 1) * rows) for at in range(2)]

        def upper(bit):
            return (lax.axis_index("dp") // bit) % 2

        for step in range(len(self.bits)):
            size = parts[0].shape[0] // 2
            for at in range(2):
                bit = order[at][step]
                keep = lax.dynamic_slice_in_dim(parts[at], upper(bit) * size, size)
                send = lax.dynamic_slice_in_dim(parts[at], (1 - upper(bit)) * size, size)
                parts[at] = (keep.astype(F32) + self.over(send, bit).astype(F32)).astype(BF)
        for step in reversed(range(len(self.bits))):
            for at in range(2):
                bit = order[at][step]
                other = self.over(parts[at], bit)
                parts[at] = jnp.where(
                    upper(bit) == 0,
                    jnp.concatenate([parts[at], other]),
                    jnp.concatenate([other, parts[at]]),
                )
        return jnp.concatenate(parts)


def after(first, *later):
    held = lax.optimization_barrier((first, *later))
    return held[1:] if len(later) > 1 else held[1]


def local(plan, features, cotangent, embedding, context, lengths, norm1_gain, norm1_bias,
    conv1_weight, conv1_bias, emb_weight, emb_bias, norm2_gain, norm2_bias, conv2_weight,
    conv2_bias, norm3_gain, norm3_bias, qkv_weight, qkv_bias, context_weight, context_bias,
    out_weight, out_bias,
):
    ch, images, pixels = features.shape
    heads = ch // HEAD_DIM
    meta = plan.meta()
    moved = plan.parts == 2

    emb_act = jax.nn.silu(embedding.astype(F32)).astype(BF)
    scale_shift = (
        jnp.einsum("ie,teo->to", emb_act, emb_weight, preferred_element_type=F32) + emb_bias
    )
    length_row = jnp.broadcast_to(lengths.astype(F32)[:, None], (1, ch))
    vectors = jnp.concatenate(
        [
            jnp.stack([norm1_gain, norm1_bias, conv1_bias, norm2_gain, norm2_bias]),
            scale_shift,
            jnp.stack([conv2_bias, norm3_gain, norm3_bias, out_bias]),
            qkv_bias,
            length_row,
        ]
    )
    f_own = features.reshape(ch, pixels)
    f_got = plan.got(f_own)
    vectors, w1_own = after(scale_shift, vectors, conv1_weight)
    vectors = plan.pick(vectors, plan.got(vectors))
    w1_got = plan.got(w1_own)
    ctx_kv = (
        jnp.einsum("toe,ne->ton", context_weight, context[0], preferred_element_type=F32)
        + context_bias[:, :, None]
    ).astype(BF)
    ctx_kv = jnp.pad(ctx_kv, ((0, 0), (0, 0), (0, CTXP - CTX)))
    emb_all = jnp.where(
        jnp.arange(plan.images)[:, None] == lax.axis_index("dp"), emb_act, jnp.zeros_like(emb_act)
    )
    emb_all = plan.everywhere(emb_all)
    length = vectors[14, :1].astype(jnp.int32)
    par_one, par_two, par_three = vectors[0:2].T, vectors[2:7].T, vectors[7:10].T
    par_one = after(emb_all, par_one)
    w2_got = plan.got(after(vectors, conv2_weight))
    act_one, stat_one, f_low = first_activation(meta, f_own, f_got, par_one)
    full_one = plan.gather(act_one)
    mats_own = jnp.concatenate([qkv_weight.reshape(3 * ch, C), out_weight])
    mats_own, ctx_own, cot_own = after(
        act_one, mats_own, ctx_kv, cotangent.reshape(ch, pixels)
    )
    mats_got, ctx_got = plan.got(mats_own), plan.got(ctx_own)
    cot_got = plan.got(cot_own)

    low, stat, wide = struct((ch, HW), BF), struct((ch, 128), F32), struct((ch, HW), F32)
    weight = struct((ch, 9 * C), BF)
    act_two, stat_two, conv_one, w1 = conv_call(
        conv_one_kernel, meta, (conv1_weight, w1_got), full_one, (par_two,), (),
        [low, stat], [wide, weight], [], "conv_one",
    )
    full_two = plan.gather(act_two)
    if moved:
        full_two = after(cot_got, *full_two)
    normed, stat_three, hidden, w2 = conv_call(
        conv_two_kernel, meta, (conv2_weight, w2_got), full_two, (par_three, f_low), (),
        [low, stat], [wide, weight], [], "conv_two",
    )
    full_three = plan.gather(normed)
    mats_got, ctx_got, cot_got = after(normed, mats_got, ctx_got, cot_got)
    mats = plan.pick(mats_own, mats_got)
    w_qkv, w_out = mats[: 3 * ch], mats[3 * ch :]
    cot = folded(meta, cot_own, cot_got)
    grad_heads = plan.scatter(
        parts_product(meta, w_out.T, (cot,), plan.parts, name="grad_heads")
    )
    qkv = inputs_product(meta, w_qkv, full_three, vectors[11:14].reshape(3 * ch, 1), name="qkv")
    ctx_kv = plan.pick(ctx_own, ctx_got)
    mixed, dq, dk, dv, dkc, dvc = attention(
        4 + length,
        qkv.reshape(3, heads, HEAD_DIM, HW),
        ctx_kv.reshape(2, heads, HEAD_DIM, CTXP),
        [a.reshape(heads, HEAD_DIM, HW) for a in grad_heads],
    )

    flat = lambda a: a.reshape(ch, HW)
    dq, dk, dv = flat(dq), flat(dk), flat(dv)
    addends = plan.scatter(
        parts_product(meta, w_qkv.T, (dq, dk, dv), plan.parts, name="grad_normed")
    )
    full_heads = plan.gather(flat(mixed))
    ctx_own = jnp.concatenate([a.reshape(1, ch, CTXP) for a in (dkc, dvc)])
    ctx_got = plan.got(ctx_own)
    turned_two = plan.turn(meta, after(mixed, w2))
    dw_qkv, db_qkv = outer(meta, (dq, dk, dv), full_three, name="qkv_grad")
    dw_out, _ = outer(meta, (cot,), full_heads, name="out_grad")
    mats_own = jnp.concatenate([dw_qkv, dw_out])
    mats_got = plan.got(mats_own)
    grad_hidden, grad_two, sums_three = norm_three_back(addends, hidden, stat_three, par_three, cot)
    full_grad_two = plan.gather(grad_two)
    dw_two = conv_weight_grad(meta, grad_two, full_two, "conv_two_weight_grad")
    two_got = plan.got(dw_two)
    full_grad_two = after(dw_two, *full_grad_two) if moved else full_grad_two
    grad_one, sums_two = conv_call(
        conv_two_back_kernel, meta, (turned_two, turned_two), full_grad_two, (par_two, stat_two),
        (conv_one,), [low, stat], [], [pltpu.VMEM((ch, HW), F32)], "conv_two_back",
    )
    full_grad_one = plan.gather(grad_one)
    turned_one = plan.turn(meta, after(mixed, w1))
    mats_got, ctx_got, two_got = after(grad_one, mats_got, ctx_got, two_got)
    ctx_grad = plan.pick(ctx_own, ctx_got)[:, :, :CTX]
    dw_ctx = jnp.einsum("ton,ne->toe", ctx_grad, context[0], preferred_element_type=F32).astype(BF)
    mats = plan.pick(mats_own, mats_got)
    dw_two = plan.pick(dw_two, two_got)
    early = jnp.concatenate(
        [dw_ctx[0], dw_ctx[1], *(mats[t * ch : (t + 1) * ch] for t in range(4)), dw_two], 1
    )
    held = after(early, grad_one)
    early = lax.psum_scatter(early, "dp", scatter_dimension=0, tiled=True)
    dw_one = conv_weight_grad(meta, held, full_one, "conv_one_weight_grad")
    one_got = plan.got(dw_one)
    full_grad_one = after(dw_one, *full_grad_one) if moved else full_grad_one
    input_grad, sums_one = conv_call(
        conv_one_back_kernel, meta, (turned_one, turned_one), full_grad_one,
        (par_one, stat_one, f_low), (grad_hidden,),
        [struct((ch, HW), BF if moved else F32), stat], [],
        [pltpu.VMEM((ch, HW), F32)], "conv_one_back",
    )
    input_got = plan.got(input_grad)

    output = output_product(
        meta, w_out, full_heads, vectors[10].reshape(ch, 1), after((input_grad, one_got), hidden)
    )
    output_got = plan.got(output)
    ctx_sums = jnp.sum(ctx_own.astype(F32), axis=2)
    sums_two = sums_two[:, :5].T
    own_mod = sums_two[2:4].astype(BF).astype(F32)
    mods = jnp.where(
        (jnp.arange(plan.images) == plan.image())[:, None, None], own_mod, jnp.zeros_like(own_mod)
    ).reshape(2 * plan.images, ch)
    small = plan.total(
        jnp.concatenate(
            [
                sums_three[:, :4].T,
                db_qkv[:, 0].reshape(3, ch),
                sums_two[:2],
                sums_two[4:5],
                ctx_sums,
                sums_one[:, :2].T,
                mods,
            ]
        )
    )
    early, dw_one, one_got = after((output, small), early, dw_one, one_got)
    early = lax.all_gather(early, "dp", axis=0, tiled=True)
    dw_one = plan.sum_owned(plan.pick(dw_one, one_got))
    mods = small[14:].reshape(plan.images, 2, ch)
    mods_low = mods.astype(BF)
    dw_emb = jnp.stack(
        [
            jnp.einsum("ie,io->eo", emb_all, mods_low[:, t], preferred_element_type=F32)
            for t in range(2)
        ]
    )
    input_got, output_got = after((dw_one, small), input_got, output_got)
    input_grad = plan.pick(input_grad, input_got).astype(F32)
    output = plan.pick(output, output_got)
    early = after((dw_one, small, input_grad, output), early)
    dw_ctx = jnp.stack([early[:, n * CTX_EMB : (n + 1) * CTX_EMB] for n in range(2)])
    first = 2 * CTX_EMB
    mats = [early[:, first + n * C : first + (n + 1) * C].astype(F32) for n in range(4)]
    dw_two = early[:, first + 4 * C :]

    return (
        output.reshape(ch, images, pixels),
        input_grad.reshape(ch, images, pixels),
        small[12],
        small[13],
        dw_one.astype(F32),
        small[9],
        dw_emb,
        jnp.sum(mods, axis=0),
        small[7],
        small[8],
        dw_two.astype(F32),
        small[2],
        small[0],
        small[1],
        jnp.stack(mats[:3]),
        small[4:7],
        dw_ctx.astype(F32),
        small[10:12],
        mats[3],
        small[3],
    )


def solution(mesh):
    paired = mesh.shape["tensor"] == 2 and mesh.shape["dp"] % 2 == 0
    plan = Paired(mesh) if paired else Alone(mesh)
    specs = (
        P("tensor", "dp", None),
        P("tensor", "dp", None),
        P("dp", None),
        P("dp", None, None),
        P("dp"),
        P("tensor"),
        P("tensor"),
        P("tensor", None),
        P("tensor"),
        P(None, None, "tensor"),
        P(None, "tensor"),
        P("tensor"),
        P("tensor"),
        P("tensor", None),
        P("tensor"),
        P("tensor"),
        P("tensor"),
        P(None, "tensor", None),
        P(None, "tensor"),
        P(None, "tensor", None),
        P(None, "tensor"),
        P("tensor", None),
        P("tensor"),
    )
    return jax.shard_map(
        functools.partial(local, plan),
        mesh=mesh,
        in_specs=specs,
        out_specs=(
            P("tensor", "dp", None),
            P("tensor", "dp", None),
            P("tensor"),
            P("tensor"),
            P("tensor", None),
            P("tensor"),
            P(None, None, "tensor"),
            P(None, "tensor"),
            P("tensor"),
            P("tensor"),
            P("tensor", None),
            P("tensor"),
            P("tensor"),
            P("tensor"),
            P(None, "tensor", None),
            P(None, "tensor"),
            P(None, "tensor", None),
            P(None, "tensor"),
            P("tensor", None),
            P("tensor"),
        ),
        check_vma=False,
    )
```

```python
import functools

import jax
import jax.numpy as jnp
from jax import lax
from jax.experimental import pallas as pl
from jax.experimental.pallas import tpu as pltpu
from jax.sharding import PartitionSpec as P

C = 512
HEAD_DIM = 64
PER_GROUP = 16
SIDE = 64
HW = 4096
CTX = 260
CTXP = 384
CTX_EMB = 2048
BLOCK = 256
KEYS = 4608
PAD = 128
FILL = 32
SCALE = 100
EPSILON = 1e-05
NEG_FILL = -1e30
F32 = jnp.float32
BF = jnp.bfloat16
NT = (((1,), (1,)), ((), ()))
VMEM_BYTES = 62 << 20


def dot(a, b):
    return jnp.dot(a, b, preferred_element_type=F32)


def dot_nt(a, b):
    return lax.dot_general(a, b, NT, preferred_element_type=F32)


def whole():
    return pl.BlockSpec(memory_space=pltpu.VMEM)


def placed():
    return pl.BlockSpec(memory_space=pl.ANY)


def scalars():
    return pl.BlockSpec(memory_space=pltpu.SMEM)


def params(**kwargs):
    return pltpu.CompilerParams(vmem_limit_bytes=VMEM_BYTES, **kwargs)


def cost(flops, nbytes, transcendentals=0):
    return pl.CostEstimate(
        flops=flops // SCALE, bytes_accessed=nbytes // SCALE, transcendentals=transcendentals // SCALE
    )


def struct(shape, dtype):
    return jax.ShapeDtypeStruct(shape, dtype)


def fetch(meta, own_ref, got_ref, buf, sem):
    @pl.when(meta[1] == 1)
    def _():
        pltpu.make_async_copy(own_ref, buf, sem).start()

    @pl.when(meta[1] != 1)
    def _():
        pltpu.make_async_copy(got_ref, buf, sem).start()


def arrive(own_ref, buf, sem):
    pltpu.make_async_copy(own_ref, buf, sem).wait()


def group_scalar(column):
    return jnp.sum(column, axis=0, keepdims=True) * (1.0 / (PER_GROUP * HW))


def group_stats(vals):
    mean = group_scalar(jnp.sum(vals, axis=1, keepdims=True))
    centred = vals - mean
    var = group_scalar(jnp.sum(centred * centred, axis=1, keepdims=True))
    rstd = lax.rsqrt(var + EPSILON)
    return mean, rstd


def norm_backward(dy_sum, dyx_sum, gain):
    return group_scalar(dy_sum * gain), group_scalar(dyx_sum * gain)


def for_groups(channels, body, together=2):
    def step(g, carry):
        for u in range(together):
            first = pl.multiple_of((g * together + u) * PER_GROUP, PER_GROUP)
            body(pl.ds(first, PER_GROUP))
        return carry

    lax.fori_loop(0, channels // PER_GROUP // together, step, 0)


def columns(values):
    lane = lax.broadcasted_iota(jnp.int32, (PER_GROUP, 128), 1)
    tile = jnp.zeros((PER_GROUP, 128), F32)
    for at, val in enumerate(values):
        tile = jnp.where(lane == at, val, tile)
    return tile


ROWS = SIDE // 2


def lanes(x, n):
    return x[:, 128 * n : 128 * n + 128]


def low_lanes(x):
    return lax.broadcasted_iota(jnp.int32, (x.shape[0], 128), 1) < SIDE


def fold(x):
    low = low_lanes(x)
    out = []
    for r in range(ROWS):
        upper, lower = lanes(x, r // 2), lanes(x, r // 2 + ROWS // 2)
        if r % 2 == 0:
            out.append(jnp.where(low, upper, pltpu.roll(lower, SIDE, 1)))
        else:
            out.append(jnp.where(low, pltpu.roll(upper, SIDE, 1), lower))
    return jnp.concatenate(out, 1)


def unfold(x):
    low = low_lanes(x)
    pairs = range(x.shape[1] // 256)
    top = [jnp.where(low, lanes(x, 2 * n), pltpu.roll(lanes(x, 2 * n + 1), SIDE, 1)) for n in pairs]
    bottom = [
        jnp.where(low, pltpu.roll(lanes(x, 2 * n), SIDE, 1), lanes(x, 2 * n + 1)) for n in pairs
    ]
    return jnp.concatenate(top, 1), jnp.concatenate(bottom, 1)


def fold_kernel(meta, own_ref, got_ref, out_ref, x_buf, sem):
    fetch(meta, own_ref, got_ref, x_buf, sem)
    arrive(own_ref, x_buf, sem)

    def body(rows):
        out_ref[rows, :] = fold(x_buf[rows, :].astype(F32)).astype(BF)

    for_groups(out_ref.shape[0], body)


def folded(meta, own, got):
    return pl.pallas_call(
        fold_kernel,
        out_shape=struct(own.shape, BF),
        in_specs=[scalars(), placed(), placed()],
        out_specs=whole(),
        scratch_shapes=[pltpu.VMEM(own.shape, BF), pltpu.SemaphoreType.DMA(())],
        compiler_params=params(),
        cost_estimate=cost(8 * own.size, 4 * own.size),
        name="fold",
    )(meta, own, got)


def act_one_kernel(meta, own_ref, got_ref, par_ref, act_ref, stat_ref, fold_ref, x_buf, sem):
    fetch(meta, own_ref, got_ref, x_buf, sem)
    arrive(own_ref, x_buf, sem)

    def body(rows):
        vals = fold(x_buf[rows, :].astype(F32))
        fold_ref[rows, :] = vals.astype(BF)
        mean, rstd = group_stats(vals)
        par = par_ref[rows, :]
        out = (vals - mean) * (rstd * par[:, 0:1]) + par[:, 1:2]
        act_ref[rows, :] = (out * jax.nn.sigmoid(out)).astype(BF)
        stat_ref[rows, :] = columns([mean, rstd])

    for_groups(act_ref.shape[0], body)


def first_activation(meta, own, got, par):
    ch = own.shape[0]
    return pl.pallas_call(
        act_one_kernel,
        out_shape=[struct((ch, HW), BF), struct((ch, 128), F32), struct((ch, HW), BF)],
        in_specs=[scalars(), placed(), placed(), whole()],
        out_specs=[whole()] * 3,
        scratch_shapes=[pltpu.VMEM((ch, HW), BF), pltpu.SemaphoreType.DMA(())],
        compiler_params=params(),
        cost_estimate=cost(20 * ch * HW, 6 * ch * HW, ch * HW),
        name="act_one",
    )(meta, own, got, par)


def fill_shifted(xs, pieces, first):
    start = first
    for x_ref in pieces:
        rows = x_ref.shape[0]

        def step(r, carry, x_ref=x_ref, start=start):
            off = pl.multiple_of(r * FILL, FILL)
            at = pl.ds(pl.multiple_of(start + off, FILL), FILL)
            lane = lax.broadcasted_iota(jnp.int32, (FILL, 128), 1)
            low = lane < SIDE
            left, right = lane % SIDE == 0, lane % SIDE == SIDE - 1
            zero = jnp.zeros((FILL, 128), F32)
            here = pl.ds(off, FILL)
            for n in range(ROWS):
                x = x_ref[here, 128 * n : 128 * n + 128].astype(F32)
                kinds = (
                    jnp.where(left, zero, pltpu.roll(x, 1, 1)),
                    x,
                    jnp.where(right, zero, pltpu.roll(x, 127, 1)),
                )
                for d, y in enumerate(kinds):
                    xs[d, at, PAD + 128 * n : PAD + 128 * n + 128] = y.astype(BF)
                    if n == ROWS - 1:
                        xs[d, at, :PAD] = jnp.where(low, zero, pltpu.roll(y, SIDE, 1)).astype(BF)
                    if n == 0:
                        xs[d, at, PAD + HW :] = jnp.where(
                            low, pltpu.roll(y, SIDE, 1), zero
                        ).astype(BF)
            return carry

        lax.fori_loop(0, rows // FILL, step, 0)
        start = xs.shape[1] - rows - start if len(pieces) == 2 else start + rows


def window(xs, tap, start, width):
    first = PAD + start + (tap // 3 - 1) * 128
    if not isinstance(start, int):
        first = pl.multiple_of(first, 128)
    return xs[tap % 3, :, pl.ds(first, width)]


def convolve(xs, w_ref, out_ref, add, width=1024):
    depth = xs.shape[1]

    def step(n, carry):
        p = n * width
        acc = dot(w_ref[:, :depth], window(xs, 0, p, width))
        for tap in range(1, 9):
            acc = acc + dot(w_ref[:, tap * depth : (tap + 1) * depth], window(xs, tap, p, width))
        at = pl.ds(pl.multiple_of(p, width), width)
        out_ref[:, at] = add(acc, at)
        return carry

    lax.fori_loop(0, HW // width, step, 0)


def conv_call(kernel, meta, weights, pieces, vmem_in, any_in, outs, any_outs, scratch, name):
    out_ch, depth = weights[0].shape[0], C
    arrays = (weights[0], *pieces, *vmem_in, *any_in)
    nbytes = sum(a.size * a.dtype.itemsize for a in arrays) + out_ch * HW * 4
    return pl.pallas_call(
        functools.partial(kernel, len(pieces)),
        out_shape=[*outs, *any_outs],
        in_specs=[scalars(), placed(), placed()]
        + [whole()] * (len(pieces) + len(vmem_in))
        + [placed()] * len(any_in),
        out_specs=[whole()] * len(outs) + [placed()] * len(any_outs),
        scratch_shapes=[
            pltpu.VMEM((3, depth, HW + 2 * PAD), BF),
            pltpu.VMEM((out_ch, 9 * depth), BF),
            pltpu.VMEM((out_ch, HW), F32),
            pltpu.SemaphoreType.DMA((4,)),
            *scratch,
        ],
        compiler_params=params(),
        cost_estimate=cost(2 * out_ch * 9 * depth * HW, nbytes, out_ch * HW),
        name=name,
    )(meta, *weights, *pieces, *vmem_in, *any_in)


def conv_one_kernel(n, meta, w_own, w_got, *refs):
    pieces, refs = refs[:n], refs[n:]
    par_ref, act_ref, stat_ref, conv_ref, w_ref, xs, w_buf, acc, sems = refs
    fetch(meta, w_own, w_got, w_buf, sems.at[0])
    fill_shifted(xs, pieces, meta[0])
    arrive(w_own, w_buf, sems.at[0])
    keep = pltpu.make_async_copy(w_buf, w_ref, sems.at[2])
    keep.start()
    bias = par_ref[:, 0:1]
    convolve(xs, w_buf, acc, lambda val, at: val + bias)
    store = pltpu.make_async_copy(acc, conv_ref, sems.at[1])
    store.start()

    def body(rows):
        vals = acc[rows, :]
        mean, rstd = group_stats(vals)
        par = par_ref[rows, :]
        gain, shift, factor = par[:, 1:2], par[:, 2:3], 1.0 + par[:, 3:4]
        mid = (vals - mean) * (rstd * gain * factor) + (shift * factor + par[:, 4:5])
        act_ref[rows, :] = (mid * jax.nn.sigmoid(mid)).astype(BF)
        stat_ref[rows, :] = columns([mean, rstd])

    for_groups(acc.shape[0], body)
    store.wait()
    keep.wait()


def conv_two_kernel(n, meta, w_own, w_got, *refs):
    pieces, refs = refs[:n], refs[n:]
    par_ref, f_ref, normed_ref, stat_ref, hidden_ref, w_ref, xs, w_buf, acc, sems = refs
    fetch(meta, w_own, w_got, w_buf, sems.at[0])
    fill_shifted(xs, pieces, meta[0])
    arrive(w_own, w_buf, sems.at[0])
    keep = pltpu.make_async_copy(w_buf, w_ref, sems.at[2])
    keep.start()
    bias = par_ref[:, 0:1]
    convolve(xs, w_buf, acc, lambda val, at: val + bias + f_ref[:, at].astype(F32))
    store = pltpu.make_async_copy(acc, hidden_ref, sems.at[1])
    store.start()

    def body(rows):
        vals = acc[rows, :]
        mean, rstd = group_stats(vals)
        par = par_ref[rows, :]
        normed_ref[rows, :] = ((vals - mean) * (rstd * par[:, 1:2]) + par[:, 2:3]).astype(BF)
        stat_ref[rows, :] = columns([mean, rstd])

    for_groups(acc.shape[0], body)
    store.wait()
    keep.wait()


def silu_slope(mid):
    sig = jax.nn.sigmoid(mid)
    return sig * (1.0 + mid * (1.0 - sig))


def conv_two_back_kernel(n, meta, w_own, w_got, *refs):
    pieces, refs = refs[:n], refs[n:]
    par_ref, stat_ref, conv_ref, grad_ref, sums_ref, xs, w_buf, acc, sems, conv_buf = refs
    fetch(meta, w_own, w_got, w_buf, sems.at[0])
    load = pltpu.make_async_copy(conv_ref, conv_buf, sems.at[1])
    load.start()
    fill_shifted(xs, pieces, meta[0])
    arrive(w_own, w_buf, sems.at[0])
    convolve(xs, w_buf, acc, lambda val, at: val)
    load.wait()

    def body(rows):
        par, stat = par_ref[rows, :], stat_ref[rows, :]
        gain, shift, factor = par[:, 1:2], par[:, 2:3], 1.0 + par[:, 3:4]
        rstd = stat[:, 1:2]
        hat = (conv_buf[rows, :] - stat[:, 0:1]) * rstd
        mid = hat * (gain * factor) + (shift * factor + par[:, 4:5])
        grad = acc[rows, :] * silu_slope(mid)
        total = jnp.sum(grad, axis=1, keepdims=True)
        total_hat = jnp.sum(grad * hat, axis=1, keepdims=True)
        mean_u, mean_uhat = norm_backward(total * factor, total_hat * factor, gain)
        out = ((grad * (factor * gain) - mean_u - hat * mean_uhat) * rstd).astype(BF)
        grad_ref[rows, :] = out
        bias_grad = jnp.sum(out.astype(F32), axis=1, keepdims=True)
        sums_ref[rows, :] = columns(
            [
                total_hat * factor,
                total * factor,
                total_hat * gain + total * shift,
                total,
                bias_grad,
            ]
        )

    for_groups(acc.shape[0], body)


def conv_one_back_kernel(n, meta, w_own, w_got, *refs):
    pieces, refs = refs[:n], refs[n:]
    par_ref, stat_ref, f_ref, hid_ref, grad_ref, sums_ref, xs, w_buf, acc, sems, hid_buf = refs
    fetch(meta, w_own, w_got, w_buf, sems.at[0])
    load = pltpu.make_async_copy(hid_ref, hid_buf, sems.at[1])
    load.start()
    fill_shifted(xs, pieces, meta[0])
    arrive(w_own, w_buf, sems.at[0])
    convolve(xs, w_buf, acc, lambda val, at: val)
    load.wait()

    def body(rows):
        par, stat = par_ref[rows, :], stat_ref[rows, :]
        gain, shift = par[:, 0:1], par[:, 1:2]
        rstd = stat[:, 1:2]
        hat = (f_ref[rows, :].astype(F32) - stat[:, 0:1]) * rstd
        grad = acc[rows, :] * silu_slope(hat * gain + shift)
        total = jnp.sum(grad, axis=1, keepdims=True)
        total_hat = jnp.sum(grad * hat, axis=1, keepdims=True)
        mean_u, mean_uhat = norm_backward(total, total_hat, gain)
        out = hid_buf[rows, :] + (grad * gain - mean_u - hat * mean_uhat) * rstd
        top, bottom = unfold(out)
        grad_ref[rows, : HW // 2] = top.astype(grad_ref.dtype)
        grad_ref[rows, HW // 2 :] = bottom.astype(grad_ref.dtype)
        sums_ref[rows, :] = columns([total_hat, total])

    for_groups(acc.shape[0], body)


def weight_grad_kernel(n, meta, grad_ref, *refs):
    pieces, (out_ref, gs) = refs[:n], refs[n:]
    fill_shifted(gs, (grad_ref,), 0)
    for tap in range(9):
        moved = window(gs, 8 - tap, 0, HW)
        first = meta[0]
        for x_ref in pieces:
            rows = x_ref.shape[0]
            at = pl.ds(pl.multiple_of(tap * C + first, rows), rows)
            out_ref[:, at] = dot_nt(moved, x_ref[...]).astype(BF)
            first = C - rows - first


def conv_weight_grad(meta, grad, pieces, name):
    out_ch = grad.shape[0]
    return pl.pallas_call(
        functools.partial(weight_grad_kernel, len(pieces)),
        out_shape=struct((out_ch, 9 * C), BF),
        in_specs=[scalars()] + [whole()] * (1 + len(pieces)),
        out_specs=whole(),
        scratch_shapes=[pltpu.VMEM((3, out_ch, HW + 2 * PAD), BF)],
        compiler_params=params(),
        cost_estimate=cost(2 * out_ch * 9 * C * HW, (out_ch + C) * HW * 2 + out_ch * 9 * C * 2),
        name=name,
    )(meta, grad, *pieces)


def turn_kernel(meta, own_ref, other_ref, out_ref):
    half = own_ref.shape[0]
    for tap in range(9):
        at = pl.ds(pl.multiple_of(tap * C + meta[0], half), half)
        row = meta[0]
        for ref in (own_ref, other_ref):
            to = pl.ds(pl.multiple_of((8 - tap) * C + row, half), half)
            out_ref[:, to] = ref[:, at].astype(F32).T.astype(BF)
            row = half - row


def turned_pair(meta, own, other):
    return pl.pallas_call(
        turn_kernel,
        out_shape=struct(own.shape, BF),
        in_specs=[scalars(), whole(), whole()],
        out_specs=whole(),
        compiler_params=params(),
        cost_estimate=cost(0, 3 * own.size * 2),
        name="turn",
    )(meta, own, other)


def norm_three_back_kernel(n, *refs):
    addends, (hidden_ref, stat_ref, par_ref, cot_ref, hid_ref, grad_ref, sums_ref) = (
        refs[:n],
        refs[n:],
    )

    def body(rows):
        dy = addends[0][rows, :].astype(F32)
        for extra in addends[1:]:
            dy = dy + extra[rows, :].astype(F32)
        par, stat = par_ref[rows, :], stat_ref[rows, :]
        gain, rstd = par[:, 1:2], stat[:, 1:2]
        hat = (hidden_ref[rows, :] - stat[:, 0:1]) * rstd
        total = jnp.sum(dy, axis=1, keepdims=True)
        total_hat = jnp.sum(dy * hat, axis=1, keepdims=True)
        mean_u, mean_uhat = norm_backward(total, total_hat, gain)
        top = cot_ref[rows, :].astype(F32)
        out = top + (dy * gain - mean_u - hat * mean_uhat) * rstd
        hid_ref[rows, :] = out
        low = out.astype(BF)
        grad_ref[rows, :] = low
        sums_ref[rows, :] = columns(
            [
                total_hat,
                total,
                jnp.sum(low.astype(F32), axis=1, keepdims=True),
                jnp.sum(top, axis=1, keepdims=True),
            ]
        )

    for_groups(hidden_ref.shape[0], body)


def norm_three_back(addends, hidden, stat, par, cot):
    ch = hidden.shape[0]
    rows = 32

    def part(a):
        return pl.BlockSpec((rows, a.shape[1]), lambda r: (r, 0))

    outs = [struct((ch, HW), F32), struct((ch, HW), BF), struct((ch, 128), F32)]
    ins = (*addends, hidden, stat, par, cot)
    return pl.pallas_call(
        functools.partial(norm_three_back_kernel, len(addends)),
        grid=(ch // rows,),
        out_shape=outs,
        in_specs=[part(a) for a in ins],
        out_specs=[part(a) for a in outs],
        compiler_params=params(),
        cost_estimate=cost(20 * ch * HW, 16 * ch * HW),
        name="norm_three_back",
    )(*ins)


def piece_columns(meta, w_ref, pieces):
    first = meta[0]
    acc = None
    for x_ref in pieces:
        rows = x_ref.shape[0]
        term = dot(w_ref[:, pl.ds(pl.multiple_of(first, rows), rows)], x_ref[...])
        acc = term if acc is None else acc + term
        first = w_ref.shape[1] - rows - first
    return acc


def inputs_kernel(n, meta, w_ref, *refs):
    pieces, (bias_ref, out_ref) = refs[:n], refs[n:]
    out_ref[...] = (piece_columns(meta, w_ref, pieces) + bias_ref[...]).astype(BF)


def inputs_product(meta, weight, pieces, bias, width=1024, name=None):
    rows, depth = weight.shape
    return pl.pallas_call(
        functools.partial(inputs_kernel, len(pieces)),
        grid=(HW // width,),
        out_shape=struct((rows, HW), BF),
        in_specs=[scalars(), pl.BlockSpec((rows, depth), lambda p: (0, 0))]
        + [pl.BlockSpec((x.shape[0], width), lambda p: (0, p)) for x in pieces]
        + [pl.BlockSpec((rows, 1), lambda p: (0, 0))],
        out_specs=pl.BlockSpec((rows, width), lambda p: (0, p)),
        compiler_params=params(),
        cost_estimate=cost(2 * rows * depth * HW, (rows + depth) * HW * 2),
        name=name,
    )(meta, weight, *pieces, bias)


def parts_kernel(n, meta, w_ref, *refs):
    pieces, outs = refs[:n], refs[n:]
    first = meta[0]
    for out_ref in outs:
        rows = out_ref.shape[0]
        row = pl.ds(pl.multiple_of(first, rows), rows)
        acc = None
        at = 0
        for x_ref in pieces:
            depth = x_ref.shape[0]
            term = dot(w_ref[row, at : at + depth], x_ref[...])
            acc = term if acc is None else acc + term
            at += depth
        out_ref[...] = acc.astype(BF)
        first = w_ref.shape[0] - rows - first


def parts_product(meta, weight, pieces, count, width=1024, name=None):
    rows, depth = weight.shape
    part = struct((rows // count, HW), BF)
    return pl.pallas_call(
        functools.partial(parts_kernel, len(pieces)),
        grid=(HW // width,),
        out_shape=[part] * count,
        in_specs=[scalars(), pl.BlockSpec((rows, depth), lambda p: (0, 0))]
        + [pl.BlockSpec((x.shape[0], width), lambda p: (0, p)) for x in pieces],
        out_specs=[pl.BlockSpec((rows // count, width), lambda p: (0, p))] * count,
        compiler_params=params(),
        cost_estimate=cost(2 * rows * depth * HW, (rows + depth) * HW * 2),
        name=name,
    )(meta, weight, *pieces)


def output_kernel(n, meta, w_ref, *refs):
    pieces, (bias_ref, hidden_ref, out_ref) = refs[:n], refs[n:]
    acc = hidden_ref[...] + bias_ref[...] + piece_columns(meta, w_ref, pieces)
    half = acc.shape[1] // 2
    for base, val in zip((0, HW // 2), unfold(acc)):
        first = pl.multiple_of(base + pl.program_id(0) * half, half)
        out_ref[:, pl.ds(first, half)] = val.astype(BF)


def output_product(meta, weight, pieces, bias, hidden, width=1024):
    rows, depth = weight.shape
    return pl.pallas_call(
        functools.partial(output_kernel, len(pieces)),
        grid=(HW // width,),
        out_shape=struct((rows, HW), BF),
        in_specs=[scalars(), pl.BlockSpec((rows, depth), lambda p: (0, 0))]
        + [pl.BlockSpec((x.shape[0], width), lambda p: (0, p)) for x in pieces]
        + [
            pl.BlockSpec((rows, 1), lambda p: (0, 0)),
            pl.BlockSpec((rows, width), lambda p: (0, p)),
        ],
        out_specs=pl.BlockSpec((rows, HW), lambda p: (0, 0)),
        compiler_params=params(),
        cost_estimate=cost(2 * rows * depth * HW, (rows * 3 + depth) * HW * 2),
        name="output",
    )(meta, weight, *pieces, bias, hidden)


def outer_kernel(n_left, n_right, meta, *refs):
    lefts, rights = refs[:n_left], refs[n_left : n_left + n_right]
    out_ref, sums_ref = refs[n_left + n_right : n_left + n_right + 2]
    acc_ref, tot_ref = refs[n_left + n_right + 2 :]
    step = pl.program_id(0)

    @pl.when(step == 0)
    def _():
        acc_ref[...] = jnp.zeros_like(acc_ref)
        tot_ref[...] = jnp.zeros_like(tot_ref)

    row = 0
    for left in lefts:
        rows = left.shape[0]
        val = left[...]
        first = meta[0]
        for right in rights:
            cols = right.shape[0]
            at = pl.ds(pl.multiple_of(first, cols), cols)
            acc_ref[row : row + rows, at] += dot_nt(val, right[...])
            first = acc_ref.shape[1] - cols - first
        tot_ref[row : row + rows, :] += jnp.sum(val.astype(F32), axis=1, keepdims=True)
        row += rows

    @pl.when(step == pl.num_programs(0) - 1)
    def _():
        out_ref[...] = acc_ref[...].astype(BF)
        sums_ref[...] = tot_ref[...]


def outer(meta, lefts, rights, width=1024, name=None):
    rows, cols = sum(a.shape[0] for a in lefts), sum(a.shape[0] for a in rights)
    fixed = lambda p: (0, 0)
    return pl.pallas_call(
        functools.partial(outer_kernel, len(lefts), len(rights)),
        grid=(HW // width,),
        out_shape=[struct((rows, cols), BF), struct((rows, 128), F32)],
        in_specs=[scalars()]
        + [pl.BlockSpec((a.shape[0], width), lambda p: (0, p)) for a in (*lefts, *rights)],
        out_specs=[pl.BlockSpec((rows, cols), fixed), pl.BlockSpec((rows, 128), fixed)],
        scratch_shapes=[pltpu.VMEM((rows, cols), F32), pltpu.VMEM((rows, 128), F32)],
        compiler_params=params(),
        cost_estimate=cost(2 * rows * cols * HW, (rows + cols) * HW * 2),
        name=name,
    )(meta, *lefts, *rights)


def attention_kernel(
    n_grads, lim_ref, q_ref, k_ref, v_ref, kc_ref, vc_ref, *refs, unroll, back,
):
    g_refs, refs = refs[:n_grads], refs[n_grads:]
    o_ref, dq_ref, dk_ref, dv_ref, dkc_ref, dvc_ref = refs[:6]
    kt, vt, kn, vn, s_even, s_odd, p_sc, tops, o_acc, dk_acc, dv_acc = refs[6:]
    step, last = pl.program_id(1), pl.num_programs(1) - 1
    width = q_ref.shape[-1]
    blocks = KEYS // BLOCK

    @pl.when(step == 0)
    def _():
        spare = jnp.zeros((HEAD_DIM, KEYS - HW - CTXP), BF)
        for ref, own, ctx in ((kn, k_ref, kc_ref), (vn, v_ref, vc_ref)):
            ref[:, :HW] = own[0, 0]
            ref[:, HW : HW + CTXP] = ctx[0, 0]
            ref[:, HW + CTXP :] = spare
        row = lax.broadcasted_iota(jnp.int32, (HEAD_DIM, BLOCK), 0)
        for n in range(blocks):
            at = slice(n * BLOCK, (n + 1) * BLOCK)
            key = lax.broadcasted_iota(jnp.int32, (HEAD_DIM, BLOCK), 1) + n * BLOCK
            fill = jnp.where((row == 0) & (key >= HW + lim_ref[0]), NEG_FILL, 0.0)
            kt[at, :] = jnp.concatenate([kn[:, at].astype(F32), fill], 0).T.astype(BF)
            vt[at, :] = jnp.concatenate([vn[:, at].astype(F32), jnp.zeros_like(fill)], 0).T.astype(BF)
        dk_acc[...] = jnp.zeros_like(dk_acc)
        dv_acc[...] = jnp.zeros_like(dv_acc)

    def keys_at(n):
        return pl.ds(pl.multiple_of(n * BLOCK, BLOCK), BLOCK)

    scale = HEAD_DIM ** (-0.5)
    q = (q_ref[0, 0].astype(F32) * scale).astype(BF)
    one = jnp.where(lax.broadcasted_iota(jnp.int32, (HEAD_DIM, width), 0) == 0, 1.0, 0.0).astype(BF)
    q_more = jnp.concatenate([q, one], 0)

    def score(n, held):
        scores = dot(kt[keys_at(n), :], q_more)
        held[...] = scores
        return jnp.max(jnp.max(scores.reshape(BLOCK // 8, 8, width), axis=0), axis=0, keepdims=True)

    o_acc[...] = jnp.zeros_like(o_acc)

    def forward(n, held, top, total, shrink):
        raised = jnp.exp(held[...] - top)
        low = raised.astype(BF)
        p_sc[keys_at(n), :] = low
        tops[n, 0:1, :] = top
        sums = jnp.sum(raised.reshape(BLOCK // 8, 8, width), axis=0)
        o_acc[...] = o_acc[...] * shrink + dot(vn[:, keys_at(n)], low)
        return total * shrink + sums

    def forward_step(n, held, ahead_held, carry):
        top, total, shrink = carry
        ahead = jnp.maximum(top, score(n + 1, ahead_held))
        total = forward(n, held, top, total, shrink)
        return ahead, total, jnp.exp(top - ahead)

    held = (s_even, s_odd)

    def forward_run(j, carry):
        for u in range(unroll):
            carry = forward_step(unroll * j + u, held[u % 2], held[1 - u % 2], carry)
        return carry

    carry = (score(0, s_even), jnp.zeros((8, width), F32), jnp.ones((1, width), F32))
    carry = lax.fori_loop(0, blocks // unroll - 1, forward_run, carry)
    for n in range(blocks - unroll, blocks - 1):
        carry = forward_step(n, held[n % 2], held[1 - n % 2], carry)
    top, total, shrink = carry
    total = forward(blocks - 1, s_odd, top, total, shrink)

    inverse = 1.0 / jnp.sum(total, axis=0, keepdims=True)
    mixed = o_acc[...] * inverse
    o_ref[0] = mixed.astype(BF)
    grad = sum(g_ref[0].astype(F32) for g_ref in g_refs)
    if n_grads > 1:
        grad = grad.astype(BF).astype(F32)
    delta = jnp.sum(grad * mixed, axis=0, keepdims=True)
    dq = jnp.zeros((HEAD_DIM, width), F32)
    none = jnp.zeros((HEAD_DIM, width), BF)
    for c in range(0, KEYS, back):
        at = slice(c, c + back)
        slopes = []
        for n in range(c // BLOCK, (c + back) // BLOCK):
            sub = slice(n * BLOCK, (n + 1) * BLOCK)
            factor = inverse * jnp.exp(tops[n, 0:1, :] - top)
            grad_low = (grad * factor).astype(BF)
            both = jnp.concatenate([grad_low, none], 0)
            probs = p_sc[sub, :]
            slope = (dot(vt[sub, :], both) - delta * factor).astype(BF) * probs
            slopes.append(slope)
            dv_acc[:, sub] += dot_nt(grad_low, probs)
        slope = jnp.concatenate(slopes, 0)
        dq = dq + dot(kn[:, at], slope)
        dk_acc[:, at] += dot_nt(q, slope)
    dq_ref[0] = (dq * scale).astype(BF)

    @pl.when(step == last)
    def _():
        dk_ref[0] = dk_acc[:, :HW].astype(BF)
        dv_ref[0] = dv_acc[:, :HW].astype(BF)
        dkc_ref[0] = dk_acc[:, HW : HW + CTXP].astype(BF)
        dvc_ref[0] = dv_acc[:, HW : HW + CTXP].astype(BF)


def attention(limit, qkv, ctx_kv, grads, width=1024, unroll=6, back=256):
    heads = qkv.shape[1]
    keys = KEYS

    def part(t, w, moving):
        return pl.BlockSpec(
            (1, 1, HEAD_DIM, w), (lambda h, i: (t, h, 0, i)) if moving else (lambda h, i: (t, h, 0, 0))
        )

    def row(w, moving):
        return pl.BlockSpec(
            (1, HEAD_DIM, w), (lambda h, i: (h, 0, i)) if moving else (lambda h, i: (h, 0, 0))
        )

    big, small = struct((heads, HEAD_DIM, HW), BF), struct((heads, HEAD_DIM, CTXP), BF)
    return pl.pallas_call(
        functools.partial(attention_kernel, len(grads), unroll=unroll, back=back),
        grid=(heads, HW // width),
        in_specs=[
            pl.BlockSpec(memory_space=pltpu.SMEM),
            part(0, width, True),
            part(1, HW, False),
            part(2, HW, False),
            part(0, CTXP, False),
            part(1, CTXP, False),
        ]
        + [row(width, True)] * len(grads),
        out_specs=[
            row(width, True),
            row(width, True),
            row(HW, False),
            row(HW, False),
            row(CTXP, False),
            row(CTXP, False),
        ],
        out_shape=[big, big, big, big, small, small],
        scratch_shapes=[
            pltpu.VMEM((keys, 2 * HEAD_DIM), BF),
            pltpu.VMEM((keys, 2 * HEAD_DIM), BF),
            pltpu.VMEM((HEAD_DIM, keys), BF),
            pltpu.VMEM((HEAD_DIM, keys), BF),
            pltpu.VMEM((BLOCK, width), F32),
            pltpu.VMEM((BLOCK, width), F32),
            pltpu.VMEM((keys, width), BF),
            pltpu.VMEM((keys // BLOCK, 8, width), F32),
            pltpu.VMEM((HEAD_DIM, width), F32),
            pltpu.VMEM((HEAD_DIM, keys), F32),
            pltpu.VMEM((HEAD_DIM, keys), F32),
        ],
        compiler_params=params(dimension_semantics=("arbitrary", "arbitrary")),
        cost_estimate=cost(
            24 * heads * HW * keys * HEAD_DIM, heads * HEAD_DIM * 8 * HW * 2, heads * HW * keys
        ),
        name="attention",
    )(limit, qkv, qkv, qkv, ctx_kv, ctx_kv, *grads)


class Alone:
    parts = 1

    def __init__(self, mesh):
        self.images = mesh.shape["dp"]

    def meta(self):
        return jnp.array([0, 1], jnp.int32)

    def image(self):
        return lax.axis_index("dp")

    def got(self, x):
        return x

    def pick(self, own, got):
        return own

    def gather(self, x):
        return (lax.all_gather(x, "tensor", axis=0, tiled=True),)

    def scatter(self, parts):
        return (lax.psum_scatter(parts[0], "tensor", scatter_dimension=0, tiled=True),)

    def turn(self, meta, w):
        ch = w.shape[0]
        cut = w.reshape(ch, 9, C)
        turned = lax.all_to_all(cut, "tensor", split_axis=2, concat_axis=0, tiled=True)
        return turned[:, ::-1].transpose(2, 1, 0).reshape(ch, 9 * C)

    def total(self, x):
        return lax.psum(x, "dp")

    def everywhere(self, x):
        return lax.psum(x, "dp")

    def sum_owned(self, x, late):
        return lax.psum(x, "dp")


class Paired:
    parts = 2

    def __init__(self, mesh):
        dp = mesh.shape["dp"]
        self.images = dp
        self.far = [
            ((2 * k + core) * 2 + 1 - core, (2 * k + 1 - core) * 2 + core)
            for k in range(dp // 2)
            for core in range(2)
        ]
        self.bits = [1 << b for b in range((dp - 1).bit_length())]

    def half(self):
        return lax.axis_index("dp") % 2

    def stays(self):
        return self.half() == lax.axis_index("tensor")

    def meta(self):
        return jnp.stack([self.half() * (C // 2), self.stays().astype(jnp.int32)]).astype(jnp.int32)

    def image(self):
        return lax.axis_index("dp") // 2 * 2 + lax.axis_index("tensor")

    def got(self, x):
        return lax.ppermute(x, ("dp", "tensor"), self.far)

    def pick(self, own, got):
        return jnp.where(self.stays(), own, got)

    def over(self, x, bit):
        return lax.ppermute(x, "dp", [(i, i ^ bit) for i in range(self.images)])

    def gather(self, x):
        return (x, self.over(x, 1))

    def scatter(self, parts):
        return (parts[0], self.over(parts[1], 1))

    def turn(self, meta, w):
        return turned_pair(meta, w, self.over(w, 1))

    def total(self, x):
        x = x + lax.ppermute(x, "tensor", [(0, 1), (1, 0)])
        for bit in self.bits[1:]:
            x = x + self.over(x, bit)
        return self.pick(x, self.over(x, 1))

    def everywhere(self, x):
        for bit in self.bits:
            x = x + self.over(x, bit)
        return x

    def sum_owned(self, x, late):
        rows = x.shape[0] // 2
        order = (self.bits, [self.bits[0], *self.bits[2:], self.bits[1]])
        parts = [lax.slice_in_dim(x, at * rows, (at + 1) * rows) for at in range(2)]

        def upper(bit):
            return (lax.axis_index("dp") // bit) % 2

        for step in range(len(self.bits)):
            size = parts[0].shape[0] // 2
            for at in range(2):
                bit = order[at][step]
                keep = lax.dynamic_slice_in_dim(parts[at], upper(bit) * size, size)
                send = lax.dynamic_slice_in_dim(parts[at], (1 - upper(bit)) * size, size)
                parts[at] = (keep.astype(F32) + self.over(send, bit).astype(F32)).astype(BF)
        parts = list(after(late, *parts))
        for step in reversed(range(len(self.bits))):
            for at in range(2):
                bit = order[at][step]
                other = self.over(parts[at], bit)
                parts[at] = jnp.where(
                    upper(bit) == 0,
                    jnp.concatenate([parts[at], other]),
                    jnp.concatenate([other, parts[at]]),
                )
        return jnp.concatenate(parts)


def after(first, *later):
    held = lax.optimization_barrier((first, *later))
    return held[1:] if len(later) > 1 else held[1]


def local(plan, features, cotangent, embedding, context, lengths, norm1_gain, norm1_bias,
    conv1_weight, conv1_bias, emb_weight, emb_bias, norm2_gain, norm2_bias, conv2_weight,
    conv2_bias, norm3_gain, norm3_bias, qkv_weight, qkv_bias, context_weight, context_bias,
    out_weight, out_bias,
):
    ch, images, pixels = features.shape
    heads = ch // HEAD_DIM
    meta = plan.meta()
    moved = plan.parts == 2

    emb_act = jax.nn.silu(embedding.astype(F32)).astype(BF)
    scale_shift = (
        jnp.einsum("ie,teo->to", emb_act, emb_weight, preferred_element_type=F32) + emb_bias
    )
    length_row = jnp.broadcast_to(lengths.astype(F32)[:, None], (1, ch))
    vectors = jnp.concatenate(
        [
            jnp.stack([norm1_gain, norm1_bias, conv1_bias, norm2_gain, norm2_bias]),
            scale_shift,
            jnp.stack([conv2_bias, norm3_gain, norm3_bias, out_bias]),
            qkv_bias,
            length_row,
        ]
    )
    f_own = features.reshape(ch, pixels)
    f_got = plan.got(f_own)
    vectors, w1_own = after(scale_shift, vectors, conv1_weight)
    vectors = plan.pick(vectors, plan.got(vectors))
    w1_got = plan.got(w1_own)
    ctx_kv = (
        jnp.einsum("toe,ne->ton", context_weight, context[0], preferred_element_type=F32)
        + context_bias[:, :, None]
    ).astype(BF)
    ctx_kv = jnp.pad(ctx_kv, ((0, 0), (0, 0), (0, CTXP - CTX)))
    emb_all = jnp.where(
        jnp.arange(plan.images)[:, None] == lax.axis_index("dp"), emb_act, jnp.zeros_like(emb_act)
    )
    emb_all = plan.everywhere(emb_all)
    length = vectors[14, :1].astype(jnp.int32)
    par_one, par_two, par_three = vectors[0:2].T, vectors[2:7].T, vectors[7:10].T
    par_one = after(emb_all, par_one)
    w2_got = plan.got(after(vectors, conv2_weight))
    act_one, stat_one, f_low = first_activation(meta, f_own, f_got, par_one)
    full_one = plan.gather(act_one)
    mats_own = jnp.concatenate([qkv_weight.reshape(3 * ch, C), out_weight])
    mats_own, ctx_own = after(act_one, mats_own, ctx_kv)
    mats_got, ctx_got = plan.got(mats_own), plan.got(ctx_own)
    cot_own = after((mats_got, ctx_got), cotangent.reshape(ch, pixels))
    cot_got = plan.got(cot_own)

    low, stat, wide = struct((ch, HW), BF), struct((ch, 128), F32), struct((ch, HW), F32)
    weight = struct((ch, 9 * C), BF)
    act_two, stat_two, conv_one, w1 = conv_call(
        conv_one_kernel, meta, (conv1_weight, w1_got), full_one, (par_two,), (),
        [low, stat], [wide, weight], [], "conv_one",
    )
    full_two = plan.gather(act_two)
    if moved:
        full_two = after((mats_got, ctx_got), *full_two)
    normed, stat_three, hidden, w2 = conv_call(
        conv_two_kernel, meta, (conv2_weight, w2_got), full_two, (par_three, f_low), (),
        [low, stat], [wide, weight], [], "conv_two",
    )
    full_three = plan.gather(normed)
    cot_got = after(normed, cot_got)
    mats = plan.pick(mats_own, mats_got)
    w_qkv, w_out = mats[: 3 * ch], mats[3 * ch :]
    cot = folded(meta, cot_own, cot_got)
    grad_heads = plan.scatter(
        parts_product(meta, w_out.T, (cot,), plan.parts, name="grad_heads")
    )
    qkv = inputs_product(meta, w_qkv, full_three, vectors[11:14].reshape(3 * ch, 1), name="qkv")
    ctx_kv = plan.pick(ctx_own, ctx_got)
    mixed, dq, dk, dv, dkc, dvc = attention(
        4 + length,
        qkv.reshape(3, heads, HEAD_DIM, HW),
        ctx_kv.reshape(2, heads, HEAD_DIM, CTXP),
        [a.reshape(heads, HEAD_DIM, HW) for a in grad_heads],
    )

    flat = lambda a: a.reshape(ch, HW)
    dq, dk, dv = flat(dq), flat(dk), flat(dv)
    addends = plan.scatter(
        parts_product(meta, w_qkv.T, (dq, dk, dv), plan.parts, name="grad_normed")
    )
    full_heads = plan.gather(flat(mixed))
    ctx_own = jnp.concatenate([a.reshape(1, ch, CTXP) for a in (dkc, dvc)])
    ctx_got = plan.got(ctx_own)
    turned_two = plan.turn(meta, after(mixed, w2))
    dw_qkv, db_qkv = outer(meta, (dq, dk, dv), full_three, name="qkv_grad")
    dw_out, _ = outer(meta, (cot,), full_heads, name="out_grad")
    mats_own = jnp.concatenate([dw_qkv, dw_out])
    mats_got = plan.got(mats_own)
    grad_hidden, grad_two, sums_three = norm_three_back(addends, hidden, stat_three, par_three, cot)
    full_grad_two = plan.gather(grad_two)
    dw_two = conv_weight_grad(meta, grad_two, full_two, "conv_two_weight_grad")
    two_got = plan.got(dw_two)
    full_grad_two = after(dw_two, *full_grad_two) if moved else full_grad_two
    grad_one, sums_two = conv_call(
        conv_two_back_kernel, meta, (turned_two, turned_two), full_grad_two, (par_two, stat_two),
        (conv_one,), [low, stat], [], [pltpu.VMEM((ch, HW), F32)], "conv_two_back",
    )
    full_grad_one = plan.gather(grad_one)
    turned_one = plan.turn(meta, after(mixed, w1))
    mats_got, ctx_got, two_got = after(grad_one, mats_got, ctx_got, two_got)
    ctx_grad = plan.pick(ctx_own, ctx_got)[:, :, :CTX]
    dw_ctx = jnp.einsum("ton,ne->toe", ctx_grad, context[0], preferred_element_type=F32).astype(BF)
    mats = plan.pick(mats_own, mats_got)
    dw_two = plan.pick(dw_two, two_got)
    early = jnp.concatenate(
        [dw_ctx[0], dw_ctx[1], *(mats[t * ch : (t + 1) * ch] for t in range(4)), dw_two], 1
    )
    held = after(early, grad_one)
    early = lax.psum_scatter(early, "dp", scatter_dimension=0, tiled=True)
    dw_one = conv_weight_grad(meta, held, full_one, "conv_one_weight_grad")
    one_got = plan.got(dw_one)
    full_grad_one = after(dw_one, *full_grad_one) if moved else full_grad_one
    input_grad, sums_one = conv_call(
        conv_one_back_kernel, meta, (turned_one, turned_one), full_grad_one,
        (par_one, stat_one, f_low), (grad_hidden,),
        [struct((ch, HW), BF if moved else F32), stat], [],
        [pltpu.VMEM((ch, HW), F32)], "conv_one_back",
    )
    input_got = plan.got(input_grad)

    output = output_product(
        meta, w_out, full_heads, vectors[10].reshape(ch, 1), after((input_grad, one_got), hidden)
    )
    output_got = plan.got(output)
    ctx_sums = jnp.sum(ctx_own.astype(F32), axis=2)
    sums_two = sums_two[:, :5].T
    own_mod = sums_two[2:4].astype(BF).astype(F32)
    mods = jnp.where(
        (jnp.arange(plan.images) == plan.image())[:, None, None], own_mod, jnp.zeros_like(own_mod)
    ).reshape(2 * plan.images, ch)
    small = plan.total(
        jnp.concatenate(
            [
                sums_three[:, :4].T,
                db_qkv[:, 0].reshape(3, ch),
                sums_two[:2],
                sums_two[4:5],
                ctx_sums,
                sums_one[:, :2].T,
                mods,
            ]
        )
    )
    early, dw_one, one_got = after((output, small), early, dw_one, one_got)
    early = lax.all_gather(early, "dp", axis=0, tiled=True)
    dw_one = plan.sum_owned(plan.pick(dw_one, one_got), (input_got, output_got))
    mods = small[14:].reshape(plan.images, 2, ch)
    mods_low = mods.astype(BF)
    dw_emb = jnp.stack(
        [
            jnp.einsum("ie,io->eo", emb_all, mods_low[:, t], preferred_element_type=F32)
            for t in range(2)
        ]
    )
    input_grad = plan.pick(input_grad, input_got).astype(F32)
    output = plan.pick(output, output_got)
    early = after((dw_one, small, input_grad, output), early)
    dw_ctx = jnp.stack([early[:, n * CTX_EMB : (n + 1) * CTX_EMB] for n in range(2)])
    first = 2 * CTX_EMB
    mats = [early[:, first + n * C : first + (n + 1) * C].astype(F32) for n in range(4)]
    dw_two = early[:, first + 4 * C :]

    return (
        output.reshape(ch, images, pixels),
        input_grad.reshape(ch, images, pixels),
        small[12],
        small[13],
        dw_one.astype(F32),
        small[9],
        dw_emb,
        jnp.sum(mods, axis=0),
        small[7],
        small[8],
        dw_two.astype(F32),
        small[2],
        small[0],
        small[1],
        jnp.stack(mats[:3]),
        small[4:7],
        dw_ctx.astype(F32),
        small[10:12],
        mats[3],
        small[3],
    )


def solution(mesh):
    paired = mesh.shape["tensor"] == 2 and mesh.shape["dp"] % 2 == 0
    plan = Paired(mesh) if paired else Alone(mesh)
    specs = (
        P("tensor", "dp", None),
        P("tensor", "dp", None),
        P("dp", None),
        P("dp", None, None),
        P("dp"),
        P("tensor"),
        P("tensor"),
        P("tensor", None),
        P("tensor"),
        P(None, None, "tensor"),
        P(None, "tensor"),
        P("tensor"),
        P("tensor"),
        P("tensor", None),
        P("tensor"),
        P("tensor"),
        P("tensor"),
        P(None, "tensor", None),
        P(None, "tensor"),
        P(None, "tensor", None),
        P(None, "tensor"),
        P("tensor", None),
        P("tensor"),
    )
    return jax.shard_map(
        functools.partial(local, plan),
        mesh=mesh,
        in_specs=specs,
        out_specs=(
            P("tensor", "dp", None),
            P("tensor", "dp", None),
            P("tensor"),
            P("tensor"),
            P("tensor", None),
            P("tensor"),
            P(None, None, "tensor"),
            P(None, "tensor"),
            P("tensor"),
            P("tensor"),
            P("tensor", None),
            P("tensor"),
            P("tensor"),
            P("tensor"),
            P(None, "tensor", None),
            P(None, "tensor"),
            P(None, "tensor", None),
            P(None, "tensor"),
            P("tensor", None),
            P("tensor"),
        ),
        check_vma=False,
    )
```

```python
import functools

import jax
import jax.numpy as jnp
from jax import lax
from jax.experimental import pallas as pl
from jax.experimental.pallas import tpu as pltpu
from jax.sharding import PartitionSpec as P

C = 512
HEAD_DIM = 64
PER_GROUP = 16
SIDE = 64
HW = 4096
CTX = 260
CTXP = 384
CTX_EMB = 2048
BLOCK = 256
KEYS = 4608
PAD = 128
FILL = 32
SCALE = 100
EPSILON = 1e-05
NEG_FILL = -1e30
F32 = jnp.float32
BF = jnp.bfloat16
NT = (((1,), (1,)), ((), ()))
VMEM_BYTES = 62 << 20


def dot(a, b):
    return jnp.dot(a, b, preferred_element_type=F32)


def dot_nt(a, b):
    return lax.dot_general(a, b, NT, preferred_element_type=F32)


def whole():
    return pl.BlockSpec(memory_space=pltpu.VMEM)


def placed():
    return pl.BlockSpec(memory_space=pl.ANY)


def scalars():
    return pl.BlockSpec(memory_space=pltpu.SMEM)


def params(**kwargs):
    return pltpu.CompilerParams(vmem_limit_bytes=VMEM_BYTES, **kwargs)


def cost(flops, nbytes, transcendentals=0):
    return pl.CostEstimate(
        flops=flops // SCALE, bytes_accessed=nbytes // SCALE, transcendentals=transcendentals // SCALE
    )


def struct(shape, dtype):
    return jax.ShapeDtypeStruct(shape, dtype)


def fetch(meta, own_ref, got_ref, buf, sem):
    @pl.when(meta[1] == 1)
    def _():
        pltpu.make_async_copy(own_ref, buf, sem).start()

    @pl.when(meta[1] != 1)
    def _():
        pltpu.make_async_copy(got_ref, buf, sem).start()


def arrive(own_ref, buf, sem):
    pltpu.make_async_copy(own_ref, buf, sem).wait()


def group_scalar(column):
    return jnp.sum(column, axis=0, keepdims=True) * (1.0 / (PER_GROUP * HW))


def group_stats(vals):
    mean = group_scalar(jnp.sum(vals, axis=1, keepdims=True))
    centred = vals - mean
    var = group_scalar(jnp.sum(centred * centred, axis=1, keepdims=True))
    rstd = lax.rsqrt(var + EPSILON)
    return mean, rstd


def norm_backward(dy_sum, dyx_sum, gain):
    return group_scalar(dy_sum * gain), group_scalar(dyx_sum * gain)


def for_groups(channels, body, together=2):
    def step(g, carry):
        for u in range(together):
            first = pl.multiple_of((g * together + u) * PER_GROUP, PER_GROUP)
            body(pl.ds(first, PER_GROUP))
        return carry

    lax.fori_loop(0, channels // PER_GROUP // together, step, 0)


def columns(values):
    lane = lax.broadcasted_iota(jnp.int32, (PER_GROUP, 128), 1)
    tile = jnp.zeros((PER_GROUP, 128), F32)
    for at, val in enumerate(values):
        tile = jnp.where(lane == at, val, tile)
    return tile


ROWS = SIDE // 2


def lanes(x, n):
    return x[:, 128 * n : 128 * n + 128]


def low_lanes(x):
    return lax.broadcasted_iota(jnp.int32, (x.shape[0], 128), 1) < SIDE


def fold(x):
    low = low_lanes(x)
    out = []
    for r in range(ROWS):
        upper, lower = lanes(x, r // 2), lanes(x, r // 2 + ROWS // 2)
        if r % 2 == 0:
            out.append(jnp.where(low, upper, pltpu.roll(lower, SIDE, 1)))
        else:
            out.append(jnp.where(low, pltpu.roll(upper, SIDE, 1), lower))
    return jnp.concatenate(out, 1)


def unfold(x):
    low = low_lanes(x)
    pairs = range(x.shape[1] // 256)
    top = [jnp.where(low, lanes(x, 2 * n), pltpu.roll(lanes(x, 2 * n + 1), SIDE, 1)) for n in pairs]
    bottom = [
        jnp.where(low, pltpu.roll(lanes(x, 2 * n), SIDE, 1), lanes(x, 2 * n + 1)) for n in pairs
    ]
    return jnp.concatenate(top, 1), jnp.concatenate(bottom, 1)


def fold_kernel(meta, own_ref, got_ref, out_ref, x_buf, sem):
    fetch(meta, own_ref, got_ref, x_buf, sem)
    arrive(own_ref, x_buf, sem)

    def body(rows):
        out_ref[rows, :] = fold(x_buf[rows, :].astype(F32)).astype(BF)

    for_groups(out_ref.shape[0], body)


def folded(meta, own, got):
    return pl.pallas_call(
        fold_kernel,
        out_shape=struct(own.shape, BF),
        in_specs=[scalars(), placed(), placed()],
        out_specs=whole(),
        scratch_shapes=[pltpu.VMEM(own.shape, BF), pltpu.SemaphoreType.DMA(())],
        compiler_params=params(),
        cost_estimate=cost(8 * own.size, 4 * own.size),
        name="fold",
    )(meta, own, got)


def act_one_kernel(meta, own_ref, got_ref, par_ref, act_ref, stat_ref, fold_ref, x_buf, sem):
    fetch(meta, own_ref, got_ref, x_buf, sem)
    arrive(own_ref, x_buf, sem)

    def body(rows):
        vals = fold(x_buf[rows, :].astype(F32))
        fold_ref[rows, :] = vals.astype(BF)
        mean, rstd = group_stats(vals)
        par = par_ref[rows, :]
        out = (vals - mean) * (rstd * par[:, 0:1]) + par[:, 1:2]
        act_ref[rows, :] = (out * jax.nn.sigmoid(out)).astype(BF)
        stat_ref[rows, :] = columns([mean, rstd])

    for_groups(act_ref.shape[0], body)


def first_activation(meta, own, got, par):
    ch = own.shape[0]
    return pl.pallas_call(
        act_one_kernel,
        out_shape=[struct((ch, HW), BF), struct((ch, 128), F32), struct((ch, HW), BF)],
        in_specs=[scalars(), placed(), placed(), whole()],
        out_specs=[whole()] * 3,
        scratch_shapes=[pltpu.VMEM((ch, HW), BF), pltpu.SemaphoreType.DMA(())],
        compiler_params=params(),
        cost_estimate=cost(20 * ch * HW, 6 * ch * HW, ch * HW),
        name="act_one",
    )(meta, own, got, par)


def fill_shifted(xs, pieces, first):
    start = first
    for x_ref in pieces:
        rows = x_ref.shape[0]

        def step(r, carry, x_ref=x_ref, start=start):
            off = pl.multiple_of(r * FILL, FILL)
            at = pl.ds(pl.multiple_of(start + off, FILL), FILL)
            lane = lax.broadcasted_iota(jnp.int32, (FILL, 128), 1)
            low = lane < SIDE
            left, right = lane % SIDE == 0, lane % SIDE == SIDE - 1
            zero = jnp.zeros((FILL, 128), F32)
            here = pl.ds(off, FILL)
            for n in range(ROWS):
                x = x_ref[here, 128 * n : 128 * n + 128].astype(F32)
                kinds = (
                    jnp.where(left, zero, pltpu.roll(x, 1, 1)),
                    x,
                    jnp.where(right, zero, pltpu.roll(x, 127, 1)),
                )
                for d, y in enumerate(kinds):
                    xs[d, at, PAD + 128 * n : PAD + 128 * n + 128] = y.astype(BF)
                    if n == ROWS - 1:
                        xs[d, at, :PAD] = jnp.where(low, zero, pltpu.roll(y, SIDE, 1)).astype(BF)
                    if n == 0:
                        xs[d, at, PAD + HW :] = jnp.where(
                            low, pltpu.roll(y, SIDE, 1), zero
                        ).astype(BF)
            return carry

        lax.fori_loop(0, rows // FILL, step, 0)
        start = xs.shape[1] - rows - start if len(pieces) == 2 else start + rows


def window(xs, tap, start, width):
    first = PAD + start + (tap // 3 - 1) * 128
    if not isinstance(start, int):
        first = pl.multiple_of(first, 128)
    return xs[tap % 3, :, pl.ds(first, width)]


def convolve(xs, w_ref, out_ref, add, width=1024):
    depth = xs.shape[1]

    def step(n, carry):
        p = n * width
        acc = dot(w_ref[:, :depth], window(xs, 0, p, width))
        for tap in range(1, 9):
            acc = acc + dot(w_ref[:, tap * depth : (tap + 1) * depth], window(xs, tap, p, width))
        at = pl.ds(pl.multiple_of(p, width), width)
        out_ref[:, at] = add(acc, at)
        return carry

    lax.fori_loop(0, HW // width, step, 0)


def conv_call(kernel, meta, weights, pieces, vmem_in, any_in, outs, any_outs, scratch, name):
    out_ch, depth = weights[0].shape[0], C
    arrays = (weights[0], *pieces, *vmem_in, *any_in)
    nbytes = sum(a.size * a.dtype.itemsize for a in arrays) + out_ch * HW * 4
    return pl.pallas_call(
        functools.partial(kernel, len(pieces)),
        out_shape=[*outs, *any_outs],
        in_specs=[scalars(), placed(), placed()]
        + [whole()] * (len(pieces) + len(vmem_in))
        + [placed()] * len(any_in),
        out_specs=[whole()] * len(outs) + [placed()] * len(any_outs),
        scratch_shapes=[
            pltpu.VMEM((3, depth, HW + 2 * PAD), BF),
            pltpu.VMEM((out_ch, 9 * depth), BF),
            pltpu.VMEM((out_ch, HW), F32),
            pltpu.SemaphoreType.DMA((4,)),
            *scratch,
        ],
        compiler_params=params(),
        cost_estimate=cost(2 * out_ch * 9 * depth * HW, nbytes, out_ch * HW),
        name=name,
    )(meta, *weights, *pieces, *vmem_in, *any_in)


def conv_one_kernel(n, meta, w_own, w_got, *refs):
    pieces, refs = refs[:n], refs[n:]
    par_ref, act_ref, stat_ref, conv_ref, w_ref, xs, w_buf, acc, sems = refs
    fetch(meta, w_own, w_got, w_buf, sems.at[0])
    fill_shifted(xs, pieces, meta[0])
    arrive(w_own, w_buf, sems.at[0])
    keep = pltpu.make_async_copy(w_buf, w_ref, sems.at[2])
    keep.start()
    bias = par_ref[:, 0:1]
    convolve(xs, w_buf, acc, lambda val, at: val + bias)
    store = pltpu.make_async_copy(acc, conv_ref, sems.at[1])
    store.start()

    def body(rows):
        vals = acc[rows, :]
        mean, rstd = group_stats(vals)
        par = par_ref[rows, :]
        gain, shift, factor = par[:, 1:2], par[:, 2:3], 1.0 + par[:, 3:4]
        mid = (vals - mean) * (rstd * gain * factor) + (shift * factor + par[:, 4:5])
        act_ref[rows, :] = (mid * jax.nn.sigmoid(mid)).astype(BF)
        stat_ref[rows, :] = columns([mean, rstd])

    for_groups(acc.shape[0], body)
    store.wait()
    keep.wait()


def conv_two_kernel(n, meta, w_own, w_got, *refs):
    pieces, refs = refs[:n], refs[n:]
    par_ref, f_ref, normed_ref, stat_ref, hidden_ref, w_ref, xs, w_buf, acc, sems = refs
    fetch(meta, w_own, w_got, w_buf, sems.at[0])
    fill_shifted(xs, pieces, meta[0])
    arrive(w_own, w_buf, sems.at[0])
    keep = pltpu.make_async_copy(w_buf, w_ref, sems.at[2])
    keep.start()
    bias = par_ref[:, 0:1]
    convolve(xs, w_buf, acc, lambda val, at: val + bias + f_ref[:, at].astype(F32))
    store = pltpu.make_async_copy(acc, hidden_ref, sems.at[1])
    store.start()

    def body(rows):
        vals = acc[rows, :]
        mean, rstd = group_stats(vals)
        par = par_ref[rows, :]
        normed_ref[rows, :] = ((vals - mean) * (rstd * par[:, 1:2]) + par[:, 2:3]).astype(BF)
        stat_ref[rows, :] = columns([mean, rstd])

    for_groups(acc.shape[0], body)
    store.wait()
    keep.wait()


def silu_slope(mid):
    sig = jax.nn.sigmoid(mid)
    return sig * (1.0 + mid * (1.0 - sig))


def conv_two_back_kernel(n, meta, w_own, w_got, *refs):
    pieces, refs = refs[:n], refs[n:]
    par_ref, stat_ref, conv_ref, grad_ref, sums_ref, xs, w_buf, acc, sems, conv_buf = refs
    fetch(meta, w_own, w_got, w_buf, sems.at[0])
    load = pltpu.make_async_copy(conv_ref, conv_buf, sems.at[1])
    load.start()
    fill_shifted(xs, pieces, meta[0])
    arrive(w_own, w_buf, sems.at[0])
    convolve(xs, w_buf, acc, lambda val, at: val)
    load.wait()

    def body(rows):
        par, stat = par_ref[rows, :], stat_ref[rows, :]
        gain, shift, factor = par[:, 1:2], par[:, 2:3], 1.0 + par[:, 3:4]
        rstd = stat[:, 1:2]
        hat = (conv_buf[rows, :] - stat[:, 0:1]) * rstd
        mid = hat * (gain * factor) + (shift * factor + par[:, 4:5])
        grad = acc[rows, :] * silu_slope(mid)
        total = jnp.sum(grad, axis=1, keepdims=True)
        total_hat = jnp.sum(grad * hat, axis=1, keepdims=True)
        mean_u, mean_uhat = norm_backward(total * factor, total_hat * factor, gain)
        out = ((grad * (factor * gain) - mean_u - hat * mean_uhat) * rstd).astype(BF)
        grad_ref[rows, :] = out
        bias_grad = jnp.sum(out.astype(F32), axis=1, keepdims=True)
        sums_ref[rows, :] = columns(
            [
                total_hat * factor,
                total * factor,
                total_hat * gain + total * shift,
                total,
                bias_grad,
            ]
        )

    for_groups(acc.shape[0], body)


def conv_one_back_kernel(n, meta, w_own, w_got, *refs):
    pieces, refs = refs[:n], refs[n:]
    par_ref, stat_ref, f_ref, hid_ref, grad_ref, sums_ref, xs, w_buf, acc, sems, hid_buf = refs
    fetch(meta, w_own, w_got, w_buf, sems.at[0])
    load = pltpu.make_async_copy(hid_ref, hid_buf, sems.at[1])
    load.start()
    fill_shifted(xs, pieces, meta[0])
    arrive(w_own, w_buf, sems.at[0])
    convolve(xs, w_buf, acc, lambda val, at: val)
    load.wait()

    def body(rows):
        par, stat = par_ref[rows, :], stat_ref[rows, :]
        gain, shift = par[:, 0:1], par[:, 1:2]
        rstd = stat[:, 1:2]
        hat = (f_ref[rows, :].astype(F32) - stat[:, 0:1]) * rstd
        grad = acc[rows, :] * silu_slope(hat * gain + shift)
        total = jnp.sum(grad, axis=1, keepdims=True)
        total_hat = jnp.sum(grad * hat, axis=1, keepdims=True)
        mean_u, mean_uhat = norm_backward(total, total_hat, gain)
        out = hid_buf[rows, :] + (grad * gain - mean_u - hat * mean_uhat) * rstd
        top, bottom = unfold(out)
        grad_ref[rows, : HW // 2] = top.astype(grad_ref.dtype)
        grad_ref[rows, HW // 2 :] = bottom.astype(grad_ref.dtype)
        sums_ref[rows, :] = columns([total_hat, total])

    for_groups(acc.shape[0], body)


def weight_grad_kernel(n, meta, grad_ref, *refs):
    pieces, (out_ref, gs) = refs[:n], refs[n:]
    fill_shifted(gs, (grad_ref,), 0)
    for tap in range(9):
        moved = window(gs, 8 - tap, 0, HW)
        first = meta[0]
        for x_ref in pieces:
            rows = x_ref.shape[0]
            at = pl.ds(pl.multiple_of(tap * C + first, rows), rows)
            out_ref[:, at] = dot_nt(moved, x_ref[...]).astype(BF)
            first = C - rows - first


def conv_weight_grad(meta, grad, pieces, name):
    out_ch = grad.shape[0]
    return pl.pallas_call(
        functools.partial(weight_grad_kernel, len(pieces)),
        out_shape=struct((out_ch, 9 * C), BF),
        in_specs=[scalars()] + [whole()] * (1 + len(pieces)),
        out_specs=whole(),
        scratch_shapes=[pltpu.VMEM((3, out_ch, HW + 2 * PAD), BF)],
        compiler_params=params(),
        cost_estimate=cost(2 * out_ch * 9 * C * HW, (out_ch + C) * HW * 2 + out_ch * 9 * C * 2),
        name=name,
    )(meta, grad, *pieces)


def turn_kernel(meta, own_ref, other_ref, out_ref):
    half = own_ref.shape[0]
    for tap in range(9):
        at = pl.ds(pl.multiple_of(tap * C + meta[0], half), half)
        row = meta[0]
        for ref in (own_ref, other_ref):
            to = pl.ds(pl.multiple_of((8 - tap) * C + row, half), half)
            out_ref[:, to] = ref[:, at].astype(F32).T.astype(BF)
            row = half - row


def turned_pair(meta, own, other):
    return pl.pallas_call(
        turn_kernel,
        out_shape=struct(own.shape, BF),
        in_specs=[scalars(), whole(), whole()],
        out_specs=whole(),
        compiler_params=params(),
        cost_estimate=cost(0, 3 * own.size * 2),
        name="turn",
    )(meta, own, other)


def norm_three_back_kernel(n, *refs):
    addends, (hidden_ref, stat_ref, par_ref, cot_ref, hid_ref, grad_ref, sums_ref) = (
        refs[:n],
        refs[n:],
    )

    def body(rows):
        dy = addends[0][rows, :].astype(F32)
        for extra in addends[1:]:
            dy = dy + extra[rows, :].astype(F32)
        par, stat = par_ref[rows, :], stat_ref[rows, :]
        gain, rstd = par[:, 1:2], stat[:, 1:2]
        hat = (hidden_ref[rows, :] - stat[:, 0:1]) * rstd
        total = jnp.sum(dy, axis=1, keepdims=True)
        total_hat = jnp.sum(dy * hat, axis=1, keepdims=True)
        mean_u, mean_uhat = norm_backward(total, total_hat, gain)
        top = cot_ref[rows, :].astype(F32)
        out = top + (dy * gain - mean_u - hat * mean_uhat) * rstd
        hid_ref[rows, :] = out
        low = out.astype(BF)
        grad_ref[rows, :] = low
        sums_ref[rows, :] = columns(
            [
                total_hat,
                total,
                jnp.sum(low.astype(F32), axis=1, keepdims=True),
                jnp.sum(top, axis=1, keepdims=True),
            ]
        )

    for_groups(hidden_ref.shape[0], body)


def norm_three_back(addends, hidden, stat, par, cot):
    ch = hidden.shape[0]
    rows = 32

    def part(a):
        return pl.BlockSpec((rows, a.shape[1]), lambda r: (r, 0))

    outs = [struct((ch, HW), F32), struct((ch, HW), BF), struct((ch, 128), F32)]
    ins = (*addends, hidden, stat, par, cot)
    return pl.pallas_call(
        functools.partial(norm_three_back_kernel, len(addends)),
        grid=(ch // rows,),
        out_shape=outs,
        in_specs=[part(a) for a in ins],
        out_specs=[part(a) for a in outs],
        compiler_params=params(),
        cost_estimate=cost(20 * ch * HW, 16 * ch * HW),
        name="norm_three_back",
    )(*ins)


def piece_columns(meta, w_ref, pieces):
    first = meta[0]
    acc = None
    for x_ref in pieces:
        rows = x_ref.shape[0]
        term = dot(w_ref[:, pl.ds(pl.multiple_of(first, rows), rows)], x_ref[...])
        acc = term if acc is None else acc + term
        first = w_ref.shape[1] - rows - first
    return acc


def inputs_kernel(n, meta, w_ref, *refs):
    pieces, (bias_ref, out_ref) = refs[:n], refs[n:]
    out_ref[...] = (piece_columns(meta, w_ref, pieces) + bias_ref[...]).astype(BF)


def inputs_product(meta, weight, pieces, bias, width=1024, name=None):
    rows, depth = weight.shape
    return pl.pallas_call(
        functools.partial(inputs_kernel, len(pieces)),
        grid=(HW // width,),
        out_shape=struct((rows, HW), BF),
        in_specs=[scalars(), pl.BlockSpec((rows, depth), lambda p: (0, 0))]
        + [pl.BlockSpec((x.shape[0], width), lambda p: (0, p)) for x in pieces]
        + [pl.BlockSpec((rows, 1), lambda p: (0, 0))],
        out_specs=pl.BlockSpec((rows, width), lambda p: (0, p)),
        compiler_params=params(),
        cost_estimate=cost(2 * rows * depth * HW, (rows + depth) * HW * 2),
        name=name,
    )(meta, weight, *pieces, bias)


def parts_kernel(n, meta, w_ref, *refs):
    pieces, outs = refs[:n], refs[n:]
    first = meta[0]
    for out_ref in outs:
        rows = out_ref.shape[0]
        row = pl.ds(pl.multiple_of(first, rows), rows)
        acc = None
        at = 0
        for x_ref in pieces:
            depth = x_ref.shape[0]
            term = dot(w_ref[row, at : at + depth], x_ref[...])
            acc = term if acc is None else acc + term
            at += depth
        out_ref[...] = acc.astype(BF)
        first = w_ref.shape[0] - rows - first


def parts_product(meta, weight, pieces, count, width=1024, name=None):
    rows, depth = weight.shape
    part = struct((rows // count, HW), BF)
    return pl.pallas_call(
        functools.partial(parts_kernel, len(pieces)),
        grid=(HW // width,),
        out_shape=[part] * count,
        in_specs=[scalars(), pl.BlockSpec((rows, depth), lambda p: (0, 0))]
        + [pl.BlockSpec((x.shape[0], width), lambda p: (0, p)) for x in pieces],
        out_specs=[pl.BlockSpec((rows // count, width), lambda p: (0, p))] * count,
        compiler_params=params(),
        cost_estimate=cost(2 * rows * depth * HW, (rows + depth) * HW * 2),
        name=name,
    )(meta, weight, *pieces)


def output_kernel(n, meta, w_ref, *refs):
    pieces, (bias_ref, hidden_ref, out_ref) = refs[:n], refs[n:]
    acc = hidden_ref[...] + bias_ref[...] + piece_columns(meta, w_ref, pieces)
    half = acc.shape[1] // 2
    for base, val in zip((0, HW // 2), unfold(acc)):
        first = pl.multiple_of(base + pl.program_id(0) * half, half)
        out_ref[:, pl.ds(first, half)] = val.astype(BF)


def output_product(meta, weight, pieces, bias, hidden, width=1024):
    rows, depth = weight.shape
    return pl.pallas_call(
        functools.partial(output_kernel, len(pieces)),
        grid=(HW // width,),
        out_shape=struct((rows, HW), BF),
        in_specs=[scalars(), pl.BlockSpec((rows, depth), lambda p: (0, 0))]
        + [pl.BlockSpec((x.shape[0], width), lambda p: (0, p)) for x in pieces]
        + [
            pl.BlockSpec((rows, 1), lambda p: (0, 0)),
            pl.BlockSpec((rows, width), lambda p: (0, p)),
        ],
        out_specs=pl.BlockSpec((rows, HW), lambda p: (0, 0)),
        compiler_params=params(),
        cost_estimate=cost(2 * rows * depth * HW, (rows * 3 + depth) * HW * 2),
        name="output",
    )(meta, weight, *pieces, bias, hidden)


def outer_kernel(n_left, n_right, meta, *refs):
    lefts, rights = refs[:n_left], refs[n_left : n_left + n_right]
    out_ref, sums_ref = refs[n_left + n_right : n_left + n_right + 2]
    acc_ref, tot_ref = refs[n_left + n_right + 2 :]
    step = pl.program_id(0)

    @pl.when(step == 0)
    def _():
        acc_ref[...] = jnp.zeros_like(acc_ref)
        tot_ref[...] = jnp.zeros_like(tot_ref)

    row = 0
    for left in lefts:
        rows = left.shape[0]
        val = left[...]
        first = meta[0]
        for right in rights:
            cols = right.shape[0]
            at = pl.ds(pl.multiple_of(first, cols), cols)
            acc_ref[row : row + rows, at] += dot_nt(val, right[...])
            first = acc_ref.shape[1] - cols - first
        tot_ref[row : row + rows, :] += jnp.sum(val.astype(F32), axis=1, keepdims=True)
        row += rows

    @pl.when(step == pl.num_programs(0) - 1)
    def _():
        out_ref[...] = acc_ref[...].astype(BF)
        sums_ref[...] = tot_ref[...]


def outer(meta, lefts, rights, width=1024, name=None):
    rows, cols = sum(a.shape[0] for a in lefts), sum(a.shape[0] for a in rights)
    fixed = lambda p: (0, 0)
    return pl.pallas_call(
        functools.partial(outer_kernel, len(lefts), len(rights)),
        grid=(HW // width,),
        out_shape=[struct((rows, cols), BF), struct((rows, 128), F32)],
        in_specs=[scalars()]
        + [pl.BlockSpec((a.shape[0], width), lambda p: (0, p)) for a in (*lefts, *rights)],
        out_specs=[pl.BlockSpec((rows, cols), fixed), pl.BlockSpec((rows, 128), fixed)],
        scratch_shapes=[pltpu.VMEM((rows, cols), F32), pltpu.VMEM((rows, 128), F32)],
        compiler_params=params(),
        cost_estimate=cost(2 * rows * cols * HW, (rows + cols) * HW * 2),
        name=name,
    )(meta, *lefts, *rights)


def attention_kernel(
    n_grads, lim_ref, q_ref, k_ref, v_ref, kc_ref, vc_ref, *refs, unroll, back,
):
    g_refs, refs = refs[:n_grads], refs[n_grads:]
    o_ref, dq_ref, dk_ref, dv_ref, dkc_ref, dvc_ref = refs[:6]
    kt, vt, kn, vn, s_even, s_odd, p_sc, tops, o_acc, dk_acc, dv_acc = refs[6:]
    step, last = pl.program_id(1), pl.num_programs(1) - 1
    width = q_ref.shape[-1]
    blocks = KEYS // BLOCK

    @pl.when(step == 0)
    def _():
        spare = jnp.zeros((HEAD_DIM, KEYS - HW - CTXP), BF)
        for ref, own, ctx in ((kn, k_ref, kc_ref), (vn, v_ref, vc_ref)):
            ref[:, :HW] = own[0, 0]
            ref[:, HW : HW + CTXP] = ctx[0, 0]
            ref[:, HW + CTXP :] = spare
        row = lax.broadcasted_iota(jnp.int32, (HEAD_DIM, BLOCK), 0)
        for n in range(blocks):
            at = slice(n * BLOCK, (n + 1) * BLOCK)
            key = lax.broadcasted_iota(jnp.int32, (HEAD_DIM, BLOCK), 1) + n * BLOCK
            fill = jnp.where((row == 0) & (key >= HW + lim_ref[0]), NEG_FILL, 0.0)
            kt[at, :] = jnp.concatenate([kn[:, at].astype(F32), fill], 0).T.astype(BF)
            vt[at, :] = jnp.concatenate([vn[:, at].astype(F32), jnp.zeros_like(fill)], 0).T.astype(BF)
        dk_acc[...] = jnp.zeros_like(dk_acc)
        dv_acc[...] = jnp.zeros_like(dv_acc)

    def keys_at(n):
        return pl.ds(pl.multiple_of(n * BLOCK, BLOCK), BLOCK)

    scale = HEAD_DIM ** (-0.5)
    q = (q_ref[0, 0].astype(F32) * scale).astype(BF)
    one = jnp.where(lax.broadcasted_iota(jnp.int32, (HEAD_DIM, width), 0) == 0, 1.0, 0.0).astype(BF)
    q_more = jnp.concatenate([q, one], 0)

    def score(n, held):
        scores = dot(kt[keys_at(n), :], q_more)
        held[...] = scores
        return jnp.max(jnp.max(scores.reshape(BLOCK // 8, 8, width), axis=0), axis=0, keepdims=True)

    o_acc[...] = jnp.zeros_like(o_acc)

    def forward(n, held, top, total, shrink):
        raised = jnp.exp(held[...] - top)
        low = raised.astype(BF)
        p_sc[keys_at(n), :] = low
        tops[n, 0:1, :] = top
        sums = jnp.sum(raised.reshape(BLOCK // 8, 8, width), axis=0)
        o_acc[...] = o_acc[...] * shrink + dot(vn[:, keys_at(n)], low)
        return total * shrink + sums

    def forward_step(n, held, ahead_held, carry):
        top, total, shrink = carry
        ahead = jnp.maximum(top, score(n + 1, ahead_held))
        total = forward(n, held, top, total, shrink)
        return ahead, total, jnp.exp(top - ahead)

    held = (s_even, s_odd)

    def forward_run(j, carry):
        for u in range(unroll):
            carry = forward_step(unroll * j + u, held[u % 2], held[1 - u % 2], carry)
        return carry

    carry = (score(0, s_even), jnp.zeros((8, width), F32), jnp.ones((1, width), F32))
    carry = lax.fori_loop(0, blocks // unroll - 1, forward_run, carry)
    for n in range(blocks - unroll, blocks - 1):
        carry = forward_step(n, held[n % 2], held[1 - n % 2], carry)
    top, total, shrink = carry
    total = forward(blocks - 1, s_odd, top, total, shrink)

    inverse = 1.0 / jnp.sum(total, axis=0, keepdims=True)
    mixed = o_acc[...] * inverse
    o_ref[0] = mixed.astype(BF)
    grad = sum(g_ref[0].astype(F32) for g_ref in g_refs)
    if n_grads > 1:
        grad = grad.astype(BF).astype(F32)
    delta = jnp.sum(grad * mixed, axis=0, keepdims=True)
    dq = jnp.zeros((HEAD_DIM, width), F32)
    none = jnp.zeros((HEAD_DIM, width), BF)
    for c in range(0, KEYS, back):
        at = slice(c, c + back)
        slopes = []
        for n in range(c // BLOCK, (c + back) // BLOCK):
            sub = slice(n * BLOCK, (n + 1) * BLOCK)
            factor = inverse * jnp.exp(tops[n, 0:1, :] - top)
            grad_low = (grad * factor).astype(BF)
            both = jnp.concatenate([grad_low, none], 0)
            probs = p_sc[sub, :]
            slope = (dot(vt[sub, :], both) - delta * factor).astype(BF) * probs
            slopes.append(slope)
            dv_acc[:, sub] += dot_nt(grad_low, probs)
        slope = jnp.concatenate(slopes, 0)
        dq = dq + dot(kn[:, at], slope)
        dk_acc[:, at] += dot_nt(q, slope)
    dq_ref[0] = (dq * scale).astype(BF)

    @pl.when(step == last)
    def _():
        dk_ref[0] = dk_acc[:, :HW].astype(BF)
        dv_ref[0] = dv_acc[:, :HW].astype(BF)
        dkc_ref[0] = dk_acc[:, HW : HW + CTXP].astype(BF)
        dvc_ref[0] = dv_acc[:, HW : HW + CTXP].astype(BF)


def attention(limit, qkv, ctx_kv, grads, width=1024, unroll=6, back=256):
    heads = qkv.shape[1]
    keys = KEYS

    def part(t, w, moving):
        return pl.BlockSpec(
            (1, 1, HEAD_DIM, w), (lambda h, i: (t, h, 0, i)) if moving else (lambda h, i: (t, h, 0, 0))
        )

    def row(w, moving):
        return pl.BlockSpec(
            (1, HEAD_DIM, w), (lambda h, i: (h, 0, i)) if moving else (lambda h, i: (h, 0, 0))
        )

    big, small = struct((heads, HEAD_DIM, HW), BF), struct((heads, HEAD_DIM, CTXP), BF)
    return pl.pallas_call(
        functools.partial(attention_kernel, len(grads), unroll=unroll, back=back),
        grid=(heads, HW // width),
        in_specs=[
            pl.BlockSpec(memory_space=pltpu.SMEM),
            part(0, width, True),
            part(1, HW, False),
            part(2, HW, False),
            part(0, CTXP, False),
            part(1, CTXP, False),
        ]
        + [row(width, True)] * len(grads),
        out_specs=[
            row(width, True),
            row(width, True),
            row(HW, False),
            row(HW, False),
            row(CTXP, False),
            row(CTXP, False),
        ],
        out_shape=[big, big, big, big, small, small],
        scratch_shapes=[
            pltpu.VMEM((keys, 2 * HEAD_DIM), BF),
            pltpu.VMEM((keys, 2 * HEAD_DIM), BF),
            pltpu.VMEM((HEAD_DIM, keys), BF),
            pltpu.VMEM((HEAD_DIM, keys), BF),
            pltpu.VMEM((BLOCK, width), F32),
            pltpu.VMEM((BLOCK, width), F32),
            pltpu.VMEM((keys, width), BF),
            pltpu.VMEM((keys // BLOCK, 8, width), F32),
            pltpu.VMEM((HEAD_DIM, width), F32),
            pltpu.VMEM((HEAD_DIM, keys), F32),
            pltpu.VMEM((HEAD_DIM, keys), F32),
        ],
        compiler_params=params(dimension_semantics=("arbitrary", "arbitrary")),
        cost_estimate=cost(
            24 * heads * HW * keys * HEAD_DIM, heads * HEAD_DIM * 8 * HW * 2, heads * HW * keys
        ),
        name="attention",
    )(limit, qkv, qkv, qkv, ctx_kv, ctx_kv, *grads)


class Alone:
    parts = 1

    def __init__(self, mesh):
        self.images = mesh.shape["dp"]

    def meta(self):
        return jnp.array([0, 1], jnp.int32)

    def image(self):
        return lax.axis_index("dp")

    def got(self, x):
        return x

    def pick(self, own, got):
        return own

    def gather(self, x):
        return (lax.all_gather(x, "tensor", axis=0, tiled=True),)

    def scatter(self, parts):
        return (lax.psum_scatter(parts[0], "tensor", scatter_dimension=0, tiled=True),)

    def turn(self, meta, w):
        ch = w.shape[0]
        cut = w.reshape(ch, 9, C)
        turned = lax.all_to_all(cut, "tensor", split_axis=2, concat_axis=0, tiled=True)
        return turned[:, ::-1].transpose(2, 1, 0).reshape(ch, 9 * C)

    def total(self, x, beside):
        return lax.psum(x, "dp")

    def everywhere(self, x):
        return lax.psum(x, "dp")

    def sum_owned(self, x, late):
        return lax.psum(x, "dp")


class Paired:
    parts = 2

    def __init__(self, mesh):
        dp = mesh.shape["dp"]
        self.images = dp
        self.far = [
            ((2 * k + core) * 2 + 1 - core, (2 * k + 1 - core) * 2 + core)
            for k in range(dp // 2)
            for core in range(2)
        ]
        self.bits = [1 << b for b in range((dp - 1).bit_length())]

    def half(self):
        return lax.axis_index("dp") % 2

    def stays(self):
        return self.half() == lax.axis_index("tensor")

    def meta(self):
        return jnp.stack([self.half() * (C // 2), self.stays().astype(jnp.int32)]).astype(jnp.int32)

    def image(self):
        return lax.axis_index("dp") // 2 * 2 + lax.axis_index("tensor")

    def got(self, x):
        return lax.ppermute(x, ("dp", "tensor"), self.far)

    def pick(self, own, got):
        return jnp.where(self.stays(), own, got)

    def over(self, x, bit):
        return lax.ppermute(x, "dp", [(i, i ^ bit) for i in range(self.images)])

    def gather(self, x):
        return (x, self.over(x, 1))

    def scatter(self, parts):
        return (parts[0], self.over(parts[1], 1))

    def turn(self, meta, w):
        return turned_pair(meta, w, self.over(w, 1))

    def total(self, x, beside):
        x = after(beside, x + lax.ppermute(x, "tensor", [(0, 1), (1, 0)]))
        for bit in self.bits[1:]:
            x = x + self.over(x, bit)
        return self.pick(x, self.over(x, 1))

    def everywhere(self, x):
        for bit in self.bits:
            x = x + self.over(x, bit)
        return x

    def sum_owned(self, x, late):
        rows = x.shape[0] // 2
        order = (self.bits, [self.bits[0], *self.bits[2:], self.bits[1]])
        parts = [lax.slice_in_dim(x, at * rows, (at + 1) * rows) for at in range(2)]

        def upper(bit):
            return (lax.axis_index("dp") // bit) % 2

        for step in range(len(self.bits)):
            size = parts[0].shape[0] // 2
            for at in range(2):
                bit = order[at][step]
                keep = lax.dynamic_slice_in_dim(parts[at], upper(bit) * size, size)
                send = lax.dynamic_slice_in_dim(parts[at], (1 - upper(bit)) * size, size)
                parts[at] = (keep.astype(F32) + self.over(send, bit).astype(F32)).astype(BF)
        parts = list(after(late, *parts))
        for step in reversed(range(len(self.bits))):
            for at in range(2):
                bit = order[at][step]
                other = self.over(parts[at], bit)
                parts[at] = jnp.where(
                    upper(bit) == 0,
                    jnp.concatenate([parts[at], other]),
                    jnp.concatenate([other, parts[at]]),
                )
        return jnp.concatenate(parts)


def after(first, *later):
    held = lax.optimization_barrier((first, *later))
    return held[1:] if len(later) > 1 else held[1]


def local(plan, features, cotangent, embedding, context, lengths, norm1_gain, norm1_bias,
    conv1_weight, conv1_bias, emb_weight, emb_bias, norm2_gain, norm2_bias, conv2_weight,
    conv2_bias, norm3_gain, norm3_bias, qkv_weight, qkv_bias, context_weight, context_bias,
    out_weight, out_bias,
):
    ch, images, pixels = features.shape
    heads = ch // HEAD_DIM
    meta = plan.meta()
    moved = plan.parts == 2

    emb_act = jax.nn.silu(embedding.astype(F32)).astype(BF)
    scale_shift = (
        jnp.einsum("ie,teo->to", emb_act, emb_weight, preferred_element_type=F32) + emb_bias
    )
    length_row = jnp.broadcast_to(lengths.astype(F32)[:, None], (1, ch))
    vectors = jnp.concatenate(
        [
            jnp.stack([norm1_gain, norm1_bias, conv1_bias, norm2_gain, norm2_bias]),
            scale_shift,
            jnp.stack([conv2_bias, norm3_gain, norm3_bias, out_bias]),
            qkv_bias,
            length_row,
        ]
    )
    f_own = features.reshape(ch, pixels)
    f_got = plan.got(f_own)
    vectors, w1_own = after(scale_shift, vectors, conv1_weight)
    vectors = plan.pick(vectors, plan.got(vectors))
    w1_got = plan.got(w1_own)
    ctx_kv = (
        jnp.einsum("toe,ne->ton", context_weight, context[0], preferred_element_type=F32)
        + context_bias[:, :, None]
    ).astype(BF)
    ctx_kv = jnp.pad(ctx_kv, ((0, 0), (0, 0), (0, CTXP - CTX)))
    emb_all = jnp.where(
        jnp.arange(plan.images)[:, None] == lax.axis_index("dp"), emb_act, jnp.zeros_like(emb_act)
    )
    emb_all = plan.everywhere(emb_all)
    length = vectors[14, :1].astype(jnp.int32)
    par_one, par_two, par_three = vectors[0:2].T, vectors[2:7].T, vectors[7:10].T
    bias_qkv, bias_out = vectors[11:14].reshape(3 * ch, 1), vectors[10].reshape(ch, 1)
    par_one = after(emb_all, par_one)
    w2_got = plan.got(after(vectors, conv2_weight))
    act_one, stat_one, f_low = first_activation(meta, f_own, f_got, par_one)
    full_one = plan.gather(act_one)
    mats_own = jnp.concatenate([qkv_weight.reshape(3 * ch, C), out_weight])
    mats_own, ctx_own, cot_own = after(
        act_one, mats_own, ctx_kv, cotangent.reshape(ch, pixels)
    )
    mats_got, ctx_got = plan.got(mats_own), plan.got(ctx_own)
    cot_got = plan.got(cot_own)

    par_two, par_three, bias_qkv, bias_out = after(act_one, par_two, par_three, bias_qkv, bias_out)
    par_two = after((par_three, bias_qkv, bias_out), par_two)
    low, stat, wide = struct((ch, HW), BF), struct((ch, 128), F32), struct((ch, HW), F32)
    weight = struct((ch, 9 * C), BF)
    act_two, stat_two, conv_one, w1 = conv_call(
        conv_one_kernel, meta, (conv1_weight, w1_got), full_one, (par_two,), (),
        [low, stat], [wide, weight], [], "conv_one",
    )
    full_two = plan.gather(act_two)
    normed, stat_three, hidden, w2 = conv_call(
        conv_two_kernel, meta, (conv2_weight, w2_got), full_two, (par_three, f_low), (),
        [low, stat], [wide, weight], [], "conv_two",
    )
    full_three = plan.gather(normed)
    mats_got, ctx_got, cot_got = after(normed, mats_got, ctx_got, cot_got)
    mats = plan.pick(mats_own, mats_got)
    w_qkv, w_out = mats[: 3 * ch], mats[3 * ch :]
    cot = folded(meta, cot_own, cot_got)
    grad_heads = plan.scatter(
        parts_product(meta, w_out.T, (cot,), plan.parts, name="grad_heads")
    )
    qkv = inputs_product(meta, w_qkv, full_three, bias_qkv, name="qkv")
    ctx_kv = plan.pick(ctx_own, ctx_got)
    mixed, dq, dk, dv, dkc, dvc = attention(
        4 + length,
        qkv.reshape(3, heads, HEAD_DIM, HW),
        ctx_kv.reshape(2, heads, HEAD_DIM, CTXP),
        [a.reshape(heads, HEAD_DIM, HW) for a in grad_heads],
    )

    flat = lambda a: a.reshape(ch, HW)
    dq, dk, dv = flat(dq), flat(dk), flat(dv)
    addends = plan.scatter(
        parts_product(meta, w_qkv.T, (dq, dk, dv), plan.parts, name="grad_normed")
    )
    full_heads = plan.gather(flat(mixed))
    ctx_own = jnp.concatenate([a.reshape(1, ch, CTXP) for a in (dkc, dvc)])
    ctx_got = plan.got(ctx_own)
    turned_two = plan.turn(meta, after(mixed, w2))
    dw_qkv, db_qkv = outer(meta, (dq, dk, dv), full_three, name="qkv_grad")
    dw_out, _ = outer(meta, (cot,), full_heads, name="out_grad")
    mats_own = jnp.concatenate([dw_qkv, dw_out])
    mats_got = plan.got(mats_own)
    grad_hidden, grad_two, sums_three = norm_three_back(addends, hidden, stat_three, par_three, cot)
    full_grad_two = plan.gather(grad_two)
    dw_two = conv_weight_grad(meta, grad_two, full_two, "conv_two_weight_grad")
    two_got = plan.got(dw_two)
    full_grad_two = after(dw_two, *full_grad_two) if moved else full_grad_two
    grad_one, sums_two = conv_call(
        conv_two_back_kernel, meta, (turned_two, turned_two), full_grad_two, (par_two, stat_two),
        (conv_one,), [low, stat], [], [pltpu.VMEM((ch, HW), F32)], "conv_two_back",
    )
    full_grad_one = plan.gather(grad_one)
    turned_one = plan.turn(meta, after(mixed, w1))
    mats_got, ctx_got, two_got = after(grad_one, mats_got, ctx_got, two_got)
    ctx_grad = plan.pick(ctx_own, ctx_got)[:, :, :CTX]
    dw_ctx = jnp.einsum("ton,ne->toe", ctx_grad, context[0], preferred_element_type=F32).astype(BF)
    mats = plan.pick(mats_own, mats_got)
    dw_two = plan.pick(dw_two, two_got)
    early = jnp.concatenate(
        [dw_ctx[0], dw_ctx[1], *(mats[t * ch : (t + 1) * ch] for t in range(4)), dw_two], 1
    )
    held = after(early, grad_one)
    early = lax.psum_scatter(early, "dp", scatter_dimension=0, tiled=True)
    dw_one = conv_weight_grad(meta, held, full_one, "conv_one_weight_grad")
    one_got = plan.got(dw_one)
    full_grad_one = after(dw_one, *full_grad_one) if moved else full_grad_one
    input_grad, sums_one = conv_call(
        conv_one_back_kernel, meta, (turned_one, turned_one), full_grad_one,
        (par_one, stat_one, f_low), (grad_hidden,),
        [struct((ch, HW), BF if moved else F32), stat], [],
        [pltpu.VMEM((ch, HW), F32)], "conv_one_back",
    )
    input_got = plan.got(input_grad)

    one_got = after(input_grad, one_got)
    output = output_product(
        meta, w_out, full_heads, bias_out, after(input_grad, hidden)
    )
    output_got = plan.got(output)
    ctx_sums = jnp.sum(ctx_own.astype(F32), axis=2)
    sums_two = sums_two[:, :5].T
    own_mod = sums_two[2:4].astype(BF).astype(F32)
    mods = jnp.where(
        (jnp.arange(plan.images) == plan.image())[:, None, None], own_mod, jnp.zeros_like(own_mod)
    ).reshape(2 * plan.images, ch)
    small = plan.total(
        jnp.concatenate(
            [
                sums_three[:, :4].T,
                db_qkv[:, 0].reshape(3, ch),
                sums_two[:2],
                sums_two[4:5],
                ctx_sums,
                sums_one[:, :2].T,
                mods,
            ]
        ),
        output,
    )
    early, dw_one, one_got = after(small, early, dw_one, one_got)
    dw_one = plan.sum_owned(plan.pick(dw_one, one_got), (input_got, output_got))
    early = lax.all_gather(early, "dp", axis=0, tiled=True)
    mods = small[14:].reshape(plan.images, 2, ch)
    mods_low = mods.astype(BF)
    dw_emb = jnp.stack(
        [
            jnp.einsum("ie,io->eo", emb_all, mods_low[:, t], preferred_element_type=F32)
            for t in range(2)
        ]
    )
    input_grad = plan.pick(input_grad, input_got).astype(F32)
    output = plan.pick(output, output_got)
    early = after((dw_one, small, input_grad, output), early)
    dw_ctx = jnp.stack([early[:, n * CTX_EMB : (n + 1) * CTX_EMB] for n in range(2)])
    first = 2 * CTX_EMB
    mats = [early[:, first + n * C : first + (n + 1) * C].astype(F32) for n in range(4)]
    dw_two = early[:, first + 4 * C :]

    return (
        output.reshape(ch, images, pixels),
        input_grad.reshape(ch, images, pixels),
        small[12],
        small[13],
        dw_one.astype(F32),
        small[9],
        dw_emb,
        jnp.sum(mods, axis=0),
        small[7],
        small[8],
        dw_two.astype(F32),
        small[2],
        small[0],
        small[1],
        jnp.stack(mats[:3]),
        small[4:7],
        dw_ctx.astype(F32),
        small[10:12],
        mats[3],
        small[3],
    )


def solution(mesh):
    paired = mesh.shape["tensor"] == 2 and mesh.shape["dp"] % 2 == 0
    plan = Paired(mesh) if paired else Alone(mesh)
    specs = (
        P("tensor", "dp", None),
        P("tensor", "dp", None),
        P("dp", None),
        P("dp", None, None),
        P("dp"),
        P("tensor"),
        P("tensor"),
        P("tensor", None),
        P("tensor"),
        P(None, None, "tensor"),
        P(None, "tensor"),
        P("tensor"),
        P("tensor"),
        P("tensor", None),
        P("tensor"),
        P("tensor"),
        P("tensor"),
        P(None, "tensor", None),
        P(None, "tensor"),
        P(None, "tensor", None),
        P(None, "tensor"),
        P("tensor", None),
        P("tensor"),
    )
    return jax.shard_map(
        functools.partial(local, plan),
        mesh=mesh,
        in_specs=specs,
        out_specs=(
            P("tensor", "dp", None),
            P("tensor", "dp", None),
            P("tensor"),
            P("tensor"),
            P("tensor", None),
            P("tensor"),
            P(None, None, "tensor"),
            P(None, "tensor"),
            P("tensor"),
            P("tensor"),
            P("tensor", None),
            P("tensor"),
            P("tensor"),
            P("tensor"),
            P(None, "tensor", None),
            P(None, "tensor"),
            P(None, "tensor", None),
            P(None, "tensor"),
            P("tensor", None),
            P("tensor"),
        ),
        check_vma=False,
    )
```

```python
import functools

import jax
import jax.numpy as jnp
from jax import lax
from jax.experimental import pallas as pl
from jax.experimental.pallas import tpu as pltpu
from jax.sharding import PartitionSpec as P

C = 512
HEAD_DIM = 64
PER_GROUP = 16
SIDE = 64
HW = 4096
CTX = 260
CTXP = 384
CTX_EMB = 2048
BLOCK = 256
KEYS = 4608
PAD = 128
FILL = 32
SCALE = 100
EPSILON = 1e-05
NEG_FILL = -1e30
F32 = jnp.float32
BF = jnp.bfloat16
NT = (((1,), (1,)), ((), ()))
VMEM_BYTES = 62 << 20


def dot(a, b):
    return jnp.dot(a, b, preferred_element_type=F32)


def dot_nt(a, b):
    return lax.dot_general(a, b, NT, preferred_element_type=F32)


def whole():
    return pl.BlockSpec(memory_space=pltpu.VMEM)


def placed():
    return pl.BlockSpec(memory_space=pl.ANY)


def scalars():
    return pl.BlockSpec(memory_space=pltpu.SMEM)


def params(**kwargs):
    return pltpu.CompilerParams(vmem_limit_bytes=VMEM_BYTES, **kwargs)


def cost(flops, nbytes, transcendentals=0):
    return pl.CostEstimate(
        flops=flops // SCALE, bytes_accessed=nbytes // SCALE, transcendentals=transcendentals // SCALE
    )


def struct(shape, dtype):
    return jax.ShapeDtypeStruct(shape, dtype)


def fetch(meta, own_ref, got_ref, buf, sem):
    @pl.when(meta[1] == 1)
    def _():
        pltpu.make_async_copy(own_ref, buf, sem).start()

    @pl.when(meta[1] != 1)
    def _():
        pltpu.make_async_copy(got_ref, buf, sem).start()


def arrive(own_ref, buf, sem):
    pltpu.make_async_copy(own_ref, buf, sem).wait()


def group_scalar(column):
    return jnp.sum(column, axis=0, keepdims=True) * (1.0 / (PER_GROUP * HW))


def group_stats(vals):
    mean = group_scalar(jnp.sum(vals, axis=1, keepdims=True))
    centred = vals - mean
    var = group_scalar(jnp.sum(centred * centred, axis=1, keepdims=True))
    rstd = lax.rsqrt(var + EPSILON)
    return mean, rstd


def norm_backward(dy_sum, dyx_sum, gain):
    return group_scalar(dy_sum * gain), group_scalar(dyx_sum * gain)


def for_groups(channels, body, together=2):
    def step(g, carry):
        for u in range(together):
            first = pl.multiple_of((g * together + u) * PER_GROUP, PER_GROUP)
            body(pl.ds(first, PER_GROUP))
        return carry

    lax.fori_loop(0, channels // PER_GROUP // together, step, 0)


def columns(values):
    lane = lax.broadcasted_iota(jnp.int32, (PER_GROUP, 128), 1)
    tile = jnp.zeros((PER_GROUP, 128), F32)
    for at, val in enumerate(values):
        tile = jnp.where(lane == at, val, tile)
    return tile


ROWS = SIDE // 2


def lanes(x, n):
    return x[:, 128 * n : 128 * n + 128]


def low_lanes(x):
    return lax.broadcasted_iota(jnp.int32, (x.shape[0], 128), 1) < SIDE


def fold(x):
    low = low_lanes(x)
    out = []
    for r in range(ROWS):
        upper, lower = lanes(x, r // 2), lanes(x, r // 2 + ROWS // 2)
        if r % 2 == 0:
            out.append(jnp.where(low, upper, pltpu.roll(lower, SIDE, 1)))
        else:
            out.append(jnp.where(low, pltpu.roll(upper, SIDE, 1), lower))
    return jnp.concatenate(out, 1)


def unfold(x):
    low = low_lanes(x)
    pairs = range(x.shape[1] // 256)
    top = [jnp.where(low, lanes(x, 2 * n), pltpu.roll(lanes(x, 2 * n + 1), SIDE, 1)) for n in pairs]
    bottom = [
        jnp.where(low, pltpu.roll(lanes(x, 2 * n), SIDE, 1), lanes(x, 2 * n + 1)) for n in pairs
    ]
    return jnp.concatenate(top, 1), jnp.concatenate(bottom, 1)


def fold_kernel(meta, own_ref, got_ref, out_ref, x_buf, sem):
    fetch(meta, own_ref, got_ref, x_buf, sem)
    arrive(own_ref, x_buf, sem)

    def body(rows):
        out_ref[rows, :] = fold(x_buf[rows, :].astype(F32)).astype(BF)

    for_groups(out_ref.shape[0], body)


def folded(meta, own, got):
    return pl.pallas_call(
        fold_kernel,
        out_shape=struct(own.shape, BF),
        in_specs=[scalars(), placed(), placed()],
        out_specs=whole(),
        scratch_shapes=[pltpu.VMEM(own.shape, BF), pltpu.SemaphoreType.DMA(())],
        compiler_params=params(),
        cost_estimate=cost(8 * own.size, 4 * own.size),
        name="fold",
    )(meta, own, got)


def act_one_kernel(meta, own_ref, got_ref, par_ref, act_ref, stat_ref, fold_ref, x_buf, sem):
    fetch(meta, own_ref, got_ref, x_buf, sem)
    arrive(own_ref, x_buf, sem)

    def body(rows):
        vals = fold(x_buf[rows, :].astype(F32))
        fold_ref[rows, :] = vals.astype(BF)
        mean, rstd = group_stats(vals)
        par = par_ref[rows, :]
        out = (vals - mean) * (rstd * par[:, 0:1]) + par[:, 1:2]
        act_ref[rows, :] = (out * jax.nn.sigmoid(out)).astype(BF)
        stat_ref[rows, :] = columns([mean, rstd])

    for_groups(act_ref.shape[0], body)


def first_activation(meta, own, got, par):
    ch = own.shape[0]
    return pl.pallas_call(
        act_one_kernel,
        out_shape=[struct((ch, HW), BF), struct((ch, 128), F32), struct((ch, HW), BF)],
        in_specs=[scalars(), placed(), placed(), whole()],
        out_specs=[whole()] * 3,
        scratch_shapes=[pltpu.VMEM((ch, HW), BF), pltpu.SemaphoreType.DMA(())],
        compiler_params=params(),
        cost_estimate=cost(20 * ch * HW, 6 * ch * HW, ch * HW),
        name="act_one",
    )(meta, own, got, par)


def fill_shifted(xs, pieces, first):
    start = first
    for x_ref in pieces:
        rows = x_ref.shape[0]

        def step(r, carry, x_ref=x_ref, start=start):
            off = pl.multiple_of(r * FILL, FILL)
            at = pl.ds(pl.multiple_of(start + off, FILL), FILL)
            lane = lax.broadcasted_iota(jnp.int32, (FILL, 128), 1)
            low = lane < SIDE
            left, right = lane % SIDE == 0, lane % SIDE == SIDE - 1
            zero = jnp.zeros((FILL, 128), F32)
            here = pl.ds(off, FILL)
            for n in range(ROWS):
                x = x_ref[here, 128 * n : 128 * n + 128].astype(F32)
                kinds = (
                    jnp.where(left, zero, pltpu.roll(x, 1, 1)),
                    x,
                    jnp.where(right, zero, pltpu.roll(x, 127, 1)),
                )
                for d, y in enumerate(kinds):
                    xs[d, at, PAD + 128 * n : PAD + 128 * n + 128] = y.astype(BF)
                    if n == ROWS - 1:
                        xs[d, at, :PAD] = jnp.where(low, zero, pltpu.roll(y, SIDE, 1)).astype(BF)
                    if n == 0:
                        xs[d, at, PAD + HW :] = jnp.where(
                            low, pltpu.roll(y, SIDE, 1), zero
                        ).astype(BF)
            return carry

        lax.fori_loop(0, rows // FILL, step, 0)
        start = xs.shape[1] - rows - start if len(pieces) == 2 else start + rows


def window(xs, tap, start, width):
    first = PAD + start + (tap // 3 - 1) * 128
    if not isinstance(start, int):
        first = pl.multiple_of(first, 128)
    return xs[tap % 3, :, pl.ds(first, width)]


def convolve(xs, w_ref, out_ref, add, width=1024):
    depth = xs.shape[1]

    def step(n, carry):
        p = n * width
        acc = dot(w_ref[:, :depth], window(xs, 0, p, width))
        for tap in range(1, 9):
            acc = acc + dot(w_ref[:, tap * depth : (tap + 1) * depth], window(xs, tap, p, width))
        at = pl.ds(pl.multiple_of(p, width), width)
        out_ref[:, at] = add(acc, at)
        return carry

    lax.fori_loop(0, HW // width, step, 0)


def conv_call(kernel, meta, weights, pieces, vmem_in, any_in, outs, any_outs, scratch, name):
    out_ch, depth = weights[0].shape[0], C
    arrays = (weights[0], *pieces, *vmem_in, *any_in)
    nbytes = sum(a.size * a.dtype.itemsize for a in arrays) + out_ch * HW * 4
    return pl.pallas_call(
        functools.partial(kernel, len(pieces)),
        out_shape=[*outs, *any_outs],
        in_specs=[scalars(), placed(), placed()]
        + [whole()] * (len(pieces) + len(vmem_in))
        + [placed()] * len(any_in),
        out_specs=[whole()] * len(outs) + [placed()] * len(any_outs),
        scratch_shapes=[
            pltpu.VMEM((3, depth, HW + 2 * PAD), BF),
            pltpu.VMEM((out_ch, 9 * depth), BF),
            pltpu.VMEM((out_ch, HW), F32),
            pltpu.SemaphoreType.DMA((4,)),
            *scratch,
        ],
        compiler_params=params(),
        cost_estimate=cost(2 * out_ch * 9 * depth * HW, nbytes, out_ch * HW),
        name=name,
    )(meta, *weights, *pieces, *vmem_in, *any_in)


def conv_one_kernel(n, meta, w_own, w_got, *refs):
    pieces, refs = refs[:n], refs[n:]
    par_ref, act_ref, stat_ref, conv_ref, w_ref, xs, w_buf, acc, sems = refs
    fetch(meta, w_own, w_got, w_buf, sems.at[0])
    fill_shifted(xs, pieces, meta[0])
    arrive(w_own, w_buf, sems.at[0])
    keep = pltpu.make_async_copy(w_buf, w_ref, sems.at[2])
    keep.start()
    bias = par_ref[:, 0:1]
    convolve(xs, w_buf, acc, lambda val, at: val + bias)
    store = pltpu.make_async_copy(acc, conv_ref, sems.at[1])
    store.start()

    def body(rows):
        vals = acc[rows, :]
        mean, rstd = group_stats(vals)
        par = par_ref[rows, :]
        gain, shift, factor = par[:, 1:2], par[:, 2:3], 1.0 + par[:, 3:4]
        mid = (vals - mean) * (rstd * gain * factor) + (shift * factor + par[:, 4:5])
        act_ref[rows, :] = (mid * jax.nn.sigmoid(mid)).astype(BF)
        stat_ref[rows, :] = columns([mean, rstd])

    for_groups(acc.shape[0], body)
    store.wait()
    keep.wait()


def conv_two_kernel(n, meta, w_own, w_got, *refs):
    pieces, refs = refs[:n], refs[n:]
    par_ref, f_ref, normed_ref, stat_ref, hidden_ref, w_ref, xs, w_buf, acc, sems = refs
    fetch(meta, w_own, w_got, w_buf, sems.at[0])
    fill_shifted(xs, pieces, meta[0])
    arrive(w_own, w_buf, sems.at[0])
    keep = pltpu.make_async_copy(w_buf, w_ref, sems.at[2])
    keep.start()
    bias = par_ref[:, 0:1]
    convolve(xs, w_buf, acc, lambda val, at: val + bias + f_ref[:, at].astype(F32))
    store = pltpu.make_async_copy(acc, hidden_ref, sems.at[1])
    store.start()

    def body(rows):
        vals = acc[rows, :]
        mean, rstd = group_stats(vals)
        par = par_ref[rows, :]
        normed_ref[rows, :] = ((vals - mean) * (rstd * par[:, 1:2]) + par[:, 2:3]).astype(BF)
        stat_ref[rows, :] = columns([mean, rstd])

    for_groups(acc.shape[0], body)
    store.wait()
    keep.wait()


def silu_slope(mid):
    sig = jax.nn.sigmoid(mid)
    return sig * (1.0 + mid * (1.0 - sig))


def conv_two_back_kernel(n, meta, w_own, w_got, *refs):
    pieces, refs = refs[:n], refs[n:]
    par_ref, stat_ref, conv_ref, grad_ref, sums_ref, xs, w_buf, acc, sems, conv_buf = refs
    fetch(meta, w_own, w_got, w_buf, sems.at[0])
    load = pltpu.make_async_copy(conv_ref, conv_buf, sems.at[1])
    load.start()
    fill_shifted(xs, pieces, meta[0])
    arrive(w_own, w_buf, sems.at[0])
    convolve(xs, w_buf, acc, lambda val, at: val)
    load.wait()

    def body(rows):
        par, stat = par_ref[rows, :], stat_ref[rows, :]
        gain, shift, factor = par[:, 1:2], par[:, 2:3], 1.0 + par[:, 3:4]
        rstd = stat[:, 1:2]
        hat = (conv_buf[rows, :] - stat[:, 0:1]) * rstd
        mid = hat * (gain * factor) + (shift * factor + par[:, 4:5])
        grad = acc[rows, :] * silu_slope(mid)
        total = jnp.sum(grad, axis=1, keepdims=True)
        total_hat = jnp.sum(grad * hat, axis=1, keepdims=True)
        mean_u, mean_uhat = norm_backward(total * factor, total_hat * factor, gain)
        out = ((grad * (factor * gain) - mean_u - hat * mean_uhat) * rstd).astype(BF)
        grad_ref[rows, :] = out
        bias_grad = jnp.sum(out.astype(F32), axis=1, keepdims=True)
        sums_ref[rows, :] = columns(
            [
                total_hat * factor,
                total * factor,
                total_hat * gain + total * shift,
                total,
                bias_grad,
            ]
        )

    for_groups(acc.shape[0], body)


def conv_one_back_kernel(n, meta, w_own, w_got, *refs):
    pieces, refs = refs[:n], refs[n:]
    par_ref, stat_ref, f_ref, hid_ref, grad_ref, sums_ref, xs, w_buf, acc, sems, hid_buf = refs
    fetch(meta, w_own, w_got, w_buf, sems.at[0])
    load = pltpu.make_async_copy(hid_ref, hid_buf, sems.at[1])
    load.start()
    fill_shifted(xs, pieces, meta[0])
    arrive(w_own, w_buf, sems.at[0])
    convolve(xs, w_buf, acc, lambda val, at: val)
    load.wait()

    def body(rows):
        par, stat = par_ref[rows, :], stat_ref[rows, :]
        gain, shift = par[:, 0:1], par[:, 1:2]
        rstd = stat[:, 1:2]
        hat = (f_ref[rows, :].astype(F32) - stat[:, 0:1]) * rstd
        grad = acc[rows, :] * silu_slope(hat * gain + shift)
        total = jnp.sum(grad, axis=1, keepdims=True)
        total_hat = jnp.sum(grad * hat, axis=1, keepdims=True)
        mean_u, mean_uhat = norm_backward(total, total_hat, gain)
        out = hid_buf[rows, :] + (grad * gain - mean_u - hat * mean_uhat) * rstd
        top, bottom = unfold(out)
        grad_ref[rows, : HW // 2] = top.astype(grad_ref.dtype)
        grad_ref[rows, HW // 2 :] = bottom.astype(grad_ref.dtype)
        sums_ref[rows, :] = columns([total_hat, total])

    for_groups(acc.shape[0], body)


def weight_grad_kernel(n, meta, grad_ref, *refs):
    pieces, (out_ref, gs) = refs[:n], refs[n:]
    fill_shifted(gs, (grad_ref,), 0)
    for tap in range(9):
        moved = window(gs, 8 - tap, 0, HW)
        first = meta[0]
        for x_ref in pieces:
            rows = x_ref.shape[0]
            at = pl.ds(pl.multiple_of(tap * C + first, rows), rows)
            out_ref[:, at] = dot_nt(moved, x_ref[...]).astype(BF)
            first = C - rows - first


def conv_weight_grad(meta, grad, pieces, name):
    out_ch = grad.shape[0]
    return pl.pallas_call(
        functools.partial(weight_grad_kernel, len(pieces)),
        out_shape=struct((out_ch, 9 * C), BF),
        in_specs=[scalars()] + [whole()] * (1 + len(pieces)),
        out_specs=whole(),
        scratch_shapes=[pltpu.VMEM((3, out_ch, HW + 2 * PAD), BF)],
        compiler_params=params(),
        cost_estimate=cost(2 * out_ch * 9 * C * HW, (out_ch + C) * HW * 2 + out_ch * 9 * C * 2),
        name=name,
    )(meta, grad, *pieces)


def turn_kernel(meta, own_ref, other_ref, out_ref):
    half = own_ref.shape[0]
    for tap in range(9):
        at = pl.ds(pl.multiple_of(tap * C + meta[0], half), half)
        row = meta[0]
        for ref in (own_ref, other_ref):
            to = pl.ds(pl.multiple_of((8 - tap) * C + row, half), half)
            out_ref[:, to] = ref[:, at].astype(F32).T.astype(BF)
            row = half - row


def turned_pair(meta, own, other):
    return pl.pallas_call(
        turn_kernel,
        out_shape=struct(own.shape, BF),
        in_specs=[scalars(), whole(), whole()],
        out_specs=whole(),
        compiler_params=params(),
        cost_estimate=cost(0, 3 * own.size * 2),
        name="turn",
    )(meta, own, other)


def norm_three_back_kernel(n, *refs):
    addends, (hidden_ref, stat_ref, par_ref, cot_ref, hid_ref, grad_ref, sums_ref) = (
        refs[:n],
        refs[n:],
    )

    def body(rows):
        dy = addends[0][rows, :].astype(F32)
        for extra in addends[1:]:
            dy = dy + extra[rows, :].astype(F32)
        par, stat = par_ref[rows, :], stat_ref[rows, :]
        gain, rstd = par[:, 1:2], stat[:, 1:2]
        hat = (hidden_ref[rows, :] - stat[:, 0:1]) * rstd
        total = jnp.sum(dy, axis=1, keepdims=True)
        total_hat = jnp.sum(dy * hat, axis=1, keepdims=True)
        mean_u, mean_uhat = norm_backward(total, total_hat, gain)
        top = cot_ref[rows, :].astype(F32)
        out = top + (dy * gain - mean_u - hat * mean_uhat) * rstd
        hid_ref[rows, :] = out
        low = out.astype(BF)
        grad_ref[rows, :] = low
        sums_ref[rows, :] = columns(
            [
                total_hat,
                total,
                jnp.sum(low.astype(F32), axis=1, keepdims=True),
                jnp.sum(top, axis=1, keepdims=True),
            ]
        )

    for_groups(hidden_ref.shape[0], body)


def norm_three_back(addends, hidden, stat, par, cot):
    ch = hidden.shape[0]
    rows = 32

    def part(a):
        return pl.BlockSpec((rows, a.shape[1]), lambda r: (r, 0))

    outs = [struct((ch, HW), F32), struct((ch, HW), BF), struct((ch, 128), F32)]
    ins = (*addends, hidden, stat, par, cot)
    return pl.pallas_call(
        functools.partial(norm_three_back_kernel, len(addends)),
        grid=(ch // rows,),
        out_shape=outs,
        in_specs=[part(a) for a in ins],
        out_specs=[part(a) for a in outs],
        compiler_params=params(),
        cost_estimate=cost(20 * ch * HW, 16 * ch * HW),
        name="norm_three_back",
    )(*ins)


def piece_columns(meta, w_ref, pieces):
    first = meta[0]
    acc = None
    for x_ref in pieces:
        rows = x_ref.shape[0]
        term = dot(w_ref[:, pl.ds(pl.multiple_of(first, rows), rows)], x_ref[...])
        acc = term if acc is None else acc + term
        first = w_ref.shape[1] - rows - first
    return acc


def inputs_kernel(n, meta, w_ref, *refs):
    pieces, (bias_ref, out_ref) = refs[:n], refs[n:]
    out_ref[...] = (piece_columns(meta, w_ref, pieces) + bias_ref[...]).astype(BF)


def inputs_product(meta, weight, pieces, bias, width=1024, name=None):
    rows, depth = weight.shape
    return pl.pallas_call(
        functools.partial(inputs_kernel, len(pieces)),
        grid=(HW // width,),
        out_shape=struct((rows, HW), BF),
        in_specs=[scalars(), pl.BlockSpec((rows, depth), lambda p: (0, 0))]
        + [pl.BlockSpec((x.shape[0], width), lambda p: (0, p)) for x in pieces]
        + [pl.BlockSpec((rows, 1), lambda p: (0, 0))],
        out_specs=pl.BlockSpec((rows, width), lambda p: (0, p)),
        compiler_params=params(),
        cost_estimate=cost(2 * rows * depth * HW, (rows + depth) * HW * 2),
        name=name,
    )(meta, weight, *pieces, bias)


def parts_kernel(n, meta, w_ref, *refs):
    pieces, outs = refs[:n], refs[n:]
    first = meta[0]
    for out_ref in outs:
        rows = out_ref.shape[0]
        row = pl.ds(pl.multiple_of(first, rows), rows)
        acc = None
        at = 0
        for x_ref in pieces:
            depth = x_ref.shape[0]
            term = dot(w_ref[row, at : at + depth], x_ref[...])
            acc = term if acc is None else acc + term
            at += depth
        out_ref[...] = acc.astype(BF)
        first = w_ref.shape[0] - rows - first


def parts_product(meta, weight, pieces, count, width=1024, name=None):
    rows, depth = weight.shape
    part = struct((rows // count, HW), BF)
    return pl.pallas_call(
        functools.partial(parts_kernel, len(pieces)),
        grid=(HW // width,),
        out_shape=[part] * count,
        in_specs=[scalars(), pl.BlockSpec((rows, depth), lambda p: (0, 0))]
        + [pl.BlockSpec((x.shape[0], width), lambda p: (0, p)) for x in pieces],
        out_specs=[pl.BlockSpec((rows // count, width), lambda p: (0, p))] * count,
        compiler_params=params(),
        cost_estimate=cost(2 * rows * depth * HW, (rows + depth) * HW * 2),
        name=name,
    )(meta, weight, *pieces)


def output_kernel(n, meta, w_ref, *refs):
    pieces, (bias_ref, hidden_ref, out_ref) = refs[:n], refs[n:]
    acc = hidden_ref[...] + bias_ref[...] + piece_columns(meta, w_ref, pieces)
    half = acc.shape[1] // 2
    for base, val in zip((0, HW // 2), unfold(acc)):
        first = pl.multiple_of(base + pl.program_id(0) * half, half)
        out_ref[:, pl.ds(first, half)] = val.astype(BF)


def output_product(meta, weight, pieces, bias, hidden, width=1024):
    rows, depth = weight.shape
    return pl.pallas_call(
        functools.partial(output_kernel, len(pieces)),
        grid=(HW // width,),
        out_shape=struct((rows, HW), BF),
        in_specs=[scalars(), pl.BlockSpec((rows, depth), lambda p: (0, 0))]
        + [pl.BlockSpec((x.shape[0], width), lambda p: (0, p)) for x in pieces]
        + [
            pl.BlockSpec((rows, 1), lambda p: (0, 0)),
            pl.BlockSpec((rows, width), lambda p: (0, p)),
        ],
        out_specs=pl.BlockSpec((rows, HW), lambda p: (0, 0)),
        compiler_params=params(),
        cost_estimate=cost(2 * rows * depth * HW, (rows * 3 + depth) * HW * 2),
        name="output",
    )(meta, weight, *pieces, bias, hidden)


def outer_kernel(n_left, n_right, meta, *refs):
    lefts, rights = refs[:n_left], refs[n_left : n_left + n_right]
    out_ref, sums_ref = refs[n_left + n_right : n_left + n_right + 2]
    acc_ref, tot_ref = refs[n_left + n_right + 2 :]
    step = pl.program_id(0)

    @pl.when(step == 0)
    def _():
        acc_ref[...] = jnp.zeros_like(acc_ref)
        tot_ref[...] = jnp.zeros_like(tot_ref)

    row = 0
    for left in lefts:
        rows = left.shape[0]
        val = left[...]
        first = meta[0]
        for right in rights:
            cols = right.shape[0]
            at = pl.ds(pl.multiple_of(first, cols), cols)
            acc_ref[row : row + rows, at] += dot_nt(val, right[...])
            first = acc_ref.shape[1] - cols - first
        tot_ref[row : row + rows, :] += jnp.sum(val.astype(F32), axis=1, keepdims=True)
        row += rows

    @pl.when(step == pl.num_programs(0) - 1)
    def _():
        out_ref[...] = acc_ref[...].astype(BF)
        sums_ref[...] = tot_ref[...]


def outer(meta, lefts, rights, width=1024, name=None):
    rows, cols = sum(a.shape[0] for a in lefts), sum(a.shape[0] for a in rights)
    fixed = lambda p: (0, 0)
    return pl.pallas_call(
        functools.partial(outer_kernel, len(lefts), len(rights)),
        grid=(HW // width,),
        out_shape=[struct((rows, cols), BF), struct((rows, 128), F32)],
        in_specs=[scalars()]
        + [pl.BlockSpec((a.shape[0], width), lambda p: (0, p)) for a in (*lefts, *rights)],
        out_specs=[pl.BlockSpec((rows, cols), fixed), pl.BlockSpec((rows, 128), fixed)],
        scratch_shapes=[pltpu.VMEM((rows, cols), F32), pltpu.VMEM((rows, 128), F32)],
        compiler_params=params(),
        cost_estimate=cost(2 * rows * cols * HW, (rows + cols) * HW * 2),
        name=name,
    )(meta, *lefts, *rights)


def attention_kernel(
    n_grads, lim_ref, q_ref, k_ref, v_ref, kc_ref, vc_ref, *refs, unroll, back,
):
    g_refs, refs = refs[:n_grads], refs[n_grads:]
    o_ref, dq_ref, dk_ref, dv_ref, dkc_ref, dvc_ref = refs[:6]
    kt, vt, kn, vn, s_even, s_odd, p_sc, tops, o_acc, dk_acc, dv_acc = refs[6:]
    step, last = pl.program_id(1), pl.num_programs(1) - 1
    width = q_ref.shape[-1]
    blocks = KEYS // BLOCK

    @pl.when(step == 0)
    def _():
        spare = jnp.zeros((HEAD_DIM, KEYS - HW - CTXP), BF)
        for ref, own, ctx in ((kn, k_ref, kc_ref), (vn, v_ref, vc_ref)):
            ref[:, :HW] = own[0, 0]
            ref[:, HW : HW + CTXP] = ctx[0, 0]
            ref[:, HW + CTXP :] = spare
        row = lax.broadcasted_iota(jnp.int32, (HEAD_DIM, BLOCK), 0)
        for n in range(blocks):
            at = slice(n * BLOCK, (n + 1) * BLOCK)
            key = lax.broadcasted_iota(jnp.int32, (HEAD_DIM, BLOCK), 1) + n * BLOCK
            fill = jnp.where((row == 0) & (key >= HW + lim_ref[0]), NEG_FILL, 0.0)
            kt[at, :] = jnp.concatenate([kn[:, at].astype(F32), fill], 0).T.astype(BF)
            vt[at, :] = jnp.concatenate([vn[:, at].astype(F32), jnp.zeros_like(fill)], 0).T.astype(BF)
        dk_acc[...] = jnp.zeros_like(dk_acc)
        dv_acc[...] = jnp.zeros_like(dv_acc)

    def keys_at(n):
        return pl.ds(pl.multiple_of(n * BLOCK, BLOCK), BLOCK)

    scale = HEAD_DIM ** (-0.5)
    q = (q_ref[0, 0].astype(F32) * scale).astype(BF)
    one = jnp.where(lax.broadcasted_iota(jnp.int32, (HEAD_DIM, width), 0) == 0, 1.0, 0.0).astype(BF)
    q_more = jnp.concatenate([q, one], 0)

    def score(n, held):
        scores = dot(kt[keys_at(n), :], q_more)
        held[...] = scores
        return jnp.max(jnp.max(scores.reshape(BLOCK // 8, 8, width), axis=0), axis=0, keepdims=True)

    o_acc[...] = jnp.zeros_like(o_acc)

    def forward(n, held, top, total, shrink):
        raised = jnp.exp(held[...] - top)
        low = raised.astype(BF)
        p_sc[keys_at(n), :] = low
        tops[n, 0:1, :] = top
        sums = jnp.sum(raised.reshape(BLOCK // 8, 8, width), axis=0)
        o_acc[...] = o_acc[...] * shrink + dot(vn[:, keys_at(n)], low)
        return total * shrink + sums

    def forward_step(n, held, ahead_held, carry):
        top, total, shrink = carry
        ahead = jnp.maximum(top, score(n + 1, ahead_held))
        total = forward(n, held, top, total, shrink)
        return ahead, total, jnp.exp(top - ahead)

    held = (s_even, s_odd)

    def forward_run(j, carry):
        for u in range(unroll):
            carry = forward_step(unroll * j + u, held[u % 2], held[1 - u % 2], carry)
        return carry

    carry = (score(0, s_even), jnp.zeros((8, width), F32), jnp.ones((1, width), F32))
    carry = lax.fori_loop(0, blocks // unroll - 1, forward_run, carry)
    for n in range(blocks - unroll, blocks - 1):
        carry = forward_step(n, held[n % 2], held[1 - n % 2], carry)
    top, total, shrink = carry
    total = forward(blocks - 1, s_odd, top, total, shrink)

    inverse = 1.0 / jnp.sum(total, axis=0, keepdims=True)
    mixed = o_acc[...] * inverse
    o_ref[0] = mixed.astype(BF)
    grad = sum(g_ref[0].astype(F32) for g_ref in g_refs)
    if n_grads > 1:
        grad = grad.astype(BF).astype(F32)
    delta = jnp.sum(grad * mixed, axis=0, keepdims=True)
    dq = jnp.zeros((HEAD_DIM, width), F32)
    none = jnp.zeros((HEAD_DIM, width), BF)
    for c in range(0, KEYS, back):
        at = slice(c, c + back)
        slopes = []
        for n in range(c // BLOCK, (c + back) // BLOCK):
            sub = slice(n * BLOCK, (n + 1) * BLOCK)
            factor = inverse * jnp.exp(tops[n, 0:1, :] - top)
            grad_low = (grad * factor).astype(BF)
            both = jnp.concatenate([grad_low, none], 0)
            probs = p_sc[sub, :]
            slope = (dot(vt[sub, :], both) - delta * factor).astype(BF) * probs
            slopes.append(slope)
            dv_acc[:, sub] += dot_nt(grad_low, probs)
        slope = jnp.concatenate(slopes, 0)
        dq = dq + dot(kn[:, at], slope)
        dk_acc[:, at] += dot_nt(q, slope)
    dq_ref[0] = (dq * scale).astype(BF)

    @pl.when(step == last)
    def _():
        dk_ref[0] = dk_acc[:, :HW].astype(BF)
        dv_ref[0] = dv_acc[:, :HW].astype(BF)
        dkc_ref[0] = dk_acc[:, HW : HW + CTXP].astype(BF)
        dvc_ref[0] = dv_acc[:, HW : HW + CTXP].astype(BF)


def attention(limit, qkv, ctx_kv, grads, width=1024, unroll=6, back=256):
    heads = qkv.shape[1]
    keys = KEYS

    def part(t, w, moving):
        return pl.BlockSpec(
            (1, 1, HEAD_DIM, w), (lambda h, i: (t, h, 0, i)) if moving else (lambda h, i: (t, h, 0, 0))
        )

    def row(w, moving):
        return pl.BlockSpec(
            (1, HEAD_DIM, w), (lambda h, i: (h, 0, i)) if moving else (lambda h, i: (h, 0, 0))
        )

    big, small = struct((heads, HEAD_DIM, HW), BF), struct((heads, HEAD_DIM, CTXP), BF)
    return pl.pallas_call(
        functools.partial(attention_kernel, len(grads), unroll=unroll, back=back),
        grid=(heads, HW // width),
        in_specs=[
            pl.BlockSpec(memory_space=pltpu.SMEM),
            part(0, width, True),
            part(1, HW, False),
            part(2, HW, False),
            part(0, CTXP, False),
            part(1, CTXP, False),
        ]
        + [row(width, True)] * len(grads),
        out_specs=[
            row(width, True),
            row(width, True),
            row(HW, False),
            row(HW, False),
            row(CTXP, False),
            row(CTXP, False),
        ],
        out_shape=[big, big, big, big, small, small],
        scratch_shapes=[
            pltpu.VMEM((keys, 2 * HEAD_DIM), BF),
            pltpu.VMEM((keys, 2 * HEAD_DIM), BF),
            pltpu.VMEM((HEAD_DIM, keys), BF),
            pltpu.VMEM((HEAD_DIM, keys), BF),
            pltpu.VMEM((BLOCK, width), F32),
            pltpu.VMEM((BLOCK, width), F32),
            pltpu.VMEM((keys, width), BF),
            pltpu.VMEM((keys // BLOCK, 8, width), F32),
            pltpu.VMEM((HEAD_DIM, width), F32),
            pltpu.VMEM((HEAD_DIM, keys), F32),
            pltpu.VMEM((HEAD_DIM, keys), F32),
        ],
        compiler_params=params(dimension_semantics=("arbitrary", "arbitrary")),
        cost_estimate=cost(
            24 * heads * HW * keys * HEAD_DIM, heads * HEAD_DIM * 8 * HW * 2, heads * HW * keys
        ),
        name="attention",
    )(limit, qkv, qkv, qkv, ctx_kv, ctx_kv, *grads)


class Alone:
    parts = 1

    def __init__(self, mesh):
        self.images = mesh.shape["dp"]

    def meta(self):
        return jnp.array([0, 1], jnp.int32)

    def image(self):
        return lax.axis_index("dp")

    def got(self, x):
        return x

    def pick(self, own, got):
        return own

    def gather(self, x):
        return (lax.all_gather(x, "tensor", axis=0, tiled=True),)

    def scatter(self, parts):
        return (lax.psum_scatter(parts[0], "tensor", scatter_dimension=0, tiled=True),)

    def turn(self, meta, w):
        ch = w.shape[0]
        cut = w.reshape(ch, 9, C)
        turned = lax.all_to_all(cut, "tensor", split_axis=2, concat_axis=0, tiled=True)
        return turned[:, ::-1].transpose(2, 1, 0).reshape(ch, 9 * C)

    def total(self, x, beside):
        return lax.psum(x, "dp")

    def everywhere(self, x):
        return lax.psum(x, "dp")

    def sum_owned(self, x, beside):
        return lax.psum(x, "dp"), beside(x)


class Paired:
    parts = 2

    def __init__(self, mesh):
        dp = mesh.shape["dp"]
        self.images = dp
        self.far = [
            ((2 * k + core) * 2 + 1 - core, (2 * k + 1 - core) * 2 + core)
            for k in range(dp // 2)
            for core in range(2)
        ]
        self.bits = [1 << b for b in range((dp - 1).bit_length())]

    def half(self):
        return lax.axis_index("dp") % 2

    def stays(self):
        return self.half() == lax.axis_index("tensor")

    def meta(self):
        return jnp.stack([self.half() * (C // 2), self.stays().astype(jnp.int32)]).astype(jnp.int32)

    def image(self):
        return lax.axis_index("dp") // 2 * 2 + lax.axis_index("tensor")

    def got(self, x):
        return lax.ppermute(x, ("dp", "tensor"), self.far)

    def pick(self, own, got):
        return jnp.where(self.stays(), own, got)

    def over(self, x, bit):
        return lax.ppermute(x, "dp", [(i, i ^ bit) for i in range(self.images)])

    def gather(self, x):
        return (x, self.over(x, 1))

    def scatter(self, parts):
        return (parts[0], self.over(parts[1], 1))

    def turn(self, meta, w):
        return turned_pair(meta, w, self.over(w, 1))

    def total(self, x, beside):
        x = after(beside, x + lax.ppermute(x, "tensor", [(0, 1), (1, 0)]))
        for bit in self.bits[1:]:
            x = x + self.over(x, bit)
        return self.pick(x, self.over(x, 1))

    def everywhere(self, x):
        for bit in self.bits:
            x = x + self.over(x, bit)
        return x

    def sum_owned(self, x, beside):
        rows = x.shape[0] // 2
        order = (self.bits, [self.bits[0], *self.bits[2:], self.bits[1]])
        parts = [lax.slice_in_dim(x, at * rows, (at + 1) * rows) for at in range(2)]

        def upper(bit):
            return (lax.axis_index("dp") // bit) % 2

        for step in range(len(self.bits)):
            size = parts[0].shape[0] // 2
            for at in range(2):
                bit = order[at][step]
                keep = lax.dynamic_slice_in_dim(parts[at], upper(bit) * size, size)
                send = lax.dynamic_slice_in_dim(parts[at], (1 - upper(bit)) * size, size)
                parts[at] = (keep.astype(F32) + self.over(send, bit).astype(F32)).astype(BF)
        held = beside(parts[0])
        for step in reversed(range(len(self.bits))):
            if step == 0:
                parts = list(after(held, *parts))
            for at in range(2):
                bit = order[at][step]
                other = self.over(parts[at], bit)
                parts[at] = jnp.where(
                    upper(bit) == 0,
                    jnp.concatenate([parts[at], other]),
                    jnp.concatenate([other, parts[at]]),
                )
        return jnp.concatenate(parts), held


def after(first, *later):
    held = lax.optimization_barrier((first, *later))
    return held[1:] if len(later) > 1 else held[1]


def local(plan, features, cotangent, embedding, context, lengths, norm1_gain, norm1_bias,
    conv1_weight, conv1_bias, emb_weight, emb_bias, norm2_gain, norm2_bias, conv2_weight,
    conv2_bias, norm3_gain, norm3_bias, qkv_weight, qkv_bias, context_weight, context_bias,
    out_weight, out_bias,
):
    ch, images, pixels = features.shape
    heads = ch // HEAD_DIM
    meta = plan.meta()
    moved = plan.parts == 2

    emb_act = jax.nn.silu(embedding.astype(F32)).astype(BF)
    scale_shift = (
        jnp.einsum("ie,teo->to", emb_act, emb_weight, preferred_element_type=F32) + emb_bias
    )
    length_row = jnp.broadcast_to(lengths.astype(F32)[:, None], (1, ch))
    vectors = jnp.concatenate(
        [
            jnp.stack([norm1_gain, norm1_bias, conv1_bias, norm2_gain, norm2_bias]),
            scale_shift,
            jnp.stack([conv2_bias, norm3_gain, norm3_bias, out_bias]),
            qkv_bias,
            length_row,
        ]
    )
    f_own = features.reshape(ch, pixels)
    f_got = plan.got(f_own)
    vectors, w1_own = after(scale_shift, vectors, conv1_weight)
    vectors = plan.pick(vectors, plan.got(vectors))
    w1_got = plan.got(w1_own)
    ctx_kv = (
        jnp.einsum("toe,ne->ton", context_weight, context[0], preferred_element_type=F32)
        + context_bias[:, :, None]
    ).astype(BF)
    ctx_kv = jnp.pad(ctx_kv, ((0, 0), (0, 0), (0, CTXP - CTX)))
    emb_all = jnp.where(
        jnp.arange(plan.images)[:, None] == lax.axis_index("dp"), emb_act, jnp.zeros_like(emb_act)
    )
    emb_all = plan.everywhere(emb_all)
    length = vectors[14, :1].astype(jnp.int32)
    par_one, par_two, par_three = vectors[0:2].T, vectors[2:7].T, vectors[7:10].T
    bias_qkv, bias_out = vectors[11:14].reshape(3 * ch, 1), vectors[10].reshape(ch, 1)
    par_one = after(emb_all, par_one)
    w2_got = plan.got(after(vectors, conv2_weight))
    act_one, stat_one, f_low = first_activation(meta, f_own, f_got, par_one)
    full_one = plan.gather(act_one)
    mats_own = jnp.concatenate([qkv_weight.reshape(3 * ch, C), out_weight])
    mats_own, ctx_own, cot_own = after(
        act_one, mats_own, ctx_kv, cotangent.reshape(ch, pixels)
    )
    mats_got, ctx_got = plan.got(mats_own), plan.got(ctx_own)
    cot_got = plan.got(cot_own)

    par_two, par_three, bias_qkv, bias_out = after(act_one, par_two, par_three, bias_qkv, bias_out)
    par_two = after((par_three, bias_qkv, bias_out), par_two)
    low, stat, wide = struct((ch, HW), BF), struct((ch, 128), F32), struct((ch, HW), F32)
    weight = struct((ch, 9 * C), BF)
    act_two, stat_two, conv_one, w1 = conv_call(
        conv_one_kernel, meta, (conv1_weight, w1_got), full_one, (par_two,), (),
        [low, stat], [wide, weight], [], "conv_one",
    )
    full_two = plan.gather(act_two)
    normed, stat_three, hidden, w2 = conv_call(
        conv_two_kernel, meta, (conv2_weight, w2_got), full_two, (par_three, f_low), (),
        [low, stat], [wide, weight], [], "conv_two",
    )
    full_three = plan.gather(normed)
    mats_got, ctx_got, cot_got = after(normed, mats_got, ctx_got, cot_got)
    mats = plan.pick(mats_own, mats_got)
    w_qkv, w_out = mats[: 3 * ch], mats[3 * ch :]
    cot = folded(meta, cot_own, cot_got)
    grad_heads = plan.scatter(
        parts_product(meta, w_out.T, (cot,), plan.parts, name="grad_heads")
    )
    qkv = inputs_product(meta, w_qkv, full_three, bias_qkv, name="qkv")
    ctx_kv = plan.pick(ctx_own, ctx_got)
    mixed, dq, dk, dv, dkc, dvc = attention(
        4 + length,
        qkv.reshape(3, heads, HEAD_DIM, HW),
        ctx_kv.reshape(2, heads, HEAD_DIM, CTXP),
        [a.reshape(heads, HEAD_DIM, HW) for a in grad_heads],
    )

    flat = lambda a: a.reshape(ch, HW)
    dq, dk, dv = flat(dq), flat(dk), flat(dv)
    addends = plan.scatter(
        parts_product(meta, w_qkv.T, (dq, dk, dv), plan.parts, name="grad_normed")
    )
    full_heads = plan.gather(flat(mixed))
    ctx_own = jnp.concatenate([a.reshape(1, ch, CTXP) for a in (dkc, dvc)])
    ctx_got = plan.got(ctx_own)
    turned_two = plan.turn(meta, after(mixed, w2))
    turned_one = plan.turn(meta, after(mixed, w1))
    dw_qkv, db_qkv = outer(meta, (dq, dk, dv), full_three, name="qkv_grad")
    dw_out, _ = outer(meta, (cot,), full_heads, name="out_grad")
    mats_own = jnp.concatenate([dw_qkv, dw_out])
    mats_got = plan.got(mats_own)
    grad_hidden, grad_two, sums_three = norm_three_back(addends, hidden, stat_three, par_three, cot)
    full_grad_two = plan.gather(grad_two)
    dw_two = conv_weight_grad(meta, grad_two, full_two, "conv_two_weight_grad")
    two_got = plan.got(dw_two)
    full_grad_two = after((dw_two, turned_one), *full_grad_two) if moved else full_grad_two
    grad_one, sums_two = conv_call(
        conv_two_back_kernel, meta, (turned_two, turned_two), full_grad_two, (par_two, stat_two),
        (conv_one,), [low, stat], [], [pltpu.VMEM((ch, HW), F32)], "conv_two_back",
    )
    full_grad_one = plan.gather(grad_one)
    mats_got, ctx_got, two_got = after(grad_one, mats_got, ctx_got, two_got)
    ctx_grad = plan.pick(ctx_own, ctx_got)[:, :, :CTX]
    dw_ctx = jnp.einsum("ton,ne->toe", ctx_grad, context[0], preferred_element_type=F32).astype(BF)
    mats = plan.pick(mats_own, mats_got)
    dw_two = plan.pick(dw_two, two_got)
    early = jnp.concatenate(
        [dw_ctx[0], dw_ctx[1], *(mats[t * ch : (t + 1) * ch] for t in range(4)), dw_two], 1
    )
    held = after(early, grad_one)
    early = lax.psum_scatter(early, "dp", scatter_dimension=0, tiled=True)
    dw_one = conv_weight_grad(meta, held, full_one, "conv_one_weight_grad")
    one_got = plan.got(dw_one)
    full_grad_one = after(dw_one, *full_grad_one) if moved else full_grad_one
    input_grad, sums_one = conv_call(
        conv_one_back_kernel, meta, (turned_one, turned_one), full_grad_one,
        (par_one, stat_one, f_low), (grad_hidden,),
        [struct((ch, HW), BF if moved else F32), stat], [],
        [pltpu.VMEM((ch, HW), F32)], "conv_one_back",
    )
    input_got = plan.got(input_grad)

    one_got = after(input_grad, one_got)
    output = output_product(
        meta, w_out, full_heads, bias_out, after(input_grad, hidden)
    )
    output_got = plan.got(output)
    ctx_sums = jnp.sum(ctx_own.astype(F32), axis=2)
    sums_two = sums_two[:, :5].T
    own_mod = sums_two[2:4].astype(BF).astype(F32)
    mods = jnp.where(
        (jnp.arange(plan.images) == plan.image())[:, None, None], own_mod, jnp.zeros_like(own_mod)
    ).reshape(2 * plan.images, ch)
    small = plan.total(
        jnp.concatenate(
            [
                sums_three[:, :4].T,
                db_qkv[:, 0].reshape(3, ch),
                sums_two[:2],
                sums_two[4:5],
                ctx_sums,
                sums_one[:, :2].T,
                mods,
            ]
        ),
        output,
    )
    early, dw_one, one_got = after(small, early, dw_one, one_got)

    def finish(token):
        out_got, in_got, sums = after(token, output_got, input_got, small)
        per_image = sums[14:].reshape(plan.images, 2, ch).astype(BF)
        return (
            plan.pick(input_grad, in_got).astype(F32).reshape(ch, images, pixels),
            plan.pick(output, out_got),
            jnp.stack(
                [
                    jnp.einsum("ie,io->eo", emb_all, per_image[:, t], preferred_element_type=F32)
                    for t in range(2)
                ]
            ),
        )

    dw_one, done = plan.sum_owned(plan.pick(dw_one, one_got), finish)
    early = lax.all_gather(early, "dp", axis=0, tiled=True)
    mods = small[14:].reshape(plan.images, 2, ch)
    input_grad, output, dw_emb = done
    early = after((dw_one, small, input_grad, output), early)
    dw_ctx = jnp.stack([early[:, n * CTX_EMB : (n + 1) * CTX_EMB] for n in range(2)])
    first = 2 * CTX_EMB
    mats = [early[:, first + n * C : first + (n + 1) * C].astype(F32) for n in range(4)]
    dw_two = early[:, first + 4 * C :]

    return (
        output.reshape(ch, images, pixels),
        input_grad,
        small[12],
        small[13],
        dw_one.astype(F32),
        small[9],
        dw_emb,
        jnp.sum(mods, axis=0),
        small[7],
        small[8],
        dw_two.astype(F32),
        small[2],
        small[0],
        small[1],
        jnp.stack(mats[:3]),
        small[4:7],
        dw_ctx.astype(F32),
        small[10:12],
        mats[3],
        small[3],
    )


def solution(mesh):
    paired = mesh.shape["tensor"] == 2 and mesh.shape["dp"] % 2 == 0
    plan = Paired(mesh) if paired else Alone(mesh)
    specs = (
        P("tensor", "dp", None),
        P("tensor", "dp", None),
        P("dp", None),
        P("dp", None, None),
        P("dp"),
        P("tensor"),
        P("tensor"),
        P("tensor", None),
        P("tensor"),
        P(None, None, "tensor"),
        P(None, "tensor"),
        P("tensor"),
        P("tensor"),
        P("tensor", None),
        P("tensor"),
        P("tensor"),
        P("tensor"),
        P(None, "tensor", None),
        P(None, "tensor"),
        P(None, "tensor", None),
        P(None, "tensor"),
        P("tensor", None),
        P("tensor"),
    )
    return jax.shard_map(
        functools.partial(local, plan),
        mesh=mesh,
        in_specs=specs,
        out_specs=(
            P("tensor", "dp", None),
            P("tensor", "dp", None),
            P("tensor"),
            P("tensor"),
            P("tensor", None),
            P("tensor"),
            P(None, None, "tensor"),
            P(None, "tensor"),
            P("tensor"),
            P("tensor"),
            P("tensor", None),
            P("tensor"),
            P("tensor"),
            P("tensor"),
            P(None, "tensor", None),
            P(None, "tensor"),
            P(None, "tensor", None),
            P(None, "tensor"),
            P("tensor", None),
            P("tensor"),
        ),
        check_vma=False,
    )
```

```python
import functools

import jax
import jax.numpy as jnp
from jax import lax
from jax.experimental import pallas as pl
from jax.experimental.pallas import tpu as pltpu
from jax.sharding import PartitionSpec as P

C = 512
HEAD_DIM = 64
PER_GROUP = 16
SIDE = 64
HW = 4096
CTX = 260
CTXP = 384
CTX_EMB = 2048
BLOCK = 256
KEYS = 4608
PAD = 128
FILL = 32
SCALE = 100
EPSILON = 1e-05
NEG_FILL = -1e30
F32 = jnp.float32
BF = jnp.bfloat16
NT = (((1,), (1,)), ((), ()))
VMEM_BYTES = 62 << 20


def dot(a, b):
    return jnp.dot(a, b, preferred_element_type=F32)


def dot_nt(a, b):
    return lax.dot_general(a, b, NT, preferred_element_type=F32)


def whole():
    return pl.BlockSpec(memory_space=pltpu.VMEM)


def placed():
    return pl.BlockSpec(memory_space=pl.ANY)


def scalars():
    return pl.BlockSpec(memory_space=pltpu.SMEM)


def params(**kwargs):
    return pltpu.CompilerParams(vmem_limit_bytes=VMEM_BYTES, **kwargs)


def cost(flops, nbytes, transcendentals=0):
    return pl.CostEstimate(
        flops=flops // SCALE, bytes_accessed=nbytes // SCALE, transcendentals=transcendentals // SCALE
    )


def struct(shape, dtype):
    return jax.ShapeDtypeStruct(shape, dtype)


def fetch(meta, own_ref, got_ref, buf, sem):
    @pl.when(meta[1] == 1)
    def _():
        pltpu.make_async_copy(own_ref, buf, sem).start()

    @pl.when(meta[1] != 1)
    def _():
        pltpu.make_async_copy(got_ref, buf, sem).start()


def arrive(own_ref, buf, sem):
    pltpu.make_async_copy(own_ref, buf, sem).wait()


def group_scalar(column):
    return jnp.sum(column, axis=0, keepdims=True) * (1.0 / (PER_GROUP * HW))


def group_stats(vals):
    mean = group_scalar(jnp.sum(vals, axis=1, keepdims=True))
    centred = vals - mean
    var = group_scalar(jnp.sum(centred * centred, axis=1, keepdims=True))
    rstd = lax.rsqrt(var + EPSILON)
    return mean, rstd


def norm_backward(dy_sum, dyx_sum, gain):
    return group_scalar(dy_sum * gain), group_scalar(dyx_sum * gain)


def for_groups(channels, body, together=2):
    def step(g, carry):
        for u in range(together):
            first = pl.multiple_of((g * together + u) * PER_GROUP, PER_GROUP)
            body(pl.ds(first, PER_GROUP))
        return carry

    lax.fori_loop(0, channels // PER_GROUP // together, step, 0)


def columns(values):
    lane = lax.broadcasted_iota(jnp.int32, (PER_GROUP, 128), 1)
    tile = jnp.zeros((PER_GROUP, 128), F32)
    for at, val in enumerate(values):
        tile = jnp.where(lane == at, val, tile)
    return tile


ROWS = SIDE // 2


def lanes(x, n):
    return x[:, 128 * n : 128 * n + 128]


def low_lanes(x):
    return lax.broadcasted_iota(jnp.int32, (x.shape[0], 128), 1) < SIDE


def fold(x):
    low = low_lanes(x)
    out = []
    for r in range(ROWS):
        upper, lower = lanes(x, r // 2), lanes(x, r // 2 + ROWS // 2)
        if r % 2 == 0:
            out.append(jnp.where(low, upper, pltpu.roll(lower, SIDE, 1)))
        else:
            out.append(jnp.where(low, pltpu.roll(upper, SIDE, 1), lower))
    return jnp.concatenate(out, 1)


def unfold(x):
    low = low_lanes(x)
    pairs = range(x.shape[1] // 256)
    top = [jnp.where(low, lanes(x, 2 * n), pltpu.roll(lanes(x, 2 * n + 1), SIDE, 1)) for n in pairs]
    bottom = [
        jnp.where(low, pltpu.roll(lanes(x, 2 * n), SIDE, 1), lanes(x, 2 * n + 1)) for n in pairs
    ]
    return jnp.concatenate(top, 1), jnp.concatenate(bottom, 1)


def fold_kernel(meta, own_ref, got_ref, out_ref, x_buf, sem):
    fetch(meta, own_ref, got_ref, x_buf, sem)
    arrive(own_ref, x_buf, sem)

    def body(rows):
        out_ref[rows, :] = fold(x_buf[rows, :].astype(F32)).astype(BF)

    for_groups(out_ref.shape[0], body)


def folded(meta, own, got):
    return pl.pallas_call(
        fold_kernel,
        out_shape=struct(own.shape, BF),
        in_specs=[scalars(), placed(), placed()],
        out_specs=whole(),
        scratch_shapes=[pltpu.VMEM(own.shape, BF), pltpu.SemaphoreType.DMA(())],
        compiler_params=params(),
        cost_estimate=cost(8 * own.size, 4 * own.size),
        name="fold",
    )(meta, own, got)


def act_one_kernel(meta, own_ref, got_ref, par_ref, act_ref, stat_ref, fold_ref, x_buf, sem):
    fetch(meta, own_ref, got_ref, x_buf, sem)
    arrive(own_ref, x_buf, sem)

    def body(rows):
        vals = fold(x_buf[rows, :].astype(F32))
        fold_ref[rows, :] = vals.astype(BF)
        mean, rstd = group_stats(vals)
        par = par_ref[rows, :]
        out = (vals - mean) * (rstd * par[:, 0:1]) + par[:, 1:2]
        act_ref[rows, :] = (out * jax.nn.sigmoid(out)).astype(BF)
        stat_ref[rows, :] = columns([mean, rstd])

    for_groups(act_ref.shape[0], body)


def first_activation(meta, own, got, par):
    ch = own.shape[0]
    return pl.pallas_call(
        act_one_kernel,
        out_shape=[struct((ch, HW), BF), struct((ch, 128), F32), struct((ch, HW), BF)],
        in_specs=[scalars(), placed(), placed(), whole()],
        out_specs=[whole()] * 3,
        scratch_shapes=[pltpu.VMEM((ch, HW), BF), pltpu.SemaphoreType.DMA(())],
        compiler_params=params(),
        cost_estimate=cost(20 * ch * HW, 6 * ch * HW, ch * HW),
        name="act_one",
    )(meta, own, got, par)


def fill_shifted(xs, pieces, first):
    start = first
    for x_ref in pieces:
        rows = x_ref.shape[0]

        def step(r, carry, x_ref=x_ref, start=start):
            off = pl.multiple_of(r * FILL, FILL)
            at = pl.ds(pl.multiple_of(start + off, FILL), FILL)
            lane = lax.broadcasted_iota(jnp.int32, (FILL, 128), 1)
            low = lane < SIDE
            left, right = lane % SIDE == 0, lane % SIDE == SIDE - 1
            zero = jnp.zeros((FILL, 128), F32)
            here = pl.ds(off, FILL)
            for n in range(ROWS):
                x = x_ref[here, 128 * n : 128 * n + 128].astype(F32)
                kinds = (
                    jnp.where(left, zero, pltpu.roll(x, 1, 1)),
                    x,
                    jnp.where(right, zero, pltpu.roll(x, 127, 1)),
                )
                for d, y in enumerate(kinds):
                    xs[d, at, PAD + 128 * n : PAD + 128 * n + 128] = y.astype(BF)
                    if n == ROWS - 1:
                        xs[d, at, :PAD] = jnp.where(low, zero, pltpu.roll(y, SIDE, 1)).astype(BF)
                    if n == 0:
                        xs[d, at, PAD + HW :] = jnp.where(
                            low, pltpu.roll(y, SIDE, 1), zero
                        ).astype(BF)
            return carry

        lax.fori_loop(0, rows // FILL, step, 0)
        start = xs.shape[1] - rows - start if len(pieces) == 2 else start + rows


def window(xs, tap, start, width):
    first = PAD + start + (tap // 3 - 1) * 128
    if not isinstance(start, int):
        first = pl.multiple_of(first, 128)
    return xs[tap % 3, :, pl.ds(first, width)]


def convolve(xs, w_ref, out_ref, add, width=1024):
    depth = xs.shape[1]

    def step(n, carry):
        p = n * width
        acc = dot(w_ref[:, :depth], window(xs, 0, p, width))
        for tap in range(1, 9):
            acc = acc + dot(w_ref[:, tap * depth : (tap + 1) * depth], window(xs, tap, p, width))
        at = pl.ds(pl.multiple_of(p, width), width)
        out_ref[:, at] = add(acc, at)
        return carry

    lax.fori_loop(0, HW // width, step, 0)


def conv_call(kernel, meta, weights, pieces, vmem_in, any_in, outs, any_outs, scratch, name):
    out_ch, depth = weights[0].shape[0], C
    arrays = (weights[0], *pieces, *vmem_in, *any_in)
    nbytes = sum(a.size * a.dtype.itemsize for a in arrays) + out_ch * HW * 4
    return pl.pallas_call(
        functools.partial(kernel, len(pieces)),
        out_shape=[*outs, *any_outs],
        in_specs=[scalars(), placed(), placed()]
        + [whole()] * (len(pieces) + len(vmem_in))
        + [placed()] * len(any_in),
        out_specs=[whole()] * len(outs) + [placed()] * len(any_outs),
        scratch_shapes=[
            pltpu.VMEM((3, depth, HW + 2 * PAD), BF),
            pltpu.VMEM((out_ch, 9 * depth), BF),
            pltpu.VMEM((out_ch, HW), F32),
            pltpu.SemaphoreType.DMA((4,)),
            *scratch,
        ],
        compiler_params=params(),
        cost_estimate=cost(2 * out_ch * 9 * depth * HW, nbytes, out_ch * HW),
        name=name,
    )(meta, *weights, *pieces, *vmem_in, *any_in)


def conv_one_kernel(n, meta, w_own, w_got, *refs):
    pieces, refs = refs[:n], refs[n:]
    par_ref, act_ref, stat_ref, conv_ref, w_ref, xs, w_buf, acc, sems = refs
    fetch(meta, w_own, w_got, w_buf, sems.at[0])
    fill_shifted(xs, pieces, meta[0])
    arrive(w_own, w_buf, sems.at[0])
    keep = pltpu.make_async_copy(w_buf, w_ref, sems.at[2])
    keep.start()
    bias = par_ref[:, 0:1]
    convolve(xs, w_buf, acc, lambda val, at: val + bias)
    store = pltpu.make_async_copy(acc, conv_ref, sems.at[1])
    store.start()

    def body(rows):
        vals = acc[rows, :]
        mean, rstd = group_stats(vals)
        par = par_ref[rows, :]
        gain, shift, factor = par[:, 1:2], par[:, 2:3], 1.0 + par[:, 3:4]
        mid = (vals - mean) * (rstd * gain * factor) + (shift * factor + par[:, 4:5])
        act_ref[rows, :] = (mid * jax.nn.sigmoid(mid)).astype(BF)
        stat_ref[rows, :] = columns([mean, rstd])

    for_groups(acc.shape[0], body)
    store.wait()
    keep.wait()


def conv_two_kernel(n, meta, w_own, w_got, *refs):
    pieces, refs = refs[:n], refs[n:]
    par_ref, f_ref, normed_ref, stat_ref, hidden_ref, w_ref, xs, w_buf, acc, sems = refs
    fetch(meta, w_own, w_got, w_buf, sems.at[0])
    fill_shifted(xs, pieces, meta[0])
    arrive(w_own, w_buf, sems.at[0])
    keep = pltpu.make_async_copy(w_buf, w_ref, sems.at[2])
    keep.start()
    bias = par_ref[:, 0:1]
    convolve(xs, w_buf, acc, lambda val, at: val + bias + f_ref[:, at].astype(F32))
    store = pltpu.make_async_copy(acc, hidden_ref, sems.at[1])
    store.start()

    def body(rows):
        vals = acc[rows, :]
        mean, rstd = group_stats(vals)
        par = par_ref[rows, :]
        normed_ref[rows, :] = ((vals - mean) * (rstd * par[:, 1:2]) + par[:, 2:3]).astype(BF)
        stat_ref[rows, :] = columns([mean, rstd])

    for_groups(acc.shape[0], body)
    store.wait()
    keep.wait()


def silu_slope(mid):
    sig = jax.nn.sigmoid(mid)
    return sig * (1.0 + mid * (1.0 - sig))


def conv_two_back_kernel(n, meta, w_own, w_got, *refs):
    pieces, refs = refs[:n], refs[n:]
    par_ref, stat_ref, conv_ref, grad_ref, sums_ref, xs, w_buf, acc, sems, conv_buf = refs
    fetch(meta, w_own, w_got, w_buf, sems.at[0])
    load = pltpu.make_async_copy(conv_ref, conv_buf, sems.at[1])
    load.start()
    fill_shifted(xs, pieces, meta[0])
    arrive(w_own, w_buf, sems.at[0])
    convolve(xs, w_buf, acc, lambda val, at: val)
    load.wait()

    def body(rows):
        par, stat = par_ref[rows, :], stat_ref[rows, :]
        gain, shift, factor = par[:, 1:2], par[:, 2:3], 1.0 + par[:, 3:4]
        rstd = stat[:, 1:2]
        hat = (conv_buf[rows, :] - stat[:, 0:1]) * rstd
        mid = hat * (gain * factor) + (shift * factor + par[:, 4:5])
        grad = acc[rows, :] * silu_slope(mid)
        total = jnp.sum(grad, axis=1, keepdims=True)
        total_hat = jnp.sum(grad * hat, axis=1, keepdims=True)
        mean_u, mean_uhat = norm_backward(total * factor, total_hat * factor, gain)
        out = ((grad * (factor * gain) - mean_u - hat * mean_uhat) * rstd).astype(BF)
        grad_ref[rows, :] = out
        bias_grad = jnp.sum(out.astype(F32), axis=1, keepdims=True)
        sums_ref[rows, :] = columns(
            [
                total_hat * factor,
                total * factor,
                total_hat * gain + total * shift,
                total,
                bias_grad,
            ]
        )

    for_groups(acc.shape[0], body)


def conv_one_back_kernel(n, meta, w_own, w_got, *refs):
    pieces, refs = refs[:n], refs[n:]
    par_ref, stat_ref, f_ref, hid_ref, grad_ref, sums_ref, xs, w_buf, acc, sems, hid_buf = refs
    fetch(meta, w_own, w_got, w_buf, sems.at[0])
    load = pltpu.make_async_copy(hid_ref, hid_buf, sems.at[1])
    load.start()
    fill_shifted(xs, pieces, meta[0])
    arrive(w_own, w_buf, sems.at[0])
    convolve(xs, w_buf, acc, lambda val, at: val)
    load.wait()

    def body(rows):
        par, stat = par_ref[rows, :], stat_ref[rows, :]
        gain, shift = par[:, 0:1], par[:, 1:2]
        rstd = stat[:, 1:2]
        hat = (f_ref[rows, :].astype(F32) - stat[:, 0:1]) * rstd
        grad = acc[rows, :] * silu_slope(hat * gain + shift)
        total = jnp.sum(grad, axis=1, keepdims=True)
        total_hat = jnp.sum(grad * hat, axis=1, keepdims=True)
        mean_u, mean_uhat = norm_backward(total, total_hat, gain)
        out = hid_buf[rows, :] + (grad * gain - mean_u - hat * mean_uhat) * rstd
        top, bottom = unfold(out)
        grad_ref[rows, : HW // 2] = top.astype(grad_ref.dtype)
        grad_ref[rows, HW // 2 :] = bottom.astype(grad_ref.dtype)
        sums_ref[rows, :] = columns([total_hat, total])

    for_groups(acc.shape[0], body)


def weight_grad_kernel(n, meta, grad_ref, *refs):
    pieces, (out_ref, gs) = refs[:n], refs[n:]
    fill_shifted(gs, (grad_ref,), 0)
    for tap in range(9):
        moved = window(gs, 8 - tap, 0, HW)
        first = meta[0]
        for x_ref in pieces:
            rows = x_ref.shape[0]
            at = pl.ds(pl.multiple_of(tap * C + first, rows), rows)
            out_ref[:, at] = dot_nt(moved, x_ref[...]).astype(BF)
            first = C - rows - first


def conv_weight_grad(meta, grad, pieces, name):
    out_ch = grad.shape[0]
    return pl.pallas_call(
        functools.partial(weight_grad_kernel, len(pieces)),
        out_shape=struct((out_ch, 9 * C), BF),
        in_specs=[scalars()] + [whole()] * (1 + len(pieces)),
        out_specs=whole(),
        scratch_shapes=[pltpu.VMEM((3, out_ch, HW + 2 * PAD), BF)],
        compiler_params=params(),
        cost_estimate=cost(2 * out_ch * 9 * C * HW, (out_ch + C) * HW * 2 + out_ch * 9 * C * 2),
        name=name,
    )(meta, grad, *pieces)


def turn_kernel(meta, own_ref, other_ref, out_ref):
    half = own_ref.shape[0]
    for tap in range(9):
        at = pl.ds(pl.multiple_of(tap * C + meta[0], half), half)
        row = meta[0]
        for ref in (own_ref, other_ref):
            to = pl.ds(pl.multiple_of((8 - tap) * C + row, half), half)
            out_ref[:, to] = ref[:, at].astype(F32).T.astype(BF)
            row = half - row


def turned_pair(meta, own, other):
    return pl.pallas_call(
        turn_kernel,
        out_shape=struct(own.shape, BF),
        in_specs=[scalars(), whole(), whole()],
        out_specs=whole(),
        compiler_params=params(),
        cost_estimate=cost(0, 3 * own.size * 2),
        name="turn",
    )(meta, own, other)


def norm_three_back_kernel(n, *refs):
    addends, (hidden_ref, stat_ref, par_ref, cot_ref, hid_ref, grad_ref, sums_ref) = (
        refs[:n],
        refs[n:],
    )

    def body(rows):
        dy = addends[0][rows, :].astype(F32)
        for extra in addends[1:]:
            dy = dy + extra[rows, :].astype(F32)
        par, stat = par_ref[rows, :], stat_ref[rows, :]
        gain, rstd = par[:, 1:2], stat[:, 1:2]
        hat = (hidden_ref[rows, :] - stat[:, 0:1]) * rstd
        total = jnp.sum(dy, axis=1, keepdims=True)
        total_hat = jnp.sum(dy * hat, axis=1, keepdims=True)
        mean_u, mean_uhat = norm_backward(total, total_hat, gain)
        top = cot_ref[rows, :].astype(F32)
        out = top + (dy * gain - mean_u - hat * mean_uhat) * rstd
        hid_ref[rows, :] = out
        low = out.astype(BF)
        grad_ref[rows, :] = low
        sums_ref[rows, :] = columns(
            [
                total_hat,
                total,
                jnp.sum(low.astype(F32), axis=1, keepdims=True),
                jnp.sum(top, axis=1, keepdims=True),
            ]
        )

    for_groups(hidden_ref.shape[0], body)


def norm_three_back(addends, hidden, stat, par, cot):
    ch = hidden.shape[0]
    rows = 32

    def part(a):
        return pl.BlockSpec((rows, a.shape[1]), lambda r: (r, 0))

    outs = [struct((ch, HW), F32), struct((ch, HW), BF), struct((ch, 128), F32)]
    ins = (*addends, hidden, stat, par, cot)
    return pl.pallas_call(
        functools.partial(norm_three_back_kernel, len(addends)),
        grid=(ch // rows,),
        out_shape=outs,
        in_specs=[part(a) for a in ins],
        out_specs=[part(a) for a in outs],
        compiler_params=params(),
        cost_estimate=cost(20 * ch * HW, 16 * ch * HW),
        name="norm_three_back",
    )(*ins)


def piece_columns(meta, w_ref, pieces):
    first = meta[0]
    acc = None
    for x_ref in pieces:
        rows = x_ref.shape[0]
        term = dot(w_ref[:, pl.ds(pl.multiple_of(first, rows), rows)], x_ref[...])
        acc = term if acc is None else acc + term
        first = w_ref.shape[1] - rows - first
    return acc


def inputs_kernel(n, meta, w_ref, *refs):
    pieces, (bias_ref, out_ref) = refs[:n], refs[n:]
    out_ref[...] = (piece_columns(meta, w_ref, pieces) + bias_ref[...]).astype(BF)


def inputs_product(meta, weight, pieces, bias, width=1024, name=None):
    rows, depth = weight.shape
    return pl.pallas_call(
        functools.partial(inputs_kernel, len(pieces)),
        grid=(HW // width,),
        out_shape=struct((rows, HW), BF),
        in_specs=[scalars(), pl.BlockSpec((rows, depth), lambda p: (0, 0))]
        + [pl.BlockSpec((x.shape[0], width), lambda p: (0, p)) for x in pieces]
        + [pl.BlockSpec((rows, 1), lambda p: (0, 0))],
        out_specs=pl.BlockSpec((rows, width), lambda p: (0, p)),
        compiler_params=params(),
        cost_estimate=cost(2 * rows * depth * HW, (rows + depth) * HW * 2),
        name=name,
    )(meta, weight, *pieces, bias)


def parts_kernel(n, meta, w_ref, *refs):
    pieces, outs = refs[:n], refs[n:]
    first = meta[0]
    for out_ref in outs:
        rows = out_ref.shape[0]
        row = pl.ds(pl.multiple_of(first, rows), rows)
        acc = None
        at = 0
        for x_ref in pieces:
            depth = x_ref.shape[0]
            term = dot(w_ref[row, at : at + depth], x_ref[...])
            acc = term if acc is None else acc + term
            at += depth
        out_ref[...] = acc.astype(BF)
        first = w_ref.shape[0] - rows - first


def parts_product(meta, weight, pieces, count, width=1024, name=None):
    rows, depth = weight.shape
    part = struct((rows // count, HW), BF)
    return pl.pallas_call(
        functools.partial(parts_kernel, len(pieces)),
        grid=(HW // width,),
        out_shape=[part] * count,
        in_specs=[scalars(), pl.BlockSpec((rows, depth), lambda p: (0, 0))]
        + [pl.BlockSpec((x.shape[0], width), lambda p: (0, p)) for x in pieces],
        out_specs=[pl.BlockSpec((rows // count, width), lambda p: (0, p))] * count,
        compiler_params=params(),
        cost_estimate=cost(2 * rows * depth * HW, (rows + depth) * HW * 2),
        name=name,
    )(meta, weight, *pieces)


def output_kernel(n, meta, w_ref, *refs):
    pieces, (bias_ref, hidden_ref, out_ref) = refs[:n], refs[n:]
    acc = hidden_ref[...] + bias_ref[...] + piece_columns(meta, w_ref, pieces)
    half = acc.shape[1] // 2
    for base, val in zip((0, HW // 2), unfold(acc)):
        first = pl.multiple_of(base + pl.program_id(0) * half, half)
        out_ref[:, pl.ds(first, half)] = val.astype(BF)


def output_product(meta, weight, pieces, bias, hidden, width=1024):
    rows, depth = weight.shape
    return pl.pallas_call(
        functools.partial(output_kernel, len(pieces)),
        grid=(HW // width,),
        out_shape=struct((rows, HW), BF),
        in_specs=[scalars(), pl.BlockSpec((rows, depth), lambda p: (0, 0))]
        + [pl.BlockSpec((x.shape[0], width), lambda p: (0, p)) for x in pieces]
        + [
            pl.BlockSpec((rows, 1), lambda p: (0, 0)),
            pl.BlockSpec((rows, width), lambda p: (0, p)),
        ],
        out_specs=pl.BlockSpec((rows, HW), lambda p: (0, 0)),
        compiler_params=params(),
        cost_estimate=cost(2 * rows * depth * HW, (rows * 3 + depth) * HW * 2),
        name="output",
    )(meta, weight, *pieces, bias, hidden)


def outer_kernel(n_left, n_right, meta, *refs):
    lefts, rights = refs[:n_left], refs[n_left : n_left + n_right]
    out_ref, sums_ref = refs[n_left + n_right : n_left + n_right + 2]
    acc_ref, tot_ref = refs[n_left + n_right + 2 :]
    step = pl.program_id(0)

    @pl.when(step == 0)
    def _():
        acc_ref[...] = jnp.zeros_like(acc_ref)
        tot_ref[...] = jnp.zeros_like(tot_ref)

    row = 0
    for left in lefts:
        rows = left.shape[0]
        val = left[...]
        first = meta[0]
        for right in rights:
            cols = right.shape[0]
            at = pl.ds(pl.multiple_of(first, cols), cols)
            acc_ref[row : row + rows, at] += dot_nt(val, right[...])
            first = acc_ref.shape[1] - cols - first
        tot_ref[row : row + rows, :] += jnp.sum(val.astype(F32), axis=1, keepdims=True)
        row += rows

    @pl.when(step == pl.num_programs(0) - 1)
    def _():
        out_ref[...] = acc_ref[...].astype(BF)
        sums_ref[...] = tot_ref[...]


def outer(meta, lefts, rights, width=1024, name=None):
    rows, cols = sum(a.shape[0] for a in lefts), sum(a.shape[0] for a in rights)
    fixed = lambda p: (0, 0)
    return pl.pallas_call(
        functools.partial(outer_kernel, len(lefts), len(rights)),
        grid=(HW // width,),
        out_shape=[struct((rows, cols), BF), struct((rows, 128), F32)],
        in_specs=[scalars()]
        + [pl.BlockSpec((a.shape[0], width), lambda p: (0, p)) for a in (*lefts, *rights)],
        out_specs=[pl.BlockSpec((rows, cols), fixed), pl.BlockSpec((rows, 128), fixed)],
        scratch_shapes=[pltpu.VMEM((rows, cols), F32), pltpu.VMEM((rows, 128), F32)],
        compiler_params=params(),
        cost_estimate=cost(2 * rows * cols * HW, (rows + cols) * HW * 2),
        name=name,
    )(meta, *lefts, *rights)


def attention_kernel(
    n_grads, lim_ref, q_ref, k_ref, v_ref, kc_ref, vc_ref, *refs, unroll, back,
):
    g_refs, refs = refs[:n_grads], refs[n_grads:]
    o_ref, dq_ref, dk_ref, dv_ref, dkc_ref, dvc_ref = refs[:6]
    kt, vt, kn, vn, s_even, s_odd, p_sc, tops, o_acc, dk_acc, dv_acc = refs[6:]
    step, last = pl.program_id(1), pl.num_programs(1) - 1
    width = q_ref.shape[-1]
    blocks = KEYS // BLOCK

    @pl.when(step == 0)
    def _():
        spare = jnp.zeros((HEAD_DIM, KEYS - HW - CTXP), BF)
        for ref, own, ctx in ((kn, k_ref, kc_ref), (vn, v_ref, vc_ref)):
            ref[:, :HW] = own[0, 0]
            ref[:, HW : HW + CTXP] = ctx[0, 0]
            ref[:, HW + CTXP :] = spare
        row = lax.broadcasted_iota(jnp.int32, (HEAD_DIM, BLOCK), 0)
        for n in range(blocks):
            at = slice(n * BLOCK, (n + 1) * BLOCK)
            key = lax.broadcasted_iota(jnp.int32, (HEAD_DIM, BLOCK), 1) + n * BLOCK
            fill = jnp.where((row == 0) & (key >= HW + lim_ref[0]), NEG_FILL, 0.0)
            kt[at, :] = jnp.concatenate([kn[:, at].astype(F32), fill], 0).T.astype(BF)
            vt[at, :] = jnp.concatenate([vn[:, at].astype(F32), jnp.zeros_like(fill)], 0).T.astype(BF)
        dk_acc[...] = jnp.zeros_like(dk_acc)
        dv_acc[...] = jnp.zeros_like(dv_acc)

    def keys_at(n):
        return pl.ds(pl.multiple_of(n * BLOCK, BLOCK), BLOCK)

    scale = HEAD_DIM ** (-0.5)
    q = (q_ref[0, 0].astype(F32) * scale).astype(BF)
    one = jnp.where(lax.broadcasted_iota(jnp.int32, (HEAD_DIM, width), 0) == 0, 1.0, 0.0).astype(BF)
    q_more = jnp.concatenate([q, one], 0)

    def score(n, held):
        scores = dot(kt[keys_at(n), :], q_more)
        held[...] = scores
        return jnp.max(jnp.max(scores.reshape(BLOCK // 8, 8, width), axis=0), axis=0, keepdims=True)

    o_acc[...] = jnp.zeros_like(o_acc)

    def forward(n, held, top, total, shrink):
        raised = jnp.exp(held[...] - top)
        low = raised.astype(BF)
        p_sc[keys_at(n), :] = low
        tops[n, 0:1, :] = top
        sums = jnp.sum(raised.reshape(BLOCK // 8, 8, width), axis=0)
        o_acc[...] = o_acc[...] * shrink + dot(vn[:, keys_at(n)], low)
        return total * shrink + sums

    def forward_step(n, held, ahead_held, carry):
        top, total, shrink = carry
        ahead = jnp.maximum(top, score(n + 1, ahead_held))
        total = forward(n, held, top, total, shrink)
        return ahead, total, jnp.exp(top - ahead)

    held = (s_even, s_odd)

    def forward_run(j, carry):
        for u in range(unroll):
            carry = forward_step(unroll * j + u, held[u % 2], held[1 - u % 2], carry)
        return carry

    carry = (score(0, s_even), jnp.zeros((8, width), F32), jnp.ones((1, width), F32))
    carry = lax.fori_loop(0, blocks // unroll - 1, forward_run, carry)
    for n in range(blocks - unroll, blocks - 1):
        carry = forward_step(n, held[n % 2], held[1 - n % 2], carry)
    top, total, shrink = carry
    total = forward(blocks - 1, s_odd, top, total, shrink)

    inverse = 1.0 / jnp.sum(total, axis=0, keepdims=True)
    mixed = o_acc[...] * inverse
    o_ref[0] = mixed.astype(BF)
    grad = sum(g_ref[0].astype(F32) for g_ref in g_refs)
    if n_grads > 1:
        grad = grad.astype(BF).astype(F32)
    delta = jnp.sum(grad * mixed, axis=0, keepdims=True)
    dq = jnp.zeros((HEAD_DIM, width), F32)
    none = jnp.zeros((HEAD_DIM, width), BF)
    for c in range(0, KEYS, back):
        at = slice(c, c + back)
        slopes = []
        for n in range(c // BLOCK, (c + back) // BLOCK):
            sub = slice(n * BLOCK, (n + 1) * BLOCK)
            factor = inverse * jnp.exp(tops[n, 0:1, :] - top)
            grad_low = (grad * factor).astype(BF)
            both = jnp.concatenate([grad_low, none], 0)
            probs = p_sc[sub, :]
            slope = (dot(vt[sub, :], both) - delta * factor).astype(BF) * probs
            slopes.append(slope)
            dv_acc[:, sub] += dot_nt(grad_low, probs)
        slope = jnp.concatenate(slopes, 0)
        dq = dq + dot(kn[:, at], slope)
        dk_acc[:, at] += dot_nt(q, slope)
    dq_ref[0] = (dq * scale).astype(BF)

    @pl.when(step == last)
    def _():
        dk_ref[0] = dk_acc[:, :HW].astype(BF)
        dv_ref[0] = dv_acc[:, :HW].astype(BF)
        dkc_ref[0] = dk_acc[:, HW : HW + CTXP].astype(BF)
        dvc_ref[0] = dv_acc[:, HW : HW + CTXP].astype(BF)


def attention(limit, qkv, ctx_kv, grads, width=1024, unroll=6, back=256):
    heads = qkv.shape[1]
    keys = KEYS

    def part(t, w, moving):
        return pl.BlockSpec(
            (1, 1, HEAD_DIM, w), (lambda h, i: (t, h, 0, i)) if moving else (lambda h, i: (t, h, 0, 0))
        )

    def row(w, moving):
        return pl.BlockSpec(
            (1, HEAD_DIM, w), (lambda h, i: (h, 0, i)) if moving else (lambda h, i: (h, 0, 0))
        )

    big, small = struct((heads, HEAD_DIM, HW), BF), struct((heads, HEAD_DIM, CTXP), BF)
    return pl.pallas_call(
        functools.partial(attention_kernel, len(grads), unroll=unroll, back=back),
        grid=(heads, HW // width),
        in_specs=[
            pl.BlockSpec(memory_space=pltpu.SMEM),
            part(0, width, True),
            part(1, HW, False),
            part(2, HW, False),
            part(0, CTXP, False),
            part(1, CTXP, False),
        ]
        + [row(width, True)] * len(grads),
        out_specs=[
            row(width, True),
            row(width, True),
            row(HW, False),
            row(HW, False),
            row(CTXP, False),
            row(CTXP, False),
        ],
        out_shape=[big, big, big, big, small, small],
        scratch_shapes=[
            pltpu.VMEM((keys, 2 * HEAD_DIM), BF),
            pltpu.VMEM((keys, 2 * HEAD_DIM), BF),
            pltpu.VMEM((HEAD_DIM, keys), BF),
            pltpu.VMEM((HEAD_DIM, keys), BF),
            pltpu.VMEM((BLOCK, width), F32),
            pltpu.VMEM((BLOCK, width), F32),
            pltpu.VMEM((keys, width), BF),
            pltpu.VMEM((keys // BLOCK, 8, width), F32),
            pltpu.VMEM((HEAD_DIM, width), F32),
            pltpu.VMEM((HEAD_DIM, keys), F32),
            pltpu.VMEM((HEAD_DIM, keys), F32),
        ],
        compiler_params=params(dimension_semantics=("arbitrary", "arbitrary")),
        cost_estimate=cost(
            24 * heads * HW * keys * HEAD_DIM, heads * HEAD_DIM * 8 * HW * 2, heads * HW * keys
        ),
        name="attention",
    )(limit, qkv, qkv, qkv, ctx_kv, ctx_kv, *grads)


class Alone:
    parts = 1

    def __init__(self, mesh):
        self.images = mesh.shape["dp"]

    def meta(self):
        return jnp.array([0, 1], jnp.int32)

    def image(self):
        return lax.axis_index("dp")

    def got(self, x):
        return x

    def pick(self, own, got):
        return own

    def gather(self, x):
        return (lax.all_gather(x, "tensor", axis=0, tiled=True),)

    def scatter(self, parts):
        return (lax.psum_scatter(parts[0], "tensor", scatter_dimension=0, tiled=True),)

    def turn(self, meta, w):
        ch = w.shape[0]
        cut = w.reshape(ch, 9, C)
        turned = lax.all_to_all(cut, "tensor", split_axis=2, concat_axis=0, tiled=True)
        return turned[:, ::-1].transpose(2, 1, 0).reshape(ch, 9 * C)

    def total(self, x, beside):
        return lax.psum(x, "dp")

    def everywhere(self, x):
        return lax.psum(x, "dp")

    def sum_owned(self, x, beside):
        return lax.psum(x, "dp"), beside(x)


class Paired:
    parts = 2

    def __init__(self, mesh):
        dp = mesh.shape["dp"]
        self.images = dp
        self.far = [
            ((2 * k + core) * 2 + 1 - core, (2 * k + 1 - core) * 2 + core)
            for k in range(dp // 2)
            for core in range(2)
        ]
        self.bits = [1 << b for b in range((dp - 1).bit_length())]

    def half(self):
        return lax.axis_index("dp") % 2

    def stays(self):
        return self.half() == lax.axis_index("tensor")

    def meta(self):
        return jnp.stack([self.half() * (C // 2), self.stays().astype(jnp.int32)]).astype(jnp.int32)

    def image(self):
        return lax.axis_index("dp") // 2 * 2 + lax.axis_index("tensor")

    def got(self, x):
        return lax.ppermute(x, ("dp", "tensor"), self.far)

    def pick(self, own, got):
        return jnp.where(self.stays(), own, got)

    def over(self, x, bit):
        return lax.ppermute(x, "dp", [(i, i ^ bit) for i in range(self.images)])

    def gather(self, x):
        return (x, self.over(x, 1))

    def scatter(self, parts):
        return (parts[0], self.over(parts[1], 1))

    def turn(self, meta, w):
        return turned_pair(meta, w, self.over(w, 1))

    def total(self, x, beside):
        x = after(beside, x + lax.ppermute(x, "tensor", [(0, 1), (1, 0)]))
        for bit in self.bits[1:]:
            x = x + self.over(x, bit)
        return self.pick(x, self.over(x, 1))

    def everywhere(self, x):
        for bit in self.bits:
            x = x + self.over(x, bit)
        return x

    def sum_owned(self, x, beside):
        rows = x.shape[0] // 2
        order = (self.bits, [self.bits[0], *self.bits[2:], self.bits[1]])
        parts = [lax.slice_in_dim(x, at * rows, (at + 1) * rows) for at in range(2)]

        def upper(bit):
            return (lax.axis_index("dp") // bit) % 2

        for step in range(len(self.bits)):
            size = parts[0].shape[0] // 2
            for at in range(2):
                bit = order[at][step]
                keep = lax.dynamic_slice_in_dim(parts[at], upper(bit) * size, size)
                send = lax.dynamic_slice_in_dim(parts[at], (1 - upper(bit)) * size, size)
                parts[at] = (keep.astype(F32) + self.over(send, bit).astype(F32)).astype(BF)
        held = beside(parts[0])
        for step in reversed(range(len(self.bits))):
            if step == 0:
                parts = list(after(held, *parts))
            for at in range(2):
                bit = order[at][step]
                other = self.over(parts[at], bit)
                parts[at] = jnp.where(
                    upper(bit) == 0,
                    jnp.concatenate([parts[at], other]),
                    jnp.concatenate([other, parts[at]]),
                )
        return jnp.concatenate(parts), held


def after(first, *later):
    held = lax.optimization_barrier((first, *later))
    return held[1:] if len(later) > 1 else held[1]


def local(plan, features, cotangent, embedding, context, lengths, norm1_gain, norm1_bias,
    conv1_weight, conv1_bias, emb_weight, emb_bias, norm2_gain, norm2_bias, conv2_weight,
    conv2_bias, norm3_gain, norm3_bias, qkv_weight, qkv_bias, context_weight, context_bias,
    out_weight, out_bias,
):
    ch, images, pixels = features.shape
    heads = ch // HEAD_DIM
    meta = plan.meta()
    moved = plan.parts == 2

    emb_act = jax.nn.silu(embedding.astype(F32)).astype(BF)
    scale_shift = (
        jnp.einsum("ie,teo->to", emb_act, emb_weight, preferred_element_type=F32) + emb_bias
    )
    length_row = jnp.broadcast_to(lengths.astype(F32)[:, None], (1, ch))
    vectors = jnp.concatenate(
        [
            jnp.stack([norm1_gain, norm1_bias, conv1_bias, norm2_gain, norm2_bias]),
            scale_shift,
            jnp.stack([conv2_bias, norm3_gain, norm3_bias, out_bias]),
            qkv_bias,
            length_row,
        ]
    )
    f_own = features.reshape(ch, pixels)
    f_got = plan.got(f_own)
    vectors, w1_own = after(scale_shift, vectors, conv1_weight)
    vectors = plan.pick(vectors, plan.got(vectors))
    w1_got = plan.got(w1_own)
    ctx_kv = (
        jnp.einsum("toe,ne->ton", context_weight, context[0], preferred_element_type=F32)
        + context_bias[:, :, None]
    ).astype(BF)
    ctx_kv = jnp.pad(ctx_kv, ((0, 0), (0, 0), (0, CTXP - CTX)))
    emb_all = jnp.where(
        jnp.arange(plan.images)[:, None] == lax.axis_index("dp"), emb_act, jnp.zeros_like(emb_act)
    )
    emb_all = plan.everywhere(emb_all)
    length = vectors[14, :1].astype(jnp.int32)
    par_one, par_two, par_three = vectors[0:2].T, vectors[2:7].T, vectors[7:10].T
    bias_qkv, bias_out = vectors[11:14].reshape(3 * ch, 1), vectors[10].reshape(ch, 1)
    par_one = after(emb_all, par_one)
    w2_got = plan.got(after(vectors, conv2_weight))
    act_one, stat_one, f_low = first_activation(meta, f_own, f_got, par_one)
    full_one = plan.gather(act_one)
    mats_own = jnp.concatenate([qkv_weight.reshape(3 * ch, C), out_weight])
    mats_own, ctx_own, cot_own = after(
        act_one, mats_own, ctx_kv, cotangent.reshape(ch, pixels)
    )
    mats_got, ctx_got = plan.got(mats_own), plan.got(ctx_own)
    cot_got = plan.got(cot_own)

    par_two, par_three, bias_qkv, bias_out = after(act_one, par_two, par_three, bias_qkv, bias_out)
    par_two = after((par_three, bias_qkv, bias_out), par_two)
    low, stat, wide = struct((ch, HW), BF), struct((ch, 128), F32), struct((ch, HW), F32)
    weight = struct((ch, 9 * C), BF)
    act_two, stat_two, conv_one, w1 = conv_call(
        conv_one_kernel, meta, (conv1_weight, w1_got), full_one, (par_two,), (),
        [low, stat], [wide, weight], [], "conv_one",
    )
    full_two = plan.gather(act_two)
    normed, stat_three, hidden, w2 = conv_call(
        conv_two_kernel, meta, (conv2_weight, w2_got), full_two, (par_three, f_low), (),
        [low, stat], [wide, weight], [], "conv_two",
    )
    full_three = plan.gather(normed)
    mats_got, ctx_got, cot_got = after(normed, mats_got, ctx_got, cot_got)
    mats = plan.pick(mats_own, mats_got)
    w_qkv, w_out = mats[: 3 * ch], mats[3 * ch :]
    cot = folded(meta, cot_own, cot_got)
    grad_heads = plan.scatter(
        parts_product(meta, w_out.T, (cot,), plan.parts, name="grad_heads")
    )
    qkv = inputs_product(meta, w_qkv, full_three, bias_qkv, name="qkv")
    ctx_kv = plan.pick(ctx_own, ctx_got)
    mixed, dq, dk, dv, dkc, dvc = attention(
        4 + length,
        qkv.reshape(3, heads, HEAD_DIM, HW),
        ctx_kv.reshape(2, heads, HEAD_DIM, CTXP),
        [a.reshape(heads, HEAD_DIM, HW) for a in grad_heads],
    )

    flat = lambda a: a.reshape(ch, HW)
    dq, dk, dv = flat(dq), flat(dk), flat(dv)
    addends = plan.scatter(
        parts_product(meta, w_qkv.T, (dq, dk, dv), plan.parts, name="grad_normed")
    )
    full_heads = plan.gather(flat(mixed))
    ctx_own = jnp.concatenate([a.reshape(1, ch, CTXP) for a in (dkc, dvc)])
    ctx_got = plan.got(ctx_own)
    turned_two = plan.turn(meta, after(mixed, w2))
    turned_one = plan.turn(meta, after(mixed, w1))
    dw_qkv, db_qkv = outer(meta, (dq, dk, dv), full_three, name="qkv_grad")
    dw_out, _ = outer(meta, (cot,), full_heads, name="out_grad")
    mats_own = jnp.concatenate([dw_qkv, dw_out])
    mats_got = plan.got(mats_own)
    grad_hidden, grad_two, sums_three = norm_three_back(addends, hidden, stat_three, par_three, cot)
    full_grad_two = plan.gather(grad_two)
    dw_two = conv_weight_grad(meta, grad_two, full_two, "conv_two_weight_grad")
    two_got = plan.got(dw_two)
    full_grad_two = after((dw_two, turned_one), *full_grad_two) if moved else full_grad_two
    grad_one, sums_two = conv_call(
        conv_two_back_kernel, meta, (turned_two, turned_two), full_grad_two, (par_two, stat_two),
        (conv_one,), [low, stat], [], [pltpu.VMEM((ch, HW), F32)], "conv_two_back",
    )
    full_grad_one = plan.gather(grad_one)
    mats_got, ctx_got, two_got = after(grad_one, mats_got, ctx_got, two_got)
    ctx_grad = plan.pick(ctx_own, ctx_got)[:, :, :CTX]
    dw_ctx = jnp.einsum("ton,ne->toe", ctx_grad, context[0], preferred_element_type=F32).astype(BF)
    mats = plan.pick(mats_own, mats_got)
    dw_two = plan.pick(dw_two, two_got)
    early = jnp.concatenate(
        [dw_ctx[0], dw_ctx[1], *(mats[t * ch : (t + 1) * ch] for t in range(4)), dw_two], 1
    )
    held = after(early, grad_one)
    early = lax.psum_scatter(early, "dp", scatter_dimension=0, tiled=True)
    dw_one = conv_weight_grad(meta, held, full_one, "conv_one_weight_grad")
    one_got = plan.got(dw_one)
    full_grad_one = after(dw_one, *full_grad_one) if moved else full_grad_one
    input_grad, sums_one = conv_call(
        conv_one_back_kernel, meta, (turned_one, turned_one), full_grad_one,
        (par_one, stat_one, f_low), (grad_hidden,),
        [struct((ch, HW), BF if moved else F32), stat], [],
        [pltpu.VMEM((ch, HW), F32)], "conv_one_back",
    )
    input_got = plan.got(input_grad)

    one_got = after(input_grad, one_got)
    output = output_product(
        meta, w_out, full_heads, bias_out, after(input_grad, hidden)
    )
    output_got = plan.got(output)
    ctx_sums = jnp.sum(ctx_own.astype(F32), axis=2)
    sums_two = sums_two[:, :5].T
    own_mod = sums_two[2:4].astype(BF).astype(F32)
    mods = jnp.where(
        (jnp.arange(plan.images) == plan.image())[:, None, None], own_mod, jnp.zeros_like(own_mod)
    ).reshape(2 * plan.images, ch)
    small = plan.total(
        jnp.concatenate(
            [
                sums_three[:, :4].T,
                db_qkv[:, 0].reshape(3, ch),
                sums_two[:2],
                sums_two[4:5],
                ctx_sums,
                sums_one[:, :2].T,
                mods,
            ]
        ),
        output,
    )
    early, dw_one, one_got = after((small, input_got), early, dw_one, one_got)

    def finish(token):
        out_got, in_got, sums = after(token, output_got, input_got, small)
        per_image = sums[14:].reshape(plan.images, 2, ch).astype(BF)
        return (
            plan.pick(
                input_grad.reshape(ch, images, pixels), in_got.reshape(ch, images, pixels)
            ).astype(F32),
            plan.pick(output, out_got),
            jnp.stack(
                [
                    jnp.einsum("ie,io->eo", emb_all, per_image[:, t], preferred_element_type=F32)
                    for t in range(2)
                ]
            ),
        )

    dw_one, done = plan.sum_owned(plan.pick(dw_one, one_got), finish)
    early = lax.all_gather(early, "dp", axis=0, tiled=True)
    mods = small[14:].reshape(plan.images, 2, ch)
    input_grad, output, dw_emb = done
    early = after((dw_one, small, input_grad, output), early)
    dw_ctx = jnp.stack([early[:, n * CTX_EMB : (n + 1) * CTX_EMB] for n in range(2)])
    first = 2 * CTX_EMB
    mats = [early[:, first + n * C : first + (n + 1) * C].astype(F32) for n in range(4)]
    dw_two = early[:, first + 4 * C :]

    return (
        output.reshape(ch, images, pixels),
        input_grad,
        small[12],
        small[13],
        dw_one.astype(F32),
        small[9],
        dw_emb,
        jnp.sum(mods, axis=0),
        small[7],
        small[8],
        dw_two.astype(F32),
        small[2],
        small[0],
        small[1],
        jnp.stack(mats[:3]),
        small[4:7],
        dw_ctx.astype(F32),
        small[10:12],
        mats[3],
        small[3],
    )


def solution(mesh):
    paired = mesh.shape["tensor"] == 2 and mesh.shape["dp"] % 2 == 0
    plan = Paired(mesh) if paired else Alone(mesh)
    specs = (
        P("tensor", "dp", None),
        P("tensor", "dp", None),
        P("dp", None),
        P("dp", None, None),
        P("dp"),
        P("tensor"),
        P("tensor"),
        P("tensor", None),
        P("tensor"),
        P(None, None, "tensor"),
        P(None, "tensor"),
        P("tensor"),
        P("tensor"),
        P("tensor", None),
        P("tensor"),
        P("tensor"),
        P("tensor"),
        P(None, "tensor", None),
        P(None, "tensor"),
        P(None, "tensor", None),
        P(None, "tensor"),
        P("tensor", None),
        P("tensor"),
    )
    return jax.shard_map(
        functools.partial(local, plan),
        mesh=mesh,
        in_specs=specs,
        out_specs=(
            P("tensor", "dp", None),
            P("tensor", "dp", None),
            P("tensor"),
            P("tensor"),
            P("tensor", None),
            P("tensor"),
            P(None, None, "tensor"),
            P(None, "tensor"),
            P("tensor"),
            P("tensor"),
            P("tensor", None),
            P("tensor"),
            P("tensor"),
            P("tensor"),
            P(None, "tensor", None),
            P(None, "tensor"),
            P(None, "tensor", None),
            P(None, "tensor"),
            P("tensor", None),
            P("tensor"),
        ),
        check_vma=False,
    )
```

```python
import functools

import jax
import jax.numpy as jnp
from jax import lax
from jax.experimental import pallas as pl
from jax.experimental.pallas import tpu as pltpu
from jax.sharding import PartitionSpec as P

C = 512
HEAD_DIM = 64
PER_GROUP = 16
SIDE = 64
HW = 4096
CTX = 260
CTXP = 384
CTX_EMB = 2048
BLOCK = 256
KEYS = 4608
PAD = 128
FILL = 32
SCALE = 100
EPSILON = 1e-05
NEG_FILL = -1e30
F32 = jnp.float32
BF = jnp.bfloat16
NT = (((1,), (1,)), ((), ()))
VMEM_BYTES = 62 << 20


def dot(a, b):
    return jnp.dot(a, b, preferred_element_type=F32)


def dot_nt(a, b):
    return lax.dot_general(a, b, NT, preferred_element_type=F32)


def whole():
    return pl.BlockSpec(memory_space=pltpu.VMEM)


def placed():
    return pl.BlockSpec(memory_space=pl.ANY)


def scalars():
    return pl.BlockSpec(memory_space=pltpu.SMEM)


def params(**kwargs):
    return pltpu.CompilerParams(vmem_limit_bytes=VMEM_BYTES, **kwargs)


def cost(flops, nbytes, transcendentals=0):
    return pl.CostEstimate(
        flops=flops // SCALE, bytes_accessed=nbytes // SCALE, transcendentals=transcendentals // SCALE
    )


def struct(shape, dtype):
    return jax.ShapeDtypeStruct(shape, dtype)


def fetch(meta, own_ref, got_ref, buf, sem):
    @pl.when(meta[1] == 1)
    def _():
        pltpu.make_async_copy(own_ref, buf, sem).start()

    @pl.when(meta[1] != 1)
    def _():
        pltpu.make_async_copy(got_ref, buf, sem).start()


def arrive(own_ref, buf, sem):
    pltpu.make_async_copy(own_ref, buf, sem).wait()


def group_scalar(column):
    return jnp.sum(column, axis=0, keepdims=True) * (1.0 / (PER_GROUP * HW))


def group_stats(vals):
    mean = group_scalar(jnp.sum(vals, axis=1, keepdims=True))
    centred = vals - mean
    var = group_scalar(jnp.sum(centred * centred, axis=1, keepdims=True))
    rstd = lax.rsqrt(var + EPSILON)
    return mean, rstd


def norm_backward(dy_sum, dyx_sum, gain):
    return group_scalar(dy_sum * gain), group_scalar(dyx_sum * gain)


def for_groups(channels, body, together=2):
    def step(g, carry):
        for u in range(together):
            first = pl.multiple_of((g * together + u) * PER_GROUP, PER_GROUP)
            body(pl.ds(first, PER_GROUP))
        return carry

    lax.fori_loop(0, channels // PER_GROUP // together, step, 0)


def columns(values):
    lane = lax.broadcasted_iota(jnp.int32, (PER_GROUP, 128), 1)
    tile = jnp.zeros((PER_GROUP, 128), F32)
    for at, val in enumerate(values):
        tile = jnp.where(lane == at, val, tile)
    return tile


ROWS = SIDE // 2


def lanes(x, n):
    return x[:, 128 * n : 128 * n + 128]


def low_lanes(x):
    return lax.broadcasted_iota(jnp.int32, (x.shape[0], 128), 1) < SIDE


def fold(x):
    low = low_lanes(x)
    out = []
    for r in range(ROWS):
        upper, lower = lanes(x, r // 2), lanes(x, r // 2 + ROWS // 2)
        if r % 2 == 0:
            out.append(jnp.where(low, upper, pltpu.roll(lower, SIDE, 1)))
        else:
            out.append(jnp.where(low, pltpu.roll(upper, SIDE, 1), lower))
    return jnp.concatenate(out, 1)


def unfold(x):
    low = low_lanes(x)
    pairs = range(x.shape[1] // 256)
    top = [jnp.where(low, lanes(x, 2 * n), pltpu.roll(lanes(x, 2 * n + 1), SIDE, 1)) for n in pairs]
    bottom = [
        jnp.where(low, pltpu.roll(lanes(x, 2 * n), SIDE, 1), lanes(x, 2 * n + 1)) for n in pairs
    ]
    return jnp.concatenate(top, 1), jnp.concatenate(bottom, 1)


def fold_kernel(meta, own_ref, got_ref, out_ref, x_buf, sem):
    fetch(meta, own_ref, got_ref, x_buf, sem)
    arrive(own_ref, x_buf, sem)

    def body(rows):
        out_ref[rows, :] = fold(x_buf[rows, :].astype(F32)).astype(BF)

    for_groups(out_ref.shape[0], body)


def folded(meta, own, got):
    return pl.pallas_call(
        fold_kernel,
        out_shape=struct(own.shape, BF),
        in_specs=[scalars(), placed(), placed()],
        out_specs=whole(),
        scratch_shapes=[pltpu.VMEM(own.shape, BF), pltpu.SemaphoreType.DMA(())],
        compiler_params=params(),
        cost_estimate=cost(8 * own.size, 4 * own.size),
        name="fold",
    )(meta, own, got)


def act_one_kernel(meta, own_ref, got_ref, par_ref, act_ref, stat_ref, fold_ref, x_buf, sem):
    fetch(meta, own_ref, got_ref, x_buf, sem)
    arrive(own_ref, x_buf, sem)

    def body(rows):
        vals = fold(x_buf[rows, :].astype(F32))
        fold_ref[rows, :] = vals.astype(BF)
        mean, rstd = group_stats(vals)
        par = par_ref[rows, :]
        out = (vals - mean) * (rstd * par[:, 0:1]) + par[:, 1:2]
        act_ref[rows, :] = (out * jax.nn.sigmoid(out)).astype(BF)
        stat_ref[rows, :] = columns([mean, rstd])

    for_groups(act_ref.shape[0], body)


def first_activation(meta, own, got, par):
    ch = own.shape[0]
    return pl.pallas_call(
        act_one_kernel,
        out_shape=[struct((ch, HW), BF), struct((ch, 128), F32), struct((ch, HW), BF)],
        in_specs=[scalars(), placed(), placed(), whole()],
        out_specs=[whole()] * 3,
        scratch_shapes=[pltpu.VMEM((ch, HW), BF), pltpu.SemaphoreType.DMA(())],
        compiler_params=params(),
        cost_estimate=cost(20 * ch * HW, 6 * ch * HW, ch * HW),
        name="act_one",
    )(meta, own, got, par)


def fill_shifted(xs, pieces, first):
    start = first
    for x_ref in pieces:
        rows = x_ref.shape[0]

        def step(r, carry, x_ref=x_ref, start=start):
            off = pl.multiple_of(r * FILL, FILL)
            at = pl.ds(pl.multiple_of(start + off, FILL), FILL)
            lane = lax.broadcasted_iota(jnp.int32, (FILL, 128), 1)
            low = lane < SIDE
            left, right = lane % SIDE == 0, lane % SIDE == SIDE - 1
            zero = jnp.zeros((FILL, 128), F32)
            here = pl.ds(off, FILL)
            for n in range(ROWS):
                x = x_ref[here, 128 * n : 128 * n + 128].astype(F32)
                kinds = (
                    jnp.where(left, zero, pltpu.roll(x, 1, 1)),
                    x,
                    jnp.where(right, zero, pltpu.roll(x, 127, 1)),
                )
                for d, y in enumerate(kinds):
                    xs[d, at, PAD + 128 * n : PAD + 128 * n + 128] = y.astype(BF)
                    if n == ROWS - 1:
                        xs[d, at, :PAD] = jnp.where(low, zero, pltpu.roll(y, SIDE, 1)).astype(BF)
                    if n == 0:
                        xs[d, at, PAD + HW :] = jnp.where(
                            low, pltpu.roll(y, SIDE, 1), zero
                        ).astype(BF)
            return carry

        lax.fori_loop(0, rows // FILL, step, 0)
        start = xs.shape[1] - rows - start if len(pieces) == 2 else start + rows


def window(xs, tap, start, width):
    first = PAD + start + (tap // 3 - 1) * 128
    if not isinstance(start, int):
        first = pl.multiple_of(first, 128)
    return xs[tap % 3, :, pl.ds(first, width)]


def convolve(xs, w_ref, out_ref, add, width=1024):
    depth = xs.shape[1]

    def step(n, carry):
        p = n * width
        acc = dot(w_ref[:, :depth], window(xs, 0, p, width))
        for tap in range(1, 9):
            acc = acc + dot(w_ref[:, tap * depth : (tap + 1) * depth], window(xs, tap, p, width))
        at = pl.ds(pl.multiple_of(p, width), width)
        out_ref[:, at] = add(acc, at)
        return carry

    lax.fori_loop(0, HW // width, step, 0)


def conv_call(kernel, meta, weights, pieces, vmem_in, any_in, outs, any_outs, scratch, name):
    out_ch, depth = weights[0].shape[0], C
    arrays = (weights[0], *pieces, *vmem_in, *any_in)
    nbytes = sum(a.size * a.dtype.itemsize for a in arrays) + out_ch * HW * 4
    return pl.pallas_call(
        functools.partial(kernel, len(pieces)),
        out_shape=[*outs, *any_outs],
        in_specs=[scalars(), placed(), placed()]
        + [whole()] * (len(pieces) + len(vmem_in))
        + [placed()] * len(any_in),
        out_specs=[whole()] * len(outs) + [placed()] * len(any_outs),
        scratch_shapes=[
            pltpu.VMEM((3, depth, HW + 2 * PAD), BF),
            pltpu.VMEM((out_ch, 9 * depth), BF),
            pltpu.VMEM((out_ch, HW), F32),
            pltpu.SemaphoreType.DMA((4,)),
            *scratch,
        ],
        compiler_params=params(),
        cost_estimate=cost(2 * out_ch * 9 * depth * HW, nbytes, out_ch * HW),
        name=name,
    )(meta, *weights, *pieces, *vmem_in, *any_in)


def conv_one_kernel(n, meta, w_own, w_got, *refs):
    pieces, refs = refs[:n], refs[n:]
    par_ref, act_ref, stat_ref, conv_ref, w_ref, xs, w_buf, acc, sems = refs
    fetch(meta, w_own, w_got, w_buf, sems.at[0])
    fill_shifted(xs, pieces, meta[0])
    arrive(w_own, w_buf, sems.at[0])
    keep = pltpu.make_async_copy(w_buf, w_ref, sems.at[2])
    keep.start()
    bias = par_ref[:, 0:1]
    convolve(xs, w_buf, acc, lambda val, at: val + bias)
    store = pltpu.make_async_copy(acc, conv_ref, sems.at[1])
    store.start()

    def body(rows):
        vals = acc[rows, :]
        mean, rstd = group_stats(vals)
        par = par_ref[rows, :]
        gain, shift, factor = par[:, 1:2], par[:, 2:3], 1.0 + par[:, 3:4]
        mid = (vals - mean) * (rstd * gain * factor) + (shift * factor + par[:, 4:5])
        act_ref[rows, :] = (mid * jax.nn.sigmoid(mid)).astype(BF)
        stat_ref[rows, :] = columns([mean, rstd])

    for_groups(acc.shape[0], body)
    store.wait()
    keep.wait()


def conv_two_kernel(n, meta, w_own, w_got, *refs):
    pieces, refs = refs[:n], refs[n:]
    par_ref, f_ref, normed_ref, stat_ref, hidden_ref, w_ref, xs, w_buf, acc, sems = refs
    fetch(meta, w_own, w_got, w_buf, sems.at[0])
    fill_shifted(xs, pieces, meta[0])
    arrive(w_own, w_buf, sems.at[0])
    keep = pltpu.make_async_copy(w_buf, w_ref, sems.at[2])
    keep.start()
    bias = par_ref[:, 0:1]
    convolve(xs, w_buf, acc, lambda val, at: val + bias + f_ref[:, at].astype(F32))
    store = pltpu.make_async_copy(acc, hidden_ref, sems.at[1])
    store.start()

    def body(rows):
        vals = acc[rows, :]
        mean, rstd = group_stats(vals)
        par = par_ref[rows, :]
        normed_ref[rows, :] = ((vals - mean) * (rstd * par[:, 1:2]) + par[:, 2:3]).astype(BF)
        stat_ref[rows, :] = columns([mean, rstd])

    for_groups(acc.shape[0], body)
    store.wait()
    keep.wait()


def silu_slope(mid):
    sig = jax.nn.sigmoid(mid)
    return sig * (1.0 + mid * (1.0 - sig))


def conv_two_back_kernel(n, meta, w_own, w_got, *refs):
    pieces, refs = refs[:n], refs[n:]
    par_ref, stat_ref, conv_ref, grad_ref, sums_ref, xs, w_buf, acc, sems, conv_buf = refs
    fetch(meta, w_own, w_got, w_buf, sems.at[0])
    load = pltpu.make_async_copy(conv_ref, conv_buf, sems.at[1])
    load.start()
    fill_shifted(xs, pieces, meta[0])
    arrive(w_own, w_buf, sems.at[0])
    convolve(xs, w_buf, acc, lambda val, at: val)
    load.wait()

    def body(rows):
        par, stat = par_ref[rows, :], stat_ref[rows, :]
        gain, shift, factor = par[:, 1:2], par[:, 2:3], 1.0 + par[:, 3:4]
        rstd = stat[:, 1:2]
        hat = (conv_buf[rows, :] - stat[:, 0:1]) * rstd
        mid = hat * (gain * factor) + (shift * factor + par[:, 4:5])
        grad = acc[rows, :] * silu_slope(mid)
        total = jnp.sum(grad, axis=1, keepdims=True)
        total_hat = jnp.sum(grad * hat, axis=1, keepdims=True)
        mean_u, mean_uhat = norm_backward(total * factor, total_hat * factor, gain)
        out = ((grad * (factor * gain) - mean_u - hat * mean_uhat) * rstd).astype(BF)
        grad_ref[rows, :] = out
        bias_grad = jnp.sum(out.astype(F32), axis=1, keepdims=True)
        sums_ref[rows, :] = columns(
            [
                total_hat * factor,
                total * factor,
                total_hat * gain + total * shift,
                total,
                bias_grad,
            ]
        )

    for_groups(acc.shape[0], body)


def conv_one_back_kernel(n, meta, w_own, w_got, *refs):
    pieces, refs = refs[:n], refs[n:]
    par_ref, stat_ref, f_ref, hid_ref, grad_ref, sums_ref, xs, w_buf, acc, sems, hid_buf = refs
    fetch(meta, w_own, w_got, w_buf, sems.at[0])
    load = pltpu.make_async_copy(hid_ref, hid_buf, sems.at[1])
    load.start()
    fill_shifted(xs, pieces, meta[0])
    arrive(w_own, w_buf, sems.at[0])
    convolve(xs, w_buf, acc, lambda val, at: val)
    load.wait()

    def body(rows):
        par, stat = par_ref[rows, :], stat_ref[rows, :]
        gain, shift = par[:, 0:1], par[:, 1:2]
        rstd = stat[:, 1:2]
        hat = (f_ref[rows, :].astype(F32) - stat[:, 0:1]) * rstd
        grad = acc[rows, :] * silu_slope(hat * gain + shift)
        total = jnp.sum(grad, axis=1, keepdims=True)
        total_hat = jnp.sum(grad * hat, axis=1, keepdims=True)
        mean_u, mean_uhat = norm_backward(total, total_hat, gain)
        out = hid_buf[rows, :] + (grad * gain - mean_u - hat * mean_uhat) * rstd
        top, bottom = unfold(out)
        grad_ref[rows, : HW // 2] = top.astype(grad_ref.dtype)
        grad_ref[rows, HW // 2 :] = bottom.astype(grad_ref.dtype)
        sums_ref[rows, :] = columns([total_hat, total])

    for_groups(acc.shape[0], body)


def weight_grad_kernel(n, meta, grad_ref, *refs):
    pieces, (out_ref, gs) = refs[:n], refs[n:]
    fill_shifted(gs, (grad_ref,), 0)
    for tap in range(9):
        moved = window(gs, 8 - tap, 0, HW)
        first = meta[0]
        for x_ref in pieces:
            rows = x_ref.shape[0]
            at = pl.ds(pl.multiple_of(tap * C + first, rows), rows)
            out_ref[:, at] = dot_nt(moved, x_ref[...]).astype(BF)
            first = C - rows - first


def conv_weight_grad(meta, grad, pieces, name):
    out_ch = grad.shape[0]
    return pl.pallas_call(
        functools.partial(weight_grad_kernel, len(pieces)),
        out_shape=struct((out_ch, 9 * C), BF),
        in_specs=[scalars()] + [whole()] * (1 + len(pieces)),
        out_specs=whole(),
        scratch_shapes=[pltpu.VMEM((3, out_ch, HW + 2 * PAD), BF)],
        compiler_params=params(),
        cost_estimate=cost(2 * out_ch * 9 * C * HW, (out_ch + C) * HW * 2 + out_ch * 9 * C * 2),
        name=name,
    )(meta, grad, *pieces)


def turn_kernel(meta, own_ref, other_ref, out_ref):
    half = own_ref.shape[0]
    for tap in range(9):
        at = pl.ds(pl.multiple_of(tap * C + meta[0], half), half)
        row = meta[0]
        for ref in (own_ref, other_ref):
            to = pl.ds(pl.multiple_of((8 - tap) * C + row, half), half)
            out_ref[:, to] = ref[:, at].astype(F32).T.astype(BF)
            row = half - row


def turned_pair(meta, own, other):
    return pl.pallas_call(
        turn_kernel,
        out_shape=struct(own.shape, BF),
        in_specs=[scalars(), whole(), whole()],
        out_specs=whole(),
        compiler_params=params(),
        cost_estimate=cost(0, 3 * own.size * 2),
        name="turn",
    )(meta, own, other)


def norm_three_back_kernel(n, *refs):
    addends, (hidden_ref, stat_ref, par_ref, cot_ref, hid_ref, grad_ref, sums_ref) = (
        refs[:n],
        refs[n:],
    )

    def body(rows):
        dy = addends[0][rows, :].astype(F32)
        for extra in addends[1:]:
            dy = dy + extra[rows, :].astype(F32)
        par, stat = par_ref[rows, :], stat_ref[rows, :]
        gain, rstd = par[:, 1:2], stat[:, 1:2]
        hat = (hidden_ref[rows, :] - stat[:, 0:1]) * rstd
        total = jnp.sum(dy, axis=1, keepdims=True)
        total_hat = jnp.sum(dy * hat, axis=1, keepdims=True)
        mean_u, mean_uhat = norm_backward(total, total_hat, gain)
        top = cot_ref[rows, :].astype(F32)
        out = top + (dy * gain - mean_u - hat * mean_uhat) * rstd
        hid_ref[rows, :] = out
        low = out.astype(BF)
        grad_ref[rows, :] = low
        sums_ref[rows, :] = columns(
            [
                total_hat,
                total,
                jnp.sum(low.astype(F32), axis=1, keepdims=True),
                jnp.sum(top, axis=1, keepdims=True),
            ]
        )

    for_groups(hidden_ref.shape[0], body)


def norm_three_back(addends, hidden, stat, par, cot):
    ch = hidden.shape[0]
    rows = 32

    def part(a):
        return pl.BlockSpec((rows, a.shape[1]), lambda r: (r, 0))

    outs = [struct((ch, HW), F32), struct((ch, HW), BF), struct((ch, 128), F32)]
    ins = (*addends, hidden, stat, par, cot)
    return pl.pallas_call(
        functools.partial(norm_three_back_kernel, len(addends)),
        grid=(ch // rows,),
        out_shape=outs,
        in_specs=[part(a) for a in ins],
        out_specs=[part(a) for a in outs],
        compiler_params=params(),
        cost_estimate=cost(20 * ch * HW, 16 * ch * HW),
        name="norm_three_back",
    )(*ins)


def piece_columns(meta, w_ref, pieces):
    first = meta[0]
    acc = None
    for x_ref in pieces:
        rows = x_ref.shape[0]
        term = dot(w_ref[:, pl.ds(pl.multiple_of(first, rows), rows)], x_ref[...])
        acc = term if acc is None else acc + term
        first = w_ref.shape[1] - rows - first
    return acc


def inputs_kernel(n, meta, w_ref, *refs):
    pieces, (bias_ref, out_ref) = refs[:n], refs[n:]
    out_ref[...] = (piece_columns(meta, w_ref, pieces) + bias_ref[...]).astype(BF)


def inputs_product(meta, weight, pieces, bias, width=1024, name=None):
    rows, depth = weight.shape
    return pl.pallas_call(
        functools.partial(inputs_kernel, len(pieces)),
        grid=(HW // width,),
        out_shape=struct((rows, HW), BF),
        in_specs=[scalars(), pl.BlockSpec((rows, depth), lambda p: (0, 0))]
        + [pl.BlockSpec((x.shape[0], width), lambda p: (0, p)) for x in pieces]
        + [pl.BlockSpec((rows, 1), lambda p: (0, 0))],
        out_specs=pl.BlockSpec((rows, width), lambda p: (0, p)),
        compiler_params=params(),
        cost_estimate=cost(2 * rows * depth * HW, (rows + depth) * HW * 2),
        name=name,
    )(meta, weight, *pieces, bias)


def parts_kernel(n, meta, w_ref, *refs):
    pieces, outs = refs[:n], refs[n:]
    first = meta[0]
    for out_ref in outs:
        rows = out_ref.shape[0]
        row = pl.ds(pl.multiple_of(first, rows), rows)
        acc = None
        at = 0
        for x_ref in pieces:
            depth = x_ref.shape[0]
            term = dot(w_ref[row, at : at + depth], x_ref[...])
            acc = term if acc is None else acc + term
            at += depth
        out_ref[...] = acc.astype(BF)
        first = w_ref.shape[0] - rows - first


def parts_product(meta, weight, pieces, count, width=1024, name=None):
    rows, depth = weight.shape
    part = struct((rows // count, HW), BF)
    return pl.pallas_call(
        functools.partial(parts_kernel, len(pieces)),
        grid=(HW // width,),
        out_shape=[part] * count,
        in_specs=[scalars(), pl.BlockSpec((rows, depth), lambda p: (0, 0))]
        + [pl.BlockSpec((x.shape[0], width), lambda p: (0, p)) for x in pieces],
        out_specs=[pl.BlockSpec((rows // count, width), lambda p: (0, p))] * count,
        compiler_params=params(),
        cost_estimate=cost(2 * rows * depth * HW, (rows + depth) * HW * 2),
        name=name,
    )(meta, weight, *pieces)


def output_kernel(n, meta, w_ref, *refs):
    pieces, (bias_ref, hidden_ref, out_ref) = refs[:n], refs[n:]
    acc = hidden_ref[...] + bias_ref[...] + piece_columns(meta, w_ref, pieces)
    half = acc.shape[1] // 2
    for base, val in zip((0, HW // 2), unfold(acc)):
        first = pl.multiple_of(base + pl.program_id(0) * half, half)
        out_ref[:, pl.ds(first, half)] = val.astype(BF)


def output_product(meta, weight, pieces, bias, hidden, width=1024):
    rows, depth = weight.shape
    return pl.pallas_call(
        functools.partial(output_kernel, len(pieces)),
        grid=(HW // width,),
        out_shape=struct((rows, HW), BF),
        in_specs=[scalars(), pl.BlockSpec((rows, depth), lambda p: (0, 0))]
        + [pl.BlockSpec((x.shape[0], width), lambda p: (0, p)) for x in pieces]
        + [
            pl.BlockSpec((rows, 1), lambda p: (0, 0)),
            pl.BlockSpec((rows, width), lambda p: (0, p)),
        ],
        out_specs=pl.BlockSpec((rows, HW), lambda p: (0, 0)),
        compiler_params=params(),
        cost_estimate=cost(2 * rows * depth * HW, (rows * 3 + depth) * HW * 2),
        name="output",
    )(meta, weight, *pieces, bias, hidden)


def outer_kernel(n_left, n_right, meta, *refs):
    lefts, rights = refs[:n_left], refs[n_left : n_left + n_right]
    out_ref, sums_ref = refs[n_left + n_right : n_left + n_right + 2]
    acc_ref, tot_ref = refs[n_left + n_right + 2 :]
    step = pl.program_id(0)

    @pl.when(step == 0)
    def _():
        acc_ref[...] = jnp.zeros_like(acc_ref)
        tot_ref[...] = jnp.zeros_like(tot_ref)

    row = 0
    for left in lefts:
        rows = left.shape[0]
        val = left[...]
        first = meta[0]
        for right in rights:
            cols = right.shape[0]
            at = pl.ds(pl.multiple_of(first, cols), cols)
            acc_ref[row : row + rows, at] += dot_nt(val, right[...])
            first = acc_ref.shape[1] - cols - first
        tot_ref[row : row + rows, :] += jnp.sum(val.astype(F32), axis=1, keepdims=True)
        row += rows

    @pl.when(step == pl.num_programs(0) - 1)
    def _():
        out_ref[...] = acc_ref[...].astype(BF)
        sums_ref[...] = tot_ref[...]


def outer(meta, lefts, rights, width=1024, name=None):
    rows, cols = sum(a.shape[0] for a in lefts), sum(a.shape[0] for a in rights)
    fixed = lambda p: (0, 0)
    return pl.pallas_call(
        functools.partial(outer_kernel, len(lefts), len(rights)),
        grid=(HW // width,),
        out_shape=[struct((rows, cols), BF), struct((rows, 128), F32)],
        in_specs=[scalars()]
        + [pl.BlockSpec((a.shape[0], width), lambda p: (0, p)) for a in (*lefts, *rights)],
        out_specs=[pl.BlockSpec((rows, cols), fixed), pl.BlockSpec((rows, 128), fixed)],
        scratch_shapes=[pltpu.VMEM((rows, cols), F32), pltpu.VMEM((rows, 128), F32)],
        compiler_params=params(),
        cost_estimate=cost(2 * rows * cols * HW, (rows + cols) * HW * 2),
        name=name,
    )(meta, *lefts, *rights)


def attention_kernel(
    n_grads, lim_ref, q_ref, k_ref, v_ref, kc_ref, vc_ref, *refs, unroll, back,
):
    g_refs, refs = refs[:n_grads], refs[n_grads:]
    o_ref, dq_ref, dk_ref, dv_ref, dkc_ref, dvc_ref = refs[:6]
    kt, vt, kn, vn, s_even, s_odd, p_sc, tops, o_acc, dk_acc, dv_acc = refs[6:]
    step, last = pl.program_id(1), pl.num_programs(1) - 1
    width = q_ref.shape[-1]
    blocks = KEYS // BLOCK

    @pl.when(step == 0)
    def _():
        spare = jnp.zeros((HEAD_DIM, KEYS - HW - CTXP), BF)
        for ref, own, ctx in ((kn, k_ref, kc_ref), (vn, v_ref, vc_ref)):
            ref[:, :HW] = own[0, 0]
            ref[:, HW : HW + CTXP] = ctx[0, 0]
            ref[:, HW + CTXP :] = spare
        row = lax.broadcasted_iota(jnp.int32, (HEAD_DIM, BLOCK), 0)
        for n in range(blocks):
            at = slice(n * BLOCK, (n + 1) * BLOCK)
            key = lax.broadcasted_iota(jnp.int32, (HEAD_DIM, BLOCK), 1) + n * BLOCK
            fill = jnp.where((row == 0) & (key >= HW + lim_ref[0]), NEG_FILL, 0.0)
            kt[at, :] = jnp.concatenate([kn[:, at].astype(F32), fill], 0).T.astype(BF)
            vt[at, :] = jnp.concatenate([vn[:, at].astype(F32), jnp.zeros_like(fill)], 0).T.astype(BF)
        dk_acc[...] = jnp.zeros_like(dk_acc)
        dv_acc[...] = jnp.zeros_like(dv_acc)

    def keys_at(n):
        return pl.ds(pl.multiple_of(n * BLOCK, BLOCK), BLOCK)

    scale = HEAD_DIM ** (-0.5)
    q = (q_ref[0, 0].astype(F32) * scale).astype(BF)
    one = jnp.where(lax.broadcasted_iota(jnp.int32, (HEAD_DIM, width), 0) == 0, 1.0, 0.0).astype(BF)
    q_more = jnp.concatenate([q, one], 0)

    def score(n, held):
        scores = dot(kt[keys_at(n), :], q_more)
        held[...] = scores
        return jnp.max(jnp.max(scores.reshape(BLOCK // 8, 8, width), axis=0), axis=0, keepdims=True)

    o_acc[...] = jnp.zeros_like(o_acc)

    def forward(n, held, top, total, shrink):
        raised = jnp.exp(held[...] - top)
        low = raised.astype(BF)
        p_sc[keys_at(n), :] = low
        tops[n, 0:1, :] = top
        sums = jnp.sum(raised.reshape(BLOCK // 8, 8, width), axis=0)
        o_acc[...] = o_acc[...] * shrink + dot(vn[:, keys_at(n)], low)
        return total * shrink + sums

    def forward_step(n, held, ahead_held, carry):
        top, total, shrink = carry
        ahead = jnp.maximum(top, score(n + 1, ahead_held))
        total = forward(n, held, top, total, shrink)
        return ahead, total, jnp.exp(top - ahead)

    held = (s_even, s_odd)

    def forward_run(j, carry):
        for u in range(unroll):
            carry = forward_step(unroll * j + u, held[u % 2], held[1 - u % 2], carry)
        return carry

    carry = (score(0, s_even), jnp.zeros((8, width), F32), jnp.ones((1, width), F32))
    carry = lax.fori_loop(0, blocks // unroll - 1, forward_run, carry)
    for n in range(blocks - unroll, blocks - 1):
        carry = forward_step(n, held[n % 2], held[1 - n % 2], carry)
    top, total, shrink = carry
    total = forward(blocks - 1, s_odd, top, total, shrink)

    inverse = 1.0 / jnp.sum(total, axis=0, keepdims=True)
    mixed = o_acc[...] * inverse
    o_ref[0] = mixed.astype(BF)
    grad = sum(g_ref[0].astype(F32) for g_ref in g_refs)
    if n_grads > 1:
        grad = grad.astype(BF).astype(F32)
    delta = jnp.sum(grad * mixed, axis=0, keepdims=True)
    dq = jnp.zeros((HEAD_DIM, width), F32)
    none = jnp.zeros((HEAD_DIM, width), BF)
    for c in range(0, KEYS, back):
        at = slice(c, c + back)
        slopes = []
        for n in range(c // BLOCK, (c + back) // BLOCK):
            sub = slice(n * BLOCK, (n + 1) * BLOCK)
            factor = inverse * jnp.exp(tops[n, 0:1, :] - top)
            grad_low = (grad * factor).astype(BF)
            both = jnp.concatenate([grad_low, none], 0)
            probs = p_sc[sub, :]
            slope = (dot(vt[sub, :], both) - delta * factor).astype(BF) * probs
            slopes.append(slope)
            dv_acc[:, sub] += dot_nt(grad_low, probs)
        slope = jnp.concatenate(slopes, 0)
        dq = dq + dot(kn[:, at], slope)
        dk_acc[:, at] += dot_nt(q, slope)
    dq_ref[0] = (dq * scale).astype(BF)

    @pl.when(step == last)
    def _():
        dk_ref[0] = dk_acc[:, :HW].astype(BF)
        dv_ref[0] = dv_acc[:, :HW].astype(BF)
        dkc_ref[0] = dk_acc[:, HW : HW + CTXP].astype(BF)
        dvc_ref[0] = dv_acc[:, HW : HW + CTXP].astype(BF)


def attention(limit, qkv, ctx_kv, grads, width=1024, unroll=6, back=256):
    heads = qkv.shape[1]
    keys = KEYS

    def part(t, w, moving):
        return pl.BlockSpec(
            (1, 1, HEAD_DIM, w), (lambda h, i: (t, h, 0, i)) if moving else (lambda h, i: (t, h, 0, 0))
        )

    def row(w, moving):
        return pl.BlockSpec(
            (1, HEAD_DIM, w), (lambda h, i: (h, 0, i)) if moving else (lambda h, i: (h, 0, 0))
        )

    big, small = struct((heads, HEAD_DIM, HW), BF), struct((heads, HEAD_DIM, CTXP), BF)
    return pl.pallas_call(
        functools.partial(attention_kernel, len(grads), unroll=unroll, back=back),
        grid=(heads, HW // width),
        in_specs=[
            pl.BlockSpec(memory_space=pltpu.SMEM),
            part(0, width, True),
            part(1, HW, False),
            part(2, HW, False),
            part(0, CTXP, False),
            part(1, CTXP, False),
        ]
        + [row(width, True)] * len(grads),
        out_specs=[
            row(width, True),
            row(width, True),
            row(HW, False),
            row(HW, False),
            row(CTXP, False),
            row(CTXP, False),
        ],
        out_shape=[big, big, big, big, small, small],
        scratch_shapes=[
            pltpu.VMEM((keys, 2 * HEAD_DIM), BF),
            pltpu.VMEM((keys, 2 * HEAD_DIM), BF),
            pltpu.VMEM((HEAD_DIM, keys), BF),
            pltpu.VMEM((HEAD_DIM, keys), BF),
            pltpu.VMEM((BLOCK, width), F32),
            pltpu.VMEM((BLOCK, width), F32),
            pltpu.VMEM((keys, width), BF),
            pltpu.VMEM((keys // BLOCK, 8, width), F32),
            pltpu.VMEM((HEAD_DIM, width), F32),
            pltpu.VMEM((HEAD_DIM, keys), F32),
            pltpu.VMEM((HEAD_DIM, keys), F32),
        ],
        compiler_params=params(dimension_semantics=("arbitrary", "arbitrary")),
        cost_estimate=cost(
            24 * heads * HW * keys * HEAD_DIM, heads * HEAD_DIM * 8 * HW * 2, heads * HW * keys
        ),
        name="attention",
    )(limit, qkv, qkv, qkv, ctx_kv, ctx_kv, *grads)


class Alone:
    parts = 1

    def __init__(self, mesh):
        self.images = mesh.shape["dp"]

    def meta(self):
        return jnp.array([0, 1], jnp.int32)

    def image(self):
        return lax.axis_index("dp")

    def got(self, x):
        return x

    def pick(self, own, got):
        return own

    def gather(self, x):
        return (lax.all_gather(x, "tensor", axis=0, tiled=True),)

    def scatter(self, parts):
        return (lax.psum_scatter(parts[0], "tensor", scatter_dimension=0, tiled=True),)

    def turn(self, meta, w):
        ch = w.shape[0]
        cut = w.reshape(ch, 9, C)
        turned = lax.all_to_all(cut, "tensor", split_axis=2, concat_axis=0, tiled=True)
        return turned[:, ::-1].transpose(2, 1, 0).reshape(ch, 9 * C)

    def total(self, x):
        return lax.psum(x, "dp")

    def everywhere(self, x):
        return lax.psum(x, "dp")

    def sum_owned(self, x, late):
        return lax.psum(x, "dp")


class Paired:
    parts = 2

    def __init__(self, mesh):
        dp = mesh.shape["dp"]
        self.images = dp
        self.far = [
            ((2 * k + core) * 2 + 1 - core, (2 * k + 1 - core) * 2 + core)
            for k in range(dp // 2)
            for core in range(2)
        ]
        self.bits = [1 << b for b in range((dp - 1).bit_length())]

    def half(self):
        return lax.axis_index("dp") % 2

    def stays(self):
        return self.half() == lax.axis_index("tensor")

    def meta(self):
        return jnp.stack([self.half() * (C // 2), self.stays().astype(jnp.int32)]).astype(jnp.int32)

    def image(self):
        return lax.axis_index("dp") // 2 * 2 + lax.axis_index("tensor")

    def got(self, x):
        return lax.ppermute(x, ("dp", "tensor"), self.far)

    def pick(self, own, got):
        return jnp.where(self.stays(), own, got)

    def over(self, x, bit):
        return lax.ppermute(x, "dp", [(i, i ^ bit) for i in range(self.images)])

    def gather(self, x):
        return (x, self.over(x, 1))

    def scatter(self, parts):
        return (parts[0], self.over(parts[1], 1))

    def turn(self, meta, w):
        return turned_pair(meta, w, self.over(w, 1))

    def total(self, x):
        x = x + lax.ppermute(x, "tensor", [(0, 1), (1, 0)])
        for bit in self.bits[1:]:
            x = x + self.over(x, bit)
        return self.pick(x, self.over(x, 1))

    def everywhere(self, x):
        for bit in self.bits:
            x = x + self.over(x, bit)
        return x

    def sum_owned(self, x, late):
        rows = x.shape[0] // 2
        order = (self.bits, [self.bits[0], *self.bits[2:], self.bits[1]])
        parts = [lax.slice_in_dim(x, at * rows, (at + 1) * rows) for at in range(2)]

        def upper(bit):
            return (lax.axis_index("dp") // bit) % 2

        for step in range(len(self.bits)):
            size = parts[0].shape[0] // 2
            for at in range(2):
                bit = order[at][step]
                keep = lax.dynamic_slice_in_dim(parts[at], upper(bit) * size, size)
                send = lax.dynamic_slice_in_dim(parts[at], (1 - upper(bit)) * size, size)
                parts[at] = (keep.astype(F32) + self.over(send, bit).astype(F32)).astype(BF)
        parts = list(after(late, *parts))
        for step in reversed(range(len(self.bits))):
            for at in range(2):
                bit = order[at][step]
                other = self.over(parts[at], bit)
                parts[at] = jnp.where(
                    upper(bit) == 0,
                    jnp.concatenate([parts[at], other]),
                    jnp.concatenate([other, parts[at]]),
                )
        return jnp.concatenate(parts)


def after(first, *later):
    held = lax.optimization_barrier((first, *later))
    return held[1:] if len(later) > 1 else held[1]


def local(plan, features, cotangent, embedding, context, lengths, norm1_gain, norm1_bias,
    conv1_weight, conv1_bias, emb_weight, emb_bias, norm2_gain, norm2_bias, conv2_weight,
    conv2_bias, norm3_gain, norm3_bias, qkv_weight, qkv_bias, context_weight, context_bias,
    out_weight, out_bias,
):
    ch, images, pixels = features.shape
    heads = ch // HEAD_DIM
    meta = plan.meta()
    moved = plan.parts == 2

    emb_act = jax.nn.silu(embedding.astype(F32)).astype(BF)
    scale_shift = (
        jnp.einsum("ie,teo->to", emb_act, emb_weight, preferred_element_type=F32) + emb_bias
    )
    length_row = jnp.broadcast_to(lengths.astype(F32)[:, None], (1, ch))
    vectors = jnp.concatenate(
        [
            jnp.stack([norm1_gain, norm1_bias, conv1_bias, norm2_gain, norm2_bias]),
            scale_shift,
            jnp.stack([conv2_bias, norm3_gain, norm3_bias, out_bias]),
            qkv_bias,
            length_row,
        ]
    )
    f_own = features.reshape(ch, pixels)
    f_got = plan.got(f_own)
    vectors, w1_own = after(scale_shift, vectors, conv1_weight)
    vectors = plan.pick(vectors, plan.got(vectors))
    w1_got = plan.got(w1_own)
    ctx_kv = (
        jnp.einsum("toe,ne->ton", context_weight, context[0], preferred_element_type=F32)
        + context_bias[:, :, None]
    ).astype(BF)
    ctx_kv = jnp.pad(ctx_kv, ((0, 0), (0, 0), (0, CTXP - CTX)))
    emb_all = jnp.where(
        jnp.arange(plan.images)[:, None] == lax.axis_index("dp"), emb_act, jnp.zeros_like(emb_act)
    )
    emb_all = plan.everywhere(emb_all)
    length = vectors[14, :1].astype(jnp.int32)
    par_one, par_two, par_three = vectors[0:2].T, vectors[2:7].T, vectors[7:10].T
    bias_qkv, bias_out = vectors[11:14].reshape(3 * ch, 1), vectors[10].reshape(ch, 1)
    par_one = after(emb_all, par_one)
    w2_got = plan.got(after(vectors, conv2_weight))
    act_one, stat_one, f_low = first_activation(meta, f_own, f_got, par_one)
    full_one = plan.gather(act_one)
    mats_own = jnp.concatenate([qkv_weight.reshape(3 * ch, C), out_weight])
    mats_own, ctx_own, cot_own = after(
        act_one, mats_own, ctx_kv, cotangent.reshape(ch, pixels)
    )
    mats_got, ctx_got = plan.got(mats_own), plan.got(ctx_own)
    cot_got = plan.got(cot_own)

    par_two, par_three, bias_qkv, bias_out = after(act_one, par_two, par_three, bias_qkv, bias_out)
    par_two = after((par_three, bias_qkv, bias_out), par_two)
    low, stat, wide = struct((ch, HW), BF), struct((ch, 128), F32), struct((ch, HW), F32)
    weight = struct((ch, 9 * C), BF)
    act_two, stat_two, conv_one, w1 = conv_call(
        conv_one_kernel, meta, (conv1_weight, w1_got), full_one, (par_two,), (),
        [low, stat], [wide, weight], [], "conv_one",
    )
    full_two = plan.gather(act_two)
    normed, stat_three, hidden, w2 = conv_call(
        conv_two_kernel, meta, (conv2_weight, w2_got), full_two, (par_three, f_low), (),
        [low, stat], [wide, weight], [], "conv_two",
    )
    full_three = plan.gather(normed)
    mats_got, ctx_got, cot_got = after(normed, mats_got, ctx_got, cot_got)
    mats = plan.pick(mats_own, mats_got)
    w_qkv, w_out = mats[: 3 * ch], mats[3 * ch :]
    cot = folded(meta, cot_own, cot_got)
    grad_heads = plan.scatter(
        parts_product(meta, w_out.T, (cot,), plan.parts, name="grad_heads")
    )
    qkv = inputs_product(meta, w_qkv, full_three, bias_qkv, name="qkv")
    ctx_kv = plan.pick(ctx_own, ctx_got)
    mixed, dq, dk, dv, dkc, dvc = attention(
        4 + length,
        qkv.reshape(3, heads, HEAD_DIM, HW),
        ctx_kv.reshape(2, heads, HEAD_DIM, CTXP),
        [a.reshape(heads, HEAD_DIM, HW) for a in grad_heads],
    )

    flat = lambda a: a.reshape(ch, HW)
    dq, dk, dv = flat(dq), flat(dk), flat(dv)
    addends = plan.scatter(
        parts_product(meta, w_qkv.T, (dq, dk, dv), plan.parts, name="grad_normed")
    )
    full_heads = plan.gather(flat(mixed))
    ctx_own = jnp.concatenate([a.reshape(1, ch, CTXP) for a in (dkc, dvc)])
    ctx_got = plan.got(ctx_own)
    turned_two = plan.turn(meta, after(mixed, w2))
    turned_one = plan.turn(meta, after(mixed, w1))
    dw_qkv, db_qkv = outer(meta, (dq, dk, dv), full_three, name="qkv_grad")
    dw_out, _ = outer(meta, (cot,), full_heads, name="out_grad")
    mats_own = jnp.concatenate([dw_qkv, dw_out])
    mats_got = plan.got(mats_own)
    grad_hidden, grad_two, sums_three = norm_three_back(addends, hidden, stat_three, par_three, cot)
    full_grad_two = plan.gather(grad_two)
    dw_two = conv_weight_grad(meta, grad_two, full_two, "conv_two_weight_grad")
    two_got = plan.got(dw_two)
    full_grad_two = after((dw_two, turned_one), *full_grad_two) if moved else full_grad_two
    grad_one, sums_two = conv_call(
        conv_two_back_kernel, meta, (turned_two, turned_two), full_grad_two, (par_two, stat_two),
        (conv_one,), [low, stat], [], [pltpu.VMEM((ch, HW), F32)], "conv_two_back",
    )
    full_grad_one = plan.gather(grad_one)
    mats_got, ctx_got, two_got = after(grad_one, mats_got, ctx_got, two_got)
    ctx_grad = plan.pick(ctx_own, ctx_got)[:, :, :CTX]
    dw_ctx = jnp.einsum("ton,ne->toe", ctx_grad, context[0], preferred_element_type=F32).astype(BF)
    mats = plan.pick(mats_own, mats_got)
    dw_two = plan.pick(dw_two, two_got)
    early = jnp.concatenate(
        [dw_ctx[0], dw_ctx[1], *(mats[t * ch : (t + 1) * ch] for t in range(4)), dw_two], 1
    )
    held = after(early, grad_one)
    early = lax.psum_scatter(early, "dp", scatter_dimension=0, tiled=True)
    dw_one = conv_weight_grad(meta, held, full_one, "conv_one_weight_grad")
    one_got = plan.got(dw_one)
    full_grad_one = after(dw_one, *full_grad_one) if moved else full_grad_one
    input_grad, sums_one = conv_call(
        conv_one_back_kernel, meta, (turned_one, turned_one), full_grad_one,
        (par_one, stat_one, f_low), (grad_hidden,),
        [struct((ch, HW), BF if moved else F32), stat], [],
        [pltpu.VMEM((ch, HW), F32)], "conv_one_back",
    )
    input_got = plan.got(input_grad)

    output = output_product(
        meta, w_out, full_heads, bias_out, after((input_grad, one_got), hidden)
    )
    output_got = plan.got(output)
    ctx_sums = jnp.sum(ctx_own.astype(F32), axis=2)
    sums_two = sums_two[:, :5].T
    own_mod = sums_two[2:4].astype(BF).astype(F32)
    mods = jnp.where(
        (jnp.arange(plan.images) == plan.image())[:, None, None], own_mod, jnp.zeros_like(own_mod)
    ).reshape(2 * plan.images, ch)
    small = plan.total(
        jnp.concatenate(
            [
                sums_three[:, :4].T,
                db_qkv[:, 0].reshape(3, ch),
                sums_two[:2],
                sums_two[4:5],
                ctx_sums,
                sums_one[:, :2].T,
                mods,
            ]
        )
    )
    early, dw_one, one_got = after((output, small), early, dw_one, one_got)
    early = lax.all_gather(early, "dp", axis=0, tiled=True)
    dw_one = plan.sum_owned(plan.pick(dw_one, one_got), (input_got, output_got))
    mods = small[14:].reshape(plan.images, 2, ch)
    mods_low = mods.astype(BF)
    dw_emb = jnp.stack(
        [
            jnp.einsum("ie,io->eo", emb_all, mods_low[:, t], preferred_element_type=F32)
            for t in range(2)
        ]
    )
    input_grad = plan.pick(input_grad, input_got).astype(F32)
    output = plan.pick(output, output_got)
    early = after((dw_one, small, input_grad, output), early)
    dw_ctx = jnp.stack([early[:, n * CTX_EMB : (n + 1) * CTX_EMB] for n in range(2)])
    first = 2 * CTX_EMB
    mats = [early[:, first + n * C : first + (n + 1) * C].astype(F32) for n in range(4)]
    dw_two = early[:, first + 4 * C :]

    return (
        output.reshape(ch, images, pixels),
        input_grad.reshape(ch, images, pixels),
        small[12],
        small[13],
        dw_one.astype(F32),
        small[9],
        dw_emb,
        jnp.sum(mods, axis=0),
        small[7],
        small[8],
        dw_two.astype(F32),
        small[2],
        small[0],
        small[1],
        jnp.stack(mats[:3]),
        small[4:7],
        dw_ctx.astype(F32),
        small[10:12],
        mats[3],
        small[3],
    )


def solution(mesh):
    paired = mesh.shape["tensor"] == 2 and mesh.shape["dp"] % 2 == 0
    plan = Paired(mesh) if paired else Alone(mesh)
    specs = (
        P("tensor", "dp", None),
        P("tensor", "dp", None),
        P("dp", None),
        P("dp", None, None),
        P("dp"),
        P("tensor"),
        P("tensor"),
        P("tensor", None),
        P("tensor"),
        P(None, None, "tensor"),
        P(None, "tensor"),
        P("tensor"),
        P("tensor"),
        P("tensor", None),
        P("tensor"),
        P("tensor"),
        P("tensor"),
        P(None, "tensor", None),
        P(None, "tensor"),
        P(None, "tensor", None),
        P(None, "tensor"),
        P("tensor", None),
        P("tensor"),
    )
    return jax.shard_map(
        functools.partial(local, plan),
        mesh=mesh,
        in_specs=specs,
        out_specs=(
            P("tensor", "dp", None),
            P("tensor", "dp", None),
            P("tensor"),
            P("tensor"),
            P("tensor", None),
            P("tensor"),
            P(None, None, "tensor"),
            P(None, "tensor"),
            P("tensor"),
            P("tensor"),
            P("tensor", None),
            P("tensor"),
            P("tensor"),
            P("tensor"),
            P(None, "tensor", None),
            P(None, "tensor"),
            P(None, "tensor", None),
            P(None, "tensor"),
            P("tensor", None),
            P("tensor"),
        ),
        check_vma=False,
    )
```
